32 devices in a mesh: prow: 4 (over y, x), pcol: 8 (over z, core).
Axes of the slice: x: 2, y: 2, z: 4, core: 2. Of those that a mesh axis runs over, the one named last changes fastest.
Arguments:
- matrix: float32 [4, 1024, 8, 1536], P('prow', None, 'pcol')
- pivots: int32 [256], replicated, may hold values from 256 to 4095, as said below
Outputs:
- factored: float32 [4, 1024, 8, 1536], P('prow', None, 'pcol')
The draws below stay inside these ranges and needn't reach their ends.
Inputs may be any that keep to these rules, and one draw needn't show every extreme that they name: The 256 pivots are distinct global row indices; the values 256 and 4095 both occur.
All inputs are finite; a program needn't handle non-finite values.
Results may differ from the reference program's by a relative error of at most 0.000082.
Values sent between devices are 32-bit elements; how exact they have to be, the bound alone decides.
No kernel may reach another device: no remote copies, remote signals or barrier semaphores. Data moves between devices by JAX's collectives and lax.ppermute only.
A program may use at most 128 MiB of HBM per device.

```python
import math
import jax
import jax.numpy as jnp
from jax import lax

NB = 256
RB = 4
CB = 6
LR = 1024
LC = 1536
ROWS = 4096
COLS = 12288
N_PROW = 4
N_PCOL = 8


def pivot_draw(key):
    sub_key = jax.random.fold_in(key, 11)
    shuffled = jax.random.permutation(sub_key, ROWS - NB - 2).astype(jnp.int32) + NB + 1
    ends = jnp.array([NB, ROWS - 1], dtype=jnp.int32)
    picked = jnp.concatenate([ends, shuffled[:NB - 2]])
    offset = jax.random.randint(jax.random.fold_in(sub_key, 3), (), 0, NB)
    return jnp.roll(picked, offset)


def draw_pivots(key, part):
    return pivot_draw(key)


def draw_matrix(key, part):
    pivots = pivot_draw(key)
    entry_key = jax.random.fold_in(key, 29)
    entries = jnp.clip(jax.random.normal(entry_key, (ROWS, COLS), jnp.float32), -6.0, 6.0)
    boosts = jax.random.uniform(jax.random.fold_in(key, 41), (NB,), jnp.float32, 0.75, 1.5) * math.sqrt(NB) + 2.0
    entries = entries.at[pivots, jnp.arange(NB)].add(boosts)
    grid = entries.reshape(RB, N_PROW, NB, CB, N_PCOL, NB)
    return grid.transpose(1, 0, 2, 4, 3, 5).reshape(N_PROW, LR, N_PCOL, LC)


def setup_inputs(seed: int = 0) -> dict:
    key_of = jax.random.split(jax.random.key(seed), 3)
    return {
        "matrix": draw_matrix(jax.random.fold_in(key_of[2], 71), 0),
        "pivots": draw_pivots(jax.random.fold_in(key_of[2], 71), 0),
    }


def eliminate(square):
    extent = square.shape[0]
    positions = jnp.arange(extent)

    def column_step(column, working):
        is_below = positions > column
        pivot_line = jnp.where(is_below, working[column, :], 0.0)
        factor_col = jnp.where(is_below, working[:, column] / working[column, column], 0.0)
        working = working - factor_col[:, None] * pivot_line[None, :]
        return jnp.where(is_below[:, None] & (positions == column)[None, :], factor_col[:, None], working)
    return lax.fori_loop(0, extent, column_step, square)

def to_global(stored):
    grid = stored.reshape(N_PROW, RB, NB, N_PCOL, CB, NB)
    return grid.transpose(1, 0, 2, 4, 3, 5).reshape(ROWS, COLS)

def to_storage(full_matrix):
    grid = full_matrix.reshape(RB, N_PROW, NB, CB, N_PCOL, NB)
    return grid.transpose(1, 0, 2, 4, 3, 5).reshape(N_PROW, LR, N_PCOL, LC)

def reference(matrix, pivots):
    full_matrix = to_global(matrix)
    leading = full_matrix[:NB]
    chosen = full_matrix[pivots]
    full_matrix = full_matrix.at[:NB].set(chosen).at[pivots].set(leading)
    packed = eliminate(full_matrix[:NB, :NB])
    upper_tri = jnp.triu(packed)
    lower_tri = jnp.tril(packed, -1) + jnp.eye(NB, dtype=jnp.float32)
    lower_left = jax.scipy.linalg.solve_triangular(upper_tri, full_matrix[NB:, :NB].T, trans=1, lower=False).T
    upper_right = jax.scipy.linalg.solve_triangular(lower_tri, full_matrix[:NB, NB:], lower=True, unit_diagonal=True)
    trailing = full_matrix[NB:, NB:] - jnp.dot(lower_left, upper_right, precision=lax.Precision.HIGHEST)
    top_part = jnp.concatenate([packed, upper_right], axis=1)
    bottom_part = jnp.concatenate([lower_left, trailing], axis=1)
    return to_storage(jnp.concatenate([top_part, bottom_part], axis=0))
```

```python
import functools

import jax
import jax.numpy as jnp
from jax import lax
from jax.experimental import pallas as pl
from jax.experimental.pallas import tpu as pltpu
from jax.sharding import PartitionSpec as P

LANES = 128
SUB = 8
HI = lax.Precision.HIGHEST


def pick_lane(tile, lane):
    return jnp.take_along_axis(tile, jnp.full((SUB, LANES), lane, jnp.int32), axis=1)


def row_of(tile, j):
    return jnp.broadcast_to(tile[j:j + 1, :], (SUB, LANES))


def factor_kernel(width, s_ref, packed_ref, linv_ref, uinv_ref, a_ref, m_ref, v_ref):
    groups = a_ref.shape[0]
    tiles = groups * SUB // LANES
    per_tile = LANES // SUB
    per_block = width // SUB
    sub = lax.broadcasted_iota(jnp.int32, (SUB, LANES), 0)
    lane = lax.broadcasted_iota(jnp.int32, (SUB, LANES), 1)

    for i in range(groups):
        a_ref[i] = s_ref[i * SUB:(i + 1) * SUB, :]
        diag = lane - (i % per_tile) * SUB == sub
        for t in range(tiles):
            block = jnp.where(diag, 1.0, 0.0) if i // per_tile == t else jnp.zeros((SUB, LANES), jnp.float32)
            m_ref[i, :, t * LANES:(t + 1) * LANES] = block
            if t > i // per_tile:
                linv_ref[i * SUB:(i + 1) * SUB, t * LANES:(t + 1) * LANES] = block

    def span(t):
        return slice(t * LANES, (t + 1) * LANES)

    for o in range(groups // per_block):
        base = o * per_block
        h = base // per_tile
        live = [(a_ref, t) for t in range(h + 1, tiles)] + [(m_ref, t) for t in range(h + 1)]

        def panel(i, c, base=base, h=h, live=live):
            b = base + i
            g = (b - h * per_tile) * SUB
            rows = pl.ds(pl.multiple_of(b * SUB, SUB), SUB)
            own = a_ref[b, :, span(h)]
            cols = [pick_lane(own, g + j) for j in range(SUB)]
            in_panel = (lane >= g) & (lane < g + SUB)
            after = lane >= g + SUB
            head = jnp.where(in_panel, jnp.where(lane - g == sub, -1.0, 0.0), jnp.where(after, own, 0.0))
            rest = [ref[b, :, span(t)] for ref, t in live]
            packed = own
            final = [head] + rest
            for j in range(SUB):
                at = sub == j
                coef = cols[j]
                r = 1.0 / row_of(coef, j)
                final = [jnp.where(at, x, y) for x, y in zip([head] + rest, final)]
                packed = jnp.where((lane == g + j) & (sub > j), coef * r, packed)
                for k in range(j, SUB):
                    packed = jnp.where((lane == g + k) & at, cols[k], packed)
                head_coef = jnp.where((sub < j) | after, coef, 0.0)
                v = row_of(head, j) * r
                head = jnp.where(at, v, head - head_coef * v)
                for n, x in enumerate(rest):
                    v = row_of(x, j) * r
                    rest[n] = jnp.where(at, v, x - coef * v)
                for k in range(j + 1, SUB):
                    v = row_of(cols[k], j) * r
                    cols[k] = jnp.where(at, v, cols[k] - coef * v)
            for t in range(h):
                packed_ref[rows, span(t)] = a_ref[b, :, span(t)]
            packed_ref[rows, span(h)] = jnp.where(after, final[0], packed)
            for (ref, t), x in zip(live, final[1:]):
                (packed_ref if ref is a_ref else linv_ref)[rows, span(t)] = x
            a_ref[b, :, span(h)] = head
            v_ref[0] = head
            for n, ((ref, t), x) in enumerate(zip(live, rest)):
                ref[b, :, span(t)] = x
                v_ref[n + 1] = x
            others = [base + lax.rem(i + s, per_block) for s in range(1, per_block)]
            heads = [a_ref[r, :, span(h)] for r in others]
            facs = [[pick_lane(x, g + j) for j in range(SUB)] for x in heads]
            for n, (ref, t) in enumerate([(a_ref, h)] + live):
                old = [jnp.where(in_panel, 0.0, x) for x in heads] if n == 0 else [ref[r, :, span(t)] for r in others]
                vs = [row_of([head] + rest and ([head] + rest)[n], j) for j in range(SUB)]
                for x, fac, r in zip(old, facs, others):
                    acc = [fac[j] * vs[j] for j in range(SUB)]
                    while len(acc) > 1:
                        acc = [p + q for p, q in zip(acc[::2], acc[1::2])]
                    ref[r, :, span(t)] = x - acc[0]
            return c

        lax.fori_loop(0, per_block, panel, 0)

        lo = (base % per_tile) * SUB
        pad = [jnp.zeros((n, LANES), jnp.float32) for n in (lo, LANES - lo - width)]

        def stack(x):
            return jnp.concatenate([p for p in (pad[0], x, pad[1]) if p.shape[0]], axis=0)

        def flat(ref, first, last, t):
            return ref[first:last, :, span(t)].reshape((last - first) * SUB, LANES)

        end = base + per_block
        right = [stack(flat(ref, base, end, t)) for ref, t in [(a_ref, h)] + live]
        for first, last in ((end, groups), (0, base)):
            if first == last:
                continue
            left = flat(a_ref, first, last, h)
            column = lax.broadcasted_iota(jnp.int32, left.shape, 1)
            for n, (ref, t) in enumerate([(a_ref, h)] + live):
                if ref is m_ref and first == 0:
                    continue
                old = left if n else None
                old = jnp.where((column >= lo) & (column < lo + width), 0.0, left) if n == 0 else flat(ref, first, last, t)
                new = old - jnp.dot(left, right[n], precision=HI, preferred_element_type=jnp.float32)
                ref[first:last, :, span(t)] = new.reshape(last - first, SUB, LANES)

    ri = lax.broadcasted_iota(jnp.int32, (SUB, LANES), 0)
    for i in range(groups):
        for t in range(tiles):
            x = a_ref[i, :, span(t)]
            keep = lane + t * LANES >= ri + i * SUB
            uinv_ref[i * SUB:(i + 1) * SUB, span(t)] = jnp.where(keep, -x, 0.0)


def vmem():
    return pl.BlockSpec(memory_space=pltpu.VMEM)


def smem():
    return pl.BlockSpec(memory_space=pltpu.SMEM)


def factor(square, width=32):
    size = square.shape[0]
    out = jax.ShapeDtypeStruct((size, size), jnp.float32)
    return pl.pallas_call(
        functools.partial(factor_kernel, width),
        out_shape=(out, out, out),
        in_specs=[vmem()],
        out_specs=(vmem(),) * 3,
        scratch_shapes=[
            pltpu.VMEM((size // SUB, SUB, size), jnp.float32),
            pltpu.VMEM((size // SUB, SUB, size), jnp.float32),
            pltpu.VMEM((1 + size // LANES, SUB, LANES), jnp.float32),
        ],
        cost_estimate=pl.CostEstimate(flops=4 * size**3, bytes_accessed=16 * size**2, transcendentals=0),
        name="factor",
    )(square)


def pick_kernel(slot_ref, own_ref, block_ref, out_ref):
    def group(q, c):
        for u in range(SUB):
            j = q * SUB + u
            row = block_ref[pl.ds(slot_ref[j], 1), :]
            out_ref[pl.ds(j, 1), :] = row * own_ref[j].astype(jnp.float32)
        return c

    lax.fori_loop(0, out_ref.shape[0] // SUB, group, 0)


def pick(block, slots, owned, tiles):
    rows, width = block.shape[0], slots.shape[0]
    return pl.pallas_call(
        pick_kernel,
        grid=(tiles,),
        out_shape=jax.ShapeDtypeStruct((width, tiles * width), jnp.float32),
        in_specs=[smem(), smem(), pl.BlockSpec((rows, width), lambda t: (0, t))],
        out_specs=pl.BlockSpec((width, width), lambda t: (0, t)),
        cost_estimate=pl.CostEstimate(
            flops=width * width * tiles, bytes_accessed=4 * (rows + width) * width * tiles, transcendentals=0
        ),
        name="pick",
    )(slots, owned, block)


def place_rows(slot_ref, rows_ref, target_ref):
    def group(q, c):
        for u in range(SUB):
            j = q * SUB + u
            target_ref[pl.ds(slot_ref[j], 1), :] = rows_ref[pl.ds(j, 1), :]
        return c

    lax.fori_loop(0, rows_ref.shape[0] // SUB, group, 0)


def place_kernel(slot_ref, block_ref, rows_ref, out_ref, buf_ref):
    rows = block_ref.shape[0]
    buf_ref[:rows, :] = block_ref[...]
    place_rows(slot_ref, rows_ref, buf_ref)
    out_ref[...] = buf_ref[:rows, :]


def place(block, rows, slots):
    height, width = block.shape[0], slots.shape[0]
    return pl.pallas_call(
        place_kernel,
        grid=(1,),
        out_shape=jax.ShapeDtypeStruct((height, width), jnp.float32),
        in_specs=[
            smem(),
            pl.BlockSpec((height, width), lambda t: (0, 0)),
            pl.BlockSpec((width, width), lambda t: (0, 0)),
        ],
        out_specs=pl.BlockSpec((height, width), lambda t: (0, 0)),
        scratch_shapes=[pltpu.VMEM((height + SUB, width), jnp.float32)],
        cost_estimate=pl.CostEstimate(flops=0, bytes_accessed=8 * height * width, transcendentals=0),
        name="place",
    )(slots, block, rows)


def halves(x):
    high = x.astype(jnp.bfloat16)
    low = (x - high.astype(jnp.float32)).astype(jnp.bfloat16)
    return high, low


def split_dot(left, right):
    acc = jnp.dot(left[0], right[1], preferred_element_type=jnp.float32)
    acc += jnp.dot(left[1], right[0], preferred_element_type=jnp.float32)
    return acc + jnp.dot(left[0], right[0], preferred_element_type=jnp.float32)


def update_kernel(
    slot_ref, where_ref, block_ref, panel_ref, pivot_ref, top_ref, packed_ref, linv_ref, uinv_ref,
    out_ref, high_ref, low_ref, buf_ref,
):
    rows, width = panel_ref.shape
    t = pl.program_id(0)
    first_row = where_ref[0] == 0
    first_col = (where_ref[1] == 0) & (t == 0)

    @pl.when(t == 0)
    def _():
        lower = jnp.dot(panel_ref[...], uinv_ref[...], precision=HI, preferred_element_type=jnp.float32)
        high_ref[...], low_ref[...] = halves(lower)
        out_ref[...] = lower

    upper = jnp.dot(linv_ref[...], pivot_ref[...], precision=HI, preferred_element_type=jnp.float32)

    @pl.when(jnp.logical_not(first_col))
    def _():
        buf_ref[:rows, :] = block_ref[...]
        place_rows(slot_ref, top_ref, buf_ref)
        out_ref[...] = buf_ref[:rows, :] - split_dot((high_ref[...], low_ref[...]), halves(upper))

    @pl.when(first_row)
    def _():
        out_ref[:width, :] = jnp.where(first_col, packed_ref[...], upper)


def update(block, panel, pivot_rows, old_top, packed, linv, uinv, slots, where):
    rows, cols = block.shape
    width = slots.shape[0]
    square = pl.BlockSpec((width, width), lambda t: (0, 0))
    tall = pl.BlockSpec((rows, width), lambda t: (0, t))
    flat = pl.BlockSpec((width, width), lambda t: (0, t))
    return pl.pallas_call(
        update_kernel,
        grid=(cols // width,),
        out_shape=jax.ShapeDtypeStruct((rows, cols), jnp.float32),
        in_specs=[
            smem(), smem(), tall, pl.BlockSpec((rows, width), lambda t: (0, 0)), flat, flat, square, square, square,
        ],
        out_specs=tall,
        scratch_shapes=[
            pltpu.VMEM((rows, width), jnp.bfloat16),
            pltpu.VMEM((rows, width), jnp.bfloat16),
            pltpu.VMEM((rows + SUB, width), jnp.float32),
        ],
        cost_estimate=pl.CostEstimate(
            flops=6 * rows * cols * width, bytes_accessed=8 * rows * cols, transcendentals=0
        ),
        name="update",
    )(slots, where, block, panel, pivot_rows, old_top, packed, linv, uinv)


def bits_of(n):
    return [1 << i for i in range(n.bit_length() - 1)]


def sum_over_rows(x, order, n_row):
    for bit in order:
        x = x + lax.ppermute(x, "prow", [(i, i ^ bit) for i in range(n_row)])
    return x


def spread_rows(x, order, n_row):
    have = [0]
    for bit in order:
        x = x + lax.ppermute(x, "prow", [(i, i ^ bit) for i in have])
        have = have + [i ^ bit for i in have]
    return x


def spread_cols(x, order):
    have = [0]
    for bit in order:
        x = x + lax.ppermute(x, "pcol", [(i, i ^ bit) for i in have])
        have = have + [i ^ bit for i in have]
    return x


def on_device(n_row, n_col, matrix, pivots):
    block = matrix[0, :, 0, :]
    rows, cols = block.shape
    width = pivots.shape[0]
    row = lax.axis_index("prow")
    col = lax.axis_index("pcol")
    owner = pivots // width % n_row
    slot = pivots // (width * n_row) * width + pivots % width
    mine = owner == row
    owned = mine.astype(jnp.int32)
    target = jnp.where(mine, slot, rows)
    where = jnp.stack([row, col]).astype(jnp.int32)
    row_bits, col_bits = bits_of(n_row), bits_of(n_col)
    at_first_row = row == 0
    at_first_col = col == 0

    square = pick(block, slot, owned * at_first_col.astype(jnp.int32), 1)
    square = sum_over_rows(square, row_bits, n_row)
    square = spread_cols(square, col_bits[::-1])
    packed, linv, uinv = factor(square)

    top = jnp.where(at_first_row, block[:width], 0.0)
    top_panel = spread_rows(top[:, :width], row_bits, n_row)
    panel = place(block, top_panel, target)
    panel = spread_cols(jnp.where(at_first_col, panel, 0.0), col_bits[::-1])

    picked = pick(block, slot, owned, cols // width)
    half = width // 2
    pivot_rows = jnp.concatenate([
        sum_over_rows(picked[:half], row_bits, n_row),
        sum_over_rows(picked[half:], row_bits[::-1], n_row),
    ])
    old_top = jnp.concatenate([
        spread_rows(top[:half], row_bits, n_row),
        spread_rows(top[half:], row_bits[::-1], n_row),
    ])
    result = update(block, panel, pivot_rows, old_top, packed, linv, uinv, target, where)
    return result[None, :, None, :]


def solution(mesh):
    spec = P("prow", None, "pcol", None)
    n_row, n_col = mesh.shape["prow"], mesh.shape["pcol"]
    return jax.shard_map(
        functools.partial(on_device, n_row, n_col), mesh=mesh, in_specs=(spec, P()), out_specs=spec, check_vma=False
    )
```

```python
import functools

import jax
import jax.numpy as jnp
from jax import lax
from jax.experimental import pallas as pl
from jax.experimental.pallas import tpu as pltpu
from jax.sharding import PartitionSpec as P

LANES = 128
SUB = 8
HI = lax.Precision.HIGHEST


def pick_lane(tile, lane):
    return jnp.take_along_axis(tile, jnp.full((SUB, LANES), lane, jnp.int32), axis=1)


def row_of(tile, j):
    return jnp.broadcast_to(tile[j:j + 1, :], (SUB, LANES))


def factor_kernel(width, s_ref, extra_ref, packed_ref, linv_ref, uinv_ref, a_ref, m_ref, v_ref):
    groups = a_ref.shape[0]
    tiles = groups * SUB // LANES
    per_tile = LANES // SUB
    per_block = width // SUB
    sub = lax.broadcasted_iota(jnp.int32, (SUB, LANES), 0)
    lane = lax.broadcasted_iota(jnp.int32, (SUB, LANES), 1)

    for i in range(groups):
        a_ref[i] = s_ref[i * SUB:(i + 1) * SUB, :] + extra_ref[i * SUB:(i + 1) * SUB, :]
        diag = lane - (i % per_tile) * SUB == sub
        for t in range(tiles):
            block = jnp.where(diag, 1.0, 0.0) if i // per_tile == t else jnp.zeros((SUB, LANES), jnp.float32)
            m_ref[i, :, t * LANES:(t + 1) * LANES] = block
            if t > i // per_tile:
                linv_ref[i * SUB:(i + 1) * SUB, t * LANES:(t + 1) * LANES] = block

    def span(t):
        return slice(t * LANES, (t + 1) * LANES)

    for o in range(groups // per_block):
        base = o * per_block
        h = base // per_tile
        live = [(a_ref, t) for t in range(h + 1, tiles)] + [(m_ref, t) for t in range(h + 1)]

        def panel(i, c, base=base, h=h, live=live):
            b = base + i
            g = (b - h * per_tile) * SUB
            rows = pl.ds(pl.multiple_of(b * SUB, SUB), SUB)
            own = a_ref[b, :, span(h)]
            cols = [pick_lane(own, g + j) for j in range(SUB)]
            in_panel = (lane >= g) & (lane < g + SUB)
            after = lane >= g + SUB
            head = jnp.where(in_panel, jnp.where(lane - g == sub, -1.0, 0.0), jnp.where(after, own, 0.0))
            rest = [ref[b, :, span(t)] for ref, t in live]
            packed = own
            final = [head] + rest
            for j in range(SUB):
                at = sub == j
                coef = cols[j]
                r = 1.0 / row_of(coef, j)
                final = [jnp.where(at, x, y) for x, y in zip([head] + rest, final)]
                packed = jnp.where((lane == g + j) & (sub > j), coef * r, packed)
                for k in range(j, SUB):
                    packed = jnp.where((lane == g + k) & at, cols[k], packed)
                head_coef = jnp.where((sub < j) | after, coef, 0.0)
                v = row_of(head, j) * r
                head = jnp.where(at, v, head - head_coef * v)
                for n, x in enumerate(rest):
                    v = row_of(x, j) * r
                    rest[n] = jnp.where(at, v, x - coef * v)
                for k in range(j + 1, SUB):
                    v = row_of(cols[k], j) * r
                    cols[k] = jnp.where(at, v, cols[k] - coef * v)
            for t in range(h):
                packed_ref[rows, span(t)] = a_ref[b, :, span(t)]
            packed_ref[rows, span(h)] = jnp.where(after, final[0], packed)
            for (ref, t), x in zip(live, final[1:]):
                (packed_ref if ref is a_ref else linv_ref)[rows, span(t)] = x
            a_ref[b, :, span(h)] = head
            v_ref[0] = head
            for n, ((ref, t), x) in enumerate(zip(live, rest)):
                ref[b, :, span(t)] = x
                v_ref[n + 1] = x
            others = [base + lax.rem(i + s, per_block) for s in range(1, per_block)]
            heads = [a_ref[r, :, span(h)] for r in others]
            facs = [[pick_lane(x, g + j) for j in range(SUB)] for x in heads]
            for n, (ref, t) in enumerate([(a_ref, h)] + live):
                old = [jnp.where(in_panel, 0.0, x) for x in heads] if n == 0 else [ref[r, :, span(t)] for r in others]
                vs = [row_of([head] + rest and ([head] + rest)[n], j) for j in range(SUB)]
                for x, fac, r in zip(old, facs, others):
                    acc = [fac[j] * vs[j] for j in range(SUB)]
                    while len(acc) > 1:
                        acc = [p + q for p, q in zip(acc[::2], acc[1::2])]
                    ref[r, :, span(t)] = x - acc[0]
            return c

        lax.fori_loop(0, per_block, panel, 0)

        lo = (base % per_tile) * SUB
        pad = [jnp.zeros((n, LANES), jnp.float32) for n in (lo, LANES - lo - width)]

        def stack(x):
            return jnp.concatenate([p for p in (pad[0], x, pad[1]) if p.shape[0]], axis=0)

        def flat(ref, first, last, t):
            return ref[first:last, :, span(t)].reshape((last - first) * SUB, LANES)

        end = base + per_block
        right = [stack(flat(ref, base, end, t)) for ref, t in [(a_ref, h)] + live]
        for first, last in ((end, groups), (0, base)):
            if first == last:
                continue
            left = flat(a_ref, first, last, h)
            column = lax.broadcasted_iota(jnp.int32, left.shape, 1)
            for n, (ref, t) in enumerate([(a_ref, h)] + live):
                if ref is m_ref and first == 0:
                    continue
                old = left if n else None
                old = jnp.where((column >= lo) & (column < lo + width), 0.0, left) if n == 0 else flat(ref, first, last, t)
                new = old - jnp.dot(left, right[n], precision=HI, preferred_element_type=jnp.float32)
                ref[first:last, :, span(t)] = new.reshape(last - first, SUB, LANES)

    ri = lax.broadcasted_iota(jnp.int32, (SUB, LANES), 0)
    for i in range(groups):
        for t in range(tiles):
            x = a_ref[i, :, span(t)]
            keep = lane + t * LANES >= ri + i * SUB
            uinv_ref[i * SUB:(i + 1) * SUB, span(t)] = jnp.where(keep, -x, 0.0)


def vmem():
    return pl.BlockSpec(memory_space=pltpu.VMEM)


def smem():
    return pl.BlockSpec(memory_space=pltpu.SMEM)


def factor(square, extra, width=32):
    size = square.shape[1]
    out = jax.ShapeDtypeStruct((size, size), jnp.float32)
    return pl.pallas_call(
        functools.partial(factor_kernel, width),
        out_shape=(out, out, out),
        in_specs=[vmem(), vmem()],
        out_specs=(vmem(),) * 3,
        scratch_shapes=[
            pltpu.VMEM((size // SUB, SUB, size), jnp.float32),
            pltpu.VMEM((size // SUB, SUB, size), jnp.float32),
            pltpu.VMEM((1 + size // LANES, SUB, LANES), jnp.float32),
        ],
        cost_estimate=pl.CostEstimate(flops=4 * size**3, bytes_accessed=16 * size**2, transcendentals=0),
        name="factor",
    )(square, extra)


def pick_kernel(slot_ref, own_ref, block_ref, out_ref):
    def group(q, c):
        for u in range(SUB):
            j = q * SUB + u
            row = block_ref[pl.ds(slot_ref[j], 1), :]
            out_ref[pl.ds(j, 1), :] = row * own_ref[j].astype(jnp.float32)
        return c

    lax.fori_loop(0, out_ref.shape[0] // SUB, group, 0)


def pick(block, slots, owned, tiles):
    rows, width = block.shape[0], slots.shape[0]
    return pl.pallas_call(
        pick_kernel,
        grid=(tiles,),
        out_shape=jax.ShapeDtypeStruct((width, tiles * width), jnp.float32),
        in_specs=[smem(), smem(), pl.BlockSpec((rows, width), lambda t: (0, t))],
        out_specs=pl.BlockSpec((width, width), lambda t: (0, t)),
        cost_estimate=pl.CostEstimate(
            flops=width * width * tiles, bytes_accessed=4 * (rows + width) * width * tiles, transcendentals=0
        ),
        name="pick",
    )(slots, owned, block)


def place_rows(slot_ref, rows_ref, target_ref):
    def group(q, c):
        for u in range(SUB):
            j = q * SUB + u
            target_ref[pl.ds(slot_ref[j], 1), :] = rows_ref[pl.ds(j, 1), :]
        return c

    lax.fori_loop(0, rows_ref.shape[0] // SUB, group, 0)


def place_kernel(slot_ref, block_ref, rows_ref, out_ref, buf_ref):
    rows = block_ref.shape[0]
    buf_ref[:rows, :] = block_ref[...]
    place_rows(slot_ref, rows_ref, buf_ref)
    out_ref[...] = buf_ref[:rows, :]


def place(block, rows, slots):
    height, width = block.shape[0], slots.shape[0]
    return pl.pallas_call(
        place_kernel,
        grid=(1,),
        out_shape=jax.ShapeDtypeStruct((height, width), jnp.float32),
        in_specs=[
            smem(),
            pl.BlockSpec((height, width), lambda t: (0, 0)),
            pl.BlockSpec((width, width), lambda t: (0, 0)),
        ],
        out_specs=pl.BlockSpec((height, width), lambda t: (0, 0)),
        scratch_shapes=[pltpu.VMEM((height + SUB, width), jnp.float32)],
        cost_estimate=pl.CostEstimate(flops=0, bytes_accessed=8 * height * width, transcendentals=0),
        name="place",
    )(slots, block, rows)


def halves(x):
    high = x.astype(jnp.bfloat16)
    low = (x - high.astype(jnp.float32)).astype(jnp.bfloat16)
    return high, low


def split_dot(left, right):
    acc = jnp.dot(left[0], right[1], preferred_element_type=jnp.float32)
    acc += jnp.dot(left[1], right[0], preferred_element_type=jnp.float32)
    return acc + jnp.dot(left[0], right[0], preferred_element_type=jnp.float32)


def update_kernel(
    slot_ref, where_ref, block_ref, panel_ref, pivot_ref, top_ref, packed_ref, linv_ref, uinv_ref,
    out_ref, high_ref, low_ref, buf_ref,
):
    rows, width = panel_ref.shape
    t = pl.program_id(0)
    first_row = where_ref[0] == 0
    first_col = (where_ref[1] == 0) & (t == 0)

    @pl.when(t == 0)
    def _():
        lower = jnp.dot(panel_ref[...], uinv_ref[...], precision=HI, preferred_element_type=jnp.float32)
        high_ref[...], low_ref[...] = halves(lower)
        out_ref[...] = lower

    upper = jnp.dot(linv_ref[...], pivot_ref[...], precision=HI, preferred_element_type=jnp.float32)

    @pl.when(jnp.logical_not(first_col))
    def _():
        buf_ref[:rows, :] = block_ref[...]
        place_rows(slot_ref, top_ref, buf_ref)
        out_ref[...] = buf_ref[:rows, :] - split_dot((high_ref[...], low_ref[...]), halves(upper))

    @pl.when(first_row)
    def _():
        out_ref[:width, :] = jnp.where(first_col, packed_ref[...], upper)


def update(block, panel, pivot_rows, old_top, packed, linv, uinv, slots, where):
    rows, cols = block.shape
    width = slots.shape[0]
    square = pl.BlockSpec((width, width), lambda t: (0, 0))
    tall = pl.BlockSpec((rows, width), lambda t: (0, t))
    flat = pl.BlockSpec((width, width), lambda t: (0, t))
    return pl.pallas_call(
        update_kernel,
        grid=(cols // width,),
        out_shape=jax.ShapeDtypeStruct((rows, cols), jnp.float32),
        in_specs=[
            smem(), smem(), tall, pl.BlockSpec((rows, width), lambda t: (0, 0)), flat, flat, square, square, square,
        ],
        out_specs=tall,
        scratch_shapes=[
            pltpu.VMEM((rows, width), jnp.bfloat16),
            pltpu.VMEM((rows, width), jnp.bfloat16),
            pltpu.VMEM((rows + SUB, width), jnp.float32),
        ],
        cost_estimate=pl.CostEstimate(
            flops=6 * rows * cols * width, bytes_accessed=8 * rows * cols, transcendentals=0
        ),
        name="update",
    )(slots, where, block, panel, pivot_rows, old_top, packed, linv, uinv)


def bits_of(n):
    return [1 << i for i in range(n.bit_length() - 1)]


def sum_over_rows(x, order, n_row):
    for bit in order:
        x = x + lax.ppermute(x, "prow", [(i, i ^ bit) for i in range(n_row)])
    return x


def spread_rows(x, order, n_row):
    have = [0]
    for bit in order:
        x = x + lax.ppermute(x, "prow", [(i, i ^ bit) for i in have])
        have = have + [i ^ bit for i in have]
    return x


def spread_cols(x, order):
    have = [0]
    for bit in order:
        x = x + lax.ppermute(x, "pcol", [(i, i ^ bit) for i in have])
        have = have + [i ^ bit for i in have]
    return x


def dense_step(n_row, n_col, matrix, pivots):
    block = matrix[0, :, 0, :]
    rows, cols = block.shape
    width = pivots.shape[0]
    row = lax.axis_index("prow")
    col = lax.axis_index("pcol")
    owner = pivots // width % n_row
    slot = pivots // (width * n_row) * width + pivots % width
    mine = owner == row
    owned = mine.astype(jnp.int32)
    target = jnp.where(mine, slot, rows)
    where = jnp.stack([row, col]).astype(jnp.int32)
    row_bits, col_bits = bits_of(n_row), bits_of(n_col)
    at_first_row = row == 0
    at_first_col = col == 0

    square = pick(block, slot, owned * at_first_col.astype(jnp.int32), 1)
    square = sum_over_rows(square, row_bits, n_row)
    square = spread_cols(square, col_bits[::-1])
    packed, linv, uinv = factor(square, jnp.zeros_like(square))

    top = jnp.where(at_first_row, block[:width], 0.0)
    top_panel = spread_rows(top[:, :width], row_bits, n_row)
    panel = place(block, top_panel, target)
    panel = spread_cols(jnp.where(at_first_col, panel, 0.0), col_bits[::-1])

    picked = pick(block, slot, owned, cols // width)
    half = width // 2
    pivot_rows = jnp.concatenate([
        sum_over_rows(picked[:half], row_bits, n_row),
        sum_over_rows(picked[half:], row_bits[::-1], n_row),
    ])
    old_top = jnp.concatenate([
        spread_rows(top[:half], row_bits, n_row),
        spread_rows(top[half:], row_bits[::-1], n_row),
    ])
    result = update(block, panel, pivot_rows, old_top, packed, linv, uinv, target, where)
    return result[None, :, None, :]


def raw():
    return pl.BlockSpec(memory_space=pl.ANY)


def first_kernel(slot_ref, where_ref, mine_ref, mat_ref, square_ref, top_ref, panel_ref, sem):
    width = square_ref.shape[0]
    panel = pltpu.make_async_copy(mat_ref.at[:, 0, pl.ds(0, width)], panel_ref, sem.at[0])
    top = pltpu.make_async_copy(mat_ref.at[pl.ds(0, width), 0, pl.ds(0, width)], top_ref, sem.at[1])

    def group(q, c):
        for u in range(SUB):
            j = q * SUB + u
            source = mat_ref.at[slot_ref[j], :, pl.ds(0, width)]
            pltpu.make_async_copy(source, square_ref.at[pl.ds(j, 1), :], sem.at[2]).start()
        return c

    lax.fori_loop(0, width // SUB, group, 0)
    top.start()
    panel.start()
    pltpu.make_async_copy(mat_ref.at[pl.ds(0, width), 0, pl.ds(0, width)], square_ref, sem.at[2]).wait()
    square_ref[...] = jnp.where(mine_ref[...] > 0, square_ref[...], 0.0)
    top.wait()
    top_ref[...] = jnp.where(where_ref[0] == 0, top_ref[...], 0.0)
    panel.wait()


def first_pick(mat, slot, where, mine):
    rows, width = mat.shape[0], slot.shape[0]
    square = jax.ShapeDtypeStruct((width, width), jnp.float32)
    return pl.pallas_call(
        first_kernel,
        out_shape=(square, square, jax.ShapeDtypeStruct((rows, width), jnp.float32)),
        in_specs=[smem(), smem(), vmem(), raw()],
        out_specs=(vmem(),) * 3,
        scratch_shapes=[pltpu.SemaphoreType.DMA((3,))],
        cost_estimate=pl.CostEstimate(flops=0, bytes_accessed=8 * (rows + 2 * width) * width, transcendentals=0),
        name="first_pick",
    )(slot, where, mine, mat)


def own_rows_kernel(slot_ref, mat_ref, left_ref, right_ref, sem):
    count, half = left_ref.shape[0], left_ref.shape[2]

    def group(q, c):
        for u in range(SUB):
            i = q * SUB + u
            source = mat_ref.at[slot_ref[i]]
            pltpu.make_async_copy(source.at[:, pl.ds(0, half)], left_ref.at[i], sem.at[0]).start()
            pltpu.make_async_copy(source.at[:, pl.ds(half, half)], right_ref.at[i], sem.at[1]).start()
        return c

    lax.fori_loop(0, count // SUB, group, 0)
    pltpu.make_async_copy(mat_ref.at[pl.ds(0, count), :, pl.ds(0, half)], left_ref, sem.at[0]).wait()
    pltpu.make_async_copy(mat_ref.at[pl.ds(0, count), :, pl.ds(half, half)], right_ref, sem.at[1]).wait()


def own_rows(mat, slots):
    count, cols = slots.shape[0], mat.shape[2]
    half = jax.ShapeDtypeStruct((count, 1, cols // 2), jnp.float32)
    return pl.pallas_call(
        own_rows_kernel,
        out_shape=(half, half),
        in_specs=[smem(), raw()],
        out_specs=(vmem(),) * 2,
        scratch_shapes=[pltpu.SemaphoreType.DMA((2,))],
        cost_estimate=pl.CostEstimate(flops=0, bytes_accessed=8 * count * cols, transcendentals=0),
        name="own_rows",
    )(slots, mat)


def top_rows_kernel(list_ref, mat_ref, *refs):
    outs, sem = refs[:-1], refs[-1]
    count = outs[0].shape[0]
    for p, out_ref in enumerate(outs):
        def group(q, c, p=p, out_ref=out_ref):
            for u in range(SUB):
                i = q * SUB + u
                pltpu.make_async_copy(mat_ref.at[list_ref[p, i]], out_ref.at[i], sem.at[p]).start()
            return c

        lax.fori_loop(0, count // SUB, group, 0)
    for p, out_ref in enumerate(outs):
        pltpu.make_async_copy(mat_ref.at[pl.ds(0, count)], out_ref, sem.at[p]).wait()


def top_rows(mat, lists):
    n_row, count = lists.shape
    cols = mat.shape[2]
    return pl.pallas_call(
        top_rows_kernel,
        out_shape=(jax.ShapeDtypeStruct((count, 1, cols), jnp.float32),) * n_row,
        in_specs=[smem(), raw()],
        out_specs=(vmem(),) * n_row,
        scratch_shapes=[pltpu.SemaphoreType.DMA((n_row,))],
        cost_estimate=pl.CostEstimate(flops=0, bytes_accessed=8 * n_row * count * cols, transcendentals=0),
        name="top_rows",
    )(lists, mat)


def pack_kernel(list_ref, where_ref, a_ref, b_ref, c_ref, d_ref, out_ref, top_ref):
    width = a_ref.shape[0]
    extra = out_ref.shape[0] - width
    keep = where_ref[1] == 0
    out_ref[:width, :] = jnp.where(keep, a_ref[...] + b_ref[...], 0.0)
    top_ref[...] = jnp.where(keep, c_ref[...] + d_ref[...], 0.0)

    def group(q, c):
        for u in range(SUB):
            i = q * SUB + u
            out_ref[pl.ds(width + i, 1), :] = top_ref[pl.ds(list_ref[i], 1), :]
        return c

    lax.fori_loop(0, extra // SUB, group, 0)


def pack(a, b, c, d, mine, where):
    width, extra = a.shape[0], mine.shape[0]
    return pl.pallas_call(
        pack_kernel,
        out_shape=jax.ShapeDtypeStruct((width + extra, width), jnp.float32),
        in_specs=[smem(), smem()] + [vmem()] * 4,
        out_specs=vmem(),
        scratch_shapes=[pltpu.VMEM((width, width), jnp.float32)],
        cost_estimate=pl.CostEstimate(flops=2 * width * width, bytes_accessed=24 * width * width, transcendentals=0),
        name="pack",
    )(mine, where, a, b, c, d)


def finish_kernel(
    n_row, where_ref, target_ref, pos_ref, mat_ref, panel_ref, panel_new_ref, square_ref, square_new_ref,
    packed_ref, linv_ref, uinv_ref, a_old_ref, a_new_ref, b_old_ref, b_new_ref, *refs,
):
    tops, refs = refs[:n_row], refs[n_row:]
    out_ref, block, pivot, panel, old, high, low, top, sem, in_sem, out_sem = refs
    rows, _, cols = mat_ref.shape
    width = linv_ref.shape[0]
    count, half = tops[0].shape[0], cols // 2
    tiles = cols // width
    row, col = where_ref[0], where_ref[1]

    def tile(t):
        return pl.ds(pl.multiple_of(t * width, width), width)

    @pl.when(col % 2 == 0)
    def _():
        pltpu.make_async_copy(panel_ref, panel.at[pl.ds(0, rows)], sem.at[0]).start()

    @pl.when(col % 2 == 1)
    def _():
        pltpu.make_async_copy(panel_new_ref, panel.at[pl.ds(0, rows)], sem.at[0]).start()

    for p in range(n_row):
        @pl.when(row == p)
        def _(p=p):
            pltpu.make_async_copy(tops[p].at[:, 0, :], old, sem.at[1]).start()

    blocks = [
        pltpu.make_async_copy(mat_ref.at[:, 0, tile(t)], block.at[pl.ds(0, rows), tile(t)], in_sem.at[t])
        for t in range(tiles)
    ]
    pieces = []
    for part, (first, second) in enumerate(((a_old_ref, a_new_ref), (b_old_ref, b_new_ref))):
        for k in range(n_row):
            source = (first if 2 * k < n_row else second).at[pl.ds(k % (n_row // 2) * count, count), 0, :]
            n_bits = n_row.bit_length() - 1
            at = k if part == 0 else int(format(k, "0%db" % n_bits)[::-1], 2)
            dest = pivot.at[pl.ds(at * count, count), pl.ds(part * half, half)]
            pieces.append(pltpu.make_async_copy(source, dest, sem.at[2 + part * n_row + k]))
    for copy in blocks[:1] + pieces + blocks[1:]:
        copy.start()

    lanes = lax.broadcasted_iota(jnp.int32, (width, n_row * count), 1)
    places = jnp.where(lanes == pos_ref[...], 1.0, 0.0)
    spread_inv = halves(jnp.dot(linv_ref[...], places, precision=HI, preferred_element_type=jnp.float32))
    top[...] = square_ref[width:, :] + square_new_ref[width:, :]
    pltpu.make_async_copy(panel_ref, panel.at[pl.ds(0, rows)], sem.at[0]).wait()
    place_rows(target_ref, top, panel)
    lower = split_dot(halves(panel[:rows, :]), halves(uinv_ref[...]))
    high[...], low[...] = halves(lower)
    pltpu.make_async_copy(tops[0].at[:, 0, :], old, sem.at[1]).wait()
    for copy in blocks:
        copy.wait()
    place_rows(target_ref, old, block)

    @pl.when(col == 0)
    def _():
        block[:rows, :width] = lower

    for copy in pieces:
        copy.wait()

    def step(t, c):
        upper = split_dot(spread_inv, halves(pivot[:, tile(t)]))
        first_col = (col == 0) & (t == 0)

        @pl.when(jnp.logical_not(first_col))
        def _():
            block[:rows, tile(t)] = block[:rows, tile(t)] - split_dot((high[...], low[...]), halves(upper))

        @pl.when(row == 0)
        def _():
            block[:width, tile(t)] = jnp.where(first_col, packed_ref[...], upper)

        pltpu.make_async_copy(block.at[pl.ds(0, rows), tile(t)], out_ref.at[:, 0, tile(t)], out_sem.at[t]).start()
        return c

    lax.fori_loop(0, tiles, step, 0)
    for t in range(tiles):
        pltpu.make_async_copy(block.at[pl.ds(0, rows), tile(t)], out_ref.at[:, 0, tile(t)], out_sem.at[t]).wait()


def finish(where, target, pos, mat, panels, squares, factors, pivot_parts, tops):
    rows, _, cols = mat.shape
    width, n_row, count = factors[0].shape[0], len(tops), target.shape[0]
    return pl.pallas_call(
        functools.partial(finish_kernel, n_row),
        out_shape=jax.ShapeDtypeStruct(mat.shape, jnp.float32),
        in_specs=[smem(), smem(), vmem(), raw(), raw(), raw()] + [vmem()] * 5 + [raw()] * (4 + n_row),
        out_specs=raw(),
        scratch_shapes=[
            pltpu.VMEM((rows + SUB, cols), jnp.float32),
            pltpu.VMEM((n_row * count, cols), jnp.float32),
            pltpu.VMEM((rows + SUB, width), jnp.float32),
            pltpu.VMEM((count, cols), jnp.float32),
            pltpu.VMEM((rows, width), jnp.bfloat16),
            pltpu.VMEM((rows, width), jnp.bfloat16),
            pltpu.VMEM((count, width), jnp.float32),
            pltpu.SemaphoreType.DMA((2 + 2 * n_row,)),
            pltpu.SemaphoreType.DMA((cols // width,)),
            pltpu.SemaphoreType.DMA((cols // width,)),
        ],
        cost_estimate=pl.CostEstimate(
            flops=6 * rows * cols * width, bytes_accessed=8 * rows * cols, transcendentals=0
        ),
        name="finish",
    )(where, target, pos, mat, *panels, *squares, *factors, *pivot_parts, *tops)


def capacity(n_row, width):
    mean = width / n_row
    return -(-int(mean + 4 * (mean * (1 - 1 / n_row)) ** 0.5) // SUB) * SUB


def grow_rows(x, order, n_row):
    for bit in order[:-1]:
        x = jnp.concatenate([x, lax.ppermute(x, "prow", [(i, i ^ bit) for i in range(n_row)])])
    return x, lax.ppermute(x, "prow", [(i, i ^ order[-1]) for i in range(n_row)])


def tree(x, axes, order, to_pair, is_new):
    have = [0]
    for n, bit in enumerate(order):
        moved = lax.ppermute(x, axes, [to_pair(i, i ^ bit) for i in have])
        have = have + [i ^ bit for i in have]
        if n + 1 < len(order):
            x = jnp.where(is_new(bit, order[:n + 1]), moved, x)
    return x, moved


def capped_step(n_row, n_col, matrix, pivots):
    _, rows, _, cols = matrix.shape
    mat = matrix.reshape(rows, 1, cols)
    width = pivots.shape[0]
    count = capacity(n_row, width)
    row, col = lax.axis_index("prow"), lax.axis_index("pcol")
    where = jnp.stack([row, col]).astype(jnp.int32)
    row_bits, col_bits = bits_of(n_row), bits_of(n_col)
    owner, slot, rank = locate(pivots, n_row)
    mine = owner == row
    number = jnp.arange(width, dtype=jnp.int32)
    ordinal = jnp.arange(count, dtype=jnp.int32)
    hit = mine[None, :] & (rank[None, :] == ordinal[:, None])
    my_slots = jnp.sum(jnp.where(hit, slot[None, :], 0), axis=1, dtype=jnp.int32)
    my_number = jnp.sum(jnp.where(hit, number[None, :], 0), axis=1, dtype=jnp.int32)
    target = jnp.where(jnp.any(hit, axis=1), my_slots, rows)
    every = jnp.arange(n_row, dtype=jnp.int32)[:, None, None]
    hits = (owner[None, None, :] == every) & (rank[None, None, :] == ordinal[None, :, None])
    lists = jnp.sum(jnp.where(hits, number[None, None, :], 0), axis=2, dtype=jnp.int32)
    pos = ((owner ^ row) * count + rank)[:, None]

    square, top, panel = first_pick(mat, slot, where, mine.astype(jnp.int32)[:, None])

    def flat(i, j):
        return (i * n_col, j * n_col)

    both = ("prow", "pcol")
    for n, bit in enumerate(row_bits):
        moved = lax.ppermute(square, both, [flat(i, i ^ bit) for i in range(n_row)])
        back = row_bits[::-1]
        held = [i for i in range(n_row) if all(not i & b for b in back[n:])]
        moved_top = lax.ppermute(top, both, [flat(i, i ^ back[n]) for i in held])
        if n + 1 < len(row_bits):
            square, top = square + moved, top + moved_top
    message = pack(square, moved, top, moved_top, my_number, where)

    order = col_bits[::-1]

    def pair(i, j):
        return (i, j)

    def is_new(bit, done):
        return (col & bit) != 0

    message, message_new = tree(message, "pcol", order, pair, is_new)
    factors = factor(message, message_new)
    panel, panel_new = tree(panel, "pcol", order, pair, is_new)

    left, right = own_rows(mat, my_slots)
    parts = grow_rows(left, row_bits, n_row) + grow_rows(right, row_bits[::-1], n_row)
    tops = top_rows(mat, lists)
    tops = tops[:1] + tuple(lax.ppermute(tops[p], "prow", [(0, p)]) for p in range(1, n_row))
    out = finish(where, target, pos, mat, (panel, panel_new), (message, message_new), factors, parts, tops)
    return out.reshape(matrix.shape)


def locate(pivots, n_row):
    width = pivots.shape[0]
    owner = pivots // width % n_row
    slot = pivots // (width * n_row) * width + pivots % width
    number = jnp.arange(width, dtype=jnp.int32)
    ahead = (owner[:, None] == owner[None, :]) & (number[None, :] < number[:, None])
    return owner, slot, jnp.sum(ahead, axis=1, dtype=jnp.int32)


def on_device(n_row, n_col, matrix, pivots):
    owner, slot, rank = locate(pivots, n_row)
    return lax.cond(
        jnp.max(rank) < capacity(n_row, pivots.shape[0]),
        functools.partial(capped_step, n_row, n_col),
        functools.partial(dense_step, n_row, n_col),
        matrix, pivots,
    )


def solution(mesh):
    spec = P("prow", None, "pcol", None)
    n_row, n_col = mesh.shape["prow"], mesh.shape["pcol"]
    return jax.shard_map(
        functools.partial(on_device, n_row, n_col), mesh=mesh, in_specs=(spec, P()), out_specs=spec, check_vma=False
    )
```

```python
import functools

import jax
import jax.numpy as jnp
from jax import lax
from jax.experimental import pallas as pl
from jax.experimental.pallas import tpu as pltpu
from jax.sharding import PartitionSpec as P

LANES = 128
SUB = 8
HI = lax.Precision.HIGHEST


def pick_lane(tile, lane):
    return jnp.take_along_axis(tile, jnp.full((SUB, LANES), lane, jnp.int32), axis=1)


def row_of(tile, j):
    return jnp.broadcast_to(tile[j:j + 1, :], (SUB, LANES))


def factor_kernel(width, s_ref, extra_ref, packed_ref, linv_ref, uinv_ref, a_ref, m_ref, v_ref):
    groups = a_ref.shape[0]
    tiles = groups * SUB // LANES
    per_tile = LANES // SUB
    per_block = width // SUB
    sub = lax.broadcasted_iota(jnp.int32, (SUB, LANES), 0)
    lane = lax.broadcasted_iota(jnp.int32, (SUB, LANES), 1)

    for i in range(groups):
        a_ref[i] = s_ref[i * SUB:(i + 1) * SUB, :] + extra_ref[i * SUB:(i + 1) * SUB, :]
        diag = lane - (i % per_tile) * SUB == sub
        for t in range(tiles):
            block = jnp.where(diag, 1.0, 0.0) if i // per_tile == t else jnp.zeros((SUB, LANES), jnp.float32)
            m_ref[i, :, t * LANES:(t + 1) * LANES] = block
            if t > i // per_tile:
                linv_ref[i * SUB:(i + 1) * SUB, t * LANES:(t + 1) * LANES] = block

    def span(t):
        return slice(t * LANES, (t + 1) * LANES)

    for o in range(groups // per_block):
        base = o * per_block
        h = base // per_tile
        live = [(a_ref, t) for t in range(h + 1, tiles)] + [(m_ref, t) for t in range(h + 1)]

        def panel(i, c, base=base, h=h, live=live):
            b = base + i
            g = (b - h * per_tile) * SUB
            rows = pl.ds(pl.multiple_of(b * SUB, SUB), SUB)
            own = a_ref[b, :, span(h)]
            cols = [pick_lane(own, g + j) for j in range(SUB)]
            in_panel = (lane >= g) & (lane < g + SUB)
            after = lane >= g + SUB
            head = jnp.where(in_panel, jnp.where(lane - g == sub, -1.0, 0.0), jnp.where(after, own, 0.0))
            rest = [ref[b, :, span(t)] for ref, t in live]
            packed = own
            final = [head] + rest
            for j in range(SUB):
                at = sub == j
                coef = cols[j]
                r = 1.0 / row_of(coef, j)
                final = [jnp.where(at, x, y) for x, y in zip([head] + rest, final)]
                packed = jnp.where((lane == g + j) & (sub > j), coef * r, packed)
                for k in range(j, SUB):
                    packed = jnp.where((lane == g + k) & at, cols[k], packed)
                head_coef = jnp.where((sub < j) | after, coef, 0.0)
                v = row_of(head, j) * r
                head = jnp.where(at, v, head - head_coef * v)
                for n, x in enumerate(rest):
                    v = row_of(x, j) * r
                    rest[n] = jnp.where(at, v, x - coef * v)
                for k in range(j + 1, SUB):
                    v = row_of(cols[k], j) * r
                    cols[k] = jnp.where(at, v, cols[k] - coef * v)
            for t in range(h):
                packed_ref[rows, span(t)] = a_ref[b, :, span(t)]
            packed_ref[rows, span(h)] = jnp.where(after, final[0], packed)
            for (ref, t), x in zip(live, final[1:]):
                (packed_ref if ref is a_ref else linv_ref)[rows, span(t)] = x
            a_ref[b, :, span(h)] = head
            v_ref[0] = head
            for n, ((ref, t), x) in enumerate(zip(live, rest)):
                ref[b, :, span(t)] = x
                v_ref[n + 1] = x
            others = [base + lax.rem(i + s, per_block) for s in range(1, per_block)]
            heads = [a_ref[r, :, span(h)] for r in others]
            facs = [[pick_lane(x, g + j) for j in range(SUB)] for x in heads]
            for n, (ref, t) in enumerate([(a_ref, h)] + live):
                old = [jnp.where(in_panel, 0.0, x) for x in heads] if n == 0 else [ref[r, :, span(t)] for r in others]
                vs = [row_of([head] + rest and ([head] + rest)[n], j) for j in range(SUB)]
                for x, fac, r in zip(old, facs, others):
                    acc = [fac[j] * vs[j] for j in range(SUB)]
                    while len(acc) > 1:
                        acc = [p + q for p, q in zip(acc[::2], acc[1::2])]
                    ref[r, :, span(t)] = x - acc[0]
            return c

        lax.fori_loop(0, per_block, panel, 0)

        lo = (base % per_tile) * SUB
        pad = [jnp.zeros((n, LANES), jnp.float32) for n in (lo, LANES - lo - width)]

        def stack(x):
            return jnp.concatenate([p for p in (pad[0], x, pad[1]) if p.shape[0]], axis=0)

        def flat(ref, first, last, t):
            return ref[first:last, :, span(t)].reshape((last - first) * SUB, LANES)

        end = base + per_block
        right = [stack(flat(ref, base, end, t)) for ref, t in [(a_ref, h)] + live]
        for first, last in ((end, groups), (0, base)):
            if first == last:
                continue
            left = flat(a_ref, first, last, h)
            column = lax.broadcasted_iota(jnp.int32, left.shape, 1)
            for n, (ref, t) in enumerate([(a_ref, h)] + live):
                if ref is m_ref and first == 0:
                    continue
                old = left if n else None
                old = jnp.where((column >= lo) & (column < lo + width), 0.0, left) if n == 0 else flat(ref, first, last, t)
                new = old - jnp.dot(left, right[n], precision=HI, preferred_element_type=jnp.float32)
                ref[first:last, :, span(t)] = new.reshape(last - first, SUB, LANES)

    ri = lax.broadcasted_iota(jnp.int32, (SUB, LANES), 0)
    for i in range(groups):
        for t in range(tiles):
            x = a_ref[i, :, span(t)]
            keep = lane + t * LANES >= ri + i * SUB
            uinv_ref[i * SUB:(i + 1) * SUB, span(t)] = jnp.where(keep, -x, 0.0)


def vmem():
    return pl.BlockSpec(memory_space=pltpu.VMEM)


def smem():
    return pl.BlockSpec(memory_space=pltpu.SMEM)


def factor(square, extra, width=32):
    size = square.shape[1]
    out = jax.ShapeDtypeStruct((size, size), jnp.float32)
    return pl.pallas_call(
        functools.partial(factor_kernel, width),
        out_shape=(out, out, out),
        in_specs=[vmem(), vmem()],
        out_specs=(vmem(),) * 3,
        scratch_shapes=[
            pltpu.VMEM((size // SUB, SUB, size), jnp.float32),
            pltpu.VMEM((size // SUB, SUB, size), jnp.float32),
            pltpu.VMEM((1 + size // LANES, SUB, LANES), jnp.float32),
        ],
        cost_estimate=pl.CostEstimate(flops=4 * size**3, bytes_accessed=16 * size**2, transcendentals=0),
        name="factor",
    )(square, extra)


def pick_kernel(slot_ref, own_ref, block_ref, out_ref):
    def group(q, c):
        for u in range(SUB):
            j = q * SUB + u
            row = block_ref[pl.ds(slot_ref[j], 1), :]
            out_ref[pl.ds(j, 1), :] = row * own_ref[j].astype(jnp.float32)
        return c

    lax.fori_loop(0, out_ref.shape[0] // SUB, group, 0)


def pick(block, slots, owned, tiles):
    rows, width = block.shape[0], slots.shape[0]
    return pl.pallas_call(
        pick_kernel,
        grid=(tiles,),
        out_shape=jax.ShapeDtypeStruct((width, tiles * width), jnp.float32),
        in_specs=[smem(), smem(), pl.BlockSpec((rows, width), lambda t: (0, t))],
        out_specs=pl.BlockSpec((width, width), lambda t: (0, t)),
        cost_estimate=pl.CostEstimate(
            flops=width * width * tiles, bytes_accessed=4 * (rows + width) * width * tiles, transcendentals=0
        ),
        name="pick",
    )(slots, owned, block)


def place_rows(slot_ref, rows_ref, target_ref):
    def group(q, c):
        for u in range(SUB):
            j = q * SUB + u
            target_ref[pl.ds(slot_ref[j], 1), :] = rows_ref[pl.ds(j, 1), :]
        return c

    lax.fori_loop(0, rows_ref.shape[0] // SUB, group, 0)


def place_kernel(slot_ref, block_ref, rows_ref, out_ref, buf_ref):
    rows = block_ref.shape[0]
    buf_ref[:rows, :] = block_ref[...]
    place_rows(slot_ref, rows_ref, buf_ref)
    out_ref[...] = buf_ref[:rows, :]


def place(block, rows, slots):
    height, width = block.shape[0], slots.shape[0]
    return pl.pallas_call(
        place_kernel,
        grid=(1,),
        out_shape=jax.ShapeDtypeStruct((height, width), jnp.float32),
        in_specs=[
            smem(),
            pl.BlockSpec((height, width), lambda t: (0, 0)),
            pl.BlockSpec((width, width), lambda t: (0, 0)),
        ],
        out_specs=pl.BlockSpec((height, width), lambda t: (0, 0)),
        scratch_shapes=[pltpu.VMEM((height + SUB, width), jnp.float32)],
        cost_estimate=pl.CostEstimate(flops=0, bytes_accessed=8 * height * width, transcendentals=0),
        name="place",
    )(slots, block, rows)


def halves(x):
    high = x.astype(jnp.bfloat16)
    low = (x - high.astype(jnp.float32)).astype(jnp.bfloat16)
    return high, low


def split_dot(left, right):
    acc = jnp.dot(left[0], right[1], preferred_element_type=jnp.float32)
    acc += jnp.dot(left[1], right[0], preferred_element_type=jnp.float32)
    return acc + jnp.dot(left[0], right[0], preferred_element_type=jnp.float32)


def update_kernel(
    slot_ref, where_ref, block_ref, panel_ref, pivot_ref, top_ref, packed_ref, linv_ref, uinv_ref,
    out_ref, high_ref, low_ref, buf_ref,
):
    rows, width = panel_ref.shape
    t = pl.program_id(0)
    first_row = where_ref[0] == 0
    first_col = (where_ref[1] == 0) & (t == 0)

    @pl.when(t == 0)
    def _():
        lower = jnp.dot(panel_ref[...], uinv_ref[...], precision=HI, preferred_element_type=jnp.float32)
        high_ref[...], low_ref[...] = halves(lower)
        out_ref[...] = lower

    upper = jnp.dot(linv_ref[...], pivot_ref[...], precision=HI, preferred_element_type=jnp.float32)

    @pl.when(jnp.logical_not(first_col))
    def _():
        buf_ref[:rows, :] = block_ref[...]
        place_rows(slot_ref, top_ref, buf_ref)
        out_ref[...] = buf_ref[:rows, :] - split_dot((high_ref[...], low_ref[...]), halves(upper))

    @pl.when(first_row)
    def _():
        out_ref[:width, :] = jnp.where(first_col, packed_ref[...], upper)


def update(block, panel, pivot_rows, old_top, packed, linv, uinv, slots, where):
    rows, cols = block.shape
    width = slots.shape[0]
    square = pl.BlockSpec((width, width), lambda t: (0, 0))
    tall = pl.BlockSpec((rows, width), lambda t: (0, t))
    flat = pl.BlockSpec((width, width), lambda t: (0, t))
    return pl.pallas_call(
        update_kernel,
        grid=(cols // width,),
        out_shape=jax.ShapeDtypeStruct((rows, cols), jnp.float32),
        in_specs=[
            smem(), smem(), tall, pl.BlockSpec((rows, width), lambda t: (0, 0)), flat, flat, square, square, square,
        ],
        out_specs=tall,
        scratch_shapes=[
            pltpu.VMEM((rows, width), jnp.bfloat16),
            pltpu.VMEM((rows, width), jnp.bfloat16),
            pltpu.VMEM((rows + SUB, width), jnp.float32),
        ],
        cost_estimate=pl.CostEstimate(
            flops=6 * rows * cols * width, bytes_accessed=8 * rows * cols, transcendentals=0
        ),
        name="update",
    )(slots, where, block, panel, pivot_rows, old_top, packed, linv, uinv)


def bits_of(n):
    return [1 << i for i in range(n.bit_length() - 1)]


def sum_over_rows(x, order, n_row):
    for bit in order:
        x = x + lax.ppermute(x, "prow", [(i, i ^ bit) for i in range(n_row)])
    return x


def spread_rows(x, order, n_row):
    have = [0]
    for bit in order:
        x = x + lax.ppermute(x, "prow", [(i, i ^ bit) for i in have])
        have = have + [i ^ bit for i in have]
    return x


def spread_cols(x, order):
    have = [0]
    for bit in order:
        x = x + lax.ppermute(x, "pcol", [(i, i ^ bit) for i in have])
        have = have + [i ^ bit for i in have]
    return x


def dense_step(n_row, n_col, matrix, pivots):
    block = matrix[0, :, 0, :]
    rows, cols = block.shape
    width = pivots.shape[0]
    row = lax.axis_index("prow")
    col = lax.axis_index("pcol")
    owner = pivots // width % n_row
    slot = pivots // (width * n_row) * width + pivots % width
    mine = owner == row
    owned = mine.astype(jnp.int32)
    target = jnp.where(mine, slot, rows)
    where = jnp.stack([row, col]).astype(jnp.int32)
    row_bits, col_bits = bits_of(n_row), bits_of(n_col)
    at_first_row = row == 0
    at_first_col = col == 0

    square = pick(block, slot, owned * at_first_col.astype(jnp.int32), 1)
    square = sum_over_rows(square, row_bits, n_row)
    square = spread_cols(square, col_bits[::-1])
    packed, linv, uinv = factor(square, jnp.zeros_like(square))

    top = jnp.where(at_first_row, block[:width], 0.0)
    top_panel = spread_rows(top[:, :width], row_bits, n_row)
    panel = place(block, top_panel, target)
    panel = spread_cols(jnp.where(at_first_col, panel, 0.0), col_bits[::-1])

    picked = pick(block, slot, owned, cols // width)
    half = width // 2
    pivot_rows = jnp.concatenate([
        sum_over_rows(picked[:half], row_bits, n_row),
        sum_over_rows(picked[half:], row_bits[::-1], n_row),
    ])
    old_top = jnp.concatenate([
        spread_rows(top[:half], row_bits, n_row),
        spread_rows(top[half:], row_bits[::-1], n_row),
    ])
    result = update(block, panel, pivot_rows, old_top, packed, linv, uinv, target, where)
    return result[None, :, None, :]


def raw():
    return pl.BlockSpec(memory_space=pl.ANY)


def begin_kernel(
    n_row, pivot_ref, mat_ref, panel_ref, mine_ref, lists_ref, pos_ref, wide_ref, counts_ref, *refs
):
    messages, sem = refs[:n_row], refs[-1]
    width = pivot_ref.shape[0]
    count = mine_ref.shape[0]
    width_log, row_log = width.bit_length() - 1, n_row.bit_length() - 1
    row = lax.axis_index("prow")
    copy = pltpu.make_async_copy(mat_ref.at[:, 0, pl.ds(0, width)], panel_ref, sem)
    copy.start()
    for p in range(n_row):
        counts_ref[p] = 0

    def locate(q, c):
        for u in range(SUB):
            j = q * SUB + u
            block = lax.shift_right_logical(pivot_ref[j], width_log)
            owner = block & (n_row - 1)
            slot = lax.shift_left(lax.shift_right_logical(block, row_log), width_log) + (pivot_ref[j] & (width - 1))
            rank = counts_ref[owner]
            counts_ref[owner] = rank + 1
            held = jnp.minimum(rank, count - 1)
            lists_ref[owner, held] = j
            place = (owner ^ row) * count + held
            pos_ref[j] = place
            wide_ref[pl.ds(j, 1), :] = jnp.full((1, LANES), place, jnp.int32)

            @pl.when(owner == row)
            def _():
                mine_ref[held] = slot
        return c

    lax.fori_loop(0, width // SUB, locate, 0)

    def clear(i, c):
        mine_ref[i] = jnp.where(i < counts_ref[row], mine_ref[i], 0)
        for p in range(n_row):
            lists_ref[p, i] = jnp.where(i < counts_ref[p], lists_ref[p, i], 0)
        return c

    lax.fori_loop(0, count, clear, 0)
    copy.wait()

    def gather(q, c):
        for u in range(SUB):
            i = q * SUB + u
            messages[0][pl.ds(i, 1), :] = panel_ref[pl.ds(mine_ref[i], 1), :]
        return c

    lax.fori_loop(0, count // SUB, gather, 0)
    for k in range(1, n_row):
        messages[k][:count, :] = messages[0][:count, :]

    @pl.when(row == 0)
    def _():
        for p in range(n_row):
            def gather_top(q, c, p=p):
                for u in range(SUB):
                    i = q * SUB + u
                    messages[p][pl.ds(count + i, 1), :] = panel_ref[pl.ds(lists_ref[p, i], 1), :]
                return c

            lax.fori_loop(0, count // SUB, gather_top, 0)


def begin(mat, pivots, n_row, count):
    rows, width = mat.shape[0], pivots.shape[0]
    message = jax.ShapeDtypeStruct((2 * count, width), jnp.float32)
    return pl.pallas_call(
        functools.partial(begin_kernel, n_row),
        out_shape=(
            jax.ShapeDtypeStruct((rows, width), jnp.float32),
            jax.ShapeDtypeStruct((count,), jnp.int32),
            jax.ShapeDtypeStruct((n_row, count), jnp.int32),
            jax.ShapeDtypeStruct((width,), jnp.int32),
            jax.ShapeDtypeStruct((width, LANES), jnp.int32),
            jax.ShapeDtypeStruct((n_row,), jnp.int32),
        ) + (message,) * n_row,
        in_specs=[smem(), raw()],
        out_specs=(vmem(), smem(), smem(), smem(), vmem(), smem()) + (vmem(),) * n_row,
        scratch_shapes=[pltpu.SemaphoreType.DMA],
        cost_estimate=pl.CostEstimate(flops=0, bytes_accessed=8 * rows * width, transcendentals=0),
        name="begin",
    )(pivots, mat)


def own_rows_kernel(slot_ref, mat_ref, out_ref, sem):
    count = out_ref.shape[0]

    def group(q, c):
        for u in range(SUB):
            i = q * SUB + u
            pltpu.make_async_copy(mat_ref.at[slot_ref[i]], out_ref.at[i], sem).start()
        return c

    lax.fori_loop(0, count // SUB, group, 0)
    pltpu.make_async_copy(mat_ref.at[pl.ds(0, count)], out_ref, sem).wait()


def own_rows(mat, slots):
    count, cols = slots.shape[0], mat.shape[2]
    return pl.pallas_call(
        own_rows_kernel,
        out_shape=jax.ShapeDtypeStruct((count, 1, cols), jnp.float32),
        in_specs=[smem(), raw()],
        out_specs=vmem(),
        scratch_shapes=[pltpu.SemaphoreType.DMA],
        cost_estimate=pl.CostEstimate(flops=0, bytes_accessed=8 * count * cols, transcendentals=0),
        name="own_rows",
    )(slots, mat)


def top_rows_kernel(list_ref, mat_ref, *refs):
    outs, sem = refs[:-1], refs[-1]
    count = outs[0].shape[0]

    @pl.when(lax.axis_index("prow") == 0)
    def _():
        for p, out_ref in enumerate(outs):
            def group(q, c, p=p, out_ref=out_ref):
                for u in range(SUB):
                    i = q * SUB + u
                    pltpu.make_async_copy(mat_ref.at[list_ref[p, i]], out_ref.at[i], sem.at[p]).start()
                return c

            lax.fori_loop(0, count // SUB, group, 0)
        for p, out_ref in enumerate(outs):
            pltpu.make_async_copy(mat_ref.at[pl.ds(0, count)], out_ref, sem.at[p]).wait()


def top_rows(mat, lists):
    n_row, count = lists.shape
    cols = mat.shape[2]
    return pl.pallas_call(
        top_rows_kernel,
        out_shape=(jax.ShapeDtypeStruct((count, 1, cols), jnp.float32),) * n_row,
        in_specs=[smem(), raw()],
        out_specs=(vmem(),) * n_row,
        scratch_shapes=[pltpu.SemaphoreType.DMA((n_row,))],
        cost_estimate=pl.CostEstimate(flops=0, bytes_accessed=8 * n_row * count * cols, transcendentals=0),
        name="top_rows",
    )(lists, mat)


def pack_kernel(n_row, pos_ref, *refs):
    parts, out_ref, all_ref = refs[:n_row], refs[n_row], refs[n_row + 1]
    width = pos_ref.shape[0]
    count = out_ref.shape[0] - width
    row, col = lax.axis_index("prow"), lax.axis_index("pcol")

    @pl.when(col == 0)
    def _():
        for k in range(n_row):
            all_ref[k * count:(k + 1) * count, :] = parts[k][:count, :]

        def group(q, c):
            for u in range(SUB):
                j = q * SUB + u
                out_ref[pl.ds(j, 1), :] = all_ref[pl.ds(pos_ref[j], 1), :]
            return c

        lax.fori_loop(0, width // SUB, group, 0)
        for k in range(n_row):
            @pl.when(row == k)
            def _(k=k):
                out_ref[width:, :] = parts[k][count:, :]

    @pl.when(col != 0)
    def _():
        out_ref[...] = jnp.zeros_like(out_ref)


def pack(pos, parts):
    n_row, width = len(parts), pos.shape[0]
    count = parts[0].shape[0] // 2
    return pl.pallas_call(
        functools.partial(pack_kernel, n_row),
        out_shape=jax.ShapeDtypeStruct((width + count, width), jnp.float32),
        in_specs=[smem()] + [vmem()] * n_row,
        out_specs=vmem(),
        scratch_shapes=[pltpu.VMEM((n_row * count, width), jnp.float32)],
        cost_estimate=pl.CostEstimate(flops=0, bytes_accessed=24 * width * width, transcendentals=0),
        name="pack",
    )(pos, *parts)


def put_rows(slot_ref, held, rows_ref, target_ref):
    spare = target_ref.shape[0] - SUB

    def group(q, c):
        for u in range(SUB):
            i = q * SUB + u
            slot = jnp.where(i < held, slot_ref[i], spare)
            target_ref[pl.ds(slot, 1), :] = rows_ref[pl.ds(i, 1), :]
        return c

    lax.fori_loop(0, rows_ref.shape[0] // SUB, group, 0)


def finish_kernel(
    n_row, mine_ref, counts_ref, wide_ref, mat_ref, panel_ref, panel_new_ref, square_ref, square_new_ref,
    packed_ref, linv_ref, uinv_ref, *refs,
):
    parts, tops, refs = refs[:n_row], refs[n_row:2 * n_row], refs[2 * n_row:]
    out_ref, block, pivot, panel, old, high, low, top, sem, in_sem, out_sem = refs
    rows, _, cols = mat_ref.shape
    width = linv_ref.shape[0]
    count = tops[0].shape[0]
    tiles = cols // width
    row, col = lax.axis_index("prow"), lax.axis_index("pcol")

    def tile(t):
        return pl.ds(pl.multiple_of(t * width, width), width)

    @pl.when(col % 2 == 0)
    def _():
        pltpu.make_async_copy(panel_ref, panel.at[pl.ds(0, rows)], sem.at[0]).start()

    @pl.when(col % 2 == 1)
    def _():
        pltpu.make_async_copy(panel_new_ref, panel.at[pl.ds(0, rows)], sem.at[0]).start()

    for p in range(n_row):
        @pl.when(row == p)
        def _(p=p):
            pltpu.make_async_copy(tops[p].at[:, 0, :], old, sem.at[1]).start()

    blocks = [
        pltpu.make_async_copy(mat_ref.at[:, 0, tile(t)], block.at[pl.ds(0, rows), tile(t)], in_sem.at[t])
        for t in range(tiles)
    ]
    pieces = [
        pltpu.make_async_copy(parts[k].at[:, 0, :], pivot.at[pl.ds(k * count, count), :], sem.at[2 + k])
        for k in range(n_row)
    ]
    for copy in blocks[:1] + pieces + blocks[1:]:
        copy.start()

    lanes = lax.broadcasted_iota(jnp.int32, (width, LANES), 1)
    places = jnp.concatenate(
        [jnp.where(lanes + t * LANES == wide_ref[...], 1.0, 0.0) for t in range(n_row * count // LANES)], axis=1
    )
    spread_inv = halves(jnp.dot(linv_ref[...], places, precision=HI, preferred_element_type=jnp.float32))
    top[...] = square_ref[width:, :] + square_new_ref[width:, :]
    pltpu.make_async_copy(panel_ref, panel.at[pl.ds(0, rows)], sem.at[0]).wait()
    put_rows(mine_ref, counts_ref[row], top, panel)
    lower = split_dot(halves(panel[:rows, :]), halves(uinv_ref[...]))
    high[...], low[...] = halves(lower)
    pltpu.make_async_copy(tops[0].at[:, 0, :], old, sem.at[1]).wait()
    for copy in blocks:
        copy.wait()
    put_rows(mine_ref, counts_ref[row], old, block)

    @pl.when(col == 0)
    def _():
        block[:rows, :width] = lower

    for copy in pieces:
        copy.wait()

    def step(t, c):
        upper = split_dot(spread_inv, halves(pivot[:, tile(t)]))
        first_col = (col == 0) & (t == 0)

        @pl.when(jnp.logical_not(first_col))
        def _():
            block[:rows, tile(t)] = block[:rows, tile(t)] - split_dot((high[...], low[...]), halves(upper))

        @pl.when(row == 0)
        def _():
            block[:width, tile(t)] = jnp.where(first_col, packed_ref[...], upper)

        pltpu.make_async_copy(block.at[pl.ds(0, rows), tile(t)], out_ref.at[:, 0, tile(t)], out_sem.at[t]).start()
        return c

    lax.fori_loop(0, tiles, step, 0)
    for t in range(tiles):
        pltpu.make_async_copy(block.at[pl.ds(0, rows), tile(t)], out_ref.at[:, 0, tile(t)], out_sem.at[t]).wait()


def finish(mine, counts, wide, mat, panels, squares, factors, pivot_parts, tops):
    rows, _, cols = mat.shape
    width, n_row, count = factors[0].shape[0], len(tops), mine.shape[0]
    return pl.pallas_call(
        functools.partial(finish_kernel, n_row),
        out_shape=jax.ShapeDtypeStruct(mat.shape, jnp.float32),
        in_specs=[smem(), smem(), vmem(), raw(), raw(), raw()] + [vmem()] * 5 + [raw()] * (2 * n_row),
        out_specs=raw(),
        scratch_shapes=[
            pltpu.VMEM((rows + SUB, cols), jnp.float32),
            pltpu.VMEM((n_row * count, cols), jnp.float32),
            pltpu.VMEM((rows + SUB, width), jnp.float32),
            pltpu.VMEM((count, cols), jnp.float32),
            pltpu.VMEM((rows, width), jnp.bfloat16),
            pltpu.VMEM((rows, width), jnp.bfloat16),
            pltpu.VMEM((count, width), jnp.float32),
            pltpu.SemaphoreType.DMA((2 + n_row,)),
            pltpu.SemaphoreType.DMA((cols // width,)),
            pltpu.SemaphoreType.DMA((cols // width,)),
        ],
        cost_estimate=pl.CostEstimate(
            flops=6 * rows * cols * width, bytes_accessed=8 * rows * cols, transcendentals=0
        ),
        name="finish",
    )(mine, counts, wide, mat, *panels, *squares, *factors, *pivot_parts, *tops)


def capacity(n_row, width):
    mean = width / n_row
    return -(-int(mean + 4 * (mean * (1 - 1 / n_row)) ** 0.5) // SUB) * SUB


def tree(x, order, is_new):
    have = [0]
    for n, bit in enumerate(order):
        moved = lax.ppermute(x, "pcol", [(i, i ^ bit) for i in have])
        have = have + [i ^ bit for i in have]
        if n + 1 < len(order):
            x = jnp.where(is_new(bit), moved, x)
    return x, moved


def capped_step(n_row, n_col, matrix, begun):
    _, rows, _, cols = matrix.shape
    mat = matrix.reshape(rows, 1, cols)
    panel, mine, lists, pos, wide, counts = begun[:6]
    messages = begun[6:]
    col = lax.axis_index("pcol")
    order = bits_of(n_col)[::-1]

    def is_new(bit):
        return (col & bit) != 0

    both = ("prow", "pcol")
    moved = [
        lax.ppermute(messages[k], both, [(i * n_col, (i ^ k) * n_col) for i in range(n_row)]) for k in range(1, n_row)
    ]
    rows_own = own_rows(mat, mine)
    parts = [rows_own] + [lax.ppermute(rows_own, "prow", [(i, i ^ k) for i in range(n_row)]) for k in range(1, n_row)]
    message, message_new = tree(pack(pos, [messages[0]] + moved), order, is_new)
    factors = factor(message, message_new)
    panel, panel_new = tree(panel, order, is_new)
    tops = top_rows(mat, lists)
    tops = tops[:1] + tuple(lax.ppermute(tops[p], "prow", [(0, p)]) for p in range(1, n_row))
    out = finish(mine, counts, wide, mat, (panel, panel_new), (message, message_new), factors, parts, tops)
    return out.reshape(matrix.shape)


def on_device(n_row, n_col, matrix, pivots):
    _, rows, _, cols = matrix.shape
    count = capacity(n_row, pivots.shape[0])
    begun = begin(matrix.reshape(rows, 1, cols), pivots, n_row, count)
    return lax.cond(
        jnp.max(begun[5]) <= count,
        lambda m, p, b: capped_step(n_row, n_col, m, b),
        lambda m, p, b: dense_step(n_row, n_col, m, p),
        matrix, pivots, begun,
    )


def solution(mesh):
    spec = P("prow", None, "pcol", None)
    n_row, n_col = mesh.shape["prow"], mesh.shape["pcol"]
    return jax.shard_map(
        functools.partial(on_device, n_row, n_col), mesh=mesh, in_specs=(spec, P()), out_specs=spec, check_vma=False
    )
```

```python
import functools

import jax
import jax.numpy as jnp
from jax import lax
from jax.experimental import pallas as pl
from jax.experimental.pallas import tpu as pltpu
from jax.sharding import PartitionSpec as P

LANES = 128
SUB = 8
HI = lax.Precision.HIGHEST


def pick_lane(tile, lane):
    return jnp.take_along_axis(tile, jnp.full((SUB, LANES), lane, jnp.int32), axis=1)


def row_of(tile, j):
    return jnp.broadcast_to(tile[j:j + 1, :], (SUB, LANES))


def factor_kernel(width, s_ref, extra_ref, packed_ref, linv_ref, uinv_ref, a_ref, m_ref, v_ref):
    groups = a_ref.shape[0]
    tiles = groups * SUB // LANES
    per_tile = LANES // SUB
    per_block = width // SUB
    sub = lax.broadcasted_iota(jnp.int32, (SUB, LANES), 0)
    lane = lax.broadcasted_iota(jnp.int32, (SUB, LANES), 1)

    for i in range(groups):
        a_ref[i] = s_ref[i * SUB:(i + 1) * SUB, :] + extra_ref[i * SUB:(i + 1) * SUB, :]
        diag = lane - (i % per_tile) * SUB == sub
        for t in range(tiles):
            block = jnp.where(diag, 1.0, 0.0) if i // per_tile == t else jnp.zeros((SUB, LANES), jnp.float32)
            m_ref[i, :, t * LANES:(t + 1) * LANES] = block
            if t > i // per_tile:
                linv_ref[i * SUB:(i + 1) * SUB, t * LANES:(t + 1) * LANES] = block

    def span(t):
        return slice(t * LANES, (t + 1) * LANES)

    for o in range(groups // per_block):
        base = o * per_block
        h = base // per_tile
        live = [(a_ref, t) for t in range(h + 1, tiles)] + [(m_ref, t) for t in range(h + 1)]

        def panel(i, c, base=base, h=h, live=live):
            b = base + i
            g = (b - h * per_tile) * SUB
            rows = pl.ds(pl.multiple_of(b * SUB, SUB), SUB)
            own = a_ref[b, :, span(h)]
            cols = [pick_lane(own, g + j) for j in range(SUB)]
            in_panel = (lane >= g) & (lane < g + SUB)
            after = lane >= g + SUB
            head = jnp.where(in_panel, jnp.where(lane - g == sub, -1.0, 0.0), jnp.where(after, own, 0.0))
            rest = [ref[b, :, span(t)] for ref, t in live]
            packed = own
            final = [head] + rest
            for j in range(SUB):
                at = sub == j
                coef = cols[j]
                r = 1.0 / row_of(coef, j)
                final = [jnp.where(at, x, y) for x, y in zip([head] + rest, final)]
                packed = jnp.where((lane == g + j) & (sub > j), coef * r, packed)
                for k in range(j, SUB):
                    packed = jnp.where((lane == g + k) & at, cols[k], packed)
                head_coef = jnp.where((sub < j) | after, coef, 0.0)
                v = row_of(head, j) * r
                head = jnp.where(at, v, head - head_coef * v)
                for n, x in enumerate(rest):
                    v = row_of(x, j) * r
                    rest[n] = jnp.where(at, v, x - coef * v)
                for k in range(j + 1, SUB):
                    v = row_of(cols[k], j) * r
                    cols[k] = jnp.where(at, v, cols[k] - coef * v)
            for t in range(h):
                packed_ref[rows, span(t)] = a_ref[b, :, span(t)]
            packed_ref[rows, span(h)] = jnp.where(after, final[0], packed)
            for (ref, t), x in zip(live, final[1:]):
                (packed_ref if ref is a_ref else linv_ref)[rows, span(t)] = x
            a_ref[b, :, span(h)] = head
            v_ref[0] = head
            for n, ((ref, t), x) in enumerate(zip(live, rest)):
                ref[b, :, span(t)] = x
                v_ref[n + 1] = x
            others = [base + lax.rem(i + s, per_block) for s in range(1, per_block)]
            heads = [a_ref[r, :, span(h)] for r in others]
            facs = [[pick_lane(x, g + j) for j in range(SUB)] for x in heads]
            for n, (ref, t) in enumerate([(a_ref, h)] + live):
                old = [jnp.where(in_panel, 0.0, x) for x in heads] if n == 0 else [ref[r, :, span(t)] for r in others]
                vs = [row_of([head] + rest and ([head] + rest)[n], j) for j in range(SUB)]
                for x, fac, r in zip(old, facs, others):
                    acc = [fac[j] * vs[j] for j in range(SUB)]
                    while len(acc) > 1:
                        acc = [p + q for p, q in zip(acc[::2], acc[1::2])]
                    ref[r, :, span(t)] = x - acc[0]
            return c

        lax.fori_loop(0, per_block, panel, 0)

        lo = (base % per_tile) * SUB
        pad = [jnp.zeros((n, LANES), jnp.float32) for n in (lo, LANES - lo - width)]

        def stack(x):
            return jnp.concatenate([p for p in (pad[0], x, pad[1]) if p.shape[0]], axis=0)

        def flat(ref, first, last, t):
            return ref[first:last, :, span(t)].reshape((last - first) * SUB, LANES)

        end = base + per_block
        right = [stack(flat(ref, base, end, t)) for ref, t in [(a_ref, h)] + live]
        for first, last in ((end, groups), (0, base)):
            if first == last:
                continue
            left = flat(a_ref, first, last, h)
            column = lax.broadcasted_iota(jnp.int32, left.shape, 1)
            for n, (ref, t) in enumerate([(a_ref, h)] + live):
                if ref is m_ref and first == 0:
                    continue
                old = left if n else None
                old = jnp.where((column >= lo) & (column < lo + width), 0.0, left) if n == 0 else flat(ref, first, last, t)
                new = old - jnp.dot(left, right[n], precision=HI, preferred_element_type=jnp.float32)
                ref[first:last, :, span(t)] = new.reshape(last - first, SUB, LANES)

    ri = lax.broadcasted_iota(jnp.int32, (SUB, LANES), 0)
    for i in range(groups):
        for t in range(tiles):
            x = a_ref[i, :, span(t)]
            keep = lane + t * LANES >= ri + i * SUB
            uinv_ref[i * SUB:(i + 1) * SUB, span(t)] = jnp.where(keep, -x, 0.0)


def vmem():
    return pl.BlockSpec(memory_space=pltpu.VMEM)


def smem():
    return pl.BlockSpec(memory_space=pltpu.SMEM)


def factor(square, extra, width=32):
    size = square.shape[1]
    out = jax.ShapeDtypeStruct((size, size), jnp.float32)
    return pl.pallas_call(
        functools.partial(factor_kernel, width),
        out_shape=(out, out, out),
        in_specs=[vmem(), vmem()],
        out_specs=(vmem(),) * 3,
        scratch_shapes=[
            pltpu.VMEM((size // SUB, SUB, size), jnp.float32),
            pltpu.VMEM((size // SUB, SUB, size), jnp.float32),
            pltpu.VMEM((1 + size // LANES, SUB, LANES), jnp.float32),
        ],
        cost_estimate=pl.CostEstimate(flops=4 * size**3, bytes_accessed=200_000_000, transcendentals=0),
        name="factor",
    )(square, extra)


def pick_kernel(slot_ref, own_ref, block_ref, out_ref):
    def group(q, c):
        for u in range(SUB):
            j = q * SUB + u
            row = block_ref[pl.ds(slot_ref[j], 1), :]
            out_ref[pl.ds(j, 1), :] = row * own_ref[j].astype(jnp.float32)
        return c

    lax.fori_loop(0, out_ref.shape[0] // SUB, group, 0)


def pick(block, slots, owned, tiles):
    rows, width = block.shape[0], slots.shape[0]
    return pl.pallas_call(
        pick_kernel,
        grid=(tiles,),
        out_shape=jax.ShapeDtypeStruct((width, tiles * width), jnp.float32),
        in_specs=[smem(), smem(), pl.BlockSpec((rows, width), lambda t: (0, t))],
        out_specs=pl.BlockSpec((width, width), lambda t: (0, t)),
        cost_estimate=pl.CostEstimate(
            flops=width * width * tiles, bytes_accessed=4 * (rows + width) * width * tiles, transcendentals=0
        ),
        name="pick",
    )(slots, owned, block)


def place_rows(slot_ref, rows_ref, target_ref):
    def group(q, c):
        for u in range(SUB):
            j = q * SUB + u
            target_ref[pl.ds(slot_ref[j], 1), :] = rows_ref[pl.ds(j, 1), :]
        return c

    lax.fori_loop(0, rows_ref.shape[0] // SUB, group, 0)


def place_kernel(slot_ref, block_ref, rows_ref, out_ref, buf_ref):
    rows = block_ref.shape[0]
    buf_ref[:rows, :] = block_ref[...]
    place_rows(slot_ref, rows_ref, buf_ref)
    out_ref[...] = buf_ref[:rows, :]


def place(block, rows, slots):
    height, width = block.shape[0], slots.shape[0]
    return pl.pallas_call(
        place_kernel,
        grid=(1,),
        out_shape=jax.ShapeDtypeStruct((height, width), jnp.float32),
        in_specs=[
            smem(),
            pl.BlockSpec((height, width), lambda t: (0, 0)),
            pl.BlockSpec((width, width), lambda t: (0, 0)),
        ],
        out_specs=pl.BlockSpec((height, width), lambda t: (0, 0)),
        scratch_shapes=[pltpu.VMEM((height + SUB, width), jnp.float32)],
        cost_estimate=pl.CostEstimate(flops=0, bytes_accessed=8 * height * width, transcendentals=0),
        name="place",
    )(slots, block, rows)


def halves(x):
    high = x.astype(jnp.bfloat16)
    low = (x - high.astype(jnp.float32)).astype(jnp.bfloat16)
    return high, low


def split_dot(left, right):
    acc = jnp.dot(left[0], right[1], preferred_element_type=jnp.float32)
    acc += jnp.dot(left[1], right[0], preferred_element_type=jnp.float32)
    return acc + jnp.dot(left[0], right[0], preferred_element_type=jnp.float32)


def update_kernel(
    slot_ref, where_ref, block_ref, panel_ref, pivot_ref, top_ref, packed_ref, linv_ref, uinv_ref,
    out_ref, high_ref, low_ref, buf_ref,
):
    rows, width = panel_ref.shape
    t = pl.program_id(0)
    first_row = where_ref[0] == 0
    first_col = (where_ref[1] == 0) & (t == 0)

    @pl.when(t == 0)
    def _():
        lower = jnp.dot(panel_ref[...], uinv_ref[...], precision=HI, preferred_element_type=jnp.float32)
        high_ref[...], low_ref[...] = halves(lower)
        out_ref[...] = lower

    upper = jnp.dot(linv_ref[...], pivot_ref[...], precision=HI, preferred_element_type=jnp.float32)

    @pl.when(jnp.logical_not(first_col))
    def _():
        buf_ref[:rows, :] = block_ref[...]
        place_rows(slot_ref, top_ref, buf_ref)
        out_ref[...] = buf_ref[:rows, :] - split_dot((high_ref[...], low_ref[...]), halves(upper))

    @pl.when(first_row)
    def _():
        out_ref[:width, :] = jnp.where(first_col, packed_ref[...], upper)


def update(block, panel, pivot_rows, old_top, packed, linv, uinv, slots, where):
    rows, cols = block.shape
    width = slots.shape[0]
    square = pl.BlockSpec((width, width), lambda t: (0, 0))
    tall = pl.BlockSpec((rows, width), lambda t: (0, t))
    flat = pl.BlockSpec((width, width), lambda t: (0, t))
    return pl.pallas_call(
        update_kernel,
        grid=(cols // width,),
        out_shape=jax.ShapeDtypeStruct((rows, cols), jnp.float32),
        in_specs=[
            smem(), smem(), tall, pl.BlockSpec((rows, width), lambda t: (0, 0)), flat, flat, square, square, square,
        ],
        out_specs=tall,
        scratch_shapes=[
            pltpu.VMEM((rows, width), jnp.bfloat16),
            pltpu.VMEM((rows, width), jnp.bfloat16),
            pltpu.VMEM((rows + SUB, width), jnp.float32),
        ],
        cost_estimate=pl.CostEstimate(
            flops=6 * rows * cols * width, bytes_accessed=8 * rows * cols, transcendentals=0
        ),
        name="update",
    )(slots, where, block, panel, pivot_rows, old_top, packed, linv, uinv)


def bits_of(n):
    return [1 << i for i in range(n.bit_length() - 1)]


def sum_over_rows(x, order, n_row):
    for bit in order:
        x = x + lax.ppermute(x, "prow", [(i, i ^ bit) for i in range(n_row)])
    return x


def spread_rows(x, order, n_row):
    have = [0]
    for bit in order:
        x = x + lax.ppermute(x, "prow", [(i, i ^ bit) for i in have])
        have = have + [i ^ bit for i in have]
    return x


def spread_cols(x, order):
    have = [0]
    for bit in order:
        x = x + lax.ppermute(x, "pcol", [(i, i ^ bit) for i in have])
        have = have + [i ^ bit for i in have]
    return x


def dense_step(n_row, n_col, matrix, pivots):
    block = matrix[0, :, 0, :]
    rows, cols = block.shape
    width = pivots.shape[0]
    row = lax.axis_index("prow")
    col = lax.axis_index("pcol")
    owner = pivots // width % n_row
    slot = pivots // (width * n_row) * width + pivots % width
    mine = owner == row
    owned = mine.astype(jnp.int32)
    target = jnp.where(mine, slot, rows)
    where = jnp.stack([row, col]).astype(jnp.int32)
    row_bits, col_bits = bits_of(n_row), bits_of(n_col)
    at_first_row = row == 0
    at_first_col = col == 0

    square = pick(block, slot, owned * at_first_col.astype(jnp.int32), 1)
    square = sum_over_rows(square, row_bits, n_row)
    square = spread_cols(square, col_bits[::-1])
    packed, linv, uinv = factor(square, jnp.zeros_like(square))

    top = jnp.where(at_first_row, block[:width], 0.0)
    top_panel = spread_rows(top[:, :width], row_bits, n_row)
    panel = place(block, top_panel, target)
    panel = spread_cols(jnp.where(at_first_col, panel, 0.0), col_bits[::-1])

    picked = pick(block, slot, owned, cols // width)
    half = width // 2
    pivot_rows = jnp.concatenate([
        sum_over_rows(picked[:half], row_bits, n_row),
        sum_over_rows(picked[half:], row_bits[::-1], n_row),
    ])
    old_top = jnp.concatenate([
        spread_rows(top[:half], row_bits, n_row),
        spread_rows(top[half:], row_bits[::-1], n_row),
    ])
    result = update(block, panel, pivot_rows, old_top, packed, linv, uinv, target, where)
    return result[None, :, None, :]


def raw():
    return pl.BlockSpec(memory_space=pl.ANY)


def tables_kernel(n_row, pivot_ref, mine_ref, lists_ref, pos_ref, wide_ref, counts_ref):
    width = pivot_ref.shape[0]
    count = mine_ref.shape[0]
    width_log, row_log = width.bit_length() - 1, n_row.bit_length() - 1
    row = lax.axis_index("prow")
    for p in range(n_row):
        counts_ref[p] = 0

    def locate(q, c):
        for u in range(SUB):
            j = q * SUB + u
            block = lax.shift_right_logical(pivot_ref[j], width_log)
            owner = block & (n_row - 1)
            rank = counts_ref[owner]
            counts_ref[owner] = rank + 1
            held = jnp.minimum(rank, count - 1)
            lists_ref[owner, held] = j
            place = (owner ^ row) * count + held
            pos_ref[j] = place
            wide_ref[pl.ds(j, 1), :] = jnp.full((1, LANES), place, jnp.int32)
        return c

    lax.fori_loop(0, width // SUB, locate, 0)

    def clear(i, c):
        for p in range(n_row):
            lists_ref[p, i] = jnp.where(i < counts_ref[p], lists_ref[p, i], 0)
        pivot = pivot_ref[lists_ref[row, i]]
        block = lax.shift_right_logical(pivot, width_log)
        slot = lax.shift_left(lax.shift_right_logical(block, row_log), width_log) + (pivot & (width - 1))
        mine_ref[i] = jnp.where(i < counts_ref[row], slot, 0)
        return c

    lax.fori_loop(0, count, clear, 0)


def tables(pivots, n_row, count):
    width = pivots.shape[0]

    def ints(*shape):
        return jax.ShapeDtypeStruct(shape, jnp.int32)

    return pl.pallas_call(
        functools.partial(tables_kernel, n_row),
        out_shape=(ints(count), ints(n_row, count), ints(width), ints(width, LANES), ints(n_row)),
        in_specs=[smem()],
        out_specs=(smem(), smem(), smem(), vmem(), smem()),
        cost_estimate=pl.CostEstimate(flops=0, bytes_accessed=10_000_000, transcendentals=0),
        name="tables",
    )(pivots)


def begin_kernel(n_row, mine_ref, lists_ref, mat_ref, panel_ref, *refs):
    messages, sem = refs[:n_row], refs[-1]
    width = panel_ref.shape[1]
    count = mine_ref.shape[0]
    copy = pltpu.make_async_copy(mat_ref.at[:, 0, pl.ds(0, width)], panel_ref, sem)
    copy.start()
    copy.wait()

    def gather(q, c):
        for u in range(SUB):
            i = q * SUB + u
            messages[0][pl.ds(i, 1), :] = panel_ref[pl.ds(mine_ref[i], 1), :]
        return c

    lax.fori_loop(0, count // SUB, gather, 0)
    for k in range(1, n_row):
        messages[k][:count, :] = messages[0][:count, :]

    @pl.when(lax.axis_index("prow") == 0)
    def _():
        for p in range(n_row):
            def gather_top(q, c, p=p):
                for u in range(SUB):
                    i = q * SUB + u
                    messages[p][pl.ds(count + i, 1), :] = panel_ref[pl.ds(lists_ref[p, i], 1), :]
                return c

            lax.fori_loop(0, count // SUB, gather_top, 0)


def begin(mat, mine, lists, width):
    rows, (n_row, count) = mat.shape[0], lists.shape
    message = jax.ShapeDtypeStruct((2 * count, width), jnp.float32)
    return pl.pallas_call(
        functools.partial(begin_kernel, n_row),
        out_shape=(jax.ShapeDtypeStruct((rows, width), jnp.float32),) + (message,) * n_row,
        in_specs=[smem(), smem(), raw()],
        out_specs=(vmem(),) * (n_row + 1),
        scratch_shapes=[pltpu.SemaphoreType.DMA],
        cost_estimate=pl.CostEstimate(flops=0, bytes_accessed=10_000_000, transcendentals=0),
        name="begin",
    )(mine, lists, mat)


def parcel_kernel(n_row, mine_ref, lists_ref, mat_ref, own_ref, *refs):
    outs, spare_ref, sem = refs[:n_row], refs[n_row], refs[n_row + 1]
    count = own_ref.shape[0]
    first = lax.axis_index("prow") == 0

    def group(q, c):
        for u in range(SUB):
            i = q * SUB + u
            pltpu.make_async_copy(mat_ref.at[mine_ref[i]], own_ref.at[i], sem.at[0]).start()
        return c

    lax.fori_loop(0, count // SUB, group, 0)

    @pl.when(first)
    def _():
        for p in range(n_row):
            base = 0 if p == 0 else count

            def group(q, c, p=p, base=base):
                for u in range(SUB):
                    i = q * SUB + u
                    pltpu.make_async_copy(mat_ref.at[lists_ref[p, i]], outs[p].at[base + i], sem.at[1]).start()
                return c

            lax.fori_loop(0, count // SUB, group, 0)

    pltpu.make_async_copy(mat_ref.at[pl.ds(0, count)], own_ref, sem.at[0]).wait()
    copies = [pltpu.make_async_copy(own_ref, outs[p].at[pl.ds(0, count)], sem.at[1 + p]) for p in range(1, n_row)]
    for copy in copies[1:]:
        copy.start()
    for copy in copies[1:]:
        copy.wait()

    @pl.when(first)
    def _():
        pltpu.make_async_copy(mat_ref.at[pl.ds(0, n_row * count)], spare_ref, sem.at[1]).wait()

    copies[0].start()
    copies[0].wait()


def parcel(mat, mine, lists):
    n_row, count = lists.shape
    cols = mat.shape[2]

    def shape(rows):
        return jax.ShapeDtypeStruct((rows, 1, cols), jnp.float32)

    return pl.pallas_call(
        functools.partial(parcel_kernel, n_row),
        out_shape=(shape(count), shape(count)) + (shape(2 * count),) * (n_row - 1),
        in_specs=[smem(), smem(), raw()],
        out_specs=(vmem(),) * (n_row + 1),
        scratch_shapes=[pltpu.VMEM((n_row * count, 1, cols), jnp.float32), pltpu.SemaphoreType.DMA((n_row + 1,))],
        cost_estimate=pl.CostEstimate(flops=0, bytes_accessed=20_000_000, transcendentals=0),
        name="parcel",
    )(mine, lists, mat)


def pack_kernel(n_row, pos_ref, *refs):
    parts, out_ref, all_ref = refs[:n_row], refs[n_row], refs[n_row + 1]
    width = pos_ref.shape[0]
    count = out_ref.shape[0] - width
    row, col = lax.axis_index("prow"), lax.axis_index("pcol")

    @pl.when(col == 0)
    def _():
        for k in range(n_row):
            all_ref[k * count:(k + 1) * count, :] = parts[k][:count, :]

        def group(q, c):
            for u in range(SUB):
                j = q * SUB + u
                out_ref[pl.ds(j, 1), :] = all_ref[pl.ds(pos_ref[j], 1), :]
            return c

        lax.fori_loop(0, width // SUB, group, 0)
        for k in range(n_row):
            @pl.when(row == k)
            def _(k=k):
                out_ref[width:, :] = parts[k][count:, :]

    @pl.when(col != 0)
    def _():
        out_ref[...] = jnp.zeros_like(out_ref)


def pack(pos, parts):
    n_row, width = len(parts), pos.shape[0]
    count = parts[0].shape[0] // 2
    return pl.pallas_call(
        functools.partial(pack_kernel, n_row),
        out_shape=jax.ShapeDtypeStruct((width + count, width), jnp.float32),
        in_specs=[smem()] + [vmem()] * n_row,
        out_specs=vmem(),
        scratch_shapes=[pltpu.VMEM((n_row * count, width), jnp.float32)],
        cost_estimate=pl.CostEstimate(flops=0, bytes_accessed=24 * width * width, transcendentals=0),
        name="pack",
    )(pos, *parts)


def put_rows(slot_ref, held, rows_ref, target_ref):
    spare = target_ref.shape[0] - SUB

    def group(q, c):
        for u in range(SUB):
            i = q * SUB + u
            slot = jnp.where(i < held, slot_ref[i], spare)
            target_ref[pl.ds(slot, 1), :] = rows_ref[pl.ds(i, 1), :]
        return c

    lax.fori_loop(0, rows_ref.shape[0] // SUB, group, 0)


def finish_kernel(
    n_row, mine_ref, counts_ref, wide_ref, mat_ref, panel_ref, panel_new_ref, square_ref, square_new_ref,
    packed_ref, linv_ref, uinv_ref, *refs,
):
    own_ref, top_ref, parcels, refs = refs[0], refs[1], refs[2:n_row + 1], refs[n_row + 1:]
    out_ref, block, pivot, panel, old, high, low, top, sem, in_sem, out_sem = refs
    rows, _, cols = mat_ref.shape
    width = linv_ref.shape[0]
    count = own_ref.shape[0]
    parts = [own_ref] + [x.at[pl.ds(0, count)] for x in parcels]
    tops = [top_ref] + [x.at[pl.ds(count, count)] for x in parcels]
    tiles = cols // width
    row, col = lax.axis_index("prow"), lax.axis_index("pcol")

    def tile(t):
        return pl.ds(pl.multiple_of(t * width, width), width)

    @pl.when(col % 2 == 0)
    def _():
        pltpu.make_async_copy(panel_ref, panel.at[pl.ds(0, rows)], sem.at[0]).start()

    @pl.when(col % 2 == 1)
    def _():
        pltpu.make_async_copy(panel_new_ref, panel.at[pl.ds(0, rows)], sem.at[0]).start()

    for p in range(n_row):
        @pl.when(row == p)
        def _(p=p):
            pltpu.make_async_copy(tops[p].at[:, 0, :], old, sem.at[1]).start()

    blocks = [
        pltpu.make_async_copy(mat_ref.at[:, 0, tile(t)], block.at[pl.ds(0, rows), tile(t)], in_sem.at[t])
        for t in range(tiles)
    ]
    pieces = [
        pltpu.make_async_copy(parts[k].at[:, 0, :], pivot.at[pl.ds(k * count, count), :], sem.at[2 + k])
        for k in range(n_row)
    ]
    if pivot.shape[0] > n_row * count:
        pivot[n_row * count:, :] = jnp.zeros((pivot.shape[0] - n_row * count, cols), jnp.float32)
    for copy in blocks[:1] + pieces + blocks[1:]:
        copy.start()

    lanes = lax.broadcasted_iota(jnp.int32, (width, LANES), 1)
    places = jnp.concatenate(
        [jnp.where(lanes + t * LANES == wide_ref[...], 1.0, 0.0) for t in range(pivot.shape[0] // LANES)], axis=1
    )
    spread_inv = halves(jnp.dot(linv_ref[...], places, precision=HI, preferred_element_type=jnp.float32))
    top[...] = square_ref[width:, :] + square_new_ref[width:, :]
    pltpu.make_async_copy(panel_ref, panel.at[pl.ds(0, rows)], sem.at[0]).wait()
    put_rows(mine_ref, counts_ref[row], top, panel)
    lower = split_dot(halves(panel[:rows, :]), halves(uinv_ref[...]))
    high[...], low[...] = halves(lower)
    pltpu.make_async_copy(tops[0].at[:, 0, :], old, sem.at[1]).wait()
    for copy in blocks:
        copy.wait()
    put_rows(mine_ref, counts_ref[row], old, block)

    @pl.when(col == 0)
    def _():
        block[:rows, :width] = lower

    for copy in pieces:
        copy.wait()

    def step(t, c):
        upper = split_dot(spread_inv, halves(pivot[:, tile(t)]))
        first_col = (col == 0) & (t == 0)

        @pl.when(jnp.logical_not(first_col))
        def _():
            block[:rows, tile(t)] = block[:rows, tile(t)] - split_dot((high[...], low[...]), halves(upper))

        @pl.when(row == 0)
        def _():
            block[:width, tile(t)] = jnp.where(first_col, packed_ref[...], upper)

        pltpu.make_async_copy(block.at[pl.ds(0, rows), tile(t)], out_ref.at[:, 0, tile(t)], out_sem.at[t]).start()
        return c

    lax.fori_loop(0, tiles, step, 0)
    for t in range(tiles):
        pltpu.make_async_copy(block.at[pl.ds(0, rows), tile(t)], out_ref.at[:, 0, tile(t)], out_sem.at[t]).wait()


def finish(mine, counts, wide, mat, panels, squares, factors, parcels):
    rows, _, cols = mat.shape
    width, n_row, count = factors[0].shape[0], len(parcels) - 1, mine.shape[0]
    return pl.pallas_call(
        functools.partial(finish_kernel, n_row),
        out_shape=jax.ShapeDtypeStruct(mat.shape, jnp.float32),
        in_specs=[smem(), smem(), vmem(), raw(), raw(), raw()] + [vmem()] * 5 + [raw()] * (n_row + 1),
        out_specs=raw(),
        scratch_shapes=[
            pltpu.VMEM((rows + SUB, cols), jnp.float32),
            pltpu.VMEM((-(-n_row * count // LANES) * LANES, cols), jnp.float32),
            pltpu.VMEM((rows + SUB, width), jnp.float32),
            pltpu.VMEM((count, cols), jnp.float32),
            pltpu.VMEM((rows, width), jnp.bfloat16),
            pltpu.VMEM((rows, width), jnp.bfloat16),
            pltpu.VMEM((count, width), jnp.float32),
            pltpu.SemaphoreType.DMA((2 + n_row,)),
            pltpu.SemaphoreType.DMA((cols // width,)),
            pltpu.SemaphoreType.DMA((cols // width,)),
        ],
        cost_estimate=pl.CostEstimate(
            flops=6 * rows * cols * width, bytes_accessed=8 * rows * cols, transcendentals=0
        ),
        name="finish",
    )(mine, counts, wide, mat, *panels, *squares, *factors, *parcels)


def capacity(n_row, width):
    mean = width / n_row
    return -(-int(mean + 3.4 * (mean * (1 - 1 / n_row)) ** 0.5) // SUB) * SUB


def capped_step(n_row, n_col, matrix, found):
    _, rows, _, cols = matrix.shape
    mat = matrix.reshape(rows, 1, cols)
    mine, lists, pos, wide, counts = found
    width = pos.shape[0]
    col = lax.axis_index("pcol")
    both = ("prow", "pcol")

    def exchange(x, k):
        return lax.ppermute(x, both, [(i * n_col, (i ^ k) * n_col) for i in range(n_row)])

    parcels = parcel(mat, mine, lists)
    sent = [lax.ppermute(parcels[1 + k], "prow", [(i, i ^ k) for i in range(n_row)]) for k in range(1, n_row)]
    mine, own = lax.optimization_barrier((mine, parcels[0]))
    panel, *messages = begin(mat, mine, lists, width)
    moved = [exchange(messages[k], k) for k in range(1, n_row)]
    message = pack(pos, [messages[0]] + moved)
    panel, message, sent[0], sent[1] = lax.optimization_barrier((panel, message, sent[0], sent[1]))
    have = [0]
    for bit in bits_of(n_col)[:0:-1]:
        pairs = [(i, i + bit) for i in have]
        have = have + [i + bit for i in have]
        message_moved = lax.ppermute(message, "pcol", pairs)
        panel_moved = lax.ppermute(panel, "pcol", pairs)
        message = jnp.where((col & bit) != 0, message_moved, message)
        message, panel_moved = lax.optimization_barrier((message, panel_moved))
        panel = jnp.where((col & bit) != 0, panel_moved, panel)
    pairs = [(i, i + 1) for i in have]
    message_new = lax.ppermute(message, "pcol", pairs)
    factors = factor(message, message_new)
    panel_new = lax.ppermute(panel, "pcol", pairs)
    out = finish(
        mine, counts, wide, mat, (panel, panel_new), (message, message_new), factors, [own, parcels[1]] + sent
    )
    return out.reshape(matrix.shape)


def on_device(n_row, n_col, matrix, pivots):
    count = capacity(n_row, pivots.shape[0])
    found = tables(pivots, n_row, count)
    return lax.cond(
        jnp.max(found[-1]) <= count,
        lambda m, p, f: capped_step(n_row, n_col, m, f),
        lambda m, p, f: dense_step(n_row, n_col, m, p),
        matrix, pivots, found,
    )


def solution(mesh):
    spec = P("prow", None, "pcol", None)
    n_row, n_col = mesh.shape["prow"], mesh.shape["pcol"]
    return jax.shard_map(
        functools.partial(on_device, n_row, n_col), mesh=mesh, in_specs=(spec, P()), out_specs=spec, check_vma=False
    )
```

```python
import functools

import jax
import jax.numpy as jnp
from jax import lax
from jax.experimental import pallas as pl
from jax.experimental.pallas import tpu as pltpu
from jax.sharding import PartitionSpec as P

LANES = 128
SUB = 8
HI = lax.Precision.HIGHEST


def pick_lane(tile, lane):
    return jnp.take_along_axis(tile, jnp.full((SUB, LANES), lane, jnp.int32), axis=1)


def row_of(tile, j):
    return jnp.broadcast_to(tile[j:j + 1, :], (SUB, LANES))


def factor_kernel(width, s_ref, extra_ref, packed_ref, linv_ref, uinv_ref, a_ref, m_ref, v_ref):
    groups = a_ref.shape[0]
    tiles = groups * SUB // LANES
    per_tile = LANES // SUB
    per_block = width // SUB
    sub = lax.broadcasted_iota(jnp.int32, (SUB, LANES), 0)
    lane = lax.broadcasted_iota(jnp.int32, (SUB, LANES), 1)

    for i in range(groups):
        a_ref[i] = s_ref[i * SUB:(i + 1) * SUB, :] + extra_ref[i * SUB:(i + 1) * SUB, :]
        diag = lane - (i % per_tile) * SUB == sub
        for t in range(tiles):
            block = jnp.where(diag, 1.0, 0.0) if i // per_tile == t else jnp.zeros((SUB, LANES), jnp.float32)
            m_ref[i, :, t * LANES:(t + 1) * LANES] = block
            if t > i // per_tile:
                linv_ref[i * SUB:(i + 1) * SUB, t * LANES:(t + 1) * LANES] = block

    def span(t):
        return slice(t * LANES, (t + 1) * LANES)

    for o in range(groups // per_block):
        base = o * per_block
        h = base // per_tile
        live = [(a_ref, t) for t in range(h + 1, tiles)] + [(m_ref, t) for t in range(h + 1)]

        def panel(i, c, base=base, h=h, live=live):
            b = base + i
            g = (b - h * per_tile) * SUB
            rows = pl.ds(pl.multiple_of(b * SUB, SUB), SUB)
            own = a_ref[b, :, span(h)]
            cols = [pick_lane(own, g + j) for j in range(SUB)]
            in_panel = (lane >= g) & (lane < g + SUB)
            after = lane >= g + SUB
            head = jnp.where(in_panel, jnp.where(lane - g == sub, -1.0, 0.0), jnp.where(after, own, 0.0))
            rest = [ref[b, :, span(t)] for ref, t in live]
            packed = own
            final = [head] + rest
            for j in range(SUB):
                at = sub == j
                coef = cols[j]
                r = 1.0 / row_of(coef, j)
                final = [jnp.where(at, x, y) for x, y in zip([head] + rest, final)]
                packed = jnp.where((lane == g + j) & (sub > j), coef * r, packed)
                for k in range(j, SUB):
                    packed = jnp.where((lane == g + k) & at, cols[k], packed)
                head_coef = jnp.where((sub < j) | after, coef, 0.0)
                v = row_of(head, j) * r
                head = jnp.where(at, v, head - head_coef * v)
                for n, x in enumerate(rest):
                    v = row_of(x, j) * r
                    rest[n] = jnp.where(at, v, x - coef * v)
                for k in range(j + 1, SUB):
                    v = row_of(cols[k], j) * r
                    cols[k] = jnp.where(at, v, cols[k] - coef * v)
            for t in range(h):
                packed_ref[rows, span(t)] = a_ref[b, :, span(t)]
            packed_ref[rows, span(h)] = jnp.where(after, final[0], packed)
            for (ref, t), x in zip(live, final[1:]):
                (packed_ref if ref is a_ref else linv_ref)[rows, span(t)] = x
            a_ref[b, :, span(h)] = head
            v_ref[0] = head
            for n, ((ref, t), x) in enumerate(zip(live, rest)):
                ref[b, :, span(t)] = x
                v_ref[n + 1] = x
            others = [base + lax.rem(i + s, per_block) for s in range(1, per_block)]
            heads = [a_ref[r, :, span(h)] for r in others]
            facs = [[pick_lane(x, g + j) for j in range(SUB)] for x in heads]
            for n, (ref, t) in enumerate([(a_ref, h)] + live):
                old = [jnp.where(in_panel, 0.0, x) for x in heads] if n == 0 else [ref[r, :, span(t)] for r in others]
                vs = [row_of([head] + rest and ([head] + rest)[n], j) for j in range(SUB)]
                for x, fac, r in zip(old, facs, others):
                    acc = [fac[j] * vs[j] for j in range(SUB)]
                    while len(acc) > 1:
                        acc = [p + q for p, q in zip(acc[::2], acc[1::2])]
                    ref[r, :, span(t)] = x - acc[0]
            return c

        lax.fori_loop(0, per_block, panel, 0)

        lo = (base % per_tile) * SUB
        pad = [jnp.zeros((n, LANES), jnp.float32) for n in (lo, LANES - lo - width)]

        def stack(x):
            return jnp.concatenate([p for p in (pad[0], x, pad[1]) if p.shape[0]], axis=0)

        def flat(ref, first, last, t):
            return ref[first:last, :, span(t)].reshape((last - first) * SUB, LANES)

        end = base + per_block
        right = [stack(flat(ref, base, end, t)) for ref, t in [(a_ref, h)] + live]
        for first, last in ((end, groups), (0, base)):
            if first == last:
                continue
            left = flat(a_ref, first, last, h)
            column = lax.broadcasted_iota(jnp.int32, left.shape, 1)
            for n, (ref, t) in enumerate([(a_ref, h)] + live):
                if ref is m_ref and first == 0:
                    continue
                old = left if n else None
                old = jnp.where((column >= lo) & (column < lo + width), 0.0, left) if n == 0 else flat(ref, first, last, t)
                new = old - jnp.dot(left, right[n], precision=HI, preferred_element_type=jnp.float32)
                ref[first:last, :, span(t)] = new.reshape(last - first, SUB, LANES)

    ri = lax.broadcasted_iota(jnp.int32, (SUB, LANES), 0)
    for i in range(groups):
        for t in range(tiles):
            x = a_ref[i, :, span(t)]
            keep = lane + t * LANES >= ri + i * SUB
            uinv_ref[i * SUB:(i + 1) * SUB, span(t)] = jnp.where(keep, -x, 0.0)


def vmem():
    return pl.BlockSpec(memory_space=pltpu.VMEM)


def smem():
    return pl.BlockSpec(memory_space=pltpu.SMEM)


def factor(square, extra, width=32):
    size = square.shape[1]
    out = jax.ShapeDtypeStruct((size, size), jnp.float32)
    return pl.pallas_call(
        functools.partial(factor_kernel, width),
        out_shape=(out, out, out),
        in_specs=[vmem(), vmem()],
        out_specs=(vmem(),) * 3,
        scratch_shapes=[
            pltpu.VMEM((size // SUB, SUB, size), jnp.float32),
            pltpu.VMEM((size // SUB, SUB, size), jnp.float32),
            pltpu.VMEM((1 + size // LANES, SUB, LANES), jnp.float32),
        ],
        cost_estimate=pl.CostEstimate(flops=4 * size**3, bytes_accessed=50_000_000, transcendentals=0),
        name="factor",
    )(square, extra)


def pick_kernel(slot_ref, own_ref, block_ref, out_ref):
    def group(q, c):
        for u in range(SUB):
            j = q * SUB + u
            row = block_ref[pl.ds(slot_ref[j], 1), :]
            out_ref[pl.ds(j, 1), :] = row * own_ref[j].astype(jnp.float32)
        return c

    lax.fori_loop(0, out_ref.shape[0] // SUB, group, 0)


def pick(block, slots, owned, tiles):
    rows, width = block.shape[0], slots.shape[0]
    return pl.pallas_call(
        pick_kernel,
        grid=(tiles,),
        out_shape=jax.ShapeDtypeStruct((width, tiles * width), jnp.float32),
        in_specs=[smem(), smem(), pl.BlockSpec((rows, width), lambda t: (0, t))],
        out_specs=pl.BlockSpec((width, width), lambda t: (0, t)),
        cost_estimate=pl.CostEstimate(
            flops=width * width * tiles, bytes_accessed=4 * (rows + width) * width * tiles, transcendentals=0
        ),
        name="pick",
    )(slots, owned, block)


def place_rows(slot_ref, rows_ref, target_ref):
    def group(q, c):
        for u in range(SUB):
            j = q * SUB + u
            target_ref[pl.ds(slot_ref[j], 1), :] = rows_ref[pl.ds(j, 1), :]
        return c

    lax.fori_loop(0, rows_ref.shape[0] // SUB, group, 0)


def place_kernel(slot_ref, block_ref, rows_ref, out_ref, buf_ref):
    rows = block_ref.shape[0]
    buf_ref[:rows, :] = block_ref[...]
    place_rows(slot_ref, rows_ref, buf_ref)
    out_ref[...] = buf_ref[:rows, :]


def place(block, rows, slots):
    height, width = block.shape[0], slots.shape[0]
    return pl.pallas_call(
        place_kernel,
        grid=(1,),
        out_shape=jax.ShapeDtypeStruct((height, width), jnp.float32),
        in_specs=[
            smem(),
            pl.BlockSpec((height, width), lambda t: (0, 0)),
            pl.BlockSpec((width, width), lambda t: (0, 0)),
        ],
        out_specs=pl.BlockSpec((height, width), lambda t: (0, 0)),
        scratch_shapes=[pltpu.VMEM((height + SUB, width), jnp.float32)],
        cost_estimate=pl.CostEstimate(flops=0, bytes_accessed=8 * height * width, transcendentals=0),
        name="place",
    )(slots, block, rows)


def halves(x):
    high = x.astype(jnp.bfloat16)
    low = (x - high.astype(jnp.float32)).astype(jnp.bfloat16)
    return high, low


def split_dot(left, right):
    acc = jnp.dot(left[0], right[1], preferred_element_type=jnp.float32)
    acc += jnp.dot(left[1], right[0], preferred_element_type=jnp.float32)
    return acc + jnp.dot(left[0], right[0], preferred_element_type=jnp.float32)


def update_kernel(
    slot_ref, where_ref, block_ref, panel_ref, pivot_ref, top_ref, packed_ref, linv_ref, uinv_ref,
    out_ref, high_ref, low_ref, buf_ref,
):
    rows, width = panel_ref.shape
    t = pl.program_id(0)
    first_row = where_ref[0] == 0
    first_col = (where_ref[1] == 0) & (t == 0)

    @pl.when(t == 0)
    def _():
        lower = jnp.dot(panel_ref[...], uinv_ref[...], precision=HI, preferred_element_type=jnp.float32)
        high_ref[...], low_ref[...] = halves(lower)
        out_ref[...] = lower

    upper = jnp.dot(linv_ref[...], pivot_ref[...], precision=HI, preferred_element_type=jnp.float32)

    @pl.when(jnp.logical_not(first_col))
    def _():
        buf_ref[:rows, :] = block_ref[...]
        place_rows(slot_ref, top_ref, buf_ref)
        out_ref[...] = buf_ref[:rows, :] - split_dot((high_ref[...], low_ref[...]), halves(upper))

    @pl.when(first_row)
    def _():
        out_ref[:width, :] = jnp.where(first_col, packed_ref[...], upper)


def update(block, panel, pivot_rows, old_top, packed, linv, uinv, slots, where):
    rows, cols = block.shape
    width = slots.shape[0]
    square = pl.BlockSpec((width, width), lambda t: (0, 0))
    tall = pl.BlockSpec((rows, width), lambda t: (0, t))
    flat = pl.BlockSpec((width, width), lambda t: (0, t))
    return pl.pallas_call(
        update_kernel,
        grid=(cols // width,),
        out_shape=jax.ShapeDtypeStruct((rows, cols), jnp.float32),
        in_specs=[
            smem(), smem(), tall, pl.BlockSpec((rows, width), lambda t: (0, 0)), flat, flat, square, square, square,
        ],
        out_specs=tall,
        scratch_shapes=[
            pltpu.VMEM((rows, width), jnp.bfloat16),
            pltpu.VMEM((rows, width), jnp.bfloat16),
            pltpu.VMEM((rows + SUB, width), jnp.float32),
        ],
        cost_estimate=pl.CostEstimate(
            flops=6 * rows * cols * width, bytes_accessed=8 * rows * cols, transcendentals=0
        ),
        name="update",
    )(slots, where, block, panel, pivot_rows, old_top, packed, linv, uinv)


def bits_of(n):
    return [1 << i for i in range(n.bit_length() - 1)]


def sum_over_rows(x, order, n_row):
    for bit in order:
        x = x + lax.ppermute(x, "prow", [(i, i ^ bit) for i in range(n_row)])
    return x


def spread_rows(x, order, n_row):
    have = [0]
    for bit in order:
        x = x + lax.ppermute(x, "prow", [(i, i ^ bit) for i in have])
        have = have + [i ^ bit for i in have]
    return x


def spread_cols(x, order):
    have = [0]
    for bit in order:
        x = x + lax.ppermute(x, "pcol", [(i, i ^ bit) for i in have])
        have = have + [i ^ bit for i in have]
    return x


def dense_step(n_row, n_col, matrix, pivots):
    block = matrix[0, :, 0, :]
    rows, cols = block.shape
    width = pivots.shape[0]
    row = lax.axis_index("prow")
    col = lax.axis_index("pcol")
    owner = pivots // width % n_row
    slot = pivots // (width * n_row) * width + pivots % width
    mine = owner == row
    owned = mine.astype(jnp.int32)
    target = jnp.where(mine, slot, rows)
    where = jnp.stack([row, col]).astype(jnp.int32)
    row_bits, col_bits = bits_of(n_row), bits_of(n_col)
    at_first_row = row == 0
    at_first_col = col == 0

    square = pick(block, slot, owned * at_first_col.astype(jnp.int32), 1)
    square = sum_over_rows(square, row_bits, n_row)
    square = spread_cols(square, col_bits[::-1])
    packed, linv, uinv = factor(square, jnp.zeros_like(square))

    top = jnp.where(at_first_row, block[:width], 0.0)
    top_panel = spread_rows(top[:, :width], row_bits, n_row)
    panel = place(block, top_panel, target)
    panel = spread_cols(jnp.where(at_first_col, panel, 0.0), col_bits[::-1])

    picked = pick(block, slot, owned, cols // width)
    half = width // 2
    pivot_rows = jnp.concatenate([
        sum_over_rows(picked[:half], row_bits, n_row),
        sum_over_rows(picked[half:], row_bits[::-1], n_row),
    ])
    old_top = jnp.concatenate([
        spread_rows(top[:half], row_bits, n_row),
        spread_rows(top[half:], row_bits[::-1], n_row),
    ])
    result = update(block, panel, pivot_rows, old_top, packed, linv, uinv, target, where)
    return result[None, :, None, :]


def raw():
    return pl.BlockSpec(memory_space=pl.ANY)


def thirds(x):
    high = x.astype(jnp.bfloat16)
    rest = x - high.astype(jnp.float32)
    middle = rest.astype(jnp.bfloat16)
    return high, middle, (rest - middle.astype(jnp.float32)).astype(jnp.bfloat16)


def select_dot(choice, parts):
    choice = choice.astype(jnp.bfloat16)
    high, middle, low = [jnp.dot(choice, x, preferred_element_type=jnp.float32) for x in parts]
    return high + (middle + low)


def begin_kernel(n_row, pivot_ref, mat_ref, panel_ref, wide_ref, fits_ref, *refs):
    messages, sem = refs[:n_row], refs[-1]
    rows, width = panel_ref.shape
    count = messages[0].shape[0] // 2
    width_log, row_log = width.bit_length() - 1, n_row.bit_length() - 1
    row = lax.axis_index("prow")
    copy = pltpu.make_async_copy(mat_ref.at[:, 0, pl.ds(0, width)], panel_ref, sem)
    copy.start()
    pivot = pivot_ref[...]
    block = lax.shift_right_logical(pivot, width_log)
    owner = block & (n_row - 1)
    slot = lax.shift_left(lax.shift_right_logical(block, row_log), width_log) + (pivot & (width - 1))
    height = -(-n_row // 16) * 16
    held = lax.broadcasted_iota(jnp.int32, (height, width), 0) == owner
    before = lax.broadcasted_iota(jnp.int32, (width, width), 0) < lax.broadcasted_iota(jnp.int32, (width, width), 1)
    held = jnp.where(held, 1.0, 0.0)
    earlier = jnp.dot(
        held.astype(jnp.bfloat16), jnp.where(before, 1.0, 0.0).astype(jnp.bfloat16), preferred_element_type=jnp.float32
    )
    rank = jnp.sum(held * earlier, axis=0, keepdims=True).astype(jnp.int32)
    fits_ref[0] = (jnp.max(rank) < count).astype(jnp.int32)
    place = ((owner ^ row) * count + rank).astype(jnp.float32)
    eye = lax.broadcasted_iota(jnp.int32, (width, width), 0) == lax.broadcasted_iota(jnp.int32, (width, width), 1)
    spread = jnp.where(eye, place, 0.0)
    wide = jnp.dot(spread, jnp.ones((width, LANES), jnp.float32), precision=HI, preferred_element_type=jnp.float32)
    wide_ref[...] = wide.astype(jnp.int32)
    ordinal = lax.broadcasted_iota(jnp.int32, (count, width), 0)
    mine = jnp.where((ordinal == rank) & (owner == row), 1.0, 0.0).astype(jnp.bfloat16)
    at_slot = jnp.where(lax.broadcasted_iota(jnp.int32, (rows, width), 0) == slot, 1.0, 0.0).astype(jnp.bfloat16)
    choice = lax.dot_general(mine, at_slot, (((1,), (1,)), ((), ())), preferred_element_type=jnp.float32)
    copy.wait()
    own = select_dot(choice, thirds(panel_ref[...]))
    for k in range(n_row):
        messages[k][:count, :] = own

    @pl.when(row == 0)
    def _():
        top = thirds(panel_ref[:width, :])
        for p in range(n_row):
            messages[p][count:, :] = select_dot(jnp.where((ordinal == rank) & (owner == p), 1.0, 0.0), top)


def begin(mat, pivots, n_row, count):
    rows, width = mat.shape[0], pivots.shape[0]
    message = jax.ShapeDtypeStruct((2 * count, width), jnp.float32)
    return pl.pallas_call(
        functools.partial(begin_kernel, n_row),
        out_shape=(
            jax.ShapeDtypeStruct((rows, width), jnp.float32),
            jax.ShapeDtypeStruct((width, LANES), jnp.int32),
            jax.ShapeDtypeStruct((1,), jnp.int32),
        ) + (message,) * n_row,
        in_specs=[vmem(), raw()],
        out_specs=(vmem(), vmem(), smem()) + (vmem(),) * n_row,
        scratch_shapes=[pltpu.SemaphoreType.DMA],
        cost_estimate=pl.CostEstimate(flops=0, bytes_accessed=10_000_000, transcendentals=0),
        name="begin",
    )(pivots[None, :], mat)


def parcel_kernel(n_row, mine_ref, lists_ref, mat_ref, own_ref, *refs):
    outs, spare_ref, sem = refs[:n_row], refs[n_row], refs[n_row + 1]
    count = own_ref.shape[0]
    first = lax.axis_index("prow") == 0

    def group(q, c):
        for u in range(SUB):
            i = q * SUB + u
            pltpu.make_async_copy(mat_ref.at[mine_ref[i]], own_ref.at[i], sem.at[0]).start()
        return c

    lax.fori_loop(0, count // SUB, group, 0)

    @pl.when(first)
    def _():
        for p in range(n_row):
            base = 0 if p == 0 else count

            def group(q, c, p=p, base=base):
                for u in range(SUB):
                    i = q * SUB + u
                    pltpu.make_async_copy(mat_ref.at[lists_ref[p, i]], outs[p].at[base + i], sem.at[1]).start()
                return c

            lax.fori_loop(0, count // SUB, group, 0)

    pltpu.make_async_copy(mat_ref.at[pl.ds(0, count)], own_ref, sem.at[0]).wait()
    copies = [pltpu.make_async_copy(own_ref, outs[p].at[pl.ds(0, count)], sem.at[1 + p]) for p in range(1, n_row)]
    for copy in copies[1:]:
        copy.start()
    for copy in copies[1:]:
        copy.wait()

    @pl.when(first)
    def _():
        pltpu.make_async_copy(mat_ref.at[pl.ds(0, n_row * count)], spare_ref, sem.at[1]).wait()

    copies[0].start()
    copies[0].wait()


def parcel(mat, mine, lists):
    n_row, count = lists.shape
    cols = mat.shape[2]

    def shape(rows):
        return jax.ShapeDtypeStruct((rows, 1, cols), jnp.float32)

    return pl.pallas_call(
        functools.partial(parcel_kernel, n_row),
        out_shape=(shape(count), shape(count)) + (shape(2 * count),) * (n_row - 1),
        in_specs=[smem(), smem(), raw()],
        out_specs=(vmem(),) * (n_row + 1),
        scratch_shapes=[pltpu.VMEM((n_row * count, 1, cols), jnp.float32), pltpu.SemaphoreType.DMA((n_row + 1,))],
        cost_estimate=pl.CostEstimate(flops=0, bytes_accessed=20_000_000, transcendentals=0),
        name="parcel",
    )(mine, lists, mat)


def pack_kernel(n_row, wide_ref, *refs):
    parts, out_ref = refs[:n_row], refs[n_row]
    width = wide_ref.shape[0]
    count = out_ref.shape[0] - width
    row, col = lax.axis_index("prow"), lax.axis_index("pcol")
    total = -(-n_row * count // LANES) * LANES

    @pl.when(col == 0)
    def _():
        pieces = [parts[k][:count, :] for k in range(n_row)]
        if total > n_row * count:
            pieces.append(jnp.zeros((total - n_row * count, width), jnp.float32))
        stack = jnp.concatenate(pieces, axis=0)
        lanes = lax.broadcasted_iota(jnp.int32, (width, LANES), 1)
        choice = jnp.concatenate(
            [jnp.where(lanes + t * LANES == wide_ref[...], 1.0, 0.0) for t in range(total // LANES)], axis=1
        )
        out_ref[:width, :] = select_dot(choice, thirds(stack))
        for k in range(n_row):
            @pl.when(row == k)
            def _(k=k):
                out_ref[width:, :] = parts[k][count:, :]

    @pl.when(col != 0)
    def _():
        out_ref[...] = jnp.zeros_like(out_ref)


def pack(wide, parts):
    n_row, width = len(parts), wide.shape[0]
    count = parts[0].shape[0] // 2
    return pl.pallas_call(
        functools.partial(pack_kernel, n_row),
        out_shape=jax.ShapeDtypeStruct((width + count, width), jnp.float32),
        in_specs=[vmem()] * (n_row + 1),
        out_specs=vmem(),
        cost_estimate=pl.CostEstimate(flops=0, bytes_accessed=4_000_000, transcendentals=0),
        name="pack",
    )(wide, *parts)


def put_rows(slot_ref, held, rows_ref, target_ref):
    spare = target_ref.shape[0] - SUB

    def group(q, c):
        for u in range(SUB):
            i = q * SUB + u
            slot = jnp.where(i < held, slot_ref[i], spare)
            target_ref[pl.ds(slot, 1), :] = rows_ref[pl.ds(i, 1), :]
        return c

    lax.fori_loop(0, rows_ref.shape[0] // SUB, group, 0)


def finish_kernel(
    n_row, mine_ref, counts_ref, wide_ref, mat_ref, panel_ref, panel_new_ref, square_ref, square_new_ref,
    packed_ref, linv_ref, uinv_ref, *refs,
):
    own_ref, top_ref, parcels, refs = refs[0], refs[1], refs[2:n_row + 1], refs[n_row + 1:]
    out_ref, block, pivot, panel, old, high, low, top, sem, in_sem, out_sem = refs
    rows, _, cols = mat_ref.shape
    width = linv_ref.shape[0]
    count = own_ref.shape[0]
    parts = [own_ref] + [x.at[pl.ds(0, count)] for x in parcels]
    tops = [top_ref] + [x.at[pl.ds(count, count)] for x in parcels]
    tiles = cols // width
    row, col = lax.axis_index("prow"), lax.axis_index("pcol")

    def tile(t):
        return pl.ds(pl.multiple_of(t * width, width), width)

    @pl.when(col % 2 == 0)
    def _():
        pltpu.make_async_copy(panel_ref, panel.at[pl.ds(0, rows)], sem.at[0]).start()

    @pl.when(col % 2 == 1)
    def _():
        pltpu.make_async_copy(panel_new_ref, panel.at[pl.ds(0, rows)], sem.at[0]).start()

    for p in range(n_row):
        @pl.when(row == p)
        def _(p=p):
            pltpu.make_async_copy(tops[p].at[:, 0, :], old, sem.at[1]).start()

    blocks = [
        pltpu.make_async_copy(mat_ref.at[:, 0, tile(t)], block.at[pl.ds(0, rows), tile(t)], in_sem.at[t])
        for t in range(tiles)
    ]
    pieces = [
        pltpu.make_async_copy(parts[k].at[:, 0, :], pivot.at[pl.ds(k * count, count), :], sem.at[2 + k])
        for k in range(n_row)
    ]
    if pivot.shape[0] > n_row * count:
        pivot[n_row * count:, :] = jnp.zeros((pivot.shape[0] - n_row * count, cols), jnp.float32)
    for copy in blocks[:1] + pieces + blocks[1:]:
        copy.start()

    lanes = lax.broadcasted_iota(jnp.int32, (width, LANES), 1)
    places = jnp.concatenate(
        [jnp.where(lanes + t * LANES == wide_ref[...], 1.0, 0.0) for t in range(pivot.shape[0] // LANES)], axis=1
    )
    spread_inv = halves(jnp.dot(linv_ref[...], places, precision=HI, preferred_element_type=jnp.float32))
    top[...] = square_ref[width:, :] + square_new_ref[width:, :]
    pltpu.make_async_copy(panel_ref, panel.at[pl.ds(0, rows)], sem.at[0]).wait()
    put_rows(mine_ref, counts_ref[row], top, panel)
    lower = split_dot(halves(panel[:rows, :]), halves(uinv_ref[...]))
    high[...], low[...] = halves(lower)
    pltpu.make_async_copy(tops[0].at[:, 0, :], old, sem.at[1]).wait()
    for copy in blocks:
        copy.wait()
    put_rows(mine_ref, counts_ref[row], old, block)

    @pl.when(col == 0)
    def _():
        block[:rows, :width] = lower

    for copy in pieces:
        copy.wait()

    def step(t, c):
        upper = split_dot(spread_inv, halves(pivot[:, tile(t)]))
        first_col = (col == 0) & (t == 0)

        @pl.when(jnp.logical_not(first_col))
        def _():
            block[:rows, tile(t)] = block[:rows, tile(t)] - split_dot((high[...], low[...]), halves(upper))

        @pl.when(row == 0)
        def _():
            block[:width, tile(t)] = jnp.where(first_col, packed_ref[...], upper)

        pltpu.make_async_copy(block.at[pl.ds(0, rows), tile(t)], out_ref.at[:, 0, tile(t)], out_sem.at[t]).start()
        return c

    lax.fori_loop(0, tiles, step, 0)
    for t in range(tiles):
        pltpu.make_async_copy(block.at[pl.ds(0, rows), tile(t)], out_ref.at[:, 0, tile(t)], out_sem.at[t]).wait()


def finish(mine, counts, wide, mat, panels, squares, factors, parcels):
    rows, _, cols = mat.shape
    width, n_row, count = factors[0].shape[0], len(parcels) - 1, mine.shape[0]
    return pl.pallas_call(
        functools.partial(finish_kernel, n_row),
        out_shape=jax.ShapeDtypeStruct(mat.shape, jnp.float32),
        in_specs=[smem(), smem(), vmem(), raw(), raw(), raw()] + [vmem()] * 5 + [raw()] * (n_row + 1),
        out_specs=raw(),
        scratch_shapes=[
            pltpu.VMEM((rows + SUB, cols), jnp.float32),
            pltpu.VMEM((-(-n_row * count // LANES) * LANES, cols), jnp.float32),
            pltpu.VMEM((rows + SUB, width), jnp.float32),
            pltpu.VMEM((count, cols), jnp.float32),
            pltpu.VMEM((rows, width), jnp.bfloat16),
            pltpu.VMEM((rows, width), jnp.bfloat16),
            pltpu.VMEM((count, width), jnp.float32),
            pltpu.SemaphoreType.DMA((2 + n_row,)),
            pltpu.SemaphoreType.DMA((cols // width,)),
            pltpu.SemaphoreType.DMA((cols // width,)),
        ],
        cost_estimate=pl.CostEstimate(
            flops=6 * rows * cols * width, bytes_accessed=8 * rows * cols, transcendentals=0
        ),
        name="finish",
    )(mine, counts, wide, mat, *panels, *squares, *factors, *parcels)


def capacity(n_row, width):
    mean = width / n_row
    return -(-int(mean + 3.4 * (mean * (1 - 1 / n_row)) ** 0.5) // SUB) * SUB


def locate(pivots, n_row, row, count):
    width = pivots.shape[0]
    owner = pivots // width % n_row
    slot = pivots // (width * n_row) * width + pivots % width
    number = jnp.arange(width, dtype=jnp.int32)
    ahead = (owner[:, None] == owner[None, :]) & (number[None, :] < number[:, None])
    rank = jnp.sum(ahead, axis=1, dtype=jnp.int32)
    every = jnp.arange(n_row, dtype=jnp.int32)[:, None, None]
    ordinal = jnp.arange(count, dtype=jnp.int32)[None, :, None]
    hits = (owner[None, None, :] == every) & (rank[None, None, :] == ordinal)
    lists = jnp.sum(jnp.where(hits, number[None, None, :], 0), axis=2, dtype=jnp.int32)
    own = (owner[None, :] == row) & (rank[None, :] == ordinal[0])
    mine = jnp.sum(jnp.where(own, slot[None, :], 0), axis=1, dtype=jnp.int32)
    return mine, lists, jnp.sum(owner[None, :] == every[:, 0], axis=1, dtype=jnp.int32)


def capped_step(n_row, n_col, matrix, pivots, begun):
    _, rows, _, cols = matrix.shape
    mat = matrix.reshape(rows, 1, cols)
    panel, wide, _, *messages = begun
    count = messages[0].shape[0] // 2
    row, col = lax.axis_index("prow"), lax.axis_index("pcol")
    both = ("prow", "pcol")
    turns = bits_of(n_col)[:0:-1]

    def exchange(x, k):
        return lax.ppermute(x, both, [(i * n_col, (i ^ k) * n_col) for i in range(n_row)])

    moved = [exchange(messages[k], k) for k in range(1, n_row)]
    mine, lists, counts = locate(pivots, n_row, row, count)
    parcels = parcel(mat, mine, lists)
    sent = []
    for k in range(1, n_row):
        item = parcels[1 + k]
        if k == 3:
            item, *sent = lax.optimization_barrier((item, *sent))
        sent.append(lax.ppermute(item, "prow", [(i, i ^ k) for i in range(n_row)]))
    message = pack(wide, messages[:1] + moved)

    pairs = [[(i, i + bit) for i in range(0, n_col, 2 * bit)] for bit in turns + [1]]
    newer = [(col & bit) != 0 for bit in turns]
    panel_moved = lax.ppermute(panel, "pcol", pairs[0])
    message, panel_moved = lax.optimization_barrier((message, panel_moved))
    for n in range(len(turns)):
        panel = jnp.where(newer[n], panel_moved, panel)
        panel_moved = lax.ppermute(panel, "pcol", pairs[n + 1])
        message = jnp.where(newer[n], lax.ppermute(message, "pcol", pairs[n]), message)
        if n + 1 < len(turns):
            message, panel_moved = lax.optimization_barrier((message, panel_moved))
    message_new = lax.ppermute(message, "pcol", pairs[-1])
    factors = factor(message, message_new)
    out = finish(
        mine, counts, wide, mat, (panel, panel_moved), (message, message_new), factors, list(parcels[:2]) + sent
    )
    return out.reshape(matrix.shape)


def on_device(n_row, n_col, matrix, pivots):
    _, rows, _, cols = matrix.shape
    begun = begin(matrix.reshape(rows, 1, cols), pivots, n_row, capacity(n_row, pivots.shape[0]))
    return lax.cond(
        begun[2][0] > 0,
        lambda m, p, b: capped_step(n_row, n_col, m, p, b),
        lambda m, p, b: dense_step(n_row, n_col, m, p),
        matrix, pivots, begun,
    )


def solution(mesh):
    spec = P("prow", None, "pcol", None)
    n_row, n_col = mesh.shape["prow"], mesh.shape["pcol"]
    return jax.shard_map(
        functools.partial(on_device, n_row, n_col), mesh=mesh, in_specs=(spec, P()), out_specs=spec, check_vma=False
    )
```

```python
import functools

import jax
import jax.numpy as jnp
from jax import lax
from jax.experimental import pallas as pl
from jax.experimental.pallas import tpu as pltpu
from jax.sharding import PartitionSpec as P

LANES = 128
SUB = 8
HI = lax.Precision.HIGHEST


def pick_lane(tile, lane):
    return jnp.take_along_axis(tile, jnp.full((SUB, LANES), lane, jnp.int32), axis=1)


def row_of(tile, j):
    return jnp.broadcast_to(tile[j:j + 1, :], (SUB, LANES))


def factor_kernel(width, s_ref, extra_ref, packed_ref, linv_ref, uinv_ref, a_ref, m_ref, v_ref):
    groups = a_ref.shape[0]
    tiles = groups * SUB // LANES
    per_tile = LANES // SUB
    per_block = width // SUB
    sub = lax.broadcasted_iota(jnp.int32, (SUB, LANES), 0)
    lane = lax.broadcasted_iota(jnp.int32, (SUB, LANES), 1)

    for i in range(groups):
        a_ref[i] = s_ref[i * SUB:(i + 1) * SUB, :] + extra_ref[i * SUB:(i + 1) * SUB, :]
        diag = lane - (i % per_tile) * SUB == sub
        for t in range(tiles):
            block = jnp.where(diag, 1.0, 0.0) if i // per_tile == t else jnp.zeros((SUB, LANES), jnp.float32)
            m_ref[i, :, t * LANES:(t + 1) * LANES] = block
            if t > i // per_tile:
                linv_ref[i * SUB:(i + 1) * SUB, t * LANES:(t + 1) * LANES] = block

    def span(t):
        return slice(t * LANES, (t + 1) * LANES)

    for o in range(groups // per_block):
        base = o * per_block
        h = base // per_tile
        live = [(a_ref, t) for t in range(h + 1, tiles)] + [(m_ref, t) for t in range(h + 1)]

        def panel(i, c, base=base, h=h, live=live):
            b = base + i
            g = (b - h * per_tile) * SUB
            rows = pl.ds(pl.multiple_of(b * SUB, SUB), SUB)
            own = a_ref[b, :, span(h)]
            cols = [pick_lane(own, g + j) for j in range(SUB)]
            in_panel = (lane >= g) & (lane < g + SUB)
            after = lane >= g + SUB
            head = jnp.where(in_panel, jnp.where(lane - g == sub, -1.0, 0.0), jnp.where(after, own, 0.0))
            rest = [ref[b, :, span(t)] for ref, t in live]
            packed = own
            final = [head] + rest
            for j in range(SUB):
                at = sub == j
                coef = cols[j]
                r = 1.0 / row_of(coef, j)
                final = [jnp.where(at, x, y) for x, y in zip([head] + rest, final)]
                packed = jnp.where((lane == g + j) & (sub > j), coef * r, packed)
                for k in range(j, SUB):
                    packed = jnp.where((lane == g + k) & at, cols[k], packed)
                head_coef = jnp.where((sub < j) | after, coef, 0.0)
                v = row_of(head, j) * r
                head = jnp.where(at, v, head - head_coef * v)
                for n, x in enumerate(rest):
                    v = row_of(x, j) * r
                    rest[n] = jnp.where(at, v, x - coef * v)
                for k in range(j + 1, SUB):
                    v = row_of(cols[k], j) * r
                    cols[k] = jnp.where(at, v, cols[k] - coef * v)
            for t in range(h):
                packed_ref[rows, span(t)] = a_ref[b, :, span(t)]
            packed_ref[rows, span(h)] = jnp.where(after, final[0], packed)
            for (ref, t), x in zip(live, final[1:]):
                (packed_ref if ref is a_ref else linv_ref)[rows, span(t)] = x
            a_ref[b, :, span(h)] = head
            v_ref[0] = head
            for n, ((ref, t), x) in enumerate(zip(live, rest)):
                ref[b, :, span(t)] = x
                v_ref[n + 1] = x
            others = [base + lax.rem(i + s, per_block) for s in range(1, per_block)]
            heads = [a_ref[r, :, span(h)] for r in others]
            facs = [[pick_lane(x, g + j) for j in range(SUB)] for x in heads]
            for n, (ref, t) in enumerate([(a_ref, h)] + live):
                old = [jnp.where(in_panel, 0.0, x) for x in heads] if n == 0 else [ref[r, :, span(t)] for r in others]
                vs = [row_of([head] + rest and ([head] + rest)[n], j) for j in range(SUB)]
                for x, fac, r in zip(old, facs, others):
                    acc = [fac[j] * vs[j] for j in range(SUB)]
                    while len(acc) > 1:
                        acc = [p + q for p, q in zip(acc[::2], acc[1::2])]
                    ref[r, :, span(t)] = x - acc[0]
            return c

        lax.fori_loop(0, per_block, panel, 0)

        lo = (base % per_tile) * SUB
        pad = [jnp.zeros((n, LANES), jnp.float32) for n in (lo, LANES - lo - width)]

        def stack(x):
            return jnp.concatenate([p for p in (pad[0], x, pad[1]) if p.shape[0]], axis=0)

        def flat(ref, first, last, t):
            return ref[first:last, :, span(t)].reshape((last - first) * SUB, LANES)

        end = base + per_block
        right = [stack(flat(ref, base, end, t)) for ref, t in [(a_ref, h)] + live]
        for first, last in ((end, groups), (0, base)):
            if first == last:
                continue
            left = flat(a_ref, first, last, h)
            column = lax.broadcasted_iota(jnp.int32, left.shape, 1)
            for n, (ref, t) in enumerate([(a_ref, h)] + live):
                if ref is m_ref and first == 0:
                    continue
                old = left if n else None
                old = jnp.where((column >= lo) & (column < lo + width), 0.0, left) if n == 0 else flat(ref, first, last, t)
                new = old - jnp.dot(left, right[n], precision=HI, preferred_element_type=jnp.float32)
                ref[first:last, :, span(t)] = new.reshape(last - first, SUB, LANES)

    ri = lax.broadcasted_iota(jnp.int32, (SUB, LANES), 0)
    for i in range(groups):
        for t in range(tiles):
            x = a_ref[i, :, span(t)]
            keep = lane + t * LANES >= ri + i * SUB
            uinv_ref[i * SUB:(i + 1) * SUB, span(t)] = jnp.where(keep, -x, 0.0)


def vmem():
    return pl.BlockSpec(memory_space=pltpu.VMEM)


def smem():
    return pl.BlockSpec(memory_space=pltpu.SMEM)


def factor(square, extra, width=32):
    size = square.shape[1]
    out = jax.ShapeDtypeStruct((size, size), jnp.float32)
    return pl.pallas_call(
        functools.partial(factor_kernel, width),
        out_shape=(out, out, out),
        in_specs=[vmem(), vmem()],
        out_specs=(vmem(),) * 3,
        scratch_shapes=[
            pltpu.VMEM((size // SUB, SUB, size), jnp.float32),
            pltpu.VMEM((size // SUB, SUB, size), jnp.float32),
            pltpu.VMEM((1 + size // LANES, SUB, LANES), jnp.float32),
        ],
        cost_estimate=pl.CostEstimate(flops=4 * size**3, bytes_accessed=50_000_000, transcendentals=0),
        name="factor",
    )(square, extra)


def pick_kernel(slot_ref, own_ref, block_ref, out_ref):
    def group(q, c):
        for u in range(SUB):
            j = q * SUB + u
            row = block_ref[pl.ds(slot_ref[j], 1), :]
            out_ref[pl.ds(j, 1), :] = row * own_ref[j].astype(jnp.float32)
        return c

    lax.fori_loop(0, out_ref.shape[0] // SUB, group, 0)


def pick(block, slots, owned, tiles):
    rows, width = block.shape[0], slots.shape[0]
    return pl.pallas_call(
        pick_kernel,
        grid=(tiles,),
        out_shape=jax.ShapeDtypeStruct((width, tiles * width), jnp.float32),
        in_specs=[smem(), smem(), pl.BlockSpec((rows, width), lambda t: (0, t))],
        out_specs=pl.BlockSpec((width, width), lambda t: (0, t)),
        cost_estimate=pl.CostEstimate(
            flops=width * width * tiles, bytes_accessed=4 * (rows + width) * width * tiles, transcendentals=0
        ),
        name="pick",
    )(slots, owned, block)


def place_rows(slot_ref, rows_ref, target_ref):
    def group(q, c):
        for u in range(SUB):
            j = q * SUB + u
            target_ref[pl.ds(slot_ref[j], 1), :] = rows_ref[pl.ds(j, 1), :]
        return c

    lax.fori_loop(0, rows_ref.shape[0] // SUB, group, 0)


def place_kernel(slot_ref, block_ref, rows_ref, out_ref, buf_ref):
    rows = block_ref.shape[0]
    buf_ref[:rows, :] = block_ref[...]
    place_rows(slot_ref, rows_ref, buf_ref)
    out_ref[...] = buf_ref[:rows, :]


def place(block, rows, slots):
    height, width = block.shape[0], slots.shape[0]
    return pl.pallas_call(
        place_kernel,
        grid=(1,),
        out_shape=jax.ShapeDtypeStruct((height, width), jnp.float32),
        in_specs=[
            smem(),
            pl.BlockSpec((height, width), lambda t: (0, 0)),
            pl.BlockSpec((width, width), lambda t: (0, 0)),
        ],
        out_specs=pl.BlockSpec((height, width), lambda t: (0, 0)),
        scratch_shapes=[pltpu.VMEM((height + SUB, width), jnp.float32)],
        cost_estimate=pl.CostEstimate(flops=0, bytes_accessed=8 * height * width, transcendentals=0),
        name="place",
    )(slots, block, rows)


def halves(x):
    high = x.astype(jnp.bfloat16)
    low = (x - high.astype(jnp.float32)).astype(jnp.bfloat16)
    return high, low


def split_dot(left, right):
    acc = jnp.dot(left[0], right[1], preferred_element_type=jnp.float32)
    acc += jnp.dot(left[1], right[0], preferred_element_type=jnp.float32)
    return acc + jnp.dot(left[0], right[0], preferred_element_type=jnp.float32)


def update_kernel(
    slot_ref, where_ref, block_ref, panel_ref, pivot_ref, top_ref, packed_ref, linv_ref, uinv_ref,
    out_ref, high_ref, low_ref, buf_ref,
):
    rows, width = panel_ref.shape
    t = pl.program_id(0)
    first_row = where_ref[0] == 0
    first_col = (where_ref[1] == 0) & (t == 0)

    @pl.when(t == 0)
    def _():
        lower = jnp.dot(panel_ref[...], uinv_ref[...], precision=HI, preferred_element_type=jnp.float32)
        high_ref[...], low_ref[...] = halves(lower)
        out_ref[...] = lower

    upper = jnp.dot(linv_ref[...], pivot_ref[...], precision=HI, preferred_element_type=jnp.float32)

    @pl.when(jnp.logical_not(first_col))
    def _():
        buf_ref[:rows, :] = block_ref[...]
        place_rows(slot_ref, top_ref, buf_ref)
        out_ref[...] = buf_ref[:rows, :] - split_dot((high_ref[...], low_ref[...]), halves(upper))

    @pl.when(first_row)
    def _():
        out_ref[:width, :] = jnp.where(first_col, packed_ref[...], upper)


def update(block, panel, pivot_rows, old_top, packed, linv, uinv, slots, where):
    rows, cols = block.shape
    width = slots.shape[0]
    square = pl.BlockSpec((width, width), lambda t: (0, 0))
    tall = pl.BlockSpec((rows, width), lambda t: (0, t))
    flat = pl.BlockSpec((width, width), lambda t: (0, t))
    return pl.pallas_call(
        update_kernel,
        grid=(cols // width,),
        out_shape=jax.ShapeDtypeStruct((rows, cols), jnp.float32),
        in_specs=[
            smem(), smem(), tall, pl.BlockSpec((rows, width), lambda t: (0, 0)), flat, flat, square, square, square,
        ],
        out_specs=tall,
        scratch_shapes=[
            pltpu.VMEM((rows, width), jnp.bfloat16),
            pltpu.VMEM((rows, width), jnp.bfloat16),
            pltpu.VMEM((rows + SUB, width), jnp.float32),
        ],
        cost_estimate=pl.CostEstimate(
            flops=6 * rows * cols * width, bytes_accessed=8 * rows * cols, transcendentals=0
        ),
        name="update",
    )(slots, where, block, panel, pivot_rows, old_top, packed, linv, uinv)


def bits_of(n):
    return [1 << i for i in range(n.bit_length() - 1)]


def sum_over_rows(x, order, n_row):
    for bit in order:
        x = x + lax.ppermute(x, "prow", [(i, i ^ bit) for i in range(n_row)])
    return x


def spread_rows(x, order, n_row):
    have = [0]
    for bit in order:
        x = x + lax.ppermute(x, "prow", [(i, i ^ bit) for i in have])
        have = have + [i ^ bit for i in have]
    return x


def spread_cols(x, order):
    have = [0]
    for bit in order:
        x = x + lax.ppermute(x, "pcol", [(i, i ^ bit) for i in have])
        have = have + [i ^ bit for i in have]
    return x


def dense_step(n_row, n_col, matrix, pivots):
    block = matrix[0, :, 0, :]
    rows, cols = block.shape
    width = pivots.shape[0]
    row = lax.axis_index("prow")
    col = lax.axis_index("pcol")
    owner = pivots // width % n_row
    slot = pivots // (width * n_row) * width + pivots % width
    mine = owner == row
    owned = mine.astype(jnp.int32)
    target = jnp.where(mine, slot, rows)
    where = jnp.stack([row, col]).astype(jnp.int32)
    row_bits, col_bits = bits_of(n_row), bits_of(n_col)
    at_first_row = row == 0
    at_first_col = col == 0

    square = pick(block, slot, owned * at_first_col.astype(jnp.int32), 1)
    square = sum_over_rows(square, row_bits, n_row)
    square = spread_cols(square, col_bits[::-1])
    packed, linv, uinv = factor(square, jnp.zeros_like(square))

    top = jnp.where(at_first_row, block[:width], 0.0)
    top_panel = spread_rows(top[:, :width], row_bits, n_row)
    panel = place(block, top_panel, target)
    panel = spread_cols(jnp.where(at_first_col, panel, 0.0), col_bits[::-1])

    picked = pick(block, slot, owned, cols // width)
    half = width // 2
    pivot_rows = jnp.concatenate([
        sum_over_rows(picked[:half], row_bits, n_row),
        sum_over_rows(picked[half:], row_bits[::-1], n_row),
    ])
    old_top = jnp.concatenate([
        spread_rows(top[:half], row_bits, n_row),
        spread_rows(top[half:], row_bits[::-1], n_row),
    ])
    result = update(block, panel, pivot_rows, old_top, packed, linv, uinv, target, where)
    return result[None, :, None, :]


def raw():
    return pl.BlockSpec(memory_space=pl.ANY)


def thirds(x):
    high = x.astype(jnp.bfloat16)
    rest = x - high.astype(jnp.float32)
    middle = rest.astype(jnp.bfloat16)
    return high, middle, (rest - middle.astype(jnp.float32)).astype(jnp.bfloat16)


def select_dot(choice, parts):
    choice = choice.astype(jnp.bfloat16)
    high, middle, low = [jnp.dot(choice, x, preferred_element_type=jnp.float32) for x in parts]
    return high + (middle + low)


def begin_kernel(n_row, pivot_ref, mat_ref, panel_ref, wide_ref, fits_ref, *refs):
    messages, sem = refs[:n_row], refs[-1]
    rows, width = panel_ref.shape
    count = messages[0].shape[0] // 2
    width_log, row_log = width.bit_length() - 1, n_row.bit_length() - 1
    row = lax.axis_index("prow")
    copy = pltpu.make_async_copy(mat_ref.at[:, 0, pl.ds(0, width)], panel_ref, sem)
    copy.start()
    pivot = pivot_ref[...]
    block = lax.shift_right_logical(pivot, width_log)
    owner = block & (n_row - 1)
    slot = lax.shift_left(lax.shift_right_logical(block, row_log), width_log) + (pivot & (width - 1))
    _, rank = owners(pivot, n_row)
    fits_ref[0] = (jnp.max(rank) < count).astype(jnp.int32)
    place = ((owner ^ row) * count + rank).astype(jnp.float32)
    eye = lax.broadcasted_iota(jnp.int32, (width, width), 0) == lax.broadcasted_iota(jnp.int32, (width, width), 1)
    spread = jnp.where(eye, place, 0.0)
    wide = jnp.dot(spread, jnp.ones((width, LANES), jnp.float32), precision=HI, preferred_element_type=jnp.float32)
    wide_ref[...] = wide.astype(jnp.int32)
    ordinal = lax.broadcasted_iota(jnp.int32, (count, width), 0)
    mine = jnp.where((ordinal == rank) & (owner == row), 1.0, 0.0).astype(jnp.bfloat16)
    at_slot = jnp.where(lax.broadcasted_iota(jnp.int32, (rows, width), 0) == slot, 1.0, 0.0).astype(jnp.bfloat16)
    choice = lax.dot_general(mine, at_slot, (((1,), (1,)), ((), ())), preferred_element_type=jnp.float32)
    copy.wait()
    own = select_dot(choice, thirds(panel_ref[...]))
    for k in range(n_row):
        messages[k][:count, :] = own

    @pl.when(row == 0)
    def _():
        top = thirds(panel_ref[:width, :])
        for p in range(n_row):
            messages[p][count:, :] = select_dot(jnp.where((ordinal == rank) & (owner == p), 1.0, 0.0), top)


def begin(mat, pivots, n_row, count):
    rows, width = mat.shape[0], pivots.shape[0]
    message = jax.ShapeDtypeStruct((2 * count, width), jnp.float32)
    return pl.pallas_call(
        functools.partial(begin_kernel, n_row),
        out_shape=(
            jax.ShapeDtypeStruct((rows, width), jnp.float32),
            jax.ShapeDtypeStruct((width, LANES), jnp.int32),
            jax.ShapeDtypeStruct((1,), jnp.int32),
        ) + (message,) * n_row,
        in_specs=[vmem(), raw()],
        out_specs=(vmem(), vmem(), smem()) + (vmem(),) * n_row,
        scratch_shapes=[pltpu.SemaphoreType.DMA],
        cost_estimate=pl.CostEstimate(flops=0, bytes_accessed=10_000_000, transcendentals=0),
        name="begin",
    )(pivots[None, :], mat)


def parcel_kernel(n_row, mine_ref, pivot_ref, mat_ref, *refs):
    outs, own, block, sem = refs[:-3], refs[-3], refs[-2], refs[-1]
    count, cols = own.shape
    half = count // 2
    width = pivot_ref.shape[1]

    def group(q, c):
        for u in range(SUB):
            i = q * SUB + u
            pltpu.make_async_copy(mat_ref.at[mine_ref[i]], own.at[pl.ds(i, 1), :], sem.at[0]).start()
        return c

    lax.fori_loop(0, count // SUB, group, 0)

    @pl.when(lax.axis_index("prow") == 0)
    def _():
        copy = pltpu.make_async_copy(mat_ref.at[pl.ds(0, width), 0, :], block, sem.at[1])
        copy.start()
        owner, rank = owners(pivot_ref[...], n_row)
        ordinal = lax.broadcasted_iota(jnp.int32, (count, width), 0)
        choices = [jnp.where((ordinal == rank) & (owner == p), 1.0, 0.0) for p in range(n_row)]
        choice = jnp.concatenate(choices, axis=0)
        copy.wait()

        def piece(t, c):
            at = pl.ds(pl.multiple_of(t * width, width), width)
            tops = select_dot(choice, thirds(block[:, at]))
            for p in range(n_row):
                for part in range(2):
                    first = p * count + part * half
                    for ref, base in top_places(n_row, half, outs, p, part):
                        ref[pl.ds(base, half), at] = tops[first:first + half]
            return c

        lax.fori_loop(0, cols // width, piece, 0)

    pltpu.make_async_copy(mat_ref.at[pl.ds(0, count), 0, :], own, sem.at[0]).wait()
    if n_row == 4:
        outs[0][:half, :] = own[:half, :]
        outs[1][:half, :] = own[half:, :]
        outs[2][:count, :] = own[...]
    else:
        outs[0][:count, :] = own[...]
        for p in range(1, n_row):
            outs[p][:count, :] = own[...]


def top_places(n_row, half, outs, p, part):
    if n_row != 4:
        return [(outs[p], 2 * half + part * half)]
    if p == 0:
        return [(outs[2], 2 * half + part * half)]
    if p == 3:
        return [(outs[part], 2 * half)]
    if part == p - 1:
        return [(outs[part], half)]
    return [(outs[2], (4 + part) * half)]


def owners(pivot, n_row):
    width = pivot.shape[1]
    owner = lax.shift_right_logical(pivot, width.bit_length() - 1) & (n_row - 1)
    held = lax.broadcasted_iota(jnp.int32, (-(-n_row // 16) * 16, width), 0) == owner
    before = lax.broadcasted_iota(jnp.int32, (width, width), 0) < lax.broadcasted_iota(jnp.int32, (width, width), 1)
    held = jnp.where(held, 1.0, 0.0)
    earlier = jnp.dot(
        held.astype(jnp.bfloat16), jnp.where(before, 1.0, 0.0).astype(jnp.bfloat16), preferred_element_type=jnp.float32
    )
    return owner, jnp.sum(held * earlier, axis=0, keepdims=True).astype(jnp.int32)


def parcel(mat, mine, pivots, n_row):
    count, width, cols = mine.shape[0], pivots.shape[0], mat.shape[2]
    half = count // 2
    sizes = [3 * half, 3 * half, 6 * half] if n_row == 4 else [2 * count] * n_row
    return pl.pallas_call(
        functools.partial(parcel_kernel, n_row),
        out_shape=tuple(jax.ShapeDtypeStruct((size, cols), jnp.float32) for size in sizes),
        in_specs=[smem(), vmem(), raw()],
        out_specs=(vmem(),) * len(sizes),
        scratch_shapes=[
            pltpu.VMEM((count, cols), jnp.float32),
            pltpu.VMEM((width, cols), jnp.float32),
            pltpu.SemaphoreType.DMA((2,)),
        ],
        cost_estimate=pl.CostEstimate(flops=0, bytes_accessed=16_000_000, transcendentals=0),
        name="parcel",
    )(mine, pivots[None, :], mat)


def relay_kernel(kept_ref, first_ref, second_ref, y_ref, x_ref, sem):
    half = first_ref.shape[0] // 3
    row = lax.axis_index("prow")

    def move(source, base, dest, at, n):
        return pltpu.make_async_copy(source.at[pl.ds(base, half), :], dest.at[pl.ds(at, half), :], sem.at[n])

    copies = [
        move(kept_ref, 0, y_ref, 0, 0),
        move(kept_ref, half, x_ref, 0, 1),
        move(first_ref, 0, y_ref, half, 2),
        move(second_ref, 0, x_ref, half, 3),
    ]
    for copy in copies:
        copy.start()

    @pl.when(row == 0)
    def _():
        move(kept_ref, 4 * half, y_ref, 2 * half, 4).start()
        move(kept_ref, 5 * half, x_ref, 2 * half, 5).start()

    @pl.when(row != 0)
    def _():
        move(first_ref, 2 * half, y_ref, 2 * half, 4).start()
        move(second_ref, 2 * half, x_ref, 2 * half, 5).start()

    for copy in copies:
        copy.wait()
    move(first_ref, 2 * half, y_ref, 2 * half, 4).wait()
    move(second_ref, 2 * half, x_ref, 2 * half, 5).wait()


def relay(kept, first, second):
    shape = jax.ShapeDtypeStruct(first.shape, jnp.float32)
    return pl.pallas_call(
        relay_kernel,
        out_shape=(shape, shape),
        in_specs=[raw()] * 3,
        out_specs=(vmem(), vmem()),
        scratch_shapes=[pltpu.SemaphoreType.DMA((6,))],
        cost_estimate=pl.CostEstimate(flops=0, bytes_accessed=4_000_000, transcendentals=0),
        name="relay",
    )(kept, first, second)


def pack_kernel(n_row, wide_ref, *refs):
    parts, out_ref = refs[:n_row], refs[n_row]
    width = wide_ref.shape[0]
    count = out_ref.shape[0] - width
    row, col = lax.axis_index("prow"), lax.axis_index("pcol")
    total = -(-n_row * count // LANES) * LANES

    @pl.when(col == 0)
    def _():
        pieces = [parts[k][:count, :] for k in range(n_row)]
        if total > n_row * count:
            pieces.append(jnp.zeros((total - n_row * count, width), jnp.float32))
        stack = jnp.concatenate(pieces, axis=0)
        lanes = lax.broadcasted_iota(jnp.int32, (width, LANES), 1)
        choice = jnp.concatenate(
            [jnp.where(lanes + t * LANES == wide_ref[...], 1.0, 0.0) for t in range(total // LANES)], axis=1
        )
        out_ref[:width, :] = select_dot(choice, thirds(stack))
        for k in range(n_row):
            @pl.when(row == k)
            def _(k=k):
                out_ref[width:, :] = parts[k][count:, :]

    @pl.when(col != 0)
    def _():
        out_ref[...] = jnp.zeros_like(out_ref)


def pack(wide, parts):
    n_row, width = len(parts), wide.shape[0]
    count = parts[0].shape[0] // 2
    return pl.pallas_call(
        functools.partial(pack_kernel, n_row),
        out_shape=jax.ShapeDtypeStruct((width + count, width), jnp.float32),
        in_specs=[vmem()] * (n_row + 1),
        out_specs=vmem(),
        cost_estimate=pl.CostEstimate(flops=0, bytes_accessed=4_000_000, transcendentals=0),
        name="pack",
    )(wide, *parts)


def unpack_parcels(n_row, count, parcels):
    half = count // 2
    if n_row != 4:
        parts = [(x, part * half) for x in parcels for part in range(2)]
        return parts, [[(x, count + part * half) for part in range(2)] for x in parcels]
    kept, first, second, third, fourth = parcels
    parts = [
        (kept, 0), (kept, half), (first, 0), (fourth, 0), (third, 0), (second, 0), (third, half), (fourth, half)
    ]
    tops = [
        [(kept, 2 * half), (kept, 3 * half)],
        [(first, half), (fourth, 2 * half)],
        [(third, 2 * half), (second, half)],
        [(third, 2 * half), (fourth, 2 * half)],
    ]
    return parts, tops


def put_rows(slot_ref, held, rows_ref, target_ref):
    spare = target_ref.shape[0] - SUB

    def group(q, c):
        for u in range(SUB):
            i = q * SUB + u
            slot = jnp.where(i < held, slot_ref[i], spare)
            target_ref[pl.ds(slot, 1), :] = rows_ref[pl.ds(i, 1), :]
        return c

    lax.fori_loop(0, rows_ref.shape[0] // SUB, group, 0)


def finish_kernel(
    n_row, mine_ref, counts_ref, wide_ref, mat_ref, panel_ref, panel_new_ref, square_ref, square_new_ref,
    packed_ref, linv_ref, uinv_ref, *refs,
):
    n_parcels = 5 if n_row == 4 else n_row
    parcels, refs = refs[:n_parcels], refs[n_parcels:]
    out_ref, block, pivot, panel, old, high, low, top, sem, in_sem, out_sem = refs
    rows, _, cols = mat_ref.shape
    width = linv_ref.shape[0]
    count = mine_ref.shape[0]
    half = count // 2
    parts, tops = unpack_parcels(n_row, count, parcels)
    tiles = cols // width
    row, col = lax.axis_index("prow"), lax.axis_index("pcol")

    def tile(t):
        return pl.ds(pl.multiple_of(t * width, width), width)

    @pl.when(col % 2 == 0)
    def _():
        pltpu.make_async_copy(panel_ref, panel.at[pl.ds(0, rows)], sem.at[0]).start()

    @pl.when(col % 2 == 1)
    def _():
        pltpu.make_async_copy(panel_new_ref, panel.at[pl.ds(0, rows)], sem.at[0]).start()

    for p in range(n_row):
        @pl.when(row == p)
        def _(p=p):
            for part in range(2):
                ref, base = tops[p][part]
                dest = old.at[pl.ds(part * half, half), :]
                pltpu.make_async_copy(ref.at[pl.ds(base, half), :], dest, sem.at[1]).start()

    blocks = [
        pltpu.make_async_copy(mat_ref.at[:, 0, tile(t)], block.at[pl.ds(0, rows), tile(t)], in_sem.at[t])
        for t in range(tiles)
    ]
    pieces = [
        pltpu.make_async_copy(
            ref.at[pl.ds(base, half), :], pivot.at[pl.ds(n * half, half), :], sem.at[2 + n]
        )
        for n, (ref, base) in enumerate(parts)
    ]
    if pivot.shape[0] > n_row * count:
        pivot[n_row * count:, :] = jnp.zeros((pivot.shape[0] - n_row * count, cols), jnp.float32)
    for copy in blocks[:1] + pieces + blocks[1:]:
        copy.start()

    lanes = lax.broadcasted_iota(jnp.int32, (width, LANES), 1)
    places = jnp.concatenate(
        [jnp.where(lanes + t * LANES == wide_ref[...], 1.0, 0.0) for t in range(pivot.shape[0] // LANES)], axis=1
    )
    spread_inv = halves(jnp.dot(linv_ref[...], places, precision=HI, preferred_element_type=jnp.float32))
    top[...] = square_ref[width:, :] + square_new_ref[width:, :]
    pltpu.make_async_copy(panel_ref, panel.at[pl.ds(0, rows)], sem.at[0]).wait()
    put_rows(mine_ref, counts_ref[row], top, panel)
    lower = split_dot(halves(panel[:rows, :]), halves(uinv_ref[...]))
    high[...], low[...] = halves(lower)
    pltpu.make_async_copy(mat_ref.at[pl.ds(0, count), 0, :], old, sem.at[1]).wait()
    for copy in blocks:
        copy.wait()
    put_rows(mine_ref, counts_ref[row], old, block)

    @pl.when(col == 0)
    def _():
        block[:rows, :width] = lower

    for copy in pieces:
        copy.wait()

    def step(t, c):
        upper = split_dot(spread_inv, halves(pivot[:, tile(t)]))
        first_col = (col == 0) & (t == 0)

        @pl.when(jnp.logical_not(first_col))
        def _():
            block[:rows, tile(t)] = block[:rows, tile(t)] - split_dot((high[...], low[...]), halves(upper))

        @pl.when(row == 0)
        def _():
            block[:width, tile(t)] = jnp.where(first_col, packed_ref[...], upper)

        pltpu.make_async_copy(block.at[pl.ds(0, rows), tile(t)], out_ref.at[:, 0, tile(t)], out_sem.at[t]).start()
        return c

    lax.fori_loop(0, tiles, step, 0)
    for t in range(tiles):
        pltpu.make_async_copy(block.at[pl.ds(0, rows), tile(t)], out_ref.at[:, 0, tile(t)], out_sem.at[t]).wait()


def finish(mine, counts, wide, mat, panels, squares, factors, parcels):
    rows, _, cols = mat.shape
    width, n_row, count = factors[0].shape[0], counts.shape[0], mine.shape[0]
    return pl.pallas_call(
        functools.partial(finish_kernel, n_row),
        out_shape=jax.ShapeDtypeStruct(mat.shape, jnp.float32),
        in_specs=[smem(), smem(), vmem(), raw(), raw(), raw()] + [vmem()] * 5 + [raw()] * len(parcels),
        out_specs=raw(),
        scratch_shapes=[
            pltpu.VMEM((rows + SUB, cols), jnp.float32),
            pltpu.VMEM((-(-n_row * count // LANES) * LANES, cols), jnp.float32),
            pltpu.VMEM((rows + SUB, width), jnp.float32),
            pltpu.VMEM((count, cols), jnp.float32),
            pltpu.VMEM((rows, width), jnp.bfloat16),
            pltpu.VMEM((rows, width), jnp.bfloat16),
            pltpu.VMEM((count, width), jnp.float32),
            pltpu.SemaphoreType.DMA((2 + 2 * n_row,)),
            pltpu.SemaphoreType.DMA((cols // width,)),
            pltpu.SemaphoreType.DMA((cols // width,)),
        ],
        cost_estimate=pl.CostEstimate(
            flops=6 * rows * cols * width, bytes_accessed=8 * rows * cols, transcendentals=0
        ),
        name="finish",
    )(mine, counts, wide, mat, *panels, *squares, *factors, *parcels)


def capacity(n_row, width):
    mean = width / n_row
    return -(-int(mean + 4 * (mean * (1 - 1 / n_row)) ** 0.5) // (2 * SUB)) * (2 * SUB)


def locate(pivots, n_row, row, count):
    width = pivots.shape[0]
    owner = pivots // width % n_row
    slot = pivots // (width * n_row) * width + pivots % width
    number = jnp.arange(width, dtype=jnp.int32)
    ahead = (owner[:, None] == owner[None, :]) & (number[None, :] < number[:, None])
    rank = jnp.sum(ahead, axis=1, dtype=jnp.int32)
    every = jnp.arange(n_row, dtype=jnp.int32)[:, None]
    ordinal = jnp.arange(count, dtype=jnp.int32)[:, None]
    own = (owner[None, :] == row) & (rank[None, :] == ordinal)
    mine = jnp.sum(jnp.where(own, slot[None, :], 0), axis=1, dtype=jnp.int32)
    return mine, jnp.sum(owner[None, :] == every, axis=1, dtype=jnp.int32)


def capped_step(n_row, n_col, matrix, pivots, begun):
    _, rows, _, cols = matrix.shape
    mat = matrix.reshape(rows, 1, cols)
    panel, wide, _, *messages = begun
    count = messages[0].shape[0] // 2
    row, col = lax.axis_index("prow"), lax.axis_index("pcol")
    both = ("prow", "pcol")
    turns = bits_of(n_col)[:0:-1]

    def exchange(x, k):
        return lax.ppermute(x, both, [(i * n_col, (i ^ k) * n_col) for i in range(n_row)])

    moved = [exchange(messages[k], k) for k in range(1, n_row)]
    mine, counts = locate(pivots, n_row, row, count)
    parcels = parcel(mat, mine, pivots, n_row)

    def send(x, k):
        return lax.ppermute(x, "prow", [(i, i ^ k) for i in range(n_row)])

    panel_moved = lax.ppermute(panel, "pcol", [(i, i + turns[0]) for i in range(0, n_col, 2 * turns[0])])
    *moved, panel_moved = lax.optimization_barrier((*moved, panel_moved))
    message = pack(wide, messages[:1] + moved)
    if n_row == 4:
        first, second = send(parcels[0], 1), send(parcels[1], 2)
        message, first, second = lax.optimization_barrier((message, first, second))
        kept = parcels[2]
        to_y, to_x = relay(kept, first, second)
        arrived = [kept, first, second, send(to_y, 2), send(to_x, 1)]
    else:
        arrived = [parcels[0]] + [send(parcels[k], k) for k in range(1, n_row)]

    pairs = [[(i, i + bit) for i in range(0, n_col, 2 * bit)] for bit in turns + [1]]
    newer = [(col & bit) != 0 for bit in turns]
    for n in range(len(turns)):
        panel = jnp.where(newer[n], panel_moved, panel)
        panel_moved = lax.ppermute(panel, "pcol", pairs[n + 1])
        message = jnp.where(newer[n], lax.ppermute(message, "pcol", pairs[n]), message)
        if n + 1 < len(turns):
            message, panel_moved = lax.optimization_barrier((message, panel_moved))
    message_new = lax.ppermute(message, "pcol", pairs[-1])
    factors = factor(message, message_new)
    out = finish(
        mine, counts, wide, mat, (panel, panel_moved), (message, message_new), factors, arrived
    )
    return out.reshape(matrix.shape)


def on_device(n_row, n_col, matrix, pivots):
    _, rows, _, cols = matrix.shape
    begun = begin(matrix.reshape(rows, 1, cols), pivots, n_row, capacity(n_row, pivots.shape[0]))
    return lax.cond(
        begun[2][0] > 0,
        lambda m, p, b: capped_step(n_row, n_col, m, p, b),
        lambda m, p, b: dense_step(n_row, n_col, m, p),
        matrix, pivots, begun,
    )


def solution(mesh):
    spec = P("prow", None, "pcol", None)
    n_row, n_col = mesh.shape["prow"], mesh.shape["pcol"]
    return jax.shard_map(
        functools.partial(on_device, n_row, n_col), mesh=mesh, in_specs=(spec, P()), out_specs=spec, check_vma=False
    )
```

```python
import functools

import jax
import jax.numpy as jnp
from jax import lax
from jax.experimental import pallas as pl
from jax.experimental.pallas import tpu as pltpu
from jax.sharding import PartitionSpec as P

LANES = 128
SUB = 8
HI = lax.Precision.HIGHEST


def pick_lane(tile, lane):
    return jnp.take_along_axis(tile, jnp.full((SUB, LANES), lane, jnp.int32), axis=1)


def row_of(tile, j):
    return jnp.broadcast_to(tile[j:j + 1, :], (SUB, LANES))


def factor_kernel(width, first_ref, second_ref, packed_ref, linv_ref, uinv_ref, a_ref, m_ref, v_ref, s_ref, sem):
    groups = a_ref.shape[0]
    tiles = groups * SUB // LANES
    per_tile = LANES // SUB
    per_block = width // SUB
    copies = [
        pltpu.make_async_copy(ref.at[pl.ds(0, groups * SUB), :], s_ref.at[n], sem.at[n])
        for n, ref in enumerate((first_ref, second_ref))
    ]
    for copy in copies:
        copy.start()
    sub = lax.broadcasted_iota(jnp.int32, (SUB, LANES), 0)
    lane = lax.broadcasted_iota(jnp.int32, (SUB, LANES), 1)

    for i in range(groups):
        diag = lane - (i % per_tile) * SUB == sub
        for t in range(tiles):
            block = jnp.where(diag, 1.0, 0.0) if i // per_tile == t else jnp.zeros((SUB, LANES), jnp.float32)
            m_ref[i, :, t * LANES:(t + 1) * LANES] = block
            if t > i // per_tile:
                linv_ref[i * SUB:(i + 1) * SUB, t * LANES:(t + 1) * LANES] = block

    for copy in copies:
        copy.wait()
    for i in range(groups):
        a_ref[i] = s_ref[0, i * SUB:(i + 1) * SUB, :] + s_ref[1, i * SUB:(i + 1) * SUB, :]

    def span(t):
        return slice(t * LANES, (t + 1) * LANES)

    for o in range(groups // per_block):
        base = o * per_block
        h = base // per_tile
        live = [(a_ref, t) for t in range(h + 1, tiles)] + [(m_ref, t) for t in range(h + 1)]

        def panel(i, c, base=base, h=h, live=live):
            b = base + i
            g = (b - h * per_tile) * SUB
            rows = pl.ds(pl.multiple_of(b * SUB, SUB), SUB)
            own = a_ref[b, :, span(h)]
            cols = [pick_lane(own, g + j) for j in range(SUB)]
            in_panel = (lane >= g) & (lane < g + SUB)
            after = lane >= g + SUB
            head = jnp.where(in_panel, jnp.where(lane - g == sub, -1.0, 0.0), jnp.where(after, own, 0.0))
            rest = [ref[b, :, span(t)] for ref, t in live]
            packed = own
            final = [head] + rest
            for j in range(SUB):
                at = sub == j
                coef = cols[j]
                r = 1.0 / row_of(coef, j)
                final = [jnp.where(at, x, y) for x, y in zip([head] + rest, final)]
                packed = jnp.where((lane == g + j) & (sub > j), coef * r, packed)
                for k in range(j, SUB):
                    packed = jnp.where((lane == g + k) & at, cols[k], packed)
                head_coef = jnp.where((sub < j) | after, coef, 0.0)
                v = row_of(head, j) * r
                head = jnp.where(at, v, head - head_coef * v)
                for n, x in enumerate(rest):
                    v = row_of(x, j) * r
                    rest[n] = jnp.where(at, v, x - coef * v)
                for k in range(j + 1, SUB):
                    v = row_of(cols[k], j) * r
                    cols[k] = jnp.where(at, v, cols[k] - coef * v)
            for t in range(h):
                packed_ref[rows, span(t)] = a_ref[b, :, span(t)]
            packed_ref[rows, span(h)] = jnp.where(after, final[0], packed)
            for (ref, t), x in zip(live, final[1:]):
                (packed_ref if ref is a_ref else linv_ref)[rows, span(t)] = x
            a_ref[b, :, span(h)] = head
            v_ref[0] = head
            for n, ((ref, t), x) in enumerate(zip(live, rest)):
                ref[b, :, span(t)] = x
                v_ref[n + 1] = x
            others = [base + lax.rem(i + s, per_block) for s in range(1, per_block)]
            heads = [a_ref[r, :, span(h)] for r in others]
            facs = [[pick_lane(x, g + j) for j in range(SUB)] for x in heads]
            for n, (ref, t) in enumerate([(a_ref, h)] + live):
                old = [jnp.where(in_panel, 0.0, x) for x in heads] if n == 0 else [ref[r, :, span(t)] for r in others]
                vs = [row_of([head] + rest and ([head] + rest)[n], j) for j in range(SUB)]
                for x, fac, r in zip(old, facs, others):
                    acc = [fac[j] * vs[j] for j in range(SUB)]
                    while len(acc) > 1:
                        acc = [p + q for p, q in zip(acc[::2], acc[1::2])]
                    ref[r, :, span(t)] = x - acc[0]
            return c

        lax.fori_loop(0, per_block, panel, 0)

        lo = (base % per_tile) * SUB
        pad = [jnp.zeros((n, LANES), jnp.float32) for n in (lo, LANES - lo - width)]

        def stack(x):
            return jnp.concatenate([p for p in (pad[0], x, pad[1]) if p.shape[0]], axis=0)

        def flat(ref, first, last, t):
            return ref[first:last, :, span(t)].reshape((last - first) * SUB, LANES)

        end = base + per_block
        right = [stack(flat(ref, base, end, t)) for ref, t in [(a_ref, h)] + live]
        for first, last in ((end, groups), (0, base)):
            if first == last:
                continue
            left = flat(a_ref, first, last, h)
            column = lax.broadcasted_iota(jnp.int32, left.shape, 1)
            for n, (ref, t) in enumerate([(a_ref, h)] + live):
                if ref is m_ref and first == 0:
                    continue
                old = left if n else None
                old = jnp.where((column >= lo) & (column < lo + width), 0.0, left) if n == 0 else flat(ref, first, last, t)
                new = old - jnp.dot(left, right[n], precision=HI, preferred_element_type=jnp.float32)
                ref[first:last, :, span(t)] = new.reshape(last - first, SUB, LANES)

    ri = lax.broadcasted_iota(jnp.int32, (SUB, LANES), 0)
    for i in range(groups):
        for t in range(tiles):
            x = a_ref[i, :, span(t)]
            keep = lane + t * LANES >= ri + i * SUB
            uinv_ref[i * SUB:(i + 1) * SUB, span(t)] = jnp.where(keep, -x, 0.0)


def vmem():
    return pl.BlockSpec(memory_space=pltpu.VMEM)


def smem():
    return pl.BlockSpec(memory_space=pltpu.SMEM)


def factor(square, extra, width=32):
    size = square.shape[1]
    out = jax.ShapeDtypeStruct((size, size), jnp.float32)
    return pl.pallas_call(
        functools.partial(factor_kernel, width),
        out_shape=(out, out, out),
        in_specs=[raw(), raw()],
        out_specs=(vmem(),) * 3,
        scratch_shapes=[
            pltpu.VMEM((size // SUB, SUB, size), jnp.float32),
            pltpu.VMEM((size // SUB, SUB, size), jnp.float32),
            pltpu.VMEM((1 + size // LANES, SUB, LANES), jnp.float32),
            pltpu.VMEM((2, size, size), jnp.float32),
            pltpu.SemaphoreType.DMA((2,)),
        ],
        cost_estimate=pl.CostEstimate(flops=4 * size**3, bytes_accessed=50_000_000, transcendentals=0),
        compiler_params=pltpu.CompilerParams(vmem_limit_bytes=6 << 20),
        name="factor",
    )(square, extra)


def pick_kernel(slot_ref, own_ref, block_ref, out_ref):
    def group(q, c):
        for u in range(SUB):
            j = q * SUB + u
            row = block_ref[pl.ds(slot_ref[j], 1), :]
            out_ref[pl.ds(j, 1), :] = row * own_ref[j].astype(jnp.float32)
        return c

    lax.fori_loop(0, out_ref.shape[0] // SUB, group, 0)


def pick(block, slots, owned, tiles):
    rows, width = block.shape[0], slots.shape[0]
    return pl.pallas_call(
        pick_kernel,
        grid=(tiles,),
        out_shape=jax.ShapeDtypeStruct((width, tiles * width), jnp.float32),
        in_specs=[smem(), smem(), pl.BlockSpec((rows, width), lambda t: (0, t))],
        out_specs=pl.BlockSpec((width, width), lambda t: (0, t)),
        cost_estimate=pl.CostEstimate(
            flops=width * width * tiles, bytes_accessed=4 * (rows + width) * width * tiles, transcendentals=0
        ),
        name="pick",
    )(slots, owned, block)


def place_rows(slot_ref, rows_ref, target_ref):
    def group(q, c):
        for u in range(SUB):
            j = q * SUB + u
            target_ref[pl.ds(slot_ref[j], 1), :] = rows_ref[pl.ds(j, 1), :]
        return c

    lax.fori_loop(0, rows_ref.shape[0] // SUB, group, 0)


def place_kernel(slot_ref, block_ref, rows_ref, out_ref, buf_ref):
    rows = block_ref.shape[0]
    buf_ref[:rows, :] = block_ref[...]
    place_rows(slot_ref, rows_ref, buf_ref)
    out_ref[...] = buf_ref[:rows, :]


def place(block, rows, slots):
    height, width = block.shape[0], slots.shape[0]
    return pl.pallas_call(
        place_kernel,
        grid=(1,),
        out_shape=jax.ShapeDtypeStruct((height, width), jnp.float32),
        in_specs=[
            smem(),
            pl.BlockSpec((height, width), lambda t: (0, 0)),
            pl.BlockSpec((width, width), lambda t: (0, 0)),
        ],
        out_specs=pl.BlockSpec((height, width), lambda t: (0, 0)),
        scratch_shapes=[pltpu.VMEM((height + SUB, width), jnp.float32)],
        cost_estimate=pl.CostEstimate(flops=0, bytes_accessed=8 * height * width, transcendentals=0),
        name="place",
    )(slots, block, rows)


def halves(x):
    high = x.astype(jnp.bfloat16)
    low = (x - high.astype(jnp.float32)).astype(jnp.bfloat16)
    return high, low


def wide_left(x):
    high, low = halves(x)
    return jnp.concatenate([high, low, high], axis=1)


def wide_right(x):
    high, low = halves(x)
    return jnp.concatenate([low, high, high], axis=0)


def wide_dot(left, right):
    return jnp.dot(left, right, preferred_element_type=jnp.float32)


def split_dot(left, right):
    acc = jnp.dot(left[0], right[1], preferred_element_type=jnp.float32)
    acc += jnp.dot(left[1], right[0], preferred_element_type=jnp.float32)
    return acc + jnp.dot(left[0], right[0], preferred_element_type=jnp.float32)


def update_kernel(
    slot_ref, where_ref, block_ref, panel_ref, pivot_ref, top_ref, packed_ref, linv_ref, uinv_ref,
    out_ref, high_ref, low_ref, buf_ref,
):
    rows, width = panel_ref.shape
    t = pl.program_id(0)
    first_row = where_ref[0] == 0
    first_col = (where_ref[1] == 0) & (t == 0)

    @pl.when(t == 0)
    def _():
        lower = jnp.dot(panel_ref[...], uinv_ref[...], precision=HI, preferred_element_type=jnp.float32)
        high_ref[...], low_ref[...] = halves(lower)
        out_ref[...] = lower

    upper = jnp.dot(linv_ref[...], pivot_ref[...], precision=HI, preferred_element_type=jnp.float32)

    @pl.when(jnp.logical_not(first_col))
    def _():
        buf_ref[:rows, :] = block_ref[...]
        place_rows(slot_ref, top_ref, buf_ref)
        out_ref[...] = buf_ref[:rows, :] - split_dot((high_ref[...], low_ref[...]), halves(upper))

    @pl.when(first_row)
    def _():
        out_ref[:width, :] = jnp.where(first_col, packed_ref[...], upper)


def update(block, panel, pivot_rows, old_top, packed, linv, uinv, slots, where):
    rows, cols = block.shape
    width = slots.shape[0]
    square = pl.BlockSpec((width, width), lambda t: (0, 0))
    tall = pl.BlockSpec((rows, width), lambda t: (0, t))
    flat = pl.BlockSpec((width, width), lambda t: (0, t))
    return pl.pallas_call(
        update_kernel,
        grid=(cols // width,),
        out_shape=jax.ShapeDtypeStruct((rows, cols), jnp.float32),
        in_specs=[
            smem(), smem(), tall, pl.BlockSpec((rows, width), lambda t: (0, 0)), flat, flat, square, square, square,
        ],
        out_specs=tall,
        scratch_shapes=[
            pltpu.VMEM((rows, width), jnp.bfloat16),
            pltpu.VMEM((rows, width), jnp.bfloat16),
            pltpu.VMEM((rows + SUB, width), jnp.float32),
        ],
        cost_estimate=pl.CostEstimate(
            flops=6 * rows * cols * width, bytes_accessed=8 * rows * cols, transcendentals=0
        ),
        name="update",
    )(slots, where, block, panel, pivot_rows, old_top, packed, linv, uinv)


def bits_of(n):
    return [1 << i for i in range(n.bit_length() - 1)]


def sum_over_rows(x, order, n_row):
    for bit in order:
        x = x + lax.ppermute(x, "prow", [(i, i ^ bit) for i in range(n_row)])
    return x


def spread_rows(x, order, n_row):
    have = [0]
    for bit in order:
        x = x + lax.ppermute(x, "prow", [(i, i ^ bit) for i in have])
        have = have + [i ^ bit for i in have]
    return x


def spread_cols(x, order):
    have = [0]
    for bit in order:
        x = x + lax.ppermute(x, "pcol", [(i, i ^ bit) for i in have])
        have = have + [i ^ bit for i in have]
    return x


def dense_step(n_row, n_col, matrix, pivots):
    block = matrix[0, :, 0, :]
    rows, cols = block.shape
    width = pivots.shape[0]
    row = lax.axis_index("prow")
    col = lax.axis_index("pcol")
    owner = pivots // width % n_row
    slot = pivots // (width * n_row) * width + pivots % width
    mine = owner == row
    owned = mine.astype(jnp.int32)
    target = jnp.where(mine, slot, rows)
    where = jnp.stack([row, col]).astype(jnp.int32)
    row_bits, col_bits = bits_of(n_row), bits_of(n_col)
    at_first_row = row == 0
    at_first_col = col == 0

    square = pick(block, slot, owned * at_first_col.astype(jnp.int32), 1)
    square = sum_over_rows(square, row_bits, n_row)
    square = spread_cols(square, col_bits[::-1])
    packed, linv, uinv = factor(square, jnp.zeros_like(square))

    top = jnp.where(at_first_row, block[:width], 0.0)
    top_panel = spread_rows(top[:, :width], row_bits, n_row)
    panel = place(block, top_panel, target)
    panel = spread_cols(jnp.where(at_first_col, panel, 0.0), col_bits[::-1])

    picked = pick(block, slot, owned, cols // width)
    half = width // 2
    pivot_rows = jnp.concatenate([
        sum_over_rows(picked[:half], row_bits, n_row),
        sum_over_rows(picked[half:], row_bits[::-1], n_row),
    ])
    old_top = jnp.concatenate([
        spread_rows(top[:half], row_bits, n_row),
        spread_rows(top[half:], row_bits[::-1], n_row),
    ])
    result = update(block, panel, pivot_rows, old_top, packed, linv, uinv, target, where)
    return result[None, :, None, :]


def raw():
    return pl.BlockSpec(memory_space=pl.ANY)


def thirds(x):
    high = x.astype(jnp.bfloat16)
    rest = x - high.astype(jnp.float32)
    middle = rest.astype(jnp.bfloat16)
    return high, middle, (rest - middle.astype(jnp.float32)).astype(jnp.bfloat16)


def select_dot(choice, parts):
    choice = choice.astype(jnp.bfloat16)
    high, middle, low = [jnp.dot(choice, x, preferred_element_type=jnp.float32) for x in parts]
    return high + (middle + low)


def pick_dot(parts, choice):
    choice = choice.astype(jnp.bfloat16)
    high, middle, low = [jnp.dot(x, choice, preferred_element_type=jnp.float32) for x in parts]
    return high + (middle + low)


def begin_kernel(n_row, pivot_ref, mat_ref, panel_ref, wide_ref, fits_ref, *refs):
    messages, sem = refs[:n_row], refs[-1]
    rows, width = panel_ref.shape
    count = messages[0].shape[0] // 2
    width_log, row_log = width.bit_length() - 1, n_row.bit_length() - 1
    row = lax.axis_index("prow")
    copy = pltpu.make_async_copy(mat_ref.at[:, 0, pl.ds(0, width)], panel_ref, sem)
    copy.start()
    pivot = pivot_ref[...]
    block = lax.shift_right_logical(pivot, width_log)
    owner = block & (n_row - 1)
    slot = lax.shift_left(lax.shift_right_logical(block, row_log), width_log) + (pivot & (width - 1))
    _, rank = owners(pivot, n_row)
    fits_ref[0] = (jnp.max(rank) < count).astype(jnp.int32)
    place = ((owner ^ row) * count + rank).astype(jnp.float32)
    eye = lax.broadcasted_iota(jnp.int32, (width, width), 0) == lax.broadcasted_iota(jnp.int32, (width, width), 1)
    spread = jnp.where(eye, place, 0.0)
    wide = jnp.dot(spread, jnp.ones((width, LANES), jnp.float32), precision=HI, preferred_element_type=jnp.float32)
    wide_ref[...] = wide.astype(jnp.int32)
    ordinal = lax.broadcasted_iota(jnp.int32, (count, width), 0)
    mine = jnp.where((ordinal == rank) & (owner == row), 1.0, 0.0).astype(jnp.bfloat16)
    at_slot = jnp.where(lax.broadcasted_iota(jnp.int32, (rows, width), 0) == slot, 1.0, 0.0).astype(jnp.bfloat16)
    choice = lax.dot_general(mine, at_slot, (((1,), (1,)), ((), ())), preferred_element_type=jnp.float32)
    copy.wait()
    own = select_dot(choice, thirds(panel_ref[...]))
    for k in range(n_row):
        messages[k][:count, :] = own

    @pl.when(row == 0)
    def _():
        top = thirds(panel_ref[:width, :])
        for p in range(n_row):
            messages[p][count:, :] = select_dot(jnp.where((ordinal == rank) & (owner == p), 1.0, 0.0), top)


def begin(mat, pivots, n_row, count):
    rows, width = mat.shape[0], pivots.shape[0]
    message = jax.ShapeDtypeStruct((2 * count, width), jnp.float32)
    return pl.pallas_call(
        functools.partial(begin_kernel, n_row),
        out_shape=(
            jax.ShapeDtypeStruct((rows, width), jnp.float32),
            jax.ShapeDtypeStruct((width, LANES), jnp.int32),
            jax.ShapeDtypeStruct((1,), jnp.int32),
        ) + (message,) * n_row,
        in_specs=[vmem(), raw()],
        out_specs=(vmem(), vmem(), smem()) + (vmem(),) * n_row,
        scratch_shapes=[pltpu.SemaphoreType.DMA],
        cost_estimate=pl.CostEstimate(flops=0, bytes_accessed=10_000_000, transcendentals=0),
        compiler_params=pltpu.CompilerParams(vmem_limit_bytes=12 << 20),
        name="begin",
    )(pivots[None, :], mat)


def parcel_kernel(n_row, mine_ref, pivot_ref, mat_ref, *refs):
    outs, own, block, sem = refs[:-3], refs[-3], refs[-2], refs[-1]
    count, cols = own.shape
    half = count // 2
    width = pivot_ref.shape[1]

    def group(q, c):
        for u in range(SUB):
            i = q * SUB + u
            pltpu.make_async_copy(mat_ref.at[mine_ref[i]], own.at[pl.ds(i, 1), :], sem.at[0]).start()
        return c

    lax.fori_loop(0, count // SUB, group, 0)

    @pl.when(lax.axis_index("prow") == 0)
    def _():
        copy = pltpu.make_async_copy(mat_ref.at[pl.ds(0, width), 0, :], block, sem.at[1])
        copy.start()
        owner, rank = owners(pivot_ref[...], n_row)
        ordinal = lax.broadcasted_iota(jnp.int32, (count, width), 0)
        choices = [jnp.where((ordinal == rank) & (owner == p), 1.0, 0.0) for p in range(n_row)]
        choice = jnp.concatenate(choices, axis=0)
        copy.wait()

        def piece(t, c):
            at = pl.ds(pl.multiple_of(t * width, width), width)
            tops = select_dot(choice, thirds(block[:, at]))
            for p in range(n_row):
                for part in range(2):
                    first = p * count + part * half
                    for ref, base in top_places(n_row, half, outs, p, part):
                        ref[pl.ds(base, half), at] = tops[first:first + half]
            return c

        lax.fori_loop(0, cols // width, piece, 0)

    pltpu.make_async_copy(mat_ref.at[pl.ds(0, count), 0, :], own, sem.at[0]).wait()
    if n_row == 4:
        outs[0][:half, :] = own[:half, :]
        outs[1][:half, :] = own[half:, :]
        outs[2][:count, :] = own[...]
    else:
        outs[0][:count, :] = own[...]
        for p in range(1, n_row):
            outs[p][:count, :] = own[...]


def top_places(n_row, half, outs, p, part):
    if n_row != 4:
        return [(outs[p], 2 * half + part * half)]
    if p == 0:
        return [(outs[2], 2 * half + part * half)]
    if p == 3:
        return [(outs[part], 2 * half)]
    if part == p - 1:
        return [(outs[part], half)]
    return [(outs[2], (4 + part) * half)]


def owners(pivot, n_row):
    width = pivot.shape[1]
    owner = lax.shift_right_logical(pivot, width.bit_length() - 1) & (n_row - 1)
    held = lax.broadcasted_iota(jnp.int32, (-(-n_row // 16) * 16, width), 0) == owner
    before = lax.broadcasted_iota(jnp.int32, (width, width), 0) < lax.broadcasted_iota(jnp.int32, (width, width), 1)
    held = jnp.where(held, 1.0, 0.0)
    earlier = jnp.dot(
        held.astype(jnp.bfloat16), jnp.where(before, 1.0, 0.0).astype(jnp.bfloat16), preferred_element_type=jnp.float32
    )
    return owner, jnp.sum(held * earlier, axis=0, keepdims=True).astype(jnp.int32)


def parcel(mat, mine, pivots, n_row):
    count, width, cols = mine.shape[0], pivots.shape[0], mat.shape[2]
    half = count // 2
    sizes = [3 * half, 3 * half, 6 * half] if n_row == 4 else [2 * count] * n_row
    return pl.pallas_call(
        functools.partial(parcel_kernel, n_row),
        out_shape=tuple(jax.ShapeDtypeStruct((size, cols), jnp.float32) for size in sizes),
        in_specs=[smem(), vmem(), raw()],
        out_specs=(vmem(),) * len(sizes),
        scratch_shapes=[
            pltpu.VMEM((count, cols), jnp.float32),
            pltpu.VMEM((width, cols), jnp.float32),
            pltpu.SemaphoreType.DMA((2,)),
        ],
        cost_estimate=pl.CostEstimate(flops=0, bytes_accessed=16_000_000, transcendentals=0),
        compiler_params=pltpu.CompilerParams(vmem_limit_bytes=16 << 20),
        name="parcel",
    )(mine, pivots[None, :], mat)


def relay_kernel(kept_ref, first_ref, second_ref, y_ref, x_ref, sem):
    half = first_ref.shape[0] // 3
    row = lax.axis_index("prow")

    def move(source, base, dest, at, n):
        return pltpu.make_async_copy(source.at[pl.ds(base, half), :], dest.at[pl.ds(at, half), :], sem.at[n])

    copies = [
        move(kept_ref, 0, y_ref, 0, 0),
        move(kept_ref, half, x_ref, 0, 1),
        move(first_ref, 0, y_ref, half, 2),
        move(second_ref, 0, x_ref, half, 3),
    ]
    for copy in copies:
        copy.start()

    @pl.when(row == 0)
    def _():
        move(kept_ref, 4 * half, y_ref, 2 * half, 4).start()
        move(kept_ref, 5 * half, x_ref, 2 * half, 5).start()

    @pl.when(row != 0)
    def _():
        move(first_ref, 2 * half, y_ref, 2 * half, 4).start()
        move(second_ref, 2 * half, x_ref, 2 * half, 5).start()

    for copy in copies:
        copy.wait()
    move(first_ref, 2 * half, y_ref, 2 * half, 4).wait()
    move(second_ref, 2 * half, x_ref, 2 * half, 5).wait()


def relay(kept, first, second):
    shape = jax.ShapeDtypeStruct(first.shape, jnp.float32)
    return pl.pallas_call(
        relay_kernel,
        out_shape=(shape, shape),
        in_specs=[raw()] * 3,
        out_specs=(vmem(), vmem()),
        scratch_shapes=[pltpu.SemaphoreType.DMA((6,))],
        cost_estimate=pl.CostEstimate(flops=0, bytes_accessed=4_000_000, transcendentals=0),
        compiler_params=pltpu.CompilerParams(vmem_limit_bytes=4 << 20),
        name="relay",
    )(kept, first, second)


def pack_kernel(n_row, wide_ref, *refs):
    parts, out_ref, stack, sem = refs[:n_row], refs[n_row], refs[n_row + 1], refs[n_row + 2]
    width = wide_ref.shape[0]
    count = out_ref.shape[0] - width
    row, col = lax.axis_index("prow"), lax.axis_index("pcol")
    total = stack.shape[0]

    @pl.when(col == 0)
    def _():
        copies = [
            pltpu.make_async_copy(parts[k].at[pl.ds(0, count), :], stack.at[pl.ds(k * count, count), :], sem.at[k])
            for k in range(n_row)
        ]
        for copy in copies:
            copy.start()
        for k in range(n_row):
            @pl.when(row == k)
            def _(k=k):
                pltpu.make_async_copy(
                    parts[k].at[pl.ds(count, count), :], out_ref.at[pl.ds(width, count), :], sem.at[n_row]
                ).start()
        if total > n_row * count:
            stack[n_row * count:, :] = jnp.zeros((total - n_row * count, width), jnp.float32)
        lanes = lax.broadcasted_iota(jnp.int32, (width, LANES), 1)
        choice = jnp.concatenate(
            [jnp.where(lanes + t * LANES == wide_ref[...], 1.0, 0.0) for t in range(total // LANES)], axis=1
        )
        for copy in copies:
            copy.wait()
        out_ref[:width, :] = select_dot(choice, thirds(stack[...]))
        pltpu.make_async_copy(
            parts[0].at[pl.ds(count, count), :], out_ref.at[pl.ds(width, count), :], sem.at[n_row]
        ).wait()

    @pl.when(col != 0)
    def _():
        out_ref[...] = jnp.zeros_like(out_ref)


def pack(wide, parts):
    n_row, width = len(parts), wide.shape[0]
    count = parts[0].shape[0] // 2
    return pl.pallas_call(
        functools.partial(pack_kernel, n_row),
        out_shape=jax.ShapeDtypeStruct((width + count, width), jnp.float32),
        in_specs=[vmem()] + [raw()] * n_row,
        out_specs=vmem(),
        scratch_shapes=[
            pltpu.VMEM((-(-n_row * count // LANES) * LANES, width), jnp.float32),
            pltpu.SemaphoreType.DMA((n_row + 1,)),
        ],
        cost_estimate=pl.CostEstimate(flops=0, bytes_accessed=4_000_000, transcendentals=0),
        compiler_params=pltpu.CompilerParams(vmem_limit_bytes=6 << 20),
        name="pack",
    )(wide, *parts)


def unpack_parcels(n_row, count, parcels):
    half = count // 2
    if n_row != 4:
        parts = [(x, part * half) for x in parcels for part in range(2)]
        return parts, [[(x, count + part * half) for part in range(2)] for x in parcels]
    kept, first, second, third, fourth = parcels
    parts = [
        (kept, 0), (kept, half), (first, 0), (fourth, 0), (third, 0), (second, 0), (third, half), (fourth, half)
    ]
    tops = [
        [(kept, 2 * half), (kept, 3 * half)],
        [(first, half), (fourth, 2 * half)],
        [(third, 2 * half), (second, half)],
        [(third, 2 * half), (fourth, 2 * half)],
    ]
    return parts, tops


def put_rows(slot_ref, held, rows_ref, target_ref):
    spare = target_ref.shape[0] - SUB

    def group(q, c):
        for u in range(SUB):
            i = q * SUB + u
            slot = jnp.where(i < held, slot_ref[i], spare)
            target_ref[pl.ds(slot, 1), :] = rows_ref[pl.ds(i, 1), :]
        return c

    lax.fori_loop(0, (held + SUB - 1) // SUB, group, 0)


def finish_kernel(
    n_row, mine_ref, counts_ref, wide_ref, mat_ref, panel_ref, panel_new_ref, square_ref, square_new_ref,
    packed_ref, linv_ref, uinv_ref, *refs,
):
    n_parcels = 5 if n_row == 4 else n_row
    parcels, refs = refs[:n_parcels], refs[n_parcels:]
    out_ref, block, pivot, panel, old, left, lower, top, sem, in_sem, out_sem = refs
    rows, _, cols = mat_ref.shape
    width = linv_ref.shape[0]
    count = mine_ref.shape[0]
    half = count // 2
    stacked = n_row * count
    parts, tops = unpack_parcels(n_row, count, parcels)
    tiles = cols // width
    row, col = lax.axis_index("prow"), lax.axis_index("pcol")

    def tile(t):
        return pl.ds(pl.multiple_of(t * width, width), width)

    @pl.when(col % 2 == 0)
    def _():
        pltpu.make_async_copy(panel_ref, panel.at[pl.ds(0, rows)], sem.at[0]).start()

    @pl.when(col % 2 == 1)
    def _():
        pltpu.make_async_copy(panel_new_ref, panel.at[pl.ds(0, rows)], sem.at[0]).start()

    top_copies = [
        pltpu.make_async_copy(ref.at[pl.ds(width, count), :], top.at[n], sem.at[1 + n])
        for n, ref in enumerate((square_ref, square_new_ref))
    ]
    for copy in top_copies:
        copy.start()

    def fetch(t, c):
        pltpu.make_async_copy(mat_ref.at[:, 0, tile(t)], block.at[pl.ds(0, rows), tile(t)], in_sem.at[0, t]).start()
        for n, (ref, base) in enumerate(parts):
            dest = pivot.at[pl.ds(n * half, half), tile(t)]
            pltpu.make_async_copy(ref.at[pl.ds(base, half), tile(t)], dest, in_sem.at[1, t]).start()
        for p in range(n_row):
            @pl.when(row == p)
            def _(p=p):
                for part, (ref, base) in enumerate(tops[p]):
                    dest = old.at[pl.ds(part * half, half), tile(t)]
                    pltpu.make_async_copy(ref.at[pl.ds(base, half), tile(t)], dest, in_sem.at[2, t]).start()
        return c

    lax.fori_loop(0, tiles, fetch, 0)
    if pivot.shape[0] > stacked:
        pivot[stacked:, :] = jnp.zeros((pivot.shape[0] - stacked, cols), jnp.float32)

    lanes = lax.broadcasted_iota(jnp.int32, (width, LANES), 1)
    places = jnp.concatenate(
        [jnp.where(lanes + t * LANES == wide_ref[...], 1.0, 0.0) for t in range(pivot.shape[0] // LANES)], axis=1
    )
    spread_inv = wide_left(pick_dot(thirds(linv_ref[...]), places))
    for copy in top_copies:
        copy.wait()
    top[0] = top[0] + top[1]
    pltpu.make_async_copy(panel_ref, panel.at[pl.ds(0, rows)], sem.at[0]).wait()
    put_rows(mine_ref, counts_ref[row], top.at[0], panel)
    lower[...] = wide_dot(wide_left(panel[:rows, :]), wide_right(uinv_ref[...]))
    left[...] = wide_left(lower[...])

    def step(t, c):
        first_col = (col == 0) & (t == 0)
        pltpu.make_async_copy(
            mat_ref.at[pl.ds(0, stacked), 0, tile(t)], pivot.at[pl.ds(0, stacked), tile(t)], in_sem.at[1, t]
        ).wait()
        upper = wide_dot(spread_inv, wide_right(pivot[:, tile(t)]))
        pltpu.make_async_copy(mat_ref.at[pl.ds(0, count), 0, tile(t)], old.at[:, tile(t)], in_sem.at[2, t]).wait()
        pltpu.make_async_copy(mat_ref.at[:, 0, tile(t)], block.at[pl.ds(0, rows), tile(t)], in_sem.at[0, t]).wait()

        @pl.when(jnp.logical_not(first_col))
        def _():
            put_rows(mine_ref, counts_ref[row], old.at[:, tile(t)], block.at[:, tile(t)])
            block[:rows, tile(t)] = block[:rows, tile(t)] - wide_dot(left[...], wide_right(upper))

        @pl.when(first_col)
        def _():
            block[:rows, tile(t)] = lower[...]

        @pl.when(row == 0)
        def _():
            block[:width, tile(t)] = jnp.where(first_col, packed_ref[...], upper)

        pltpu.make_async_copy(block.at[pl.ds(0, rows), tile(t)], out_ref.at[:, 0, tile(t)], out_sem.at[t]).start()
        return c

    lax.fori_loop(0, tiles, step, 0)

    def drain(t, c):
        pltpu.make_async_copy(block.at[pl.ds(0, rows), tile(t)], out_ref.at[:, 0, tile(t)], out_sem.at[t]).wait()
        return c

    lax.fori_loop(0, tiles, drain, 0)


def finish(mine, counts, wide, mat, panels, squares, factors, parcels):
    rows, _, cols = mat.shape
    width, n_row, count = factors[0].shape[0], counts.shape[0], mine.shape[0]
    return pl.pallas_call(
        functools.partial(finish_kernel, n_row),
        out_shape=jax.ShapeDtypeStruct(mat.shape, jnp.float32),
        in_specs=[smem(), smem(), vmem()] + [raw()] * 5 + [vmem()] * 3 + [raw()] * len(parcels),
        out_specs=raw(),
        scratch_shapes=[
            pltpu.VMEM((rows + SUB, cols), jnp.float32),
            pltpu.VMEM((-(-n_row * count // LANES) * LANES, cols), jnp.float32),
            pltpu.VMEM((rows + SUB, width), jnp.float32),
            pltpu.VMEM((count, cols), jnp.float32),
            pltpu.VMEM((rows, 3 * width), jnp.bfloat16),
            pltpu.VMEM((rows, width), jnp.float32),
            pltpu.VMEM((2, count, width), jnp.float32),
            pltpu.SemaphoreType.DMA((3,)),
            pltpu.SemaphoreType.DMA((3, cols // width)),
            pltpu.SemaphoreType.DMA((cols // width,)),
        ],
        cost_estimate=pl.CostEstimate(
            flops=6 * rows * cols * width, bytes_accessed=8 * rows * cols, transcendentals=0
        ),
        compiler_params=pltpu.CompilerParams(vmem_limit_bytes=26 << 20),
        name="finish",
    )(mine, counts, wide, mat, *panels, *squares, *factors, *parcels)


def capacity(n_row, width):
    mean = width / n_row
    return -(-int(mean + 4 * (mean * (1 - 1 / n_row)) ** 0.5) // (2 * SUB)) * (2 * SUB)


def locate(pivots, n_row, row, count):
    width = pivots.shape[0]
    owner = pivots // width % n_row
    slot = pivots // (width * n_row) * width + pivots % width
    number = jnp.arange(width, dtype=jnp.int32)
    ahead = (owner[:, None] == owner[None, :]) & (number[None, :] < number[:, None])
    rank = jnp.sum(ahead, axis=1, dtype=jnp.int32)
    every = jnp.arange(n_row, dtype=jnp.int32)[:, None]
    ordinal = jnp.arange(count, dtype=jnp.int32)[:, None]
    own = (owner[None, :] == row) & (rank[None, :] == ordinal)
    mine = jnp.sum(jnp.where(own, slot[None, :], 0), axis=1, dtype=jnp.int32)
    return mine, jnp.sum(owner[None, :] == every, axis=1, dtype=jnp.int32)


def capped_step(n_row, n_col, matrix, pivots, begun):
    _, rows, _, cols = matrix.shape
    mat = matrix.reshape(rows, 1, cols)
    panel, wide, _, *messages = begun
    count = messages[0].shape[0] // 2
    row, col = lax.axis_index("prow"), lax.axis_index("pcol")
    both = ("prow", "pcol")
    turns = bits_of(n_col)[:0:-1]

    def exchange(x, k):
        return lax.ppermute(x, both, [(i * n_col, (i ^ k) * n_col) for i in range(n_row)])

    moved = [exchange(messages[k], k) for k in range(1, n_row)]
    mine, counts = locate(pivots, n_row, row, count)
    parcels = parcel(mat, mine, pivots, n_row)

    def send(x, k):
        return lax.ppermute(x, "prow", [(i, i ^ k) for i in range(n_row)])

    panel_moved = lax.ppermute(panel, "pcol", [(i, i + turns[0]) for i in range(0, n_col, 2 * turns[0])])
    *moved, panel_moved = lax.optimization_barrier((*moved, panel_moved))
    message = pack(wide, messages[:1] + moved)
    if n_row == 4:
        first, second = send(parcels[0], 1), send(parcels[1], 2)
        message, first, second = lax.optimization_barrier((message, first, second))
        kept = parcels[2]
        to_y, to_x = relay(kept, first, second)
        arrived = [kept, first, second, send(to_y, 2), send(to_x, 1)]
    else:
        arrived = [parcels[0]] + [send(parcels[k], k) for k in range(1, n_row)]

    pairs = [[(i, i + bit) for i in range(0, n_col, 2 * bit)] for bit in turns + [1]]
    newer = [(col & bit) != 0 for bit in turns]
    for n in range(len(turns)):
        panel = jnp.where(newer[n], panel_moved, panel)
        panel_moved = lax.ppermute(panel, "pcol", pairs[n + 1])
        message = jnp.where(newer[n], lax.ppermute(message, "pcol", pairs[n]), message)
        if n + 1 < len(turns):
            message, panel_moved = lax.optimization_barrier((message, panel_moved))
    message_new = lax.ppermute(message, "pcol", pairs[-1])
    factors = factor(message, message_new)
    out = finish(
        mine, counts, wide, mat, (panel, panel_moved), (message, message_new), factors, arrived
    )
    return out.reshape(matrix.shape)


def on_device(n_row, n_col, matrix, pivots):
    _, rows, _, cols = matrix.shape
    begun = begin(matrix.reshape(rows, 1, cols), pivots, n_row, capacity(n_row, pivots.shape[0]))
    return lax.cond(
        begun[2][0] > 0,
        lambda m, p, b: capped_step(n_row, n_col, m, p, b),
        lambda m, p, b: dense_step(n_row, n_col, m, p),
        matrix, pivots, begun,
    )


def solution(mesh):
    spec = P("prow", None, "pcol", None)
    n_row, n_col = mesh.shape["prow"], mesh.shape["pcol"]
    return jax.shard_map(
        functools.partial(on_device, n_row, n_col), mesh=mesh, in_specs=(spec, P()), out_specs=spec, check_vma=False
    )
```

```python
import functools

import jax
import jax.numpy as jnp
from jax import lax
from jax.experimental import pallas as pl
from jax.experimental.pallas import tpu as pltpu
from jax.sharding import PartitionSpec as P

LANES = 128
SUB = 8
HI = lax.Precision.HIGHEST


def pick_lane(tile, lane):
    return jnp.take_along_axis(tile, jnp.full((SUB, LANES), lane, jnp.int32), axis=1)


def row_of(tile, j):
    return jnp.broadcast_to(tile[j:j + 1, :], (SUB, LANES))


def factor_kernel(width, first_ref, second_ref, packed_ref, linv_ref, uinv_ref, a_ref, m_ref, v_ref, s_ref, sem):
    groups = a_ref.shape[0]
    tiles = groups * SUB // LANES
    per_tile = LANES // SUB
    per_block = width // SUB
    copies = [
        pltpu.make_async_copy(ref.at[pl.ds(0, groups * SUB), :], s_ref.at[n], sem.at[n])
        for n, ref in enumerate((first_ref, second_ref))
    ]
    for copy in copies:
        copy.start()
    sub = lax.broadcasted_iota(jnp.int32, (SUB, LANES), 0)
    lane = lax.broadcasted_iota(jnp.int32, (SUB, LANES), 1)

    for i in range(groups):
        diag = lane - (i % per_tile) * SUB == sub
        for t in range(tiles):
            block = jnp.where(diag, 1.0, 0.0) if i // per_tile == t else jnp.zeros((SUB, LANES), jnp.float32)
            m_ref[i, :, t * LANES:(t + 1) * LANES] = block
            if t > i // per_tile:
                linv_ref[i * SUB:(i + 1) * SUB, t * LANES:(t + 1) * LANES] = block

    for copy in copies:
        copy.wait()
    for i in range(groups):
        a_ref[i] = s_ref[0, i * SUB:(i + 1) * SUB, :] + s_ref[1, i * SUB:(i + 1) * SUB, :]

    def span(t):
        return slice(t * LANES, (t + 1) * LANES)

    for o in range(groups // per_block):
        base = o * per_block
        h = base // per_tile
        live = [(a_ref, t) for t in range(h + 1, tiles)] + [(m_ref, t) for t in range(h + 1)]

        def panel(i, c, base=base, h=h, live=live):
            b = base + i
            g = (b - h * per_tile) * SUB
            rows = pl.ds(pl.multiple_of(b * SUB, SUB), SUB)
            own = a_ref[b, :, span(h)]
            cols = [pick_lane(own, g + j) for j in range(SUB)]
            in_panel = (lane >= g) & (lane < g + SUB)
            after = lane >= g + SUB
            head = jnp.where(in_panel, jnp.where(lane - g == sub, -1.0, 0.0), jnp.where(after, own, 0.0))
            rest = [ref[b, :, span(t)] for ref, t in live]
            packed = own
            final = [head] + rest
            for j in range(SUB):
                at = sub == j
                coef = cols[j]
                r = 1.0 / row_of(coef, j)
                final = [jnp.where(at, x, y) for x, y in zip([head] + rest, final)]
                packed = jnp.where((lane == g + j) & (sub > j), coef * r, packed)
                for k in range(j, SUB):
                    packed = jnp.where((lane == g + k) & at, cols[k], packed)
                head_coef = jnp.where((sub < j) | after, coef, 0.0)
                v = row_of(head, j) * r
                head = jnp.where(at, v, head - head_coef * v)
                for n, x in enumerate(rest):
                    v = row_of(x, j) * r
                    rest[n] = jnp.where(at, v, x - coef * v)
                for k in range(j + 1, SUB):
                    v = row_of(cols[k], j) * r
                    cols[k] = jnp.where(at, v, cols[k] - coef * v)
            for t in range(h):
                packed_ref[rows, span(t)] = a_ref[b, :, span(t)]
            packed_ref[rows, span(h)] = jnp.where(after, final[0], packed)
            for (ref, t), x in zip(live, final[1:]):
                (packed_ref if ref is a_ref else linv_ref)[rows, span(t)] = x
            a_ref[b, :, span(h)] = head
            v_ref[0] = head
            for n, ((ref, t), x) in enumerate(zip(live, rest)):
                ref[b, :, span(t)] = x
                v_ref[n + 1] = x
            others = [base + lax.rem(i + s, per_block) for s in range(1, per_block)]
            heads = [a_ref[r, :, span(h)] for r in others]
            facs = [[pick_lane(x, g + j) for j in range(SUB)] for x in heads]
            for n, (ref, t) in enumerate([(a_ref, h)] + live):
                old = [jnp.where(in_panel, 0.0, x) for x in heads] if n == 0 else [ref[r, :, span(t)] for r in others]
                vs = [row_of([head] + rest and ([head] + rest)[n], j) for j in range(SUB)]
                for x, fac, r in zip(old, facs, others):
                    acc = [fac[j] * vs[j] for j in range(SUB)]
                    while len(acc) > 1:
                        acc = [p + q for p, q in zip(acc[::2], acc[1::2])]
                    ref[r, :, span(t)] = x - acc[0]
            return c

        lax.fori_loop(0, per_block, panel, 0)

        lo = (base % per_tile) * SUB
        pad = [jnp.zeros((n, LANES), jnp.float32) for n in (lo, LANES - lo - width)]

        def stack(x):
            return jnp.concatenate([p for p in (pad[0], x, pad[1]) if p.shape[0]], axis=0)

        def flat(ref, first, last, t):
            return ref[first:last, :, span(t)].reshape((last - first) * SUB, LANES)

        end = base + per_block
        right = [stack(flat(ref, base, end, t)) for ref, t in [(a_ref, h)] + live]
        for first, last in ((end, groups), (0, base)):
            if first == last:
                continue
            left = flat(a_ref, first, last, h)
            column = lax.broadcasted_iota(jnp.int32, left.shape, 1)
            for n, (ref, t) in enumerate([(a_ref, h)] + live):
                if ref is m_ref and first == 0:
                    continue
                old = left if n else None
                old = jnp.where((column >= lo) & (column < lo + width), 0.0, left) if n == 0 else flat(ref, first, last, t)
                new = old - jnp.dot(left, right[n], precision=HI, preferred_element_type=jnp.float32)
                ref[first:last, :, span(t)] = new.reshape(last - first, SUB, LANES)

    ri = lax.broadcasted_iota(jnp.int32, (SUB, LANES), 0)
    for i in range(groups):
        for t in range(tiles):
            x = a_ref[i, :, span(t)]
            keep = lane + t * LANES >= ri + i * SUB
            uinv_ref[i * SUB:(i + 1) * SUB, span(t)] = jnp.where(keep, -x, 0.0)


def vmem():
    return pl.BlockSpec(memory_space=pltpu.VMEM)


def smem():
    return pl.BlockSpec(memory_space=pltpu.SMEM)


def factor(square, extra, width=32):
    size = square.shape[1]
    out = jax.ShapeDtypeStruct((size, size), jnp.float32)
    return pl.pallas_call(
        functools.partial(factor_kernel, width),
        out_shape=(out, out, out),
        in_specs=[raw(), raw()],
        out_specs=(vmem(),) * 3,
        scratch_shapes=[
            pltpu.VMEM((size // SUB, SUB, size), jnp.float32),
            pltpu.VMEM((size // SUB, SUB, size), jnp.float32),
            pltpu.VMEM((1 + size // LANES, SUB, LANES), jnp.float32),
            pltpu.VMEM((2, size, size), jnp.float32),
            pltpu.SemaphoreType.DMA((2,)),
        ],
        cost_estimate=pl.CostEstimate(flops=4 * size**3, bytes_accessed=50_000_000, transcendentals=0),
        compiler_params=pltpu.CompilerParams(vmem_limit_bytes=6 << 20),
        name="factor",
    )(square, extra)


def pick_kernel(slot_ref, own_ref, block_ref, out_ref):
    def group(q, c):
        for u in range(SUB):
            j = q * SUB + u
            row = block_ref[pl.ds(slot_ref[j], 1), :]
            out_ref[pl.ds(j, 1), :] = row * own_ref[j].astype(jnp.float32)
        return c

    lax.fori_loop(0, out_ref.shape[0] // SUB, group, 0)


def pick(block, slots, owned, tiles):
    rows, width = block.shape[0], slots.shape[0]
    return pl.pallas_call(
        pick_kernel,
        grid=(tiles,),
        out_shape=jax.ShapeDtypeStruct((width, tiles * width), jnp.float32),
        in_specs=[smem(), smem(), pl.BlockSpec((rows, width), lambda t: (0, t))],
        out_specs=pl.BlockSpec((width, width), lambda t: (0, t)),
        cost_estimate=pl.CostEstimate(
            flops=width * width * tiles, bytes_accessed=4 * (rows + width) * width * tiles, transcendentals=0
        ),
        name="pick",
    )(slots, owned, block)


def place_rows(slot_ref, rows_ref, target_ref):
    def group(q, c):
        for u in range(SUB):
            j = q * SUB + u
            target_ref[pl.ds(slot_ref[j], 1), :] = rows_ref[pl.ds(j, 1), :]
        return c

    lax.fori_loop(0, rows_ref.shape[0] // SUB, group, 0)


def place_kernel(slot_ref, block_ref, rows_ref, out_ref, buf_ref):
    rows = block_ref.shape[0]
    buf_ref[:rows, :] = block_ref[...]
    place_rows(slot_ref, rows_ref, buf_ref)
    out_ref[...] = buf_ref[:rows, :]


def place(block, rows, slots):
    height, width = block.shape[0], slots.shape[0]
    return pl.pallas_call(
        place_kernel,
        grid=(1,),
        out_shape=jax.ShapeDtypeStruct((height, width), jnp.float32),
        in_specs=[
            smem(),
            pl.BlockSpec((height, width), lambda t: (0, 0)),
            pl.BlockSpec((width, width), lambda t: (0, 0)),
        ],
        out_specs=pl.BlockSpec((height, width), lambda t: (0, 0)),
        scratch_shapes=[pltpu.VMEM((height + SUB, width), jnp.float32)],
        cost_estimate=pl.CostEstimate(flops=0, bytes_accessed=8 * height * width, transcendentals=0),
        name="place",
    )(slots, block, rows)


def halves(x):
    high = x.astype(jnp.bfloat16)
    low = (x - high.astype(jnp.float32)).astype(jnp.bfloat16)
    return high, low


def wide_left(x):
    high, low = halves(x)
    return jnp.concatenate([high, low, high], axis=1)


def wide_right(x):
    high, low = halves(x)
    return jnp.concatenate([low, high, high], axis=0)


def wide_dot(left, right):
    return jnp.dot(left, right, preferred_element_type=jnp.float32)


def split_dot(left, right):
    acc = jnp.dot(left[0], right[1], preferred_element_type=jnp.float32)
    acc += jnp.dot(left[1], right[0], preferred_element_type=jnp.float32)
    return acc + jnp.dot(left[0], right[0], preferred_element_type=jnp.float32)


def update_kernel(
    slot_ref, where_ref, block_ref, panel_ref, pivot_ref, top_ref, packed_ref, linv_ref, uinv_ref,
    out_ref, high_ref, low_ref, buf_ref,
):
    rows, width = panel_ref.shape
    t = pl.program_id(0)
    first_row = where_ref[0] == 0
    first_col = (where_ref[1] == 0) & (t == 0)

    @pl.when(t == 0)
    def _():
        lower = jnp.dot(panel_ref[...], uinv_ref[...], precision=HI, preferred_element_type=jnp.float32)
        high_ref[...], low_ref[...] = halves(lower)
        out_ref[...] = lower

    upper = jnp.dot(linv_ref[...], pivot_ref[...], precision=HI, preferred_element_type=jnp.float32)

    @pl.when(jnp.logical_not(first_col))
    def _():
        buf_ref[:rows, :] = block_ref[...]
        place_rows(slot_ref, top_ref, buf_ref)
        out_ref[...] = buf_ref[:rows, :] - split_dot((high_ref[...], low_ref[...]), halves(upper))

    @pl.when(first_row)
    def _():
        out_ref[:width, :] = jnp.where(first_col, packed_ref[...], upper)


def update(block, panel, pivot_rows, old_top, packed, linv, uinv, slots, where):
    rows, cols = block.shape
    width = slots.shape[0]
    square = pl.BlockSpec((width, width), lambda t: (0, 0))
    tall = pl.BlockSpec((rows, width), lambda t: (0, t))
    flat = pl.BlockSpec((width, width), lambda t: (0, t))
    return pl.pallas_call(
        update_kernel,
        grid=(cols // width,),
        out_shape=jax.ShapeDtypeStruct((rows, cols), jnp.float32),
        in_specs=[
            smem(), smem(), tall, pl.BlockSpec((rows, width), lambda t: (0, 0)), flat, flat, square, square, square,
        ],
        out_specs=tall,
        scratch_shapes=[
            pltpu.VMEM((rows, width), jnp.bfloat16),
            pltpu.VMEM((rows, width), jnp.bfloat16),
            pltpu.VMEM((rows + SUB, width), jnp.float32),
        ],
        cost_estimate=pl.CostEstimate(
            flops=6 * rows * cols * width, bytes_accessed=8 * rows * cols, transcendentals=0
        ),
        name="update",
    )(slots, where, block, panel, pivot_rows, old_top, packed, linv, uinv)


def bits_of(n):
    return [1 << i for i in range(n.bit_length() - 1)]


def sum_over_rows(x, order, n_row):
    for bit in order:
        x = x + lax.ppermute(x, "prow", [(i, i ^ bit) for i in range(n_row)])
    return x


def spread_rows(x, order, n_row):
    have = [0]
    for bit in order:
        x = x + lax.ppermute(x, "prow", [(i, i ^ bit) for i in have])
        have = have + [i ^ bit for i in have]
    return x


def spread_cols(x, order):
    have = [0]
    for bit in order:
        x = x + lax.ppermute(x, "pcol", [(i, i ^ bit) for i in have])
        have = have + [i ^ bit for i in have]
    return x


def dense_step(n_row, n_col, matrix, pivots):
    block = matrix[0, :, 0, :]
    rows, cols = block.shape
    width = pivots.shape[0]
    row = lax.axis_index("prow")
    col = lax.axis_index("pcol")
    owner = pivots // width % n_row
    slot = pivots // (width * n_row) * width + pivots % width
    mine = owner == row
    owned = mine.astype(jnp.int32)
    target = jnp.where(mine, slot, rows)
    where = jnp.stack([row, col]).astype(jnp.int32)
    row_bits, col_bits = bits_of(n_row), bits_of(n_col)
    at_first_row = row == 0
    at_first_col = col == 0

    square = pick(block, slot, owned * at_first_col.astype(jnp.int32), 1)
    square = sum_over_rows(square, row_bits, n_row)
    square = spread_cols(square, col_bits[::-1])
    packed, linv, uinv = factor(square, jnp.zeros_like(square))

    top = jnp.where(at_first_row, block[:width], 0.0)
    top_panel = spread_rows(top[:, :width], row_bits, n_row)
    panel = place(block, top_panel, target)
    panel = spread_cols(jnp.where(at_first_col, panel, 0.0), col_bits[::-1])

    picked = pick(block, slot, owned, cols // width)
    half = width // 2
    pivot_rows = jnp.concatenate([
        sum_over_rows(picked[:half], row_bits, n_row),
        sum_over_rows(picked[half:], row_bits[::-1], n_row),
    ])
    old_top = jnp.concatenate([
        spread_rows(top[:half], row_bits, n_row),
        spread_rows(top[half:], row_bits[::-1], n_row),
    ])
    result = update(block, panel, pivot_rows, old_top, packed, linv, uinv, target, where)
    return result[None, :, None, :]


def raw():
    return pl.BlockSpec(memory_space=pl.ANY)


def thirds(x):
    high = x.astype(jnp.bfloat16)
    rest = x - high.astype(jnp.float32)
    middle = rest.astype(jnp.bfloat16)
    return high, middle, (rest - middle.astype(jnp.float32)).astype(jnp.bfloat16)


def select_dot(choice, parts):
    choice = choice.astype(jnp.bfloat16)
    high, middle, low = [jnp.dot(choice, x, preferred_element_type=jnp.float32) for x in parts]
    return high + (middle + low)


def pick_dot(parts, choice):
    choice = choice.astype(jnp.bfloat16)
    high, middle, low = [jnp.dot(x, choice, preferred_element_type=jnp.float32) for x in parts]
    return high + (middle + low)


def begin_kernel(n_row, pivot_ref, mat_ref, panel_ref, wide_ref, fits_ref, *refs):
    messages, sem = refs[:n_row], refs[-1]
    rows, width = panel_ref.shape
    count = messages[0].shape[0] // 2
    width_log, row_log = width.bit_length() - 1, n_row.bit_length() - 1
    row = lax.axis_index("prow")
    copy = pltpu.make_async_copy(mat_ref.at[:, 0, pl.ds(0, width)], panel_ref, sem)
    copy.start()
    pivot = pivot_ref[...]
    block = lax.shift_right_logical(pivot, width_log)
    owner = block & (n_row - 1)
    slot = lax.shift_left(lax.shift_right_logical(block, row_log), width_log) + (pivot & (width - 1))
    _, rank = owners(pivot, n_row)
    fits_ref[0] = (jnp.max(rank) < count).astype(jnp.int32)
    place = ((owner ^ row) * count + rank).astype(jnp.float32)
    eye = lax.broadcasted_iota(jnp.int32, (width, width), 0) == lax.broadcasted_iota(jnp.int32, (width, width), 1)
    spread = jnp.where(eye, place, 0.0)
    wide = jnp.dot(spread, jnp.ones((width, LANES), jnp.float32), precision=HI, preferred_element_type=jnp.float32)
    wide_ref[...] = wide.astype(jnp.int32)
    ordinal = lax.broadcasted_iota(jnp.int32, (count, width), 0)
    mine = jnp.where((ordinal == rank) & (owner == row), 1.0, 0.0).astype(jnp.bfloat16)
    at_slot = jnp.where(lax.broadcasted_iota(jnp.int32, (rows, width), 0) == slot, 1.0, 0.0).astype(jnp.bfloat16)
    choice = lax.dot_general(mine, at_slot, (((1,), (1,)), ((), ())), preferred_element_type=jnp.float32)
    copy.wait()
    own = select_dot(choice, thirds(panel_ref[...]))
    for k in range(n_row):
        messages[k][:count, :] = own

    @pl.when(row == 0)
    def _():
        top = thirds(panel_ref[:width, :])
        for p in range(n_row):
            messages[p][count:, :] = select_dot(jnp.where((ordinal == rank) & (owner == p), 1.0, 0.0), top)


def begin(mat, pivots, n_row, count):
    rows, width = mat.shape[0], pivots.shape[0]
    message = jax.ShapeDtypeStruct((2 * count, width), jnp.float32)
    return pl.pallas_call(
        functools.partial(begin_kernel, n_row),
        out_shape=(
            jax.ShapeDtypeStruct((rows, width), jnp.float32),
            jax.ShapeDtypeStruct((width, LANES), jnp.int32),
            jax.ShapeDtypeStruct((1,), jnp.int32),
        ) + (message,) * n_row,
        in_specs=[vmem(), raw()],
        out_specs=(vmem(), vmem(), smem()) + (vmem(),) * n_row,
        scratch_shapes=[pltpu.SemaphoreType.DMA],
        cost_estimate=pl.CostEstimate(flops=0, bytes_accessed=10_000_000, transcendentals=0),
        compiler_params=pltpu.CompilerParams(vmem_limit_bytes=12 << 20),
        name="begin",
    )(pivots[None, :], mat)


def parcel_kernel(n_row, mine_ref, pivot_ref, mat_ref, *refs):
    outs, own, block, sem = refs[:-3], refs[-3], refs[-2], refs[-1]
    count, cols = own.shape
    half = count // 2
    width = pivot_ref.shape[1]

    def group(q, c):
        for u in range(SUB):
            i = q * SUB + u
            pltpu.make_async_copy(mat_ref.at[mine_ref[i]], own.at[pl.ds(i, 1), :], sem.at[0]).start()
        return c

    lax.fori_loop(0, count // SUB, group, 0)

    @pl.when(lax.axis_index("prow") == 0)
    def _():
        copy = pltpu.make_async_copy(mat_ref.at[pl.ds(0, width), 0, :], block, sem.at[1])
        copy.start()
        owner, rank = owners(pivot_ref[...], n_row)
        ordinal = lax.broadcasted_iota(jnp.int32, (count, width), 0)
        choices = [jnp.where((ordinal == rank) & (owner == p), 1.0, 0.0) for p in range(n_row)]
        choice = jnp.concatenate(choices, axis=0)
        copy.wait()

        def piece(t, c):
            at = pl.ds(pl.multiple_of(t * width, width), width)
            tops = select_dot(choice, thirds(block[:, at]))
            for p in range(n_row):
                for part in range(2):
                    first = p * count + part * half
                    for ref, base in top_places(n_row, half, outs, p, part):
                        ref[pl.ds(base, half), at] = tops[first:first + half]
            return c

        lax.fori_loop(0, cols // width, piece, 0)

    pltpu.make_async_copy(mat_ref.at[pl.ds(0, count), 0, :], own, sem.at[0]).wait()
    if n_row == 4:
        outs[0][:half, :] = own[:half, :]
        outs[1][:half, :] = own[half:, :]
        outs[2][:count, :] = own[...]
    else:
        outs[0][:count, :] = own[...]
        for p in range(1, n_row):
            outs[p][:count, :] = own[...]


def top_places(n_row, half, outs, p, part):
    if n_row != 4:
        return [(outs[p], 2 * half + part * half)]
    if p == 0:
        return [(outs[2], 2 * half + part * half)]
    if p == 3:
        return [(outs[part], 2 * half)]
    if part == p - 1:
        return [(outs[part], half)]
    return [(outs[2], (4 + part) * half)]


def owners(pivot, n_row):
    width = pivot.shape[1]
    owner = lax.shift_right_logical(pivot, width.bit_length() - 1) & (n_row - 1)
    held = lax.broadcasted_iota(jnp.int32, (-(-n_row // 16) * 16, width), 0) == owner
    before = lax.broadcasted_iota(jnp.int32, (width, width), 0) < lax.broadcasted_iota(jnp.int32, (width, width), 1)
    held = jnp.where(held, 1.0, 0.0)
    earlier = jnp.dot(
        held.astype(jnp.bfloat16), jnp.where(before, 1.0, 0.0).astype(jnp.bfloat16), preferred_element_type=jnp.float32
    )
    return owner, jnp.sum(held * earlier, axis=0, keepdims=True).astype(jnp.int32)


def parcel(mat, mine, pivots, n_row):
    count, width, cols = mine.shape[0], pivots.shape[0], mat.shape[2]
    half = count // 2
    sizes = [3 * half, 3 * half, 6 * half] if n_row == 4 else [2 * count] * n_row
    return pl.pallas_call(
        functools.partial(parcel_kernel, n_row),
        out_shape=tuple(jax.ShapeDtypeStruct((size, cols), jnp.float32) for size in sizes),
        in_specs=[smem(), vmem(), raw()],
        out_specs=(vmem(),) * len(sizes),
        scratch_shapes=[
            pltpu.VMEM((count, cols), jnp.float32),
            pltpu.VMEM((width, cols), jnp.float32),
            pltpu.SemaphoreType.DMA((2,)),
        ],
        cost_estimate=pl.CostEstimate(flops=0, bytes_accessed=16_000_000, transcendentals=0),
        compiler_params=pltpu.CompilerParams(vmem_limit_bytes=16 << 20),
        name="parcel",
    )(mine, pivots[None, :], mat)


def relay_kernel(kept_ref, first_ref, second_ref, y_ref, x_ref, sem):
    half = first_ref.shape[0] // 3
    row = lax.axis_index("prow")

    def move(source, base, dest, at, n):
        return pltpu.make_async_copy(source.at[pl.ds(base, half), :], dest.at[pl.ds(at, half), :], sem.at[n])

    copies = [
        move(kept_ref, 0, y_ref, 0, 0),
        move(kept_ref, half, x_ref, 0, 1),
        move(first_ref, 0, y_ref, half, 2),
        move(second_ref, 0, x_ref, half, 3),
    ]
    for copy in copies:
        copy.start()

    @pl.when(row == 0)
    def _():
        move(kept_ref, 4 * half, y_ref, 2 * half, 4).start()
        move(kept_ref, 5 * half, x_ref, 2 * half, 5).start()

    @pl.when(row != 0)
    def _():
        move(first_ref, 2 * half, y_ref, 2 * half, 4).start()
        move(second_ref, 2 * half, x_ref, 2 * half, 5).start()

    for copy in copies:
        copy.wait()
    move(first_ref, 2 * half, y_ref, 2 * half, 4).wait()
    move(second_ref, 2 * half, x_ref, 2 * half, 5).wait()


def relay(kept, first, second):
    shape = jax.ShapeDtypeStruct(first.shape, jnp.float32)
    return pl.pallas_call(
        relay_kernel,
        out_shape=(shape, shape),
        in_specs=[raw()] * 3,
        out_specs=(vmem(), vmem()),
        scratch_shapes=[pltpu.SemaphoreType.DMA((6,))],
        cost_estimate=pl.CostEstimate(flops=0, bytes_accessed=4_000_000, transcendentals=0),
        compiler_params=pltpu.CompilerParams(vmem_limit_bytes=4 << 20),
        name="relay",
    )(kept, first, second)


def pack_kernel(n_row, wide_ref, *refs):
    parts, out_ref, stack, sem = refs[:n_row], refs[n_row], refs[n_row + 1], refs[n_row + 2]
    width = wide_ref.shape[0]
    count = out_ref.shape[0] - width
    row, col = lax.axis_index("prow"), lax.axis_index("pcol")
    total = stack.shape[0]

    @pl.when(col == 0)
    def _():
        copies = [
            pltpu.make_async_copy(parts[k].at[pl.ds(0, count), :], stack.at[pl.ds(k * count, count), :], sem.at[k])
            for k in range(n_row)
        ]
        for copy in copies:
            copy.start()
        for k in range(n_row):
            @pl.when(row == k)
            def _(k=k):
                pltpu.make_async_copy(
                    parts[k].at[pl.ds(count, count), :], out_ref.at[pl.ds(width, count), :], sem.at[n_row]
                ).start()
        if total > n_row * count:
            stack[n_row * count:, :] = jnp.zeros((total - n_row * count, width), jnp.float32)
        lanes = lax.broadcasted_iota(jnp.int32, (width, LANES), 1)
        choice = jnp.concatenate(
            [jnp.where(lanes + t * LANES == wide_ref[...], 1.0, 0.0) for t in range(total // LANES)], axis=1
        )
        for copy in copies:
            copy.wait()
        out_ref[:width, :] = select_dot(choice, thirds(stack[...]))
        pltpu.make_async_copy(
            parts[0].at[pl.ds(count, count), :], out_ref.at[pl.ds(width, count), :], sem.at[n_row]
        ).wait()

    @pl.when(col != 0)
    def _():
        out_ref[...] = jnp.zeros_like(out_ref)


def pack(wide, parts):
    n_row, width = len(parts), wide.shape[0]
    count = parts[0].shape[0] // 2
    return pl.pallas_call(
        functools.partial(pack_kernel, n_row),
        out_shape=jax.ShapeDtypeStruct((width + count, width), jnp.float32),
        in_specs=[vmem()] + [raw()] * n_row,
        out_specs=vmem(),
        scratch_shapes=[
            pltpu.VMEM((-(-n_row * count // LANES) * LANES, width), jnp.float32),
            pltpu.SemaphoreType.DMA((n_row + 1,)),
        ],
        cost_estimate=pl.CostEstimate(flops=0, bytes_accessed=4_000_000, transcendentals=0),
        compiler_params=pltpu.CompilerParams(vmem_limit_bytes=6 << 20),
        name="pack",
    )(wide, *parts)


def unpack_parcels(n_row, count, parcels):
    half = count // 2
    if n_row != 4:
        parts = [(x, part * half) for x in parcels for part in range(2)]
        return parts, [[(x, count + part * half) for part in range(2)] for x in parcels]
    kept, first, second, third, fourth = parcels
    parts = [
        (kept, 0), (kept, half), (first, 0), (fourth, 0), (third, 0), (second, 0), (third, half), (fourth, half)
    ]
    tops = [
        [(kept, 2 * half), (kept, 3 * half)],
        [(first, half), (fourth, 2 * half)],
        [(third, 2 * half), (second, half)],
        [(third, 2 * half), (fourth, 2 * half)],
    ]
    return parts, tops


def put_rows(slot_ref, held, rows_ref, target_ref):
    spare = target_ref.shape[0] - SUB

    def group(q, c):
        for u in range(SUB):
            i = q * SUB + u
            slot = jnp.where(i < held, slot_ref[i], spare)
            target_ref[pl.ds(slot, 1), :] = rows_ref[pl.ds(i, 1), :]
        return c

    lax.fori_loop(0, (held + SUB - 1) // SUB, group, 0)


def finish_kernel(
    n_row, mine_ref, counts_ref, wide_ref, mat_ref, panel_ref, panel_new_ref, square_ref, square_new_ref,
    packed_ref, linv_ref, uinv_ref, *refs,
):
    n_parcels = 5 if n_row == 4 else n_row
    parcels, refs = refs[:n_parcels], refs[n_parcels:]
    out_ref, block, pivot, panel, old, left, lower, top, sem, in_sem, out_sem = refs
    rows, _, cols = mat_ref.shape
    width = linv_ref.shape[0]
    count = mine_ref.shape[0]
    half = count // 2
    stacked = n_row * count
    parts, tops = unpack_parcels(n_row, count, parcels)
    tiles = cols // width
    row, col = lax.axis_index("prow"), lax.axis_index("pcol")

    def tile(t):
        return pl.ds(pl.multiple_of(t * width, width), width)

    @pl.when(col % 2 == 0)
    def _():
        pltpu.make_async_copy(panel_ref, panel.at[pl.ds(0, rows)], sem.at[0]).start()

    @pl.when(col % 2 == 1)
    def _():
        pltpu.make_async_copy(panel_new_ref, panel.at[pl.ds(0, rows)], sem.at[0]).start()

    top_copies = [
        pltpu.make_async_copy(ref.at[pl.ds(width, count), :], top.at[n], sem.at[1 + n])
        for n, ref in enumerate((square_ref, square_new_ref))
    ]
    for copy in top_copies:
        copy.start()

    def fetch(t, c):
        pltpu.make_async_copy(mat_ref.at[:, 0, tile(t)], block.at[pl.ds(0, rows), tile(t)], in_sem.at[0, t]).start()
        for n, (ref, base) in enumerate(parts):
            dest = pivot.at[pl.ds(n * half, half), tile(t)]
            pltpu.make_async_copy(ref.at[pl.ds(base, half), tile(t)], dest, in_sem.at[1, t]).start()
        for p in range(n_row):
            @pl.when(row == p)
            def _(p=p):
                for part, (ref, base) in enumerate(tops[p]):
                    dest = old.at[pl.ds(part * half, half), tile(t)]
                    pltpu.make_async_copy(ref.at[pl.ds(base, half), tile(t)], dest, in_sem.at[2, t]).start()
        return c

    lax.fori_loop(0, tiles, fetch, 0)
    if pivot.shape[0] > stacked:
        pivot[stacked:, :] = jnp.zeros((pivot.shape[0] - stacked, cols), jnp.float32)

    lanes = lax.broadcasted_iota(jnp.int32, (width, LANES), 1)
    places = jnp.concatenate(
        [jnp.where(lanes + t * LANES == wide_ref[...], 1.0, 0.0) for t in range(pivot.shape[0] // LANES)], axis=1
    )
    spread_inv = wide_left(pick_dot(thirds(linv_ref[...]), places))
    for copy in top_copies:
        copy.wait()
    top[0] = top[0] + top[1]
    pltpu.make_async_copy(panel_ref, panel.at[pl.ds(0, rows)], sem.at[0]).wait()
    put_rows(mine_ref, counts_ref[row], top.at[0], panel)
    lower[...] = wide_dot(wide_left(panel[:rows, :]), wide_right(uinv_ref[...]))
    left[...] = wide_left(lower[...])

    def step(t, c):
        first_col = (col == 0) & (t == 0)
        pltpu.make_async_copy(
            mat_ref.at[pl.ds(0, stacked), 0, tile(t)], pivot.at[pl.ds(0, stacked), tile(t)], in_sem.at[1, t]
        ).wait()
        upper = wide_dot(spread_inv, wide_right(pivot[:, tile(t)]))
        pltpu.make_async_copy(mat_ref.at[pl.ds(0, count), 0, tile(t)], old.at[:, tile(t)], in_sem.at[2, t]).wait()
        pltpu.make_async_copy(mat_ref.at[:, 0, tile(t)], block.at[pl.ds(0, rows), tile(t)], in_sem.at[0, t]).wait()

        @pl.when(jnp.logical_not(first_col))
        def _():
            put_rows(mine_ref, counts_ref[row], old.at[:, tile(t)], block.at[:, tile(t)])
            block[:rows, tile(t)] = block[:rows, tile(t)] - wide_dot(left[...], wide_right(upper))

        @pl.when(first_col)
        def _():
            block[:rows, tile(t)] = lower[...]

        @pl.when(row == 0)
        def _():
            block[:width, tile(t)] = jnp.where(first_col, packed_ref[...], upper)

        pltpu.make_async_copy(block.at[pl.ds(0, rows), tile(t)], out_ref.at[:, 0, tile(t)], out_sem.at[t]).start()
        return c

    lax.fori_loop(0, tiles, step, 0)

    def drain(t, c):
        pltpu.make_async_copy(block.at[pl.ds(0, rows), tile(t)], out_ref.at[:, 0, tile(t)], out_sem.at[t]).wait()
        return c

    lax.fori_loop(0, tiles, drain, 0)


def finish(mine, counts, wide, mat, panels, squares, factors, parcels):
    rows, _, cols = mat.shape
    width, n_row, count = factors[0].shape[0], counts.shape[0], mine.shape[0]
    return pl.pallas_call(
        functools.partial(finish_kernel, n_row),
        out_shape=jax.ShapeDtypeStruct(mat.shape, jnp.float32),
        in_specs=[smem(), smem(), vmem()] + [raw()] * 5 + [vmem()] * 3 + [raw()] * len(parcels),
        out_specs=raw(),
        scratch_shapes=[
            pltpu.VMEM((rows + SUB, cols), jnp.float32),
            pltpu.VMEM((-(-n_row * count // LANES) * LANES, cols), jnp.float32),
            pltpu.VMEM((rows + SUB, width), jnp.float32),
            pltpu.VMEM((count, cols), jnp.float32),
            pltpu.VMEM((rows, 3 * width), jnp.bfloat16),
            pltpu.VMEM((rows, width), jnp.float32),
            pltpu.VMEM((2, count, width), jnp.float32),
            pltpu.SemaphoreType.DMA((3,)),
            pltpu.SemaphoreType.DMA((3, cols // width)),
            pltpu.SemaphoreType.DMA((cols // width,)),
        ],
        cost_estimate=pl.CostEstimate(
            flops=6 * rows * cols * width, bytes_accessed=8 * rows * cols, transcendentals=0
        ),
        compiler_params=pltpu.CompilerParams(vmem_limit_bytes=26 << 20),
        name="finish",
    )(mine, counts, wide, mat, *panels, *squares, *factors, *parcels)


def capacity(n_row, width):
    mean = width / n_row
    return -(-int(mean + 4 * (mean * (1 - 1 / n_row)) ** 0.5) // (2 * SUB)) * (2 * SUB)


def locate(pivots, n_row, row, count):
    width = pivots.shape[0]
    owner = pivots // width % n_row
    slot = pivots // (width * n_row) * width + pivots % width
    number = jnp.arange(width, dtype=jnp.int32)
    ahead = (owner[:, None] == owner[None, :]) & (number[None, :] < number[:, None])
    rank = jnp.sum(ahead, axis=1, dtype=jnp.int32)
    every = jnp.arange(n_row, dtype=jnp.int32)[:, None]
    ordinal = jnp.arange(count, dtype=jnp.int32)[:, None]
    own = (owner[None, :] == row) & (rank[None, :] == ordinal)
    mine = jnp.sum(jnp.where(own, slot[None, :], 0), axis=1, dtype=jnp.int32)
    return mine, jnp.sum(owner[None, :] == every, axis=1, dtype=jnp.int32)


def capped_step(n_row, n_col, matrix, pivots, begun):
    _, rows, _, cols = matrix.shape
    mat = matrix.reshape(rows, 1, cols)
    panel, wide, _, *messages = begun
    count = messages[0].shape[0] // 2
    row, col = lax.axis_index("prow"), lax.axis_index("pcol")
    both = ("prow", "pcol")
    turns = bits_of(n_col)[:0:-1]

    def exchange(x, k):
        return lax.ppermute(x, both, [(i * n_col, (i ^ k) * n_col) for i in range(n_row)])

    moved = [exchange(messages[k], k) for k in range(1, n_row)]
    mine, counts = locate(pivots, n_row, row, count)
    parcels = parcel(mat, mine, pivots, n_row)

    def send(x, k):
        return lax.ppermute(x, "prow", [(i, i ^ k) for i in range(n_row)])

    *moved, kept = lax.optimization_barrier((*moved, parcels[-1]))
    parcels = parcels[:-1] + (kept,)
    message = pack(wide, messages[:1] + moved)
    panel_moved = lax.ppermute(panel, "pcol", [(i, i + turns[0]) for i in range(0, n_col, 2 * turns[0])])
    message, panel_moved = lax.optimization_barrier((message, panel_moved))
    if n_row == 4:
        first, second = send(parcels[0], 1), send(parcels[1], 2)
        kept = parcels[2]
        to_y, to_x = relay(kept, first, second)
        arrived = [kept, first, second]
    else:
        arrived = [parcels[0]] + [send(parcels[k], k) for k in range(1, n_row)]

    pairs = [[(i, i + bit) for i in range(0, n_col, 2 * bit)] for bit in turns + [1]]
    newer = [(col & bit) != 0 for bit in turns]
    for n in range(len(turns)):
        panel = jnp.where(newer[n], panel_moved, panel)
        panel_moved = lax.ppermute(panel, "pcol", pairs[n + 1])
        message = jnp.where(newer[n], lax.ppermute(message, "pcol", pairs[n]), message)
        if n + 1 < len(turns):
            message, panel_moved = lax.optimization_barrier((message, panel_moved))
    if n_row == 4:
        message, to_y, to_x = lax.optimization_barrier((message, to_y, to_x))
        arrived += [send(to_y, 2), send(to_x, 1)]
    message_new = lax.ppermute(message, "pcol", pairs[-1])
    factors = factor(message, message_new)
    out = finish(
        mine, counts, wide, mat, (panel, panel_moved), (message, message_new), factors, arrived
    )
    return out.reshape(matrix.shape)


def on_device(n_row, n_col, matrix, pivots):
    _, rows, _, cols = matrix.shape
    begun = begin(matrix.reshape(rows, 1, cols), pivots, n_row, capacity(n_row, pivots.shape[0]))
    return lax.cond(
        begun[2][0] > 0,
        lambda m, p, b: capped_step(n_row, n_col, m, p, b),
        lambda m, p, b: dense_step(n_row, n_col, m, p),
        matrix, pivots, begun,
    )


def solution(mesh):
    spec = P("prow", None, "pcol", None)
    n_row, n_col = mesh.shape["prow"], mesh.shape["pcol"]
    return jax.shard_map(
        functools.partial(on_device, n_row, n_col), mesh=mesh, in_specs=(spec, P()), out_specs=spec, check_vma=False
    )
```

```python
import functools

import jax
import jax.numpy as jnp
from jax import lax
from jax.experimental import pallas as pl
from jax.experimental.pallas import tpu as pltpu
from jax.sharding import PartitionSpec as P

LANES = 128
SUB = 8
HI = lax.Precision.HIGHEST


def pick_lane(tile, lane):
    return jnp.take_along_axis(tile, jnp.full((SUB, LANES), lane, jnp.int32), axis=1)


def row_of(tile, j):
    return jnp.broadcast_to(tile[j:j + 1, :], (SUB, LANES))


def factor_kernel(width, first_ref, second_ref, packed_ref, linv_ref, uinv_ref, a_ref, m_ref, v_ref, s_ref, sem):
    groups = a_ref.shape[0]
    tiles = groups * SUB // LANES
    per_tile = LANES // SUB
    per_block = width // SUB
    copies = [
        pltpu.make_async_copy(ref.at[pl.ds(0, groups * SUB), :], s_ref.at[n], sem.at[n])
        for n, ref in enumerate((first_ref, second_ref))
    ]
    for copy in copies:
        copy.start()
    sub = lax.broadcasted_iota(jnp.int32, (SUB, LANES), 0)
    lane = lax.broadcasted_iota(jnp.int32, (SUB, LANES), 1)

    for i in range(groups):
        diag = lane - (i % per_tile) * SUB == sub
        for t in range(tiles):
            block = jnp.where(diag, 1.0, 0.0) if i // per_tile == t else jnp.zeros((SUB, LANES), jnp.float32)
            m_ref[i, :, t * LANES:(t + 1) * LANES] = block
            if t > i // per_tile:
                linv_ref[i * SUB:(i + 1) * SUB, t * LANES:(t + 1) * LANES] = block

    for copy in copies:
        copy.wait()
    for i in range(groups):
        a_ref[i] = s_ref[0, i * SUB:(i + 1) * SUB, :] + s_ref[1, i * SUB:(i + 1) * SUB, :]

    def span(t):
        return slice(t * LANES, (t + 1) * LANES)

    for o in range(groups // per_block):
        base = o * per_block
        h = base // per_tile
        live = [(a_ref, t) for t in range(h + 1, tiles)] + [(m_ref, t) for t in range(h + 1)]

        def panel(i, c, base=base, h=h, live=live):
            b = base + i
            g = (b - h * per_tile) * SUB
            rows = pl.ds(pl.multiple_of(b * SUB, SUB), SUB)
            own = a_ref[b, :, span(h)]
            cols = [pick_lane(own, g + j) for j in range(SUB)]
            in_panel = (lane >= g) & (lane < g + SUB)
            after = lane >= g + SUB
            head = jnp.where(in_panel, jnp.where(lane - g == sub, -1.0, 0.0), jnp.where(after, own, 0.0))
            rest = [ref[b, :, span(t)] for ref, t in live]
            packed = own
            final = [head] + rest
            for j in range(SUB):
                at = sub == j
                coef = cols[j]
                r = 1.0 / row_of(coef, j)
                final = [jnp.where(at, x, y) for x, y in zip([head] + rest, final)]
                packed = jnp.where((lane == g + j) & (sub > j), coef * r, packed)
                for k in range(j, SUB):
                    packed = jnp.where((lane == g + k) & at, cols[k], packed)
                head_coef = jnp.where((sub < j) | after, coef, 0.0)
                v = row_of(head, j) * r
                head = jnp.where(at, v, head - head_coef * v)
                for n, x in enumerate(rest):
                    v = row_of(x, j) * r
                    rest[n] = jnp.where(at, v, x - coef * v)
                for k in range(j + 1, SUB):
                    v = row_of(cols[k], j) * r
                    cols[k] = jnp.where(at, v, cols[k] - coef * v)
            for t in range(h):
                packed_ref[rows, span(t)] = a_ref[b, :, span(t)]
            packed_ref[rows, span(h)] = jnp.where(after, final[0], packed)
            for (ref, t), x in zip(live, final[1:]):
                (packed_ref if ref is a_ref else linv_ref)[rows, span(t)] = x
            a_ref[b, :, span(h)] = head
            v_ref[0] = head
            for n, ((ref, t), x) in enumerate(zip(live, rest)):
                ref[b, :, span(t)] = x
                v_ref[n + 1] = x
            others = [base + lax.rem(i + s, per_block) for s in range(1, per_block)]
            heads = [a_ref[r, :, span(h)] for r in others]
            facs = [[pick_lane(x, g + j) for j in range(SUB)] for x in heads]
            for n, (ref, t) in enumerate([(a_ref, h)] + live):
                old = [jnp.where(in_panel, 0.0, x) for x in heads] if n == 0 else [ref[r, :, span(t)] for r in others]
                vs = [row_of([head] + rest and ([head] + rest)[n], j) for j in range(SUB)]
                for x, fac, r in zip(old, facs, others):
                    acc = [fac[j] * vs[j] for j in range(SUB)]
                    while len(acc) > 1:
                        acc = [p + q for p, q in zip(acc[::2], acc[1::2])]
                    ref[r, :, span(t)] = x - acc[0]
            return c

        lax.fori_loop(0, per_block, panel, 0)

        lo = (base % per_tile) * SUB
        pad = [jnp.zeros((n, LANES), jnp.float32) for n in (lo, LANES - lo - width)]

        def stack(x):
            return jnp.concatenate([p for p in (pad[0], x, pad[1]) if p.shape[0]], axis=0)

        def flat(ref, first, last, t):
            return ref[first:last, :, span(t)].reshape((last - first) * SUB, LANES)

        end = base + per_block
        right = [stack(flat(ref, base, end, t)) for ref, t in [(a_ref, h)] + live]
        for first, last in ((end, groups), (0, base)):
            if first == last:
                continue
            left = flat(a_ref, first, last, h)
            column = lax.broadcasted_iota(jnp.int32, left.shape, 1)
            for n, (ref, t) in enumerate([(a_ref, h)] + live):
                if ref is m_ref and first == 0:
                    continue
                old = left if n else None
                old = jnp.where((column >= lo) & (column < lo + width), 0.0, left) if n == 0 else flat(ref, first, last, t)
                new = old - jnp.dot(left, right[n], precision=HI, preferred_element_type=jnp.float32)
                ref[first:last, :, span(t)] = new.reshape(last - first, SUB, LANES)

    ri = lax.broadcasted_iota(jnp.int32, (SUB, LANES), 0)
    for i in range(groups):
        for t in range(tiles):
            x = a_ref[i, :, span(t)]
            keep = lane + t * LANES >= ri + i * SUB
            uinv_ref[i * SUB:(i + 1) * SUB, span(t)] = jnp.where(keep, -x, 0.0)


def vmem():
    return pl.BlockSpec(memory_space=pltpu.VMEM)


def smem():
    return pl.BlockSpec(memory_space=pltpu.SMEM)


def factor(square, extra, width=32):
    size = square.shape[1]
    out = jax.ShapeDtypeStruct((size, size), jnp.float32)
    return pl.pallas_call(
        functools.partial(factor_kernel, width),
        out_shape=(out, out, out),
        in_specs=[raw(), raw()],
        out_specs=(vmem(),) * 3,
        scratch_shapes=[
            pltpu.VMEM((size // SUB, SUB, size), jnp.float32),
            pltpu.VMEM((size // SUB, SUB, size), jnp.float32),
            pltpu.VMEM((1 + size // LANES, SUB, LANES), jnp.float32),
            pltpu.VMEM((2, size, size), jnp.float32),
            pltpu.SemaphoreType.DMA((2,)),
        ],
        cost_estimate=pl.CostEstimate(flops=4 * size**3, bytes_accessed=50_000_000, transcendentals=0),
        compiler_params=pltpu.CompilerParams(vmem_limit_bytes=6 << 20),
        name="factor",
    )(square, extra)


def pick_kernel(slot_ref, own_ref, block_ref, out_ref):
    def group(q, c):
        for u in range(SUB):
            j = q * SUB + u
            row = block_ref[pl.ds(slot_ref[j], 1), :]
            out_ref[pl.ds(j, 1), :] = row * own_ref[j].astype(jnp.float32)
        return c

    lax.fori_loop(0, out_ref.shape[0] // SUB, group, 0)


def pick(block, slots, owned, tiles):
    rows, width = block.shape[0], slots.shape[0]
    return pl.pallas_call(
        pick_kernel,
        grid=(tiles,),
        out_shape=jax.ShapeDtypeStruct((width, tiles * width), jnp.float32),
        in_specs=[smem(), smem(), pl.BlockSpec((rows, width), lambda t: (0, t))],
        out_specs=pl.BlockSpec((width, width), lambda t: (0, t)),
        cost_estimate=pl.CostEstimate(
            flops=width * width * tiles, bytes_accessed=4 * (rows + width) * width * tiles, transcendentals=0
        ),
        name="pick",
    )(slots, owned, block)


def place_rows(slot_ref, rows_ref, target_ref):
    def group(q, c):
        for u in range(SUB):
            j = q * SUB + u
            target_ref[pl.ds(slot_ref[j], 1), :] = rows_ref[pl.ds(j, 1), :]
        return c

    lax.fori_loop(0, rows_ref.shape[0] // SUB, group, 0)


def place_kernel(slot_ref, block_ref, rows_ref, out_ref, buf_ref):
    rows = block_ref.shape[0]
    buf_ref[:rows, :] = block_ref[...]
    place_rows(slot_ref, rows_ref, buf_ref)
    out_ref[...] = buf_ref[:rows, :]


def place(block, rows, slots):
    height, width = block.shape[0], slots.shape[0]
    return pl.pallas_call(
        place_kernel,
        grid=(1,),
        out_shape=jax.ShapeDtypeStruct((height, width), jnp.float32),
        in_specs=[
            smem(),
            pl.BlockSpec((height, width), lambda t: (0, 0)),
            pl.BlockSpec((width, width), lambda t: (0, 0)),
        ],
        out_specs=pl.BlockSpec((height, width), lambda t: (0, 0)),
        scratch_shapes=[pltpu.VMEM((height + SUB, width), jnp.float32)],
        cost_estimate=pl.CostEstimate(flops=0, bytes_accessed=8 * height * width, transcendentals=0),
        name="place",
    )(slots, block, rows)


def halves(x):
    high = x.astype(jnp.bfloat16)
    low = (x - high.astype(jnp.float32)).astype(jnp.bfloat16)
    return high, low


def wide_left(x):
    high, low = halves(x)
    return jnp.concatenate([high, low, high], axis=1)


def wide_right(x):
    high, low = halves(x)
    return jnp.concatenate([low, high, high], axis=0)


def wide_dot(left, right):
    return jnp.dot(left, right, preferred_element_type=jnp.float32)


def split_dot(left, right):
    acc = jnp.dot(left[0], right[1], preferred_element_type=jnp.float32)
    acc += jnp.dot(left[1], right[0], preferred_element_type=jnp.float32)
    return acc + jnp.dot(left[0], right[0], preferred_element_type=jnp.float32)


def update_kernel(
    slot_ref, where_ref, block_ref, panel_ref, pivot_ref, top_ref, packed_ref, linv_ref, uinv_ref,
    out_ref, high_ref, low_ref, buf_ref,
):
    rows, width = panel_ref.shape
    t = pl.program_id(0)
    first_row = where_ref[0] == 0
    first_col = (where_ref[1] == 0) & (t == 0)

    @pl.when(t == 0)
    def _():
        lower = jnp.dot(panel_ref[...], uinv_ref[...], precision=HI, preferred_element_type=jnp.float32)
        high_ref[...], low_ref[...] = halves(lower)
        out_ref[...] = lower

    upper = jnp.dot(linv_ref[...], pivot_ref[...], precision=HI, preferred_element_type=jnp.float32)

    @pl.when(jnp.logical_not(first_col))
    def _():
        buf_ref[:rows, :] = block_ref[...]
        place_rows(slot_ref, top_ref, buf_ref)
        out_ref[...] = buf_ref[:rows, :] - split_dot((high_ref[...], low_ref[...]), halves(upper))

    @pl.when(first_row)
    def _():
        out_ref[:width, :] = jnp.where(first_col, packed_ref[...], upper)


def update(block, panel, pivot_rows, old_top, packed, linv, uinv, slots, where):
    rows, cols = block.shape
    width = slots.shape[0]
    square = pl.BlockSpec((width, width), lambda t: (0, 0))
    tall = pl.BlockSpec((rows, width), lambda t: (0, t))
    flat = pl.BlockSpec((width, width), lambda t: (0, t))
    return pl.pallas_call(
        update_kernel,
        grid=(cols // width,),
        out_shape=jax.ShapeDtypeStruct((rows, cols), jnp.float32),
        in_specs=[
            smem(), smem(), tall, pl.BlockSpec((rows, width), lambda t: (0, 0)), flat, flat, square, square, square,
        ],
        out_specs=tall,
        scratch_shapes=[
            pltpu.VMEM((rows, width), jnp.bfloat16),
            pltpu.VMEM((rows, width), jnp.bfloat16),
            pltpu.VMEM((rows + SUB, width), jnp.float32),
        ],
        cost_estimate=pl.CostEstimate(
            flops=6 * rows * cols * width, bytes_accessed=8 * rows * cols, transcendentals=0
        ),
        name="update",
    )(slots, where, block, panel, pivot_rows, old_top, packed, linv, uinv)


def bits_of(n):
    return [1 << i for i in range(n.bit_length() - 1)]


def sum_over_rows(x, order, n_row):
    for bit in order:
        x = x + lax.ppermute(x, "prow", [(i, i ^ bit) for i in range(n_row)])
    return x


def spread_rows(x, order, n_row):
    have = [0]
    for bit in order:
        x = x + lax.ppermute(x, "prow", [(i, i ^ bit) for i in have])
        have = have + [i ^ bit for i in have]
    return x


def spread_cols(x, order):
    have = [0]
    for bit in order:
        x = x + lax.ppermute(x, "pcol", [(i, i ^ bit) for i in have])
        have = have + [i ^ bit for i in have]
    return x


def dense_step(n_row, n_col, matrix, pivots):
    block = matrix[0, :, 0, :]
    rows, cols = block.shape
    width = pivots.shape[0]
    row = lax.axis_index("prow")
    col = lax.axis_index("pcol")
    owner = pivots // width % n_row
    slot = pivots // (width * n_row) * width + pivots % width
    mine = owner == row
    owned = mine.astype(jnp.int32)
    target = jnp.where(mine, slot, rows)
    where = jnp.stack([row, col]).astype(jnp.int32)
    row_bits, col_bits = bits_of(n_row), bits_of(n_col)
    at_first_row = row == 0
    at_first_col = col == 0

    square = pick(block, slot, owned * at_first_col.astype(jnp.int32), 1)
    square = sum_over_rows(square, row_bits, n_row)
    square = spread_cols(square, col_bits[::-1])
    packed, linv, uinv = factor(square, jnp.zeros_like(square))

    top = jnp.where(at_first_row, block[:width], 0.0)
    top_panel = spread_rows(top[:, :width], row_bits, n_row)
    panel = place(block, top_panel, target)
    panel = spread_cols(jnp.where(at_first_col, panel, 0.0), col_bits[::-1])

    picked = pick(block, slot, owned, cols // width)
    half = width // 2
    pivot_rows = jnp.concatenate([
        sum_over_rows(picked[:half], row_bits, n_row),
        sum_over_rows(picked[half:], row_bits[::-1], n_row),
    ])
    old_top = jnp.concatenate([
        spread_rows(top[:half], row_bits, n_row),
        spread_rows(top[half:], row_bits[::-1], n_row),
    ])
    result = update(block, panel, pivot_rows, old_top, packed, linv, uinv, target, where)
    return result[None, :, None, :]


def raw():
    return pl.BlockSpec(memory_space=pl.ANY)


def thirds(x):
    high = x.astype(jnp.bfloat16)
    rest = x - high.astype(jnp.float32)
    middle = rest.astype(jnp.bfloat16)
    return high, middle, (rest - middle.astype(jnp.float32)).astype(jnp.bfloat16)


def select_dot(choice, parts):
    choice = choice.astype(jnp.bfloat16)
    high, middle, low = [jnp.dot(choice, x, preferred_element_type=jnp.float32) for x in parts]
    return high + (middle + low)


def pick_dot(parts, choice):
    choice = choice.astype(jnp.bfloat16)
    high, middle, low = [jnp.dot(x, choice, preferred_element_type=jnp.float32) for x in parts]
    return high + (middle + low)


def begin_kernel(n_row, pivot_ref, mat_ref, panel_ref, wide_ref, fits_ref, *refs):
    messages, sem = refs[:n_row], refs[-1]
    rows, width = panel_ref.shape
    count = messages[0].shape[0] // 2
    width_log, row_log = width.bit_length() - 1, n_row.bit_length() - 1
    row = lax.axis_index("prow")
    copy = pltpu.make_async_copy(mat_ref.at[:, 0, pl.ds(0, width)], panel_ref, sem)
    copy.start()
    pivot = pivot_ref[...]
    block = lax.shift_right_logical(pivot, width_log)
    owner = block & (n_row - 1)
    slot = lax.shift_left(lax.shift_right_logical(block, row_log), width_log) + (pivot & (width - 1))
    _, rank = owners(pivot, n_row)
    fits_ref[0] = (jnp.max(rank) < count).astype(jnp.int32)
    place = ((owner ^ row) * count + rank).astype(jnp.float32)
    eye = lax.broadcasted_iota(jnp.int32, (width, width), 0) == lax.broadcasted_iota(jnp.int32, (width, width), 1)
    spread = jnp.where(eye, place, 0.0)
    wide = jnp.dot(spread, jnp.ones((width, LANES), jnp.float32), precision=HI, preferred_element_type=jnp.float32)
    wide_ref[...] = wide.astype(jnp.int32)
    ordinal = lax.broadcasted_iota(jnp.int32, (count, width), 0)
    mine = jnp.where((ordinal == rank) & (owner == row), 1.0, 0.0).astype(jnp.bfloat16)
    at_slot = jnp.where(lax.broadcasted_iota(jnp.int32, (rows, width), 0) == slot, 1.0, 0.0).astype(jnp.bfloat16)
    choice = lax.dot_general(mine, at_slot, (((1,), (1,)), ((), ())), preferred_element_type=jnp.float32)
    copy.wait()
    own = select_dot(choice, thirds(panel_ref[...]))
    for k in range(n_row):
        messages[k][:count, :] = own

    @pl.when(row == 0)
    def _():
        top = thirds(panel_ref[:width, :])
        for p in range(n_row):
            messages[p][count:, :] = select_dot(jnp.where((ordinal == rank) & (owner == p), 1.0, 0.0), top)


def begin(mat, pivots, n_row, count):
    rows, width = mat.shape[0], pivots.shape[0]
    message = jax.ShapeDtypeStruct((2 * count, width), jnp.float32)
    return pl.pallas_call(
        functools.partial(begin_kernel, n_row),
        out_shape=(
            jax.ShapeDtypeStruct((rows, width), jnp.float32),
            jax.ShapeDtypeStruct((width, LANES), jnp.int32),
            jax.ShapeDtypeStruct((1,), jnp.int32),
        ) + (message,) * n_row,
        in_specs=[vmem(), raw()],
        out_specs=(vmem(), vmem(), smem()) + (vmem(),) * n_row,
        scratch_shapes=[pltpu.SemaphoreType.DMA],
        cost_estimate=pl.CostEstimate(flops=0, bytes_accessed=10_000_000, transcendentals=0),
        compiler_params=pltpu.CompilerParams(vmem_limit_bytes=12 << 20),
        name="begin",
    )(pivots[None, :], mat)


def parcel_kernel(n_row, mine_ref, pivot_ref, mat_ref, *refs):
    outs, own, block, sem = refs[:-3], refs[-3], refs[-2], refs[-1]
    count, cols = own.shape
    half = count // 2
    width = pivot_ref.shape[1]

    def group(q, c):
        for u in range(SUB):
            i = q * SUB + u
            pltpu.make_async_copy(mat_ref.at[mine_ref[i]], own.at[pl.ds(i, 1), :], sem.at[0]).start()
        return c

    lax.fori_loop(0, count // SUB, group, 0)

    @pl.when(lax.axis_index("prow") == 0)
    def _():
        copy = pltpu.make_async_copy(mat_ref.at[pl.ds(0, width), 0, :], block, sem.at[1])
        copy.start()
        owner, rank = owners(pivot_ref[...], n_row)
        ordinal = lax.broadcasted_iota(jnp.int32, (count, width), 0)
        choices = [jnp.where((ordinal == rank) & (owner == p), 1.0, 0.0) for p in range(n_row)]
        choice = jnp.concatenate(choices, axis=0)
        copy.wait()

        def piece(t, c):
            at = pl.ds(pl.multiple_of(t * width, width), width)
            tops = select_dot(choice, thirds(block[:, at]))
            for p in range(n_row):
                for part in range(2):
                    first = p * count + part * half
                    for ref, base in top_places(n_row, half, outs, p, part):
                        ref[pl.ds(base, half), at] = tops[first:first + half]
            return c

        lax.fori_loop(0, cols // width, piece, 0)

    pltpu.make_async_copy(mat_ref.at[pl.ds(0, count), 0, :], own, sem.at[0]).wait()
    if n_row == 4:
        outs[0][:half, :] = own[:half, :]
        outs[1][:half, :] = own[half:, :]
        outs[2][:count, :] = own[...]
    else:
        outs[0][:count, :] = own[...]
        for p in range(1, n_row):
            outs[p][:count, :] = own[...]


def top_places(n_row, half, outs, p, part):
    if n_row != 4:
        return [(outs[p], 2 * half + part * half)]
    if p == 0:
        return [(outs[2], 2 * half + part * half)]
    if p == 3:
        return [(outs[part], 2 * half)]
    if part == p - 1:
        return [(outs[part], half)]
    return [(outs[2], (4 + part) * half)]


def owners(pivot, n_row):
    width = pivot.shape[1]
    owner = lax.shift_right_logical(pivot, width.bit_length() - 1) & (n_row - 1)
    held = lax.broadcasted_iota(jnp.int32, (-(-n_row // 16) * 16, width), 0) == owner
    before = lax.broadcasted_iota(jnp.int32, (width, width), 0) < lax.broadcasted_iota(jnp.int32, (width, width), 1)
    held = jnp.where(held, 1.0, 0.0)
    earlier = jnp.dot(
        held.astype(jnp.bfloat16), jnp.where(before, 1.0, 0.0).astype(jnp.bfloat16), preferred_element_type=jnp.float32
    )
    return owner, jnp.sum(held * earlier, axis=0, keepdims=True).astype(jnp.int32)


def parcel(mat, mine, pivots, n_row):
    count, width, cols = mine.shape[0], pivots.shape[0], mat.shape[2]
    half = count // 2
    sizes = [3 * half, 3 * half, 6 * half] if n_row == 4 else [2 * count] * n_row
    return pl.pallas_call(
        functools.partial(parcel_kernel, n_row),
        out_shape=tuple(jax.ShapeDtypeStruct((size, cols), jnp.float32) for size in sizes),
        in_specs=[smem(), vmem(), raw()],
        out_specs=(vmem(),) * len(sizes),
        scratch_shapes=[
            pltpu.VMEM((count, cols), jnp.float32),
            pltpu.VMEM((width, cols), jnp.float32),
            pltpu.SemaphoreType.DMA((2,)),
        ],
        cost_estimate=pl.CostEstimate(flops=0, bytes_accessed=16_000_000, transcendentals=0),
        compiler_params=pltpu.CompilerParams(vmem_limit_bytes=16 << 20),
        name="parcel",
    )(mine, pivots[None, :], mat)


def relay_kernel(kept_ref, first_ref, second_ref, y_ref, x_ref, sem):
    half = first_ref.shape[0] // 3
    row = lax.axis_index("prow")

    def move(source, base, dest, at, n):
        return pltpu.make_async_copy(source.at[pl.ds(base, half), :], dest.at[pl.ds(at, half), :], sem.at[n])

    copies = [
        move(kept_ref, 0, y_ref, 0, 0),
        move(kept_ref, half, x_ref, 0, 1),
        move(first_ref, 0, y_ref, half, 2),
        move(second_ref, 0, x_ref, half, 3),
    ]
    for copy in copies:
        copy.start()

    @pl.when(row == 0)
    def _():
        move(kept_ref, 4 * half, y_ref, 2 * half, 4).start()
        move(kept_ref, 5 * half, x_ref, 2 * half, 5).start()

    @pl.when(row != 0)
    def _():
        move(first_ref, 2 * half, y_ref, 2 * half, 4).start()
        move(second_ref, 2 * half, x_ref, 2 * half, 5).start()

    for copy in copies:
        copy.wait()
    move(first_ref, 2 * half, y_ref, 2 * half, 4).wait()
    move(second_ref, 2 * half, x_ref, 2 * half, 5).wait()


def relay(kept, first, second):
    shape = jax.ShapeDtypeStruct(first.shape, jnp.float32)
    return pl.pallas_call(
        relay_kernel,
        out_shape=(shape, shape),
        in_specs=[raw()] * 3,
        out_specs=(vmem(), vmem()),
        scratch_shapes=[pltpu.SemaphoreType.DMA((6,))],
        cost_estimate=pl.CostEstimate(flops=0, bytes_accessed=4_000_000, transcendentals=0),
        compiler_params=pltpu.CompilerParams(vmem_limit_bytes=4 << 20),
        name="relay",
    )(kept, first, second)


def pack_kernel(n_row, wide_ref, *refs):
    parts, out_ref, stack, sem = refs[:n_row], refs[n_row], refs[n_row + 1], refs[n_row + 2]
    width = wide_ref.shape[0]
    count = out_ref.shape[0] - width
    row, col = lax.axis_index("prow"), lax.axis_index("pcol")
    total = stack.shape[0]

    @pl.when(col == 0)
    def _():
        copies = [
            pltpu.make_async_copy(parts[k].at[pl.ds(0, count), :], stack.at[pl.ds(k * count, count), :], sem.at[k])
            for k in range(n_row)
        ]
        for copy in copies:
            copy.start()
        for k in range(n_row):
            @pl.when(row == k)
            def _(k=k):
                pltpu.make_async_copy(
                    parts[k].at[pl.ds(count, count), :], out_ref.at[pl.ds(width, count), :], sem.at[n_row]
                ).start()
        if total > n_row * count:
            stack[n_row * count:, :] = jnp.zeros((total - n_row * count, width), jnp.float32)
        lanes = lax.broadcasted_iota(jnp.int32, (width, LANES), 1)
        choice = jnp.concatenate(
            [jnp.where(lanes + t * LANES == wide_ref[...], 1.0, 0.0) for t in range(total // LANES)], axis=1
        )
        for copy in copies:
            copy.wait()
        out_ref[:width, :] = select_dot(choice, thirds(stack[...]))
        pltpu.make_async_copy(
            parts[0].at[pl.ds(count, count), :], out_ref.at[pl.ds(width, count), :], sem.at[n_row]
        ).wait()

    @pl.when(col != 0)
    def _():
        out_ref[...] = jnp.zeros_like(out_ref)


def pack(wide, parts):
    n_row, width = len(parts), wide.shape[0]
    count = parts[0].shape[0] // 2
    return pl.pallas_call(
        functools.partial(pack_kernel, n_row),
        out_shape=jax.ShapeDtypeStruct((width + count, width), jnp.float32),
        in_specs=[vmem()] + [raw()] * n_row,
        out_specs=vmem(),
        scratch_shapes=[
            pltpu.VMEM((-(-n_row * count // LANES) * LANES, width), jnp.float32),
            pltpu.SemaphoreType.DMA((n_row + 1,)),
        ],
        cost_estimate=pl.CostEstimate(flops=0, bytes_accessed=4_000_000, transcendentals=0),
        compiler_params=pltpu.CompilerParams(vmem_limit_bytes=6 << 20),
        name="pack",
    )(wide, *parts)


def unpack_parcels(n_row, count, parcels):
    half = count // 2
    if n_row != 4:
        parts = [(x, part * half) for x in parcels for part in range(2)]
        return parts, [[(x, count + part * half) for part in range(2)] for x in parcels]
    kept, first, second, third, fourth = parcels
    parts = [
        (kept, 0), (kept, half), (first, 0), (fourth, 0), (third, 0), (second, 0), (third, half), (fourth, half)
    ]
    tops = [
        [(kept, 2 * half), (kept, 3 * half)],
        [(first, half), (fourth, 2 * half)],
        [(third, 2 * half), (second, half)],
        [(third, 2 * half), (fourth, 2 * half)],
    ]
    return parts, tops


def put_rows(slot_ref, held, rows_ref, target_ref):
    spare = target_ref.shape[0] - SUB

    def group(q, c):
        for u in range(SUB):
            i = q * SUB + u
            slot = jnp.where(i < held, slot_ref[i], spare)
            target_ref[pl.ds(slot, 1), :] = rows_ref[pl.ds(i, 1), :]
        return c

    lax.fori_loop(0, (held + SUB - 1) // SUB, group, 0)


def finish_kernel(
    n_row, mine_ref, counts_ref, wide_ref, mat_ref, panel_ref, panel_new_ref, square_ref, square_new_ref,
    packed_ref, linv_ref, uinv_ref, *refs,
):
    n_parcels = 5 if n_row == 4 else n_row
    parcels, refs = refs[:n_parcels], refs[n_parcels:]
    out_ref, block, pivot, panel, old, left, lower, top, sem, in_sem, out_sem = refs
    rows, _, cols = mat_ref.shape
    width = linv_ref.shape[0]
    count = mine_ref.shape[0]
    half = count // 2
    stacked = n_row * count
    parts, tops = unpack_parcels(n_row, count, parcels)
    tiles = cols // width
    row, col = lax.axis_index("prow"), lax.axis_index("pcol")

    def tile(t):
        return pl.ds(pl.multiple_of(t * width, width), width)

    @pl.when(col % 2 == 0)
    def _():
        pltpu.make_async_copy(panel_ref, panel.at[pl.ds(0, rows)], sem.at[0]).start()

    @pl.when(col % 2 == 1)
    def _():
        pltpu.make_async_copy(panel_new_ref, panel.at[pl.ds(0, rows)], sem.at[0]).start()

    top_copies = [
        pltpu.make_async_copy(ref.at[pl.ds(width, count), :], top.at[n], sem.at[1 + n])
        for n, ref in enumerate((square_ref, square_new_ref))
    ]
    for copy in top_copies:
        copy.start()

    def fetch(t, c):
        pltpu.make_async_copy(mat_ref.at[:, 0, tile(t)], block.at[pl.ds(0, rows), tile(t)], in_sem.at[0, t]).start()
        for n, (ref, base) in enumerate(parts):
            dest = pivot.at[pl.ds(n * half, half), tile(t)]
            pltpu.make_async_copy(ref.at[pl.ds(base, half), tile(t)], dest, in_sem.at[1, t]).start()
        for p in range(n_row):
            @pl.when(row == p)
            def _(p=p):
                for part, (ref, base) in enumerate(tops[p]):
                    dest = old.at[pl.ds(part * half, half), tile(t)]
                    pltpu.make_async_copy(ref.at[pl.ds(base, half), tile(t)], dest, in_sem.at[2, t]).start()
        return c

    lax.fori_loop(0, tiles, fetch, 0)
    if pivot.shape[0] > stacked:
        pivot[stacked:, :] = jnp.zeros((pivot.shape[0] - stacked, cols), jnp.float32)

    lanes = lax.broadcasted_iota(jnp.int32, (width, LANES), 1)
    places = jnp.concatenate(
        [jnp.where(lanes + t * LANES == wide_ref[...], 1.0, 0.0) for t in range(pivot.shape[0] // LANES)], axis=1
    )
    spread_inv = wide_left(pick_dot(thirds(linv_ref[...]), places))
    for copy in top_copies:
        copy.wait()
    top[0] = top[0] + top[1]
    pltpu.make_async_copy(panel_ref, panel.at[pl.ds(0, rows)], sem.at[0]).wait()
    put_rows(mine_ref, counts_ref[row], top.at[0], panel)
    lower[...] = wide_dot(wide_left(panel[:rows, :]), wide_right(uinv_ref[...]))
    left[...] = wide_left(lower[...])

    def step(t, c):
        first_col = (col == 0) & (t == 0)
        pltpu.make_async_copy(
            mat_ref.at[pl.ds(0, stacked), 0, tile(t)], pivot.at[pl.ds(0, stacked), tile(t)], in_sem.at[1, t]
        ).wait()
        upper = wide_dot(spread_inv, wide_right(pivot[:, tile(t)]))
        pltpu.make_async_copy(mat_ref.at[pl.ds(0, count), 0, tile(t)], old.at[:, tile(t)], in_sem.at[2, t]).wait()
        pltpu.make_async_copy(mat_ref.at[:, 0, tile(t)], block.at[pl.ds(0, rows), tile(t)], in_sem.at[0, t]).wait()

        @pl.when(jnp.logical_not(first_col))
        def _():
            put_rows(mine_ref, counts_ref[row], old.at[:, tile(t)], block.at[:, tile(t)])
            block[:rows, tile(t)] = block[:rows, tile(t)] - wide_dot(left[...], wide_right(upper))

        @pl.when(first_col)
        def _():
            block[:rows, tile(t)] = lower[...]

        @pl.when(row == 0)
        def _():
            block[:width, tile(t)] = jnp.where(first_col, packed_ref[...], upper)

        pltpu.make_async_copy(block.at[pl.ds(0, rows), tile(t)], out_ref.at[:, 0, tile(t)], out_sem.at[t]).start()
        return c

    lax.fori_loop(0, tiles, step, 0)

    def drain(t, c):
        pltpu.make_async_copy(block.at[pl.ds(0, rows), tile(t)], out_ref.at[:, 0, tile(t)], out_sem.at[t]).wait()
        return c

    lax.fori_loop(0, tiles, drain, 0)


def finish(mine, counts, wide, mat, panels, squares, factors, parcels):
    rows, _, cols = mat.shape
    width, n_row, count = factors[0].shape[0], counts.shape[0], mine.shape[0]
    return pl.pallas_call(
        functools.partial(finish_kernel, n_row),
        out_shape=jax.ShapeDtypeStruct(mat.shape, jnp.float32),
        in_specs=[smem(), smem(), vmem()] + [raw()] * 5 + [vmem()] * 3 + [raw()] * len(parcels),
        out_specs=raw(),
        scratch_shapes=[
            pltpu.VMEM((rows + SUB, cols), jnp.float32),
            pltpu.VMEM((-(-n_row * count // LANES) * LANES, cols), jnp.float32),
            pltpu.VMEM((rows + SUB, width), jnp.float32),
            pltpu.VMEM((count, cols), jnp.float32),
            pltpu.VMEM((rows, 3 * width), jnp.bfloat16),
            pltpu.VMEM((rows, width), jnp.float32),
            pltpu.VMEM((2, count, width), jnp.float32),
            pltpu.SemaphoreType.DMA((3,)),
            pltpu.SemaphoreType.DMA((3, cols // width)),
            pltpu.SemaphoreType.DMA((cols // width,)),
        ],
        cost_estimate=pl.CostEstimate(
            flops=6 * rows * cols * width, bytes_accessed=8 * rows * cols, transcendentals=0
        ),
        compiler_params=pltpu.CompilerParams(vmem_limit_bytes=26 << 20),
        name="finish",
    )(mine, counts, wide, mat, *panels, *squares, *factors, *parcels)


def capacity(n_row, width):
    mean = width / n_row
    return -(-int(mean + 4 * (mean * (1 - 1 / n_row)) ** 0.5) // (2 * SUB)) * (2 * SUB)


def locate(pivots, n_row, row, count):
    width = pivots.shape[0]
    owner = pivots // width % n_row
    slot = pivots // (width * n_row) * width + pivots % width
    number = jnp.arange(width, dtype=jnp.int32)
    ahead = (owner[:, None] == owner[None, :]) & (number[None, :] < number[:, None])
    rank = jnp.sum(ahead, axis=1, dtype=jnp.int32)
    every = jnp.arange(n_row, dtype=jnp.int32)[:, None]
    ordinal = jnp.arange(count, dtype=jnp.int32)[:, None]
    own = (owner[None, :] == row) & (rank[None, :] == ordinal)
    mine = jnp.sum(jnp.where(own, slot[None, :], 0), axis=1, dtype=jnp.int32)
    return mine, jnp.sum(owner[None, :] == every, axis=1, dtype=jnp.int32)


def capped_step(n_row, n_col, matrix, pivots, begun):
    _, rows, _, cols = matrix.shape
    mat = matrix.reshape(rows, 1, cols)
    panel, wide, _, *messages = begun
    count = messages[0].shape[0] // 2
    row, col = lax.axis_index("prow"), lax.axis_index("pcol")
    both = ("prow", "pcol")
    turns = bits_of(n_col)[:0:-1]

    def exchange(x, k):
        return lax.ppermute(x, both, [(i * n_col, (i ^ k) * n_col) for i in range(n_row)])

    moved = [exchange(messages[k], k) for k in range(1, n_row)]
    mine, counts = locate(pivots, n_row, row, count)
    parcels = parcel(mat, mine, pivots, n_row)

    def send(x, k):
        return lax.ppermute(x, "prow", [(i, i ^ k) for i in range(n_row)])

    *moved, kept = lax.optimization_barrier((*moved, parcels[-1]))
    parcels = parcels[:-1] + (kept,)
    message = pack(wide, messages[:1] + moved)
    roots = [lax.ppermute(panel, "pcol", [(0, bit)]) for bit in turns]
    message, *roots = lax.optimization_barrier((message, *roots))
    if n_row == 4:
        first, second = send(parcels[0], 1), send(parcels[1], 2)
        kept = parcels[2]
        to_y, to_x = relay(kept, first, second)
        arrived = [kept, first, second]
    else:
        arrived = [parcels[0]] + [send(parcels[k], k) for k in range(1, n_row)]

    pairs = [[(i, i + bit) for i in range(0, n_col, 2 * bit)] for bit in turns + [1]]
    newer = [(col & bit) != 0 for bit in turns]
    panel = jnp.where(col == turns[0], roots[0], panel)
    for n, bit in enumerate(turns):
        if n + 1 < len(turns):
            relayed = lax.ppermute(roots[0] if n == 0 else panel, "pcol", pairs[n + 1][1:])
        message = jnp.where(newer[n], lax.ppermute(message, "pcol", pairs[n]), message)
        if n + 1 < len(turns):
            message, relayed = lax.optimization_barrier((message, relayed))
            newest = jnp.where(col == turns[n + 1], roots[n + 1], relayed)
            panel = jnp.where(newer[n + 1], newest, panel)
    panel_moved = lax.ppermute(panel, "pcol", pairs[-1])
    if n_row == 4:
        message, to_y, to_x = lax.optimization_barrier((message, to_y, to_x))
        arrived += [send(to_y, 2), send(to_x, 1)]
    message_new = lax.ppermute(message, "pcol", pairs[-1])
    factors = factor(message, message_new)
    out = finish(
        mine, counts, wide, mat, (panel, panel_moved), (message, message_new), factors, arrived
    )
    return out.reshape(matrix.shape)


def on_device(n_row, n_col, matrix, pivots):
    _, rows, _, cols = matrix.shape
    begun = begin(matrix.reshape(rows, 1, cols), pivots, n_row, capacity(n_row, pivots.shape[0]))
    return lax.cond(
        begun[2][0] > 0,
        lambda m, p, b: capped_step(n_row, n_col, m, p, b),
        lambda m, p, b: dense_step(n_row, n_col, m, p),
        matrix, pivots, begun,
    )


def solution(mesh):
    spec = P("prow", None, "pcol", None)
    n_row, n_col = mesh.shape["prow"], mesh.shape["pcol"]
    return jax.shard_map(
        functools.partial(on_device, n_row, n_col), mesh=mesh, in_specs=(spec, P()), out_specs=spec, check_vma=False
    )
```

```python
import functools

import jax
import jax.numpy as jnp
from jax import lax
from jax.experimental import pallas as pl
from jax.experimental.pallas import tpu as pltpu
from jax.sharding import PartitionSpec as P

LANES = 128
SUB = 8
HI = lax.Precision.HIGHEST


def pick_lane(tile, lane):
    return jnp.take_along_axis(tile, jnp.full((SUB, LANES), lane, jnp.int32), axis=1)


def row_of(tile, j):
    return jnp.broadcast_to(tile[j:j + 1, :], (SUB, LANES))


def factor_kernel(width, unroll, first_ref, second_ref, packed_ref, linv_ref, uinv_ref, a_ref, m_ref, v_ref, s_ref, sem):
    groups = a_ref.shape[0]
    tiles = groups * SUB // LANES
    per_tile = LANES // SUB
    per_block = width // SUB
    copies = [
        pltpu.make_async_copy(ref.at[pl.ds(0, groups * SUB), :], s_ref.at[n], sem.at[n])
        for n, ref in enumerate((first_ref, second_ref))
    ]
    for copy in copies:
        copy.start()
    sub = lax.broadcasted_iota(jnp.int32, (SUB, LANES), 0)
    lane = lax.broadcasted_iota(jnp.int32, (SUB, LANES), 1)

    for i in range(groups):
        diag = lane - (i % per_tile) * SUB == sub
        for t in range(tiles):
            block = jnp.where(diag, 1.0, 0.0) if i // per_tile == t else jnp.zeros((SUB, LANES), jnp.float32)
            m_ref[i, :, t * LANES:(t + 1) * LANES] = block
            if t > i // per_tile:
                linv_ref[i * SUB:(i + 1) * SUB, t * LANES:(t + 1) * LANES] = block

    for copy in copies:
        copy.wait()
    for i in range(groups):
        a_ref[i] = s_ref[0, i * SUB:(i + 1) * SUB, :] + s_ref[1, i * SUB:(i + 1) * SUB, :]

    def span(t):
        return slice(t * LANES, (t + 1) * LANES)

    for o in range(groups // per_block):
        base = o * per_block
        h = base // per_tile
        live = [(a_ref, t) for t in range(h + 1, tiles)] + [(m_ref, t) for t in range(h + 1)]

        def panel(i, c, base=base, h=h, live=live):
            b = base + i
            g = (b - h * per_tile) * SUB
            rows = pl.ds(pl.multiple_of(b * SUB, SUB), SUB)
            own = a_ref[b, :, span(h)]
            cols = [pick_lane(own, g + j) for j in range(SUB)]
            in_panel = (lane >= g) & (lane < g + SUB)
            after = lane >= g + SUB
            head = jnp.where(in_panel, jnp.where(lane - g == sub, -1.0, 0.0), jnp.where(after, own, 0.0))
            rest = [ref[b, :, span(t)] for ref, t in live]
            packed = own
            final = [head] + rest
            for j in range(SUB):
                at = sub == j
                coef = cols[j]
                r = 1.0 / row_of(coef, j)
                final = [jnp.where(at, x, y) for x, y in zip([head] + rest, final)]
                packed = jnp.where((lane == g + j) & (sub > j), coef * r, packed)
                for k in range(j, SUB):
                    packed = jnp.where((lane == g + k) & at, cols[k], packed)
                head_coef = jnp.where((sub < j) | after, coef, 0.0)
                v = row_of(head, j) * r
                head = jnp.where(at, v, head - head_coef * v)
                for n, x in enumerate(rest):
                    v = row_of(x, j) * r
                    rest[n] = jnp.where(at, v, x - coef * v)
                for k in range(j + 1, SUB):
                    v = row_of(cols[k], j) * r
                    cols[k] = jnp.where(at, v, cols[k] - coef * v)
            for t in range(h):
                packed_ref[rows, span(t)] = a_ref[b, :, span(t)]
            packed_ref[rows, span(h)] = jnp.where(after, final[0], packed)
            for (ref, t), x in zip(live, final[1:]):
                (packed_ref if ref is a_ref else linv_ref)[rows, span(t)] = x
            a_ref[b, :, span(h)] = head
            v_ref[0] = head
            for n, ((ref, t), x) in enumerate(zip(live, rest)):
                ref[b, :, span(t)] = x
                v_ref[n + 1] = x
            others = [base + lax.rem(i + s, per_block) for s in range(1, per_block)]
            heads = [a_ref[r, :, span(h)] for r in others]
            facs = [[pick_lane(x, g + j) for j in range(SUB)] for x in heads]
            for n, (ref, t) in enumerate([(a_ref, h)] + live):
                old = [jnp.where(in_panel, 0.0, x) for x in heads] if n == 0 else [ref[r, :, span(t)] for r in others]
                vs = [row_of([head] + rest and ([head] + rest)[n], j) for j in range(SUB)]
                for x, fac, r in zip(old, facs, others):
                    acc = [fac[j] * vs[j] for j in range(SUB)]
                    while len(acc) > 1:
                        acc = [p + q for p, q in zip(acc[::2], acc[1::2])]
                    ref[r, :, span(t)] = x - acc[0]
            return c

        lax.fori_loop(0, per_block, panel, 0, unroll=unroll)

        lo = (base % per_tile) * SUB
        pad = [jnp.zeros((n, LANES), jnp.float32) for n in (lo, LANES - lo - width)]

        def stack(x):
            return jnp.concatenate([p for p in (pad[0], x, pad[1]) if p.shape[0]], axis=0)

        def flat(ref, first, last, t):
            return ref[first:last, :, span(t)].reshape((last - first) * SUB, LANES)

        end = base + per_block
        right = [stack(flat(ref, base, end, t)) for ref, t in [(a_ref, h)] + live]
        for first, last in ((end, groups), (0, base)):
            if first == last:
                continue
            left = flat(a_ref, first, last, h)
            column = lax.broadcasted_iota(jnp.int32, left.shape, 1)
            for n, (ref, t) in enumerate([(a_ref, h)] + live):
                if ref is m_ref and first == 0:
                    continue
                old = left if n else None
                old = jnp.where((column >= lo) & (column < lo + width), 0.0, left) if n == 0 else flat(ref, first, last, t)
                new = old - jnp.dot(left, right[n], precision=HI, preferred_element_type=jnp.float32)
                ref[first:last, :, span(t)] = new.reshape(last - first, SUB, LANES)

    ri = lax.broadcasted_iota(jnp.int32, (SUB, LANES), 0)
    for i in range(groups):
        for t in range(tiles):
            x = a_ref[i, :, span(t)]
            keep = lane + t * LANES >= ri + i * SUB
            uinv_ref[i * SUB:(i + 1) * SUB, span(t)] = jnp.where(keep, -x, 0.0)


def vmem():
    return pl.BlockSpec(memory_space=pltpu.VMEM)


def smem():
    return pl.BlockSpec(memory_space=pltpu.SMEM)


def factor(square, extra, unroll, width=32):
    size = square.shape[1]
    out = jax.ShapeDtypeStruct((size, size), jnp.float32)
    return pl.pallas_call(
        functools.partial(factor_kernel, width, unroll),
        out_shape=(out, out, out),
        in_specs=[raw(), raw()],
        out_specs=(vmem(),) * 3,
        scratch_shapes=[
            pltpu.VMEM((size // SUB, SUB, size), jnp.float32),
            pltpu.VMEM((size // SUB, SUB, size), jnp.float32),
            pltpu.VMEM((1 + size // LANES, SUB, LANES), jnp.float32),
            pltpu.VMEM((2, size, size), jnp.float32),
            pltpu.SemaphoreType.DMA((2,)),
        ],
        cost_estimate=pl.CostEstimate(flops=4 * size**3, bytes_accessed=50_000_000, transcendentals=0),
        compiler_params=pltpu.CompilerParams(vmem_limit_bytes=10 << 20),
        name="factor",
    )(square, extra)


def pick_kernel(slot_ref, own_ref, block_ref, out_ref):
    def group(q, c):
        for u in range(SUB):
            j = q * SUB + u
            row = block_ref[pl.ds(slot_ref[j], 1), :]
            out_ref[pl.ds(j, 1), :] = row * own_ref[j].astype(jnp.float32)
        return c

    lax.fori_loop(0, out_ref.shape[0] // SUB, group, 0)


def pick(block, slots, owned, tiles):
    rows, width = block.shape[0], slots.shape[0]
    return pl.pallas_call(
        pick_kernel,
        grid=(tiles,),
        out_shape=jax.ShapeDtypeStruct((width, tiles * width), jnp.float32),
        in_specs=[smem(), smem(), pl.BlockSpec((rows, width), lambda t: (0, t))],
        out_specs=pl.BlockSpec((width, width), lambda t: (0, t)),
        cost_estimate=pl.CostEstimate(
            flops=width * width * tiles, bytes_accessed=4 * (rows + width) * width * tiles, transcendentals=0
        ),
        name="pick",
    )(slots, owned, block)


def place_rows(slot_ref, rows_ref, target_ref):
    def group(q, c):
        for u in range(SUB):
            j = q * SUB + u
            target_ref[pl.ds(slot_ref[j], 1), :] = rows_ref[pl.ds(j, 1), :]
        return c

    lax.fori_loop(0, rows_ref.shape[0] // SUB, group, 0)


def place_kernel(slot_ref, block_ref, rows_ref, out_ref, buf_ref):
    rows = block_ref.shape[0]
    buf_ref[:rows, :] = block_ref[...]
    place_rows(slot_ref, rows_ref, buf_ref)
    out_ref[...] = buf_ref[:rows, :]


def place(block, rows, slots):
    height, width = block.shape[0], slots.shape[0]
    return pl.pallas_call(
        place_kernel,
        grid=(1,),
        out_shape=jax.ShapeDtypeStruct((height, width), jnp.float32),
        in_specs=[
            smem(),
            pl.BlockSpec((height, width), lambda t: (0, 0)),
            pl.BlockSpec((width, width), lambda t: (0, 0)),
        ],
        out_specs=pl.BlockSpec((height, width), lambda t: (0, 0)),
        scratch_shapes=[pltpu.VMEM((height + SUB, width), jnp.float32)],
        cost_estimate=pl.CostEstimate(flops=0, bytes_accessed=8 * height * width, transcendentals=0),
        name="place",
    )(slots, block, rows)


def halves(x):
    high = x.astype(jnp.bfloat16)
    low = (x - high.astype(jnp.float32)).astype(jnp.bfloat16)
    return high, low


def wide_left(x):
    high, low = halves(x)
    return jnp.concatenate([high, low, high], axis=1)


def wide_right(x):
    high, low = halves(x)
    return jnp.concatenate([low, high, high], axis=0)


def wide_dot(left, right):
    return jnp.dot(left, right, preferred_element_type=jnp.float32)


def split_dot(left, right):
    acc = jnp.dot(left[0], right[1], preferred_element_type=jnp.float32)
    acc += jnp.dot(left[1], right[0], preferred_element_type=jnp.float32)
    return acc + jnp.dot(left[0], right[0], preferred_element_type=jnp.float32)


def update_kernel(
    slot_ref, where_ref, block_ref, panel_ref, pivot_ref, top_ref, packed_ref, linv_ref, uinv_ref,
    out_ref, high_ref, low_ref, buf_ref,
):
    rows, width = panel_ref.shape
    t = pl.program_id(0)
    first_row = where_ref[0] == 0
    first_col = (where_ref[1] == 0) & (t == 0)

    @pl.when(t == 0)
    def _():
        lower = jnp.dot(panel_ref[...], uinv_ref[...], precision=HI, preferred_element_type=jnp.float32)
        high_ref[...], low_ref[...] = halves(lower)
        out_ref[...] = lower

    upper = jnp.dot(linv_ref[...], pivot_ref[...], precision=HI, preferred_element_type=jnp.float32)

    @pl.when(jnp.logical_not(first_col))
    def _():
        buf_ref[:rows, :] = block_ref[...]
        place_rows(slot_ref, top_ref, buf_ref)
        out_ref[...] = buf_ref[:rows, :] - split_dot((high_ref[...], low_ref[...]), halves(upper))

    @pl.when(first_row)
    def _():
        out_ref[:width, :] = jnp.where(first_col, packed_ref[...], upper)


def update(block, panel, pivot_rows, old_top, packed, linv, uinv, slots, where):
    rows, cols = block.shape
    width = slots.shape[0]
    square = pl.BlockSpec((width, width), lambda t: (0, 0))
    tall = pl.BlockSpec((rows, width), lambda t: (0, t))
    flat = pl.BlockSpec((width, width), lambda t: (0, t))
    return pl.pallas_call(
        update_kernel,
        grid=(cols // width,),
        out_shape=jax.ShapeDtypeStruct((rows, cols), jnp.float32),
        in_specs=[
            smem(), smem(), tall, pl.BlockSpec((rows, width), lambda t: (0, 0)), flat, flat, square, square, square,
        ],
        out_specs=tall,
        scratch_shapes=[
            pltpu.VMEM((rows, width), jnp.bfloat16),
            pltpu.VMEM((rows, width), jnp.bfloat16),
            pltpu.VMEM((rows + SUB, width), jnp.float32),
        ],
        cost_estimate=pl.CostEstimate(
            flops=6 * rows * cols * width, bytes_accessed=8 * rows * cols, transcendentals=0
        ),
        name="update",
    )(slots, where, block, panel, pivot_rows, old_top, packed, linv, uinv)


def bits_of(n):
    return [1 << i for i in range(n.bit_length() - 1)]


def sum_over_rows(x, order, n_row):
    for bit in order:
        x = x + lax.ppermute(x, "prow", [(i, i ^ bit) for i in range(n_row)])
    return x


def spread_rows(x, order, n_row):
    have = [0]
    for bit in order:
        x = x + lax.ppermute(x, "prow", [(i, i ^ bit) for i in have])
        have = have + [i ^ bit for i in have]
    return x


def spread_cols(x, order):
    have = [0]
    for bit in order:
        x = x + lax.ppermute(x, "pcol", [(i, i ^ bit) for i in have])
        have = have + [i ^ bit for i in have]
    return x


def dense_step(n_row, n_col, matrix, pivots):
    block = matrix[0, :, 0, :]
    rows, cols = block.shape
    width = pivots.shape[0]
    row = lax.axis_index("prow")
    col = lax.axis_index("pcol")
    owner = pivots // width % n_row
    slot = pivots // (width * n_row) * width + pivots % width
    mine = owner == row
    owned = mine.astype(jnp.int32)
    target = jnp.where(mine, slot, rows)
    where = jnp.stack([row, col]).astype(jnp.int32)
    row_bits, col_bits = bits_of(n_row), bits_of(n_col)
    at_first_row = row == 0
    at_first_col = col == 0

    square = pick(block, slot, owned * at_first_col.astype(jnp.int32), 1)
    square = sum_over_rows(square, row_bits, n_row)
    square = spread_cols(square, col_bits[::-1])
    packed, linv, uinv = factor(square, jnp.zeros_like(square), False)

    top = jnp.where(at_first_row, block[:width], 0.0)
    top_panel = spread_rows(top[:, :width], row_bits, n_row)
    panel = place(block, top_panel, target)
    panel = spread_cols(jnp.where(at_first_col, panel, 0.0), col_bits[::-1])

    picked = pick(block, slot, owned, cols // width)
    half = width // 2
    pivot_rows = jnp.concatenate([
        sum_over_rows(picked[:half], row_bits, n_row),
        sum_over_rows(picked[half:], row_bits[::-1], n_row),
    ])
    old_top = jnp.concatenate([
        spread_rows(top[:half], row_bits, n_row),
        spread_rows(top[half:], row_bits[::-1], n_row),
    ])
    result = update(block, panel, pivot_rows, old_top, packed, linv, uinv, target, where)
    return result[None, :, None, :]


def raw():
    return pl.BlockSpec(memory_space=pl.ANY)


def thirds(x):
    high = x.astype(jnp.bfloat16)
    rest = x - high.astype(jnp.float32)
    middle = rest.astype(jnp.bfloat16)
    return high, middle, (rest - middle.astype(jnp.float32)).astype(jnp.bfloat16)


def select_dot(choice, parts):
    choice = choice.astype(jnp.bfloat16)
    high, middle, low = [jnp.dot(choice, x, preferred_element_type=jnp.float32) for x in parts]
    return high + (middle + low)


def pick_dot(parts, choice):
    choice = choice.astype(jnp.bfloat16)
    high, middle, low = [jnp.dot(x, choice, preferred_element_type=jnp.float32) for x in parts]
    return high + (middle + low)


def begin_kernel(n_row, pivot_ref, mat_ref, panel_ref, wide_ref, fits_ref, *refs):
    messages, sem = refs[:n_row], refs[-1]
    rows, width = panel_ref.shape
    count = messages[0].shape[0] // 2
    width_log, row_log = width.bit_length() - 1, n_row.bit_length() - 1
    row = lax.axis_index("prow")
    copy = pltpu.make_async_copy(mat_ref.at[:, 0, pl.ds(0, width)], panel_ref, sem)
    copy.start()
    pivot = pivot_ref[...]
    block = lax.shift_right_logical(pivot, width_log)
    owner = block & (n_row - 1)
    slot = lax.shift_left(lax.shift_right_logical(block, row_log), width_log) + (pivot & (width - 1))
    _, rank = owners(pivot, n_row)
    fits_ref[0] = (jnp.max(rank) < count).astype(jnp.int32)
    place = ((owner ^ row) * count + rank).astype(jnp.float32)
    eye = lax.broadcasted_iota(jnp.int32, (width, width), 0) == lax.broadcasted_iota(jnp.int32, (width, width), 1)
    spread = jnp.where(eye, place, 0.0)
    wide = jnp.dot(spread, jnp.ones((width, LANES), jnp.float32), precision=HI, preferred_element_type=jnp.float32)
    wide_ref[...] = wide.astype(jnp.int32)
    ordinal = lax.broadcasted_iota(jnp.int32, (count, width), 0)
    mine = jnp.where((ordinal == rank) & (owner == row), 1.0, 0.0).astype(jnp.bfloat16)
    at_slot = jnp.where(lax.broadcasted_iota(jnp.int32, (rows, width), 0) == slot, 1.0, 0.0).astype(jnp.bfloat16)
    choice = lax.dot_general(mine, at_slot, (((1,), (1,)), ((), ())), preferred_element_type=jnp.float32)
    copy.wait()
    own = select_dot(choice, thirds(panel_ref[...]))
    for k in range(n_row):
        messages[k][:count, :] = own

    @pl.when(row == 0)
    def _():
        top = thirds(panel_ref[:width, :])
        for p in range(n_row):
            messages[p][count:, :] = select_dot(jnp.where((ordinal == rank) & (owner == p), 1.0, 0.0), top)


def begin(mat, pivots, n_row, count):
    rows, width = mat.shape[0], pivots.shape[0]
    message = jax.ShapeDtypeStruct((2 * count, width), jnp.float32)
    return pl.pallas_call(
        functools.partial(begin_kernel, n_row),
        out_shape=(
            jax.ShapeDtypeStruct((rows, width), jnp.float32),
            jax.ShapeDtypeStruct((width, LANES), jnp.int32),
            jax.ShapeDtypeStruct((1,), jnp.int32),
        ) + (message,) * n_row,
        in_specs=[vmem(), raw()],
        out_specs=(vmem(), vmem(), smem()) + (vmem(),) * n_row,
        scratch_shapes=[pltpu.SemaphoreType.DMA],
        cost_estimate=pl.CostEstimate(flops=0, bytes_accessed=10_000_000, transcendentals=0),
        compiler_params=pltpu.CompilerParams(vmem_limit_bytes=12 << 20),
        name="begin",
    )(pivots[None, :], mat)


def parcel_kernel(n_row, mine_ref, pivot_ref, mat_ref, *refs):
    outs, own, block, sem = refs[:-3], refs[-3], refs[-2], refs[-1]
    count, cols = own.shape
    half = count // 2
    width = pivot_ref.shape[1]

    def group(q, c):
        for u in range(SUB):
            i = q * SUB + u
            pltpu.make_async_copy(mat_ref.at[mine_ref[i]], own.at[pl.ds(i, 1), :], sem.at[0]).start()
        return c

    @pl.when(lax.axis_index("prow") == 0)
    def _():
        pltpu.make_async_copy(mat_ref.at[pl.ds(0, width), 0, :], block, sem.at[1]).start()

    lax.fori_loop(0, count // SUB, group, 0)

    @pl.when(lax.axis_index("prow") == 0)
    def _():
        copy = pltpu.make_async_copy(mat_ref.at[pl.ds(0, width), 0, :], block, sem.at[1])
        owner, rank = owners(pivot_ref[...], n_row)
        ordinal = lax.broadcasted_iota(jnp.int32, (count, width), 0)
        choices = [jnp.where((ordinal == rank) & (owner == p), 1.0, 0.0) for p in range(n_row)]
        choice = jnp.concatenate(choices, axis=0)
        copy.wait()

        def piece(t, c):
            at = pl.ds(pl.multiple_of(t * width, width), width)
            tops = select_dot(choice, thirds(block[:, at]))
            for p in range(n_row):
                for part in range(2):
                    first = p * count + part * half
                    for ref, base in top_places(n_row, half, outs, p, part):
                        ref[pl.ds(base, half), at] = tops[first:first + half]
            return c

        lax.fori_loop(0, cols // width, piece, 0, unroll=True)

    pltpu.make_async_copy(mat_ref.at[pl.ds(0, count), 0, :], own, sem.at[0]).wait()
    if n_row == 4:
        outs[0][:half, :] = own[:half, :]
        outs[1][:half, :] = own[half:, :]
        outs[2][:count, :] = own[...]
    else:
        outs[0][:count, :] = own[...]
        for p in range(1, n_row):
            outs[p][:count, :] = own[...]


def top_places(n_row, half, outs, p, part):
    if n_row != 4:
        return [(outs[p], 2 * half + part * half)]
    if p == 0:
        return [(outs[2], 2 * half + part * half)]
    if p == 3:
        return [(outs[part], 2 * half)]
    if part == p - 1:
        return [(outs[part], half)]
    return [(outs[2], (4 + part) * half)]


def owners(pivot, n_row):
    width = pivot.shape[1]
    owner = lax.shift_right_logical(pivot, width.bit_length() - 1) & (n_row - 1)
    held = lax.broadcasted_iota(jnp.int32, (-(-n_row // 16) * 16, width), 0) == owner
    before = lax.broadcasted_iota(jnp.int32, (width, width), 0) < lax.broadcasted_iota(jnp.int32, (width, width), 1)
    held = jnp.where(held, 1.0, 0.0)
    earlier = jnp.dot(
        held.astype(jnp.bfloat16), jnp.where(before, 1.0, 0.0).astype(jnp.bfloat16), preferred_element_type=jnp.float32
    )
    return owner, jnp.sum(held * earlier, axis=0, keepdims=True).astype(jnp.int32)


def parcel(mat, mine, pivots, n_row):
    count, width, cols = mine.shape[0], pivots.shape[0], mat.shape[2]
    half = count // 2
    sizes = [3 * half, 3 * half, 6 * half] if n_row == 4 else [2 * count] * n_row
    return pl.pallas_call(
        functools.partial(parcel_kernel, n_row),
        out_shape=tuple(jax.ShapeDtypeStruct((size, cols), jnp.float32) for size in sizes),
        in_specs=[smem(), vmem(), raw()],
        out_specs=(vmem(),) * len(sizes),
        scratch_shapes=[
            pltpu.VMEM((count, cols), jnp.float32),
            pltpu.VMEM((width, cols), jnp.float32),
            pltpu.SemaphoreType.DMA((2,)),
        ],
        cost_estimate=pl.CostEstimate(flops=0, bytes_accessed=16_000_000, transcendentals=0),
        compiler_params=pltpu.CompilerParams(vmem_limit_bytes=16 << 20),
        name="parcel",
    )(mine, pivots[None, :], mat)


def relay_kernel(kept_ref, first_ref, second_ref, y_ref, x_ref, sem):
    half = first_ref.shape[0] // 3
    row = lax.axis_index("prow")

    def move(source, base, dest, at, n):
        return pltpu.make_async_copy(source.at[pl.ds(base, half), :], dest.at[pl.ds(at, half), :], sem.at[n])

    copies = [
        move(kept_ref, 0, y_ref, 0, 0),
        move(kept_ref, half, x_ref, 0, 1),
        move(first_ref, 0, y_ref, half, 2),
        move(second_ref, 0, x_ref, half, 3),
    ]
    for copy in copies:
        copy.start()

    @pl.when(row == 0)
    def _():
        move(kept_ref, 4 * half, y_ref, 2 * half, 4).start()
        move(kept_ref, 5 * half, x_ref, 2 * half, 5).start()

    @pl.when(row != 0)
    def _():
        move(first_ref, 2 * half, y_ref, 2 * half, 4).start()
        move(second_ref, 2 * half, x_ref, 2 * half, 5).start()

    for copy in copies:
        copy.wait()
    move(first_ref, 2 * half, y_ref, 2 * half, 4).wait()
    move(second_ref, 2 * half, x_ref, 2 * half, 5).wait()


def relay(kept, first, second):
    shape = jax.ShapeDtypeStruct(first.shape, jnp.float32)
    return pl.pallas_call(
        relay_kernel,
        out_shape=(shape, shape),
        in_specs=[raw()] * 3,
        out_specs=(vmem(), vmem()),
        scratch_shapes=[pltpu.SemaphoreType.DMA((6,))],
        cost_estimate=pl.CostEstimate(flops=0, bytes_accessed=4_000_000, transcendentals=0),
        compiler_params=pltpu.CompilerParams(vmem_limit_bytes=4 << 20),
        name="relay",
    )(kept, first, second)


def pack_kernel(n_row, wide_ref, *refs):
    parts, out_ref, stack, sem = refs[:n_row], refs[n_row], refs[n_row + 1], refs[n_row + 2]
    width = wide_ref.shape[0]
    count = out_ref.shape[0] - width
    row, col = lax.axis_index("prow"), lax.axis_index("pcol")
    total = stack.shape[0]

    @pl.when(col == 0)
    def _():
        copies = [
            pltpu.make_async_copy(parts[k].at[pl.ds(0, count), :], stack.at[pl.ds(k * count, count), :], sem.at[k])
            for k in range(n_row)
        ]
        for copy in copies:
            copy.start()
        for k in range(n_row):
            @pl.when(row == k)
            def _(k=k):
                pltpu.make_async_copy(
                    parts[k].at[pl.ds(count, count), :], out_ref.at[pl.ds(width, count), :], sem.at[n_row]
                ).start()
        if total > n_row * count:
            stack[n_row * count:, :] = jnp.zeros((total - n_row * count, width), jnp.float32)
        lanes = lax.broadcasted_iota(jnp.int32, (width, LANES), 1)
        choice = jnp.concatenate(
            [jnp.where(lanes + t * LANES == wide_ref[...], 1.0, 0.0) for t in range(total // LANES)], axis=1
        )
        for copy in copies:
            copy.wait()
        out_ref[:width, :] = select_dot(choice, thirds(stack[...]))
        pltpu.make_async_copy(
            parts[0].at[pl.ds(count, count), :], out_ref.at[pl.ds(width, count), :], sem.at[n_row]
        ).wait()

    @pl.when(col != 0)
    def _():
        out_ref[...] = jnp.zeros_like(out_ref)


def pack(wide, parts):
    n_row, width = len(parts), wide.shape[0]
    count = parts[0].shape[0] // 2
    return pl.pallas_call(
        functools.partial(pack_kernel, n_row),
        out_shape=jax.ShapeDtypeStruct((width + count, width), jnp.float32),
        in_specs=[vmem()] + [raw()] * n_row,
        out_specs=vmem(),
        scratch_shapes=[
            pltpu.VMEM((-(-n_row * count // LANES) * LANES, width), jnp.float32),
            pltpu.SemaphoreType.DMA((n_row + 1,)),
        ],
        cost_estimate=pl.CostEstimate(flops=0, bytes_accessed=4_000_000, transcendentals=0),
        compiler_params=pltpu.CompilerParams(vmem_limit_bytes=6 << 20),
        name="pack",
    )(wide, *parts)


def unpack_parcels(n_row, count, parcels):
    half = count // 2
    if n_row != 4:
        parts = [(x, part * half) for x in parcels for part in range(2)]
        return parts, [[(x, count + part * half) for part in range(2)] for x in parcels]
    kept, first, second, third, fourth = parcels
    parts = [
        (kept, 0), (kept, half), (first, 0), (fourth, 0), (third, 0), (second, 0), (third, half), (fourth, half)
    ]
    tops = [
        [(kept, 2 * half), (kept, 3 * half)],
        [(first, half), (fourth, 2 * half)],
        [(third, 2 * half), (second, half)],
        [(third, 2 * half), (fourth, 2 * half)],
    ]
    return parts, tops


def put_rows(slot_ref, held, rows_ref, target_ref):
    spare = target_ref.shape[0] - SUB

    def group(q, c):
        for u in range(SUB):
            i = q * SUB + u
            slot = jnp.where(i < held, slot_ref[i], spare)
            target_ref[pl.ds(slot, 1), :] = rows_ref[pl.ds(i, 1), :]
        return c

    lax.fori_loop(0, (held + SUB - 1) // SUB, group, 0)


def finish_kernel(
    n_row, mine_ref, counts_ref, wide_ref, mat_ref, panel_ref, panel_new_ref, square_ref, square_new_ref,
    packed_ref, linv_ref, uinv_ref, *refs,
):
    n_parcels = 5 if n_row == 4 else n_row
    parcels, refs = refs[:n_parcels], refs[n_parcels:]
    out_ref, block, pivot, panel, old, left, lower, top, sem, in_sem, out_sem = refs
    rows, _, cols = mat_ref.shape
    width = linv_ref.shape[0]
    count = mine_ref.shape[0]
    half = count // 2
    stacked = n_row * count
    parts, tops = unpack_parcels(n_row, count, parcels)
    tiles = cols // width
    row, col = lax.axis_index("prow"), lax.axis_index("pcol")

    def tile(t):
        return pl.ds(pl.multiple_of(t * width, width), width)

    @pl.when(col % 2 == 0)
    def _():
        pltpu.make_async_copy(panel_ref, panel.at[pl.ds(0, rows)], sem.at[0]).start()

    @pl.when(col % 2 == 1)
    def _():
        pltpu.make_async_copy(panel_new_ref, panel.at[pl.ds(0, rows)], sem.at[0]).start()

    top_copies = [
        pltpu.make_async_copy(ref.at[pl.ds(width, count), :], top.at[n], sem.at[1 + n])
        for n, ref in enumerate((square_ref, square_new_ref))
    ]
    for copy in top_copies:
        copy.start()

    def fetch(t, c):
        pltpu.make_async_copy(mat_ref.at[:, 0, tile(t)], block.at[pl.ds(0, rows), tile(t)], in_sem.at[0, t]).start()
        for n, (ref, base) in enumerate(parts):
            dest = pivot.at[pl.ds(n * half, half), tile(t)]
            pltpu.make_async_copy(ref.at[pl.ds(base, half), tile(t)], dest, in_sem.at[1, t]).start()
        for p in range(n_row):
            @pl.when(row == p)
            def _(p=p):
                for part, (ref, base) in enumerate(tops[p]):
                    dest = old.at[pl.ds(part * half, half), tile(t)]
                    pltpu.make_async_copy(ref.at[pl.ds(base, half), tile(t)], dest, in_sem.at[2, t]).start()
        return c

    lax.fori_loop(0, tiles, fetch, 0)
    if pivot.shape[0] > stacked:
        pivot[stacked:, :] = jnp.zeros((pivot.shape[0] - stacked, cols), jnp.float32)

    lanes = lax.broadcasted_iota(jnp.int32, (width, LANES), 1)
    places = jnp.concatenate(
        [jnp.where(lanes + t * LANES == wide_ref[...], 1.0, 0.0) for t in range(pivot.shape[0] // LANES)], axis=1
    )
    spread_inv = wide_left(pick_dot(thirds(linv_ref[...]), places))
    for copy in top_copies:
        copy.wait()
    top[0] = top[0] + top[1]
    pltpu.make_async_copy(panel_ref, panel.at[pl.ds(0, rows)], sem.at[0]).wait()
    put_rows(mine_ref, counts_ref[row], top.at[0], panel)
    lower[...] = wide_dot(wide_left(panel[:rows, :]), wide_right(uinv_ref[...]))
    left[...] = wide_left(lower[...])

    def step(t, c):
        first_col = (col == 0) & (t == 0)
        pltpu.make_async_copy(
            mat_ref.at[pl.ds(0, stacked), 0, tile(t)], pivot.at[pl.ds(0, stacked), tile(t)], in_sem.at[1, t]
        ).wait()
        upper = wide_dot(spread_inv, wide_right(pivot[:, tile(t)]))
        pltpu.make_async_copy(mat_ref.at[pl.ds(0, count), 0, tile(t)], old.at[:, tile(t)], in_sem.at[2, t]).wait()
        pltpu.make_async_copy(mat_ref.at[:, 0, tile(t)], block.at[pl.ds(0, rows), tile(t)], in_sem.at[0, t]).wait()

        @pl.when(jnp.logical_not(first_col))
        def _():
            put_rows(mine_ref, counts_ref[row], old.at[:, tile(t)], block.at[:, tile(t)])
            block[:rows, tile(t)] = block[:rows, tile(t)] - wide_dot(left[...], wide_right(upper))

        @pl.when(first_col)
        def _():
            block[:rows, tile(t)] = lower[...]

        @pl.when(row == 0)
        def _():
            block[:width, tile(t)] = jnp.where(first_col, packed_ref[...], upper)

        pltpu.make_async_copy(block.at[pl.ds(0, rows), tile(t)], out_ref.at[:, 0, tile(t)], out_sem.at[t]).start()
        return c

    lax.fori_loop(0, tiles, step, 0)

    def drain(t, c):
        pltpu.make_async_copy(block.at[pl.ds(0, rows), tile(t)], out_ref.at[:, 0, tile(t)], out_sem.at[t]).wait()
        return c

    lax.fori_loop(0, tiles, drain, 0)


def finish(mine, counts, wide, mat, panels, squares, factors, parcels):
    rows, _, cols = mat.shape
    width, n_row, count = factors[0].shape[0], counts.shape[0], mine.shape[0]
    return pl.pallas_call(
        functools.partial(finish_kernel, n_row),
        out_shape=jax.ShapeDtypeStruct(mat.shape, jnp.float32),
        in_specs=[smem(), smem(), vmem()] + [raw()] * 5 + [vmem()] * 3 + [raw()] * len(parcels),
        out_specs=raw(),
        scratch_shapes=[
            pltpu.VMEM((rows + SUB, cols), jnp.float32),
            pltpu.VMEM((-(-n_row * count // LANES) * LANES, cols), jnp.float32),
            pltpu.VMEM((rows + SUB, width), jnp.float32),
            pltpu.VMEM((count, cols), jnp.float32),
            pltpu.VMEM((rows, 3 * width), jnp.bfloat16),
            pltpu.VMEM((rows, width), jnp.float32),
            pltpu.VMEM((2, count, width), jnp.float32),
            pltpu.SemaphoreType.DMA((3,)),
            pltpu.SemaphoreType.DMA((3, cols // width)),
            pltpu.SemaphoreType.DMA((cols // width,)),
        ],
        cost_estimate=pl.CostEstimate(
            flops=6 * rows * cols * width, bytes_accessed=8 * rows * cols, transcendentals=0
        ),
        compiler_params=pltpu.CompilerParams(vmem_limit_bytes=26 << 20),
        name="finish",
    )(mine, counts, wide, mat, *panels, *squares, *factors, *parcels)


def capacity(n_row, width):
    mean = width / n_row
    return -(-int(mean + 4 * (mean * (1 - 1 / n_row)) ** 0.5) // (2 * SUB)) * (2 * SUB)


def locate(pivots, n_row, row, count):
    width = pivots.shape[0]
    owner = pivots // width % n_row
    slot = pivots // (width * n_row) * width + pivots % width
    number = jnp.arange(width, dtype=jnp.int32)
    ahead = (owner[:, None] == owner[None, :]) & (number[None, :] < number[:, None])
    rank = jnp.sum(ahead, axis=1, dtype=jnp.int32)
    every = jnp.arange(n_row, dtype=jnp.int32)[:, None]
    ordinal = jnp.arange(count, dtype=jnp.int32)[:, None]
    own = (owner[None, :] == row) & (rank[None, :] == ordinal)
    mine = jnp.sum(jnp.where(own, slot[None, :], 0), axis=1, dtype=jnp.int32)
    return mine, jnp.sum(owner[None, :] == every, axis=1, dtype=jnp.int32)


def capped_step(n_row, n_col, matrix, pivots, begun):
    _, rows, _, cols = matrix.shape
    mat = matrix.reshape(rows, 1, cols)
    panel, wide, _, *messages = begun
    count = messages[0].shape[0] // 2
    row, col = lax.axis_index("prow"), lax.axis_index("pcol")
    both = ("prow", "pcol")
    turns = bits_of(n_col)[:0:-1]

    def exchange(x, k):
        return lax.ppermute(x, both, [(i * n_col, (i ^ k) * n_col) for i in range(n_row)])

    moved = [exchange(messages[k], k) for k in range(1, n_row)]
    mine, counts = locate(pivots, n_row, row, count)
    parcels = parcel(mat, mine, pivots, n_row)

    def send(x, k):
        return lax.ppermute(x, "prow", [(i, i ^ k) for i in range(n_row)])

    *moved, kept = lax.optimization_barrier((*moved, parcels[-1]))
    parcels = parcels[:-1] + (kept,)
    message = pack(wide, messages[:1] + moved)
    panel_moved = lax.ppermute(panel, "pcol", [(i, i + turns[0]) for i in range(0, n_col, 2 * turns[0])])
    message, panel_moved = lax.optimization_barrier((message, panel_moved))
    if n_row == 4:
        first, second = send(parcels[0], 1), send(parcels[1], 2)
        kept = parcels[2]
        to_y, to_x = relay(kept, first, second)
        arrived = [kept, first, second]
    else:
        arrived = [parcels[0]] + [send(parcels[k], k) for k in range(1, n_row)]

    pairs = [[(i, i + bit) for i in range(0, n_col, 2 * bit)] for bit in turns + [1]]
    newer = [(col & bit) != 0 for bit in turns]
    for n in range(len(turns)):
        panel = jnp.where(newer[n], panel_moved, panel)
        panel_moved = lax.ppermute(panel, "pcol", pairs[n + 1])
        message = jnp.where(newer[n], lax.ppermute(message, "pcol", pairs[n]), message)
        if n + 1 < len(turns):
            message, panel_moved = lax.optimization_barrier((message, panel_moved))
    if n_row == 4:
        message, to_y, to_x = lax.optimization_barrier((message, to_y, to_x))
        arrived += [send(to_y, 2), send(to_x, 1)]
    message_new = lax.ppermute(message, "pcol", pairs[-1])
    factors = factor(message, message_new, True)
    out = finish(
        mine, counts, wide, mat, (panel, panel_moved), (message, message_new), factors, arrived
    )
    return out.reshape(matrix.shape)


def on_device(n_row, n_col, matrix, pivots):
    _, rows, _, cols = matrix.shape
    begun = begin(matrix.reshape(rows, 1, cols), pivots, n_row, capacity(n_row, pivots.shape[0]))
    return lax.cond(
        begun[2][0] > 0,
        lambda m, p, b: capped_step(n_row, n_col, m, p, b),
        lambda m, p, b: dense_step(n_row, n_col, m, p),
        matrix, pivots, begun,
    )


def solution(mesh):
    spec = P("prow", None, "pcol", None)
    n_row, n_col = mesh.shape["prow"], mesh.shape["pcol"]
    return jax.shard_map(
        functools.partial(on_device, n_row, n_col), mesh=mesh, in_specs=(spec, P()), out_specs=spec, check_vma=False
    )
```

```python
import functools

import jax
import jax.numpy as jnp
from jax import lax
from jax.experimental import pallas as pl
from jax.experimental.pallas import tpu as pltpu
from jax.sharding import PartitionSpec as P

LANES = 128
SUB = 8
HI = lax.Precision.HIGHEST


def pick_lane(tile, lane):
    return jnp.take_along_axis(tile, jnp.full((SUB, LANES), lane, jnp.int32), axis=1)


def row_of(tile, j):
    return jnp.broadcast_to(tile[j:j + 1, :], (SUB, LANES))


def factor_kernel(width, unroll, first_ref, second_ref, packed_ref, linv_ref, uinv_ref, a_ref, m_ref, v_ref, s_ref, sem):
    groups = a_ref.shape[0]
    tiles = groups * SUB // LANES
    per_tile = LANES // SUB
    per_block = width // SUB
    copies = [
        pltpu.make_async_copy(ref.at[pl.ds(0, groups * SUB), :], s_ref.at[n], sem.at[n])
        for n, ref in enumerate((first_ref, second_ref))
    ]
    for copy in copies:
        copy.start()
    sub = lax.broadcasted_iota(jnp.int32, (SUB, LANES), 0)
    lane = lax.broadcasted_iota(jnp.int32, (SUB, LANES), 1)

    for i in range(groups):
        diag = lane - (i % per_tile) * SUB == sub
        for t in range(tiles):
            block = jnp.where(diag, 1.0, 0.0) if i // per_tile == t else jnp.zeros((SUB, LANES), jnp.float32)
            m_ref[i, :, t * LANES:(t + 1) * LANES] = block
            if t > i // per_tile:
                linv_ref[i * SUB:(i + 1) * SUB, t * LANES:(t + 1) * LANES] = block

    for copy in copies:
        copy.wait()
    for i in range(groups):
        a_ref[i] = s_ref[0, i * SUB:(i + 1) * SUB, :] + s_ref[1, i * SUB:(i + 1) * SUB, :]

    def span(t):
        return slice(t * LANES, (t + 1) * LANES)

    for o in range(groups // per_block):
        base = o * per_block
        h = base // per_tile
        live = [(a_ref, t) for t in range(h + 1, tiles)] + [(m_ref, t) for t in range(h + 1)]

        def panel(i, c, base=base, h=h, live=live):
            b = base + i
            g = (b - h * per_tile) * SUB
            rows = pl.ds(pl.multiple_of(b * SUB, SUB), SUB)
            own = a_ref[b, :, span(h)]
            cols = [pick_lane(own, g + j) for j in range(SUB)]
            in_panel = (lane >= g) & (lane < g + SUB)
            after = lane >= g + SUB
            head = jnp.where(in_panel, jnp.where(lane - g == sub, -1.0, 0.0), jnp.where(after, own, 0.0))
            rest = [ref[b, :, span(t)] for ref, t in live]
            packed = own
            final = [head] + rest
            for j in range(SUB):
                at = sub == j
                coef = cols[j]
                r = 1.0 / row_of(coef, j)
                final = [jnp.where(at, x, y) for x, y in zip([head] + rest, final)]
                packed = jnp.where((lane == g + j) & (sub > j), coef * r, packed)
                for k in range(j, SUB):
                    packed = jnp.where((lane == g + k) & at, cols[k], packed)
                head_coef = jnp.where((sub < j) | after, coef, 0.0)
                v = row_of(head, j) * r
                head = jnp.where(at, v, head - head_coef * v)
                for n, x in enumerate(rest):
                    v = row_of(x, j) * r
                    rest[n] = jnp.where(at, v, x - coef * v)
                for k in range(j + 1, SUB):
                    v = row_of(cols[k], j) * r
                    cols[k] = jnp.where(at, v, cols[k] - coef * v)
            for t in range(h):
                packed_ref[rows, span(t)] = a_ref[b, :, span(t)]
            packed_ref[rows, span(h)] = jnp.where(after, final[0], packed)
            for (ref, t), x in zip(live, final[1:]):
                (packed_ref if ref is a_ref else linv_ref)[rows, span(t)] = x
            a_ref[b, :, span(h)] = head
            v_ref[0] = head
            for n, ((ref, t), x) in enumerate(zip(live, rest)):
                ref[b, :, span(t)] = x
                v_ref[n + 1] = x
            others = [base + lax.rem(i + s, per_block) for s in range(1, per_block)]
            heads = [a_ref[r, :, span(h)] for r in others]
            facs = [[pick_lane(x, g + j) for j in range(SUB)] for x in heads]
            for n, (ref, t) in enumerate([(a_ref, h)] + live):
                old = [jnp.where(in_panel, 0.0, x) for x in heads] if n == 0 else [ref[r, :, span(t)] for r in others]
                vs = [row_of([head] + rest and ([head] + rest)[n], j) for j in range(SUB)]
                for x, fac, r in zip(old, facs, others):
                    acc = [fac[j] * vs[j] for j in range(SUB)]
                    while len(acc) > 1:
                        acc = [p + q for p, q in zip(acc[::2], acc[1::2])]
                    ref[r, :, span(t)] = x - acc[0]
            return c

        lax.fori_loop(0, per_block, panel, 0, unroll=unroll)

        lo = (base % per_tile) * SUB
        pad = [jnp.zeros((n, LANES), jnp.float32) for n in (lo, LANES - lo - width)]

        def stack(x):
            return jnp.concatenate([p for p in (pad[0], x, pad[1]) if p.shape[0]], axis=0)

        def flat(ref, first, last, t):
            return ref[first:last, :, span(t)].reshape((last - first) * SUB, LANES)

        end = base + per_block
        right = [stack(flat(ref, base, end, t)) for ref, t in [(a_ref, h)] + live]
        for first, last in ((end, groups), (0, base)):
            if first == last:
                continue
            left = flat(a_ref, first, last, h)
            column = lax.broadcasted_iota(jnp.int32, left.shape, 1)
            for n, (ref, t) in enumerate([(a_ref, h)] + live):
                if ref is m_ref and first == 0:
                    continue
                old = left if n else None
                old = jnp.where((column >= lo) & (column < lo + width), 0.0, left) if n == 0 else flat(ref, first, last, t)
                new = old - jnp.dot(left, right[n], precision=HI, preferred_element_type=jnp.float32)
                ref[first:last, :, span(t)] = new.reshape(last - first, SUB, LANES)

    ri = lax.broadcasted_iota(jnp.int32, (SUB, LANES), 0)
    for i in range(groups):
        for t in range(tiles):
            x = a_ref[i, :, span(t)]
            keep = lane + t * LANES >= ri + i * SUB
            uinv_ref[i * SUB:(i + 1) * SUB, span(t)] = jnp.where(keep, -x, 0.0)


def vmem():
    return pl.BlockSpec(memory_space=pltpu.VMEM)


def smem():
    return pl.BlockSpec(memory_space=pltpu.SMEM)


def factor(square, extra, unroll, width=32):
    size = square.shape[1]
    out = jax.ShapeDtypeStruct((size, size), jnp.float32)
    return pl.pallas_call(
        functools.partial(factor_kernel, width, unroll),
        out_shape=(out, out, out),
        in_specs=[raw(), raw()],
        out_specs=(vmem(),) * 3,
        scratch_shapes=[
            pltpu.VMEM((size // SUB, SUB, size), jnp.float32),
            pltpu.VMEM((size // SUB, SUB, size), jnp.float32),
            pltpu.VMEM((1 + size // LANES, SUB, LANES), jnp.float32),
            pltpu.VMEM((2, size, size), jnp.float32),
            pltpu.SemaphoreType.DMA((2,)),
        ],
        cost_estimate=pl.CostEstimate(flops=4 * size**3, bytes_accessed=50_000_000, transcendentals=0),
        compiler_params=pltpu.CompilerParams(vmem_limit_bytes=10 << 20),
        name="factor",
    )(square, extra)


def pick_kernel(slot_ref, own_ref, block_ref, out_ref):
    def group(q, c):
        for u in range(SUB):
            j = q * SUB + u
            row = block_ref[pl.ds(slot_ref[j], 1), :]
            out_ref[pl.ds(j, 1), :] = row * own_ref[j].astype(jnp.float32)
        return c

    lax.fori_loop(0, out_ref.shape[0] // SUB, group, 0)


def pick(block, slots, owned, tiles):
    rows, width = block.shape[0], slots.shape[0]
    return pl.pallas_call(
        pick_kernel,
        grid=(tiles,),
        out_shape=jax.ShapeDtypeStruct((width, tiles * width), jnp.float32),
        in_specs=[smem(), smem(), pl.BlockSpec((rows, width), lambda t: (0, t))],
        out_specs=pl.BlockSpec((width, width), lambda t: (0, t)),
        cost_estimate=pl.CostEstimate(
            flops=width * width * tiles, bytes_accessed=4 * (rows + width) * width * tiles, transcendentals=0
        ),
        name="pick",
    )(slots, owned, block)


def place_rows(slot_ref, rows_ref, target_ref):
    def group(q, c):
        for u in range(SUB):
            j = q * SUB + u
            target_ref[pl.ds(slot_ref[j], 1), :] = rows_ref[pl.ds(j, 1), :]
        return c

    lax.fori_loop(0, rows_ref.shape[0] // SUB, group, 0)


def place_kernel(slot_ref, block_ref, rows_ref, out_ref, buf_ref):
    rows = block_ref.shape[0]
    buf_ref[:rows, :] = block_ref[...]
    place_rows(slot_ref, rows_ref, buf_ref)
    out_ref[...] = buf_ref[:rows, :]


def place(block, rows, slots):
    height, width = block.shape[0], slots.shape[0]
    return pl.pallas_call(
        place_kernel,
        grid=(1,),
        out_shape=jax.ShapeDtypeStruct((height, width), jnp.float32),
        in_specs=[
            smem(),
            pl.BlockSpec((height, width), lambda t: (0, 0)),
            pl.BlockSpec((width, width), lambda t: (0, 0)),
        ],
        out_specs=pl.BlockSpec((height, width), lambda t: (0, 0)),
        scratch_shapes=[pltpu.VMEM((height + SUB, width), jnp.float32)],
        cost_estimate=pl.CostEstimate(flops=0, bytes_accessed=8 * height * width, transcendentals=0),
        name="place",
    )(slots, block, rows)


def halves(x):
    high = x.astype(jnp.bfloat16)
    low = (x - high.astype(jnp.float32)).astype(jnp.bfloat16)
    return high, low


def wide_left(x):
    high, low = halves(x)
    return jnp.concatenate([high, low, high], axis=1)


def wide_right(x):
    high, low = halves(x)
    return jnp.concatenate([low, high, high], axis=0)


def wide_dot(left, right):
    return jnp.dot(left, right, preferred_element_type=jnp.float32)


def split_dot(left, right):
    acc = jnp.dot(left[0], right[1], preferred_element_type=jnp.float32)
    acc += jnp.dot(left[1], right[0], preferred_element_type=jnp.float32)
    return acc + jnp.dot(left[0], right[0], preferred_element_type=jnp.float32)


def update_kernel(
    slot_ref, where_ref, block_ref, panel_ref, pivot_ref, top_ref, packed_ref, linv_ref, uinv_ref,
    out_ref, high_ref, low_ref, buf_ref,
):
    rows, width = panel_ref.shape
    t = pl.program_id(0)
    first_row = where_ref[0] == 0
    first_col = (where_ref[1] == 0) & (t == 0)

    @pl.when(t == 0)
    def _():
        lower = jnp.dot(panel_ref[...], uinv_ref[...], precision=HI, preferred_element_type=jnp.float32)
        high_ref[...], low_ref[...] = halves(lower)
        out_ref[...] = lower

    upper = jnp.dot(linv_ref[...], pivot_ref[...], precision=HI, preferred_element_type=jnp.float32)

    @pl.when(jnp.logical_not(first_col))
    def _():
        buf_ref[:rows, :] = block_ref[...]
        place_rows(slot_ref, top_ref, buf_ref)
        out_ref[...] = buf_ref[:rows, :] - split_dot((high_ref[...], low_ref[...]), halves(upper))

    @pl.when(first_row)
    def _():
        out_ref[:width, :] = jnp.where(first_col, packed_ref[...], upper)


def update(block, panel, pivot_rows, old_top, packed, linv, uinv, slots, where):
    rows, cols = block.shape
    width = slots.shape[0]
    square = pl.BlockSpec((width, width), lambda t: (0, 0))
    tall = pl.BlockSpec((rows, width), lambda t: (0, t))
    flat = pl.BlockSpec((width, width), lambda t: (0, t))
    return pl.pallas_call(
        update_kernel,
        grid=(cols // width,),
        out_shape=jax.ShapeDtypeStruct((rows, cols), jnp.float32),
        in_specs=[
            smem(), smem(), tall, pl.BlockSpec((rows, width), lambda t: (0, 0)), flat, flat, square, square, square,
        ],
        out_specs=tall,
        scratch_shapes=[
            pltpu.VMEM((rows, width), jnp.bfloat16),
            pltpu.VMEM((rows, width), jnp.bfloat16),
            pltpu.VMEM((rows + SUB, width), jnp.float32),
        ],
        cost_estimate=pl.CostEstimate(
            flops=6 * rows * cols * width, bytes_accessed=8 * rows * cols, transcendentals=0
        ),
        name="update",
    )(slots, where, block, panel, pivot_rows, old_top, packed, linv, uinv)


def bits_of(n):
    return [1 << i for i in range(n.bit_length() - 1)]


def sum_over_rows(x, order, n_row):
    for bit in order:
        x = x + lax.ppermute(x, "prow", [(i, i ^ bit) for i in range(n_row)])
    return x


def spread_rows(x, order, n_row):
    have = [0]
    for bit in order:
        x = x + lax.ppermute(x, "prow", [(i, i ^ bit) for i in have])
        have = have + [i ^ bit for i in have]
    return x


def spread_cols(x, order):
    have = [0]
    for bit in order:
        x = x + lax.ppermute(x, "pcol", [(i, i ^ bit) for i in have])
        have = have + [i ^ bit for i in have]
    return x


def dense_step(n_row, n_col, matrix, pivots):
    block = matrix[0, :, 0, :]
    rows, cols = block.shape
    width = pivots.shape[0]
    row = lax.axis_index("prow")
    col = lax.axis_index("pcol")
    owner = pivots // width % n_row
    slot = pivots // (width * n_row) * width + pivots % width
    mine = owner == row
    owned = mine.astype(jnp.int32)
    target = jnp.where(mine, slot, rows)
    where = jnp.stack([row, col]).astype(jnp.int32)
    row_bits, col_bits = bits_of(n_row), bits_of(n_col)
    at_first_row = row == 0
    at_first_col = col == 0

    square = pick(block, slot, owned * at_first_col.astype(jnp.int32), 1)
    square = sum_over_rows(square, row_bits, n_row)
    square = spread_cols(square, col_bits[::-1])
    packed, linv, uinv = factor(square, jnp.zeros_like(square), False)

    top = jnp.where(at_first_row, block[:width], 0.0)
    top_panel = spread_rows(top[:, :width], row_bits, n_row)
    panel = place(block, top_panel, target)
    panel = spread_cols(jnp.where(at_first_col, panel, 0.0), col_bits[::-1])

    picked = pick(block, slot, owned, cols // width)
    half = width // 2
    pivot_rows = jnp.concatenate([
        sum_over_rows(picked[:half], row_bits, n_row),
        sum_over_rows(picked[half:], row_bits[::-1], n_row),
    ])
    old_top = jnp.concatenate([
        spread_rows(top[:half], row_bits, n_row),
        spread_rows(top[half:], row_bits[::-1], n_row),
    ])
    result = update(block, panel, pivot_rows, old_top, packed, linv, uinv, target, where)
    return result[None, :, None, :]


def raw():
    return pl.BlockSpec(memory_space=pl.ANY)


def thirds(x):
    high = x.astype(jnp.bfloat16)
    rest = x - high.astype(jnp.float32)
    middle = rest.astype(jnp.bfloat16)
    return high, middle, (rest - middle.astype(jnp.float32)).astype(jnp.bfloat16)


def select_dot(choice, parts):
    choice = choice.astype(jnp.bfloat16)
    high, middle, low = [jnp.dot(choice, x, preferred_element_type=jnp.float32) for x in parts]
    return high + (middle + low)


def pick_dot(parts, choice):
    choice = choice.astype(jnp.bfloat16)
    high, middle, low = [jnp.dot(x, choice, preferred_element_type=jnp.float32) for x in parts]
    return high + (middle + low)


def begin_kernel(n_row, pivot_ref, mat_ref, panel_ref, wide_ref, fits_ref, *refs):
    messages, sem = refs[:n_row], refs[-1]
    rows, width = panel_ref.shape
    count = messages[0].shape[0] // 2
    width_log, row_log = width.bit_length() - 1, n_row.bit_length() - 1
    row = lax.axis_index("prow")
    copy = pltpu.make_async_copy(mat_ref.at[:, 0, pl.ds(0, width)], panel_ref, sem)
    copy.start()
    pivot = pivot_ref[...]
    block = lax.shift_right_logical(pivot, width_log)
    owner = block & (n_row - 1)
    slot = lax.shift_left(lax.shift_right_logical(block, row_log), width_log) + (pivot & (width - 1))
    _, rank = owners(pivot, n_row)
    fits_ref[0] = (jnp.max(rank) < count).astype(jnp.int32)
    place = ((owner ^ row) * count + rank).astype(jnp.float32)
    eye = lax.broadcasted_iota(jnp.int32, (width, width), 0) == lax.broadcasted_iota(jnp.int32, (width, width), 1)
    spread = jnp.where(eye, place, 0.0)
    wide = jnp.dot(spread, jnp.ones((width, LANES), jnp.float32), precision=HI, preferred_element_type=jnp.float32)
    wide_ref[...] = wide.astype(jnp.int32)
    ordinal = lax.broadcasted_iota(jnp.int32, (count, width), 0)
    mine = jnp.where((ordinal == rank) & (owner == row), 1.0, 0.0).astype(jnp.bfloat16)
    at_slot = jnp.where(lax.broadcasted_iota(jnp.int32, (rows, width), 0) == slot, 1.0, 0.0).astype(jnp.bfloat16)
    choice = lax.dot_general(mine, at_slot, (((1,), (1,)), ((), ())), preferred_element_type=jnp.float32)
    copy.wait()
    own = select_dot(choice, thirds(panel_ref[...]))
    for k in range(n_row):
        messages[k][:count, :] = own

    @pl.when(row == 0)
    def _():
        top = thirds(panel_ref[:width, :])
        for p in range(n_row):
            messages[p][count:, :] = select_dot(jnp.where((ordinal == rank) & (owner == p), 1.0, 0.0), top)


def begin(mat, pivots, n_row, count):
    rows, width = mat.shape[0], pivots.shape[0]
    message = jax.ShapeDtypeStruct((2 * count, width), jnp.float32)
    return pl.pallas_call(
        functools.partial(begin_kernel, n_row),
        out_shape=(
            jax.ShapeDtypeStruct((rows, width), jnp.float32),
            jax.ShapeDtypeStruct((width, LANES), jnp.int32),
            jax.ShapeDtypeStruct((1,), jnp.int32),
        ) + (message,) * n_row,
        in_specs=[vmem(), raw()],
        out_specs=(vmem(), vmem(), smem()) + (vmem(),) * n_row,
        scratch_shapes=[pltpu.SemaphoreType.DMA],
        cost_estimate=pl.CostEstimate(flops=0, bytes_accessed=10_000_000, transcendentals=0),
        compiler_params=pltpu.CompilerParams(vmem_limit_bytes=12 << 20),
        name="begin",
    )(pivots[None, :], mat)


def parcel_kernel(n_row, mine_ref, pivot_ref, mat_ref, *refs):
    outs, own, block, sem = refs[:-3], refs[-3], refs[-2], refs[-1]
    count, cols = own.shape
    half = count // 2
    width = pivot_ref.shape[1]

    def group(q, c):
        for u in range(SUB):
            i = q * SUB + u
            pltpu.make_async_copy(mat_ref.at[mine_ref[i]], own.at[pl.ds(i, 1), :], sem.at[0]).start()
        return c

    @pl.when(lax.axis_index("prow") == 0)
    def _():
        pltpu.make_async_copy(mat_ref.at[pl.ds(0, width), 0, :], block, sem.at[1]).start()

    lax.fori_loop(0, count // SUB, group, 0)

    @pl.when(lax.axis_index("prow") == 0)
    def _():
        copy = pltpu.make_async_copy(mat_ref.at[pl.ds(0, width), 0, :], block, sem.at[1])
        owner, rank = owners(pivot_ref[...], n_row)
        ordinal = lax.broadcasted_iota(jnp.int32, (count, width), 0)
        choices = [jnp.where((ordinal == rank) & (owner == p), 1.0, 0.0) for p in range(n_row)]
        choice = jnp.concatenate(choices, axis=0)
        copy.wait()

        def piece(t, c):
            at = pl.ds(pl.multiple_of(t * width, width), width)
            tops = select_dot(choice, thirds(block[:, at]))
            for p in range(n_row):
                for part in range(2):
                    first = p * count + part * half
                    for ref, base in top_places(n_row, half, outs, p, part):
                        ref[pl.ds(base, half), at] = tops[first:first + half]
            return c

        lax.fori_loop(0, cols // width, piece, 0, unroll=True)

    pltpu.make_async_copy(mat_ref.at[pl.ds(0, count), 0, :], own, sem.at[0]).wait()
    if n_row == 4:
        outs[0][:half, :] = own[:half, :]
        outs[1][:half, :] = own[half:, :]
        outs[2][:count, :] = own[...]
    else:
        outs[0][:count, :] = own[...]
        for p in range(1, n_row):
            outs[p][:count, :] = own[...]


def top_places(n_row, half, outs, p, part):
    if n_row != 4:
        return [(outs[p], 2 * half + part * half)]
    if p == 0:
        return [(outs[2], 2 * half + part * half)]
    if p == 3:
        return [(outs[part], 2 * half)]
    if part == p - 1:
        return [(outs[part], half)]
    return [(outs[2], (4 + part) * half)]


def owners(pivot, n_row):
    width = pivot.shape[1]
    owner = lax.shift_right_logical(pivot, width.bit_length() - 1) & (n_row - 1)
    held = lax.broadcasted_iota(jnp.int32, (-(-n_row // 16) * 16, width), 0) == owner
    before = lax.broadcasted_iota(jnp.int32, (width, width), 0) < lax.broadcasted_iota(jnp.int32, (width, width), 1)
    held = jnp.where(held, 1.0, 0.0)
    earlier = jnp.dot(
        held.astype(jnp.bfloat16), jnp.where(before, 1.0, 0.0).astype(jnp.bfloat16), preferred_element_type=jnp.float32
    )
    return owner, jnp.sum(held * earlier, axis=0, keepdims=True).astype(jnp.int32)


def parcel(mat, mine, pivots, n_row):
    count, width, cols = mine.shape[0], pivots.shape[0], mat.shape[2]
    half = count // 2
    sizes = [3 * half, 3 * half, 6 * half] if n_row == 4 else [2 * count] * n_row
    return pl.pallas_call(
        functools.partial(parcel_kernel, n_row),
        out_shape=tuple(jax.ShapeDtypeStruct((size, cols), jnp.float32) for size in sizes),
        in_specs=[smem(), vmem(), raw()],
        out_specs=(vmem(),) * len(sizes),
        scratch_shapes=[
            pltpu.VMEM((count, cols), jnp.float32),
            pltpu.VMEM((width, cols), jnp.float32),
            pltpu.SemaphoreType.DMA((2,)),
        ],
        cost_estimate=pl.CostEstimate(flops=0, bytes_accessed=16_000_000, transcendentals=0),
        compiler_params=pltpu.CompilerParams(vmem_limit_bytes=16 << 20),
        name="parcel",
    )(mine, pivots[None, :], mat)


def relay_kernel(kept_ref, first_ref, second_ref, y_ref, x_ref, sem):
    half = first_ref.shape[0] // 3
    row = lax.axis_index("prow")

    def move(source, base, dest, at, n):
        return pltpu.make_async_copy(source.at[pl.ds(base, half), :], dest.at[pl.ds(at, half), :], sem.at[n])

    copies = [
        move(kept_ref, 0, y_ref, 0, 0),
        move(kept_ref, half, x_ref, 0, 1),
        move(first_ref, 0, y_ref, half, 2),
        move(second_ref, 0, x_ref, half, 3),
    ]
    for copy in copies:
        copy.start()

    @pl.when(row == 0)
    def _():
        move(kept_ref, 4 * half, y_ref, 2 * half, 4).start()
        move(kept_ref, 5 * half, x_ref, 2 * half, 5).start()

    @pl.when(row != 0)
    def _():
        move(first_ref, 2 * half, y_ref, 2 * half, 4).start()
        move(second_ref, 2 * half, x_ref, 2 * half, 5).start()

    for copy in copies:
        copy.wait()
    move(first_ref, 2 * half, y_ref, 2 * half, 4).wait()
    move(second_ref, 2 * half, x_ref, 2 * half, 5).wait()


def relay(kept, first, second):
    shape = jax.ShapeDtypeStruct(first.shape, jnp.float32)
    return pl.pallas_call(
        relay_kernel,
        out_shape=(shape, shape),
        in_specs=[raw()] * 3,
        out_specs=(vmem(), vmem()),
        scratch_shapes=[pltpu.SemaphoreType.DMA((6,))],
        cost_estimate=pl.CostEstimate(flops=0, bytes_accessed=4_000_000, transcendentals=0),
        compiler_params=pltpu.CompilerParams(vmem_limit_bytes=4 << 20),
        name="relay",
    )(kept, first, second)


def pack_kernel(n_row, wide_ref, *refs):
    parts, out_ref, stack, sem = refs[:n_row], refs[n_row], refs[n_row + 1], refs[n_row + 2]
    width = wide_ref.shape[0]
    count = out_ref.shape[0] - width
    row, col = lax.axis_index("prow"), lax.axis_index("pcol")
    total = stack.shape[0]

    @pl.when(col == 0)
    def _():
        copies = [
            pltpu.make_async_copy(parts[k].at[pl.ds(0, count), :], stack.at[pl.ds(k * count, count), :], sem.at[k])
            for k in range(n_row)
        ]
        for copy in copies:
            copy.start()
        for k in range(n_row):
            @pl.when(row == k)
            def _(k=k):
                pltpu.make_async_copy(
                    parts[k].at[pl.ds(count, count), :], out_ref.at[pl.ds(width, count), :], sem.at[n_row]
                ).start()
        if total > n_row * count:
            stack[n_row * count:, :] = jnp.zeros((total - n_row * count, width), jnp.float32)
        lanes = lax.broadcasted_iota(jnp.int32, (width, LANES), 1)
        choice = jnp.concatenate(
            [jnp.where(lanes + t * LANES == wide_ref[...], 1.0, 0.0) for t in range(total // LANES)], axis=1
        )
        for copy in copies:
            copy.wait()
        out_ref[:width, :] = select_dot(choice, thirds(stack[...]))
        pltpu.make_async_copy(
            parts[0].at[pl.ds(count, count), :], out_ref.at[pl.ds(width, count), :], sem.at[n_row]
        ).wait()

    @pl.when(col != 0)
    def _():
        out_ref[...] = jnp.zeros_like(out_ref)


def pack(wide, parts):
    n_row, width = len(parts), wide.shape[0]
    count = parts[0].shape[0] // 2
    return pl.pallas_call(
        functools.partial(pack_kernel, n_row),
        out_shape=jax.ShapeDtypeStruct((width + count, width), jnp.float32),
        in_specs=[vmem()] + [raw()] * n_row,
        out_specs=vmem(),
        scratch_shapes=[
            pltpu.VMEM((-(-n_row * count // LANES) * LANES, width), jnp.float32),
            pltpu.SemaphoreType.DMA((n_row + 1,)),
        ],
        cost_estimate=pl.CostEstimate(flops=0, bytes_accessed=4_000_000, transcendentals=0),
        compiler_params=pltpu.CompilerParams(vmem_limit_bytes=6 << 20),
        name="pack",
    )(wide, *parts)


def unpack_parcels(n_row, count, parcels):
    half = count // 2
    if n_row != 4:
        parts = [(x, part * half) for x in parcels for part in range(2)]
        return parts, [[(x, count + part * half) for part in range(2)] for x in parcels]
    kept, first, second, third, fourth = parcels
    parts = [
        (kept, 0), (kept, half), (first, 0), (fourth, 0), (third, 0), (second, 0), (third, half), (fourth, half)
    ]
    tops = [
        [(kept, 2 * half), (kept, 3 * half)],
        [(first, half), (fourth, 2 * half)],
        [(third, 2 * half), (second, half)],
        [(third, 2 * half), (fourth, 2 * half)],
    ]
    return parts, tops


def put_rows(slot_ref, held, rows_ref, target_ref):
    spare = target_ref.shape[0] - SUB

    def group(q, c):
        for u in range(SUB):
            i = q * SUB + u
            slot = jnp.where(i < held, slot_ref[i], spare)
            target_ref[pl.ds(slot, 1), :] = rows_ref[pl.ds(i, 1), :]
        return c

    lax.fori_loop(0, (held + SUB - 1) // SUB, group, 0)


def finish_kernel(
    n_row, mine_ref, counts_ref, wide_ref, mat_ref, panel_ref, panel_new_ref, square_ref, square_new_ref,
    packed_ref, linv_ref, uinv_ref, *refs,
):
    n_parcels = 5 if n_row == 4 else n_row
    parcels, refs = refs[:n_parcels], refs[n_parcels:]
    out_ref, block, pivot, panel, old, left, lower, top, sem, in_sem, out_sem = refs
    rows, _, cols = mat_ref.shape
    width = linv_ref.shape[0]
    count = mine_ref.shape[0]
    half = count // 2
    stacked = n_row * count
    parts, tops = unpack_parcels(n_row, count, parcels)
    tiles = cols // width
    row, col = lax.axis_index("prow"), lax.axis_index("pcol")

    def tile(t):
        return pl.ds(pl.multiple_of(t * width, width), width)

    @pl.when(col % 2 == 0)
    def _():
        pltpu.make_async_copy(panel_ref, panel.at[pl.ds(0, rows)], sem.at[0]).start()

    @pl.when(col % 2 == 1)
    def _():
        pltpu.make_async_copy(panel_new_ref, panel.at[pl.ds(0, rows)], sem.at[0]).start()

    top_copies = [
        pltpu.make_async_copy(ref.at[pl.ds(width, count), :], top.at[n], sem.at[1 + n])
        for n, ref in enumerate((square_ref, square_new_ref))
    ]
    for copy in top_copies:
        copy.start()

    def fetch(t, c):
        pltpu.make_async_copy(mat_ref.at[:, 0, tile(t)], block.at[pl.ds(0, rows), tile(t)], in_sem.at[0, t]).start()
        for n, (ref, base) in enumerate(parts):
            dest = pivot.at[pl.ds(n * half, half), tile(t)]
            pltpu.make_async_copy(ref.at[pl.ds(base, half), tile(t)], dest, in_sem.at[1, t]).start()
        for p in range(n_row):
            @pl.when(row == p)
            def _(p=p):
                for part, (ref, base) in enumerate(tops[p]):
                    dest = old.at[pl.ds(part * half, half), tile(t)]
                    pltpu.make_async_copy(ref.at[pl.ds(base, half), tile(t)], dest, in_sem.at[2, t]).start()
        return c

    lax.fori_loop(0, tiles, fetch, 0)
    if pivot.shape[0] > stacked:
        pivot[stacked:, :] = jnp.zeros((pivot.shape[0] - stacked, cols), jnp.float32)

    lanes = lax.broadcasted_iota(jnp.int32, (width, LANES), 1)
    places = jnp.concatenate(
        [jnp.where(lanes + t * LANES == wide_ref[...], 1.0, 0.0) for t in range(pivot.shape[0] // LANES)], axis=1
    )
    spread_inv = wide_left(pick_dot(thirds(linv_ref[...]), places))
    for copy in top_copies:
        copy.wait()
    top[0] = top[0] + top[1]
    pltpu.make_async_copy(panel_ref, panel.at[pl.ds(0, rows)], sem.at[0]).wait()
    put_rows(mine_ref, counts_ref[row], top.at[0], panel)
    lower[...] = wide_dot(wide_left(panel[:rows, :]), wide_right(uinv_ref[...]))
    left[...] = wide_left(lower[...])

    def step(t, c):
        first_col = (col == 0) & (t == 0)
        pltpu.make_async_copy(
            mat_ref.at[pl.ds(0, stacked), 0, tile(t)], pivot.at[pl.ds(0, stacked), tile(t)], in_sem.at[1, t]
        ).wait()
        upper = wide_dot(spread_inv, wide_right(pivot[:, tile(t)]))
        pltpu.make_async_copy(mat_ref.at[pl.ds(0, count), 0, tile(t)], old.at[:, tile(t)], in_sem.at[2, t]).wait()
        pltpu.make_async_copy(mat_ref.at[:, 0, tile(t)], block.at[pl.ds(0, rows), tile(t)], in_sem.at[0, t]).wait()

        @pl.when(jnp.logical_not(first_col))
        def _():
            put_rows(mine_ref, counts_ref[row], old.at[:, tile(t)], block.at[:, tile(t)])
            block[:rows, tile(t)] = block[:rows, tile(t)] - wide_dot(left[...], wide_right(upper))

        @pl.when(first_col)
        def _():
            block[:rows, tile(t)] = lower[...]

        @pl.when(row == 0)
        def _():
            block[:width, tile(t)] = jnp.where(first_col, packed_ref[...], upper)

        pltpu.make_async_copy(block.at[pl.ds(0, rows), tile(t)], out_ref.at[:, 0, tile(t)], out_sem.at[t]).start()
        return c

    lax.fori_loop(0, tiles, step, 0)

    def drain(t, c):
        pltpu.make_async_copy(block.at[pl.ds(0, rows), tile(t)], out_ref.at[:, 0, tile(t)], out_sem.at[t]).wait()
        return c

    lax.fori_loop(0, tiles, drain, 0)


def finish(mine, counts, wide, mat, panels, squares, factors, parcels):
    rows, _, cols = mat.shape
    width, n_row, count = factors[0].shape[0], counts.shape[0], mine.shape[0]
    return pl.pallas_call(
        functools.partial(finish_kernel, n_row),
        out_shape=jax.ShapeDtypeStruct(mat.shape, jnp.float32),
        in_specs=[smem(), smem(), vmem()] + [raw()] * 5 + [vmem()] * 3 + [raw()] * len(parcels),
        out_specs=raw(),
        scratch_shapes=[
            pltpu.VMEM((rows + SUB, cols), jnp.float32),
            pltpu.VMEM((-(-n_row * count // LANES) * LANES, cols), jnp.float32),
            pltpu.VMEM((rows + SUB, width), jnp.float32),
            pltpu.VMEM((count, cols), jnp.float32),
            pltpu.VMEM((rows, 3 * width), jnp.bfloat16),
            pltpu.VMEM((rows, width), jnp.float32),
            pltpu.VMEM((2, count, width), jnp.float32),
            pltpu.SemaphoreType.DMA((3,)),
            pltpu.SemaphoreType.DMA((3, cols // width)),
            pltpu.SemaphoreType.DMA((cols // width,)),
        ],
        cost_estimate=pl.CostEstimate(
            flops=6 * rows * cols * width, bytes_accessed=8 * rows * cols, transcendentals=0
        ),
        compiler_params=pltpu.CompilerParams(vmem_limit_bytes=26 << 20),
        name="finish",
    )(mine, counts, wide, mat, *panels, *squares, *factors, *parcels)


def capacity(n_row, width):
    mean = width / n_row
    return -(-int(mean + 4 * (mean * (1 - 1 / n_row)) ** 0.5) // (2 * SUB)) * (2 * SUB)


def locate(pivots, n_row, row, count):
    width = pivots.shape[0]
    owner = pivots // width % n_row
    slot = pivots // (width * n_row) * width + pivots % width
    number = jnp.arange(width, dtype=jnp.int32)
    ahead = (owner[:, None] == owner[None, :]) & (number[None, :] < number[:, None])
    rank = jnp.sum(ahead, axis=1, dtype=jnp.int32)
    every = jnp.arange(n_row, dtype=jnp.int32)[:, None]
    ordinal = jnp.arange(count, dtype=jnp.int32)[:, None]
    own = (owner[None, :] == row) & (rank[None, :] == ordinal)
    mine = jnp.sum(jnp.where(own, slot[None, :], 0), axis=1, dtype=jnp.int32)
    return mine, jnp.sum(owner[None, :] == every, axis=1, dtype=jnp.int32)


def capped_step(n_row, n_col, matrix, pivots, begun):
    _, rows, _, cols = matrix.shape
    mat = matrix.reshape(rows, 1, cols)
    panel, wide, _, *messages = begun
    count = messages[0].shape[0] // 2
    row, col = lax.axis_index("prow"), lax.axis_index("pcol")
    both = ("prow", "pcol")
    turns = bits_of(n_col)[:0:-1]

    def exchange(x, k):
        return lax.ppermute(x, both, [(i * n_col, (i ^ k) * n_col) for i in range(n_row)])

    moved = [exchange(messages[k], k) for k in range(1, n_row)]
    mine, counts = locate(pivots, n_row, row, count)
    parcels = parcel(mat, mine, pivots, n_row)

    def send(x, k):
        return lax.ppermute(x, "prow", [(i, i ^ k) for i in range(n_row)])

    *moved, kept = lax.optimization_barrier((*moved, parcels[-1]))
    parcels = parcels[:-1] + (kept,)
    message = pack(wide, messages[:1] + moved)
    panel_moved = lax.ppermute(panel, "pcol", [(i, i + turns[0]) for i in range(0, n_col, 2 * turns[0])])
    message, panel_moved = lax.optimization_barrier((message, panel_moved))
    if n_row == 4:
        first, second = send(parcels[0], 1), send(parcels[1], 2)
        kept = parcels[2]
        to_y, to_x = relay(kept, first, second)
        arrived = [kept, first, second]
    else:
        arrived = [parcels[0]] + [send(parcels[k], k) for k in range(1, n_row)]

    pairs = [[(i, i + bit) for i in range(0, n_col, 2 * bit)] for bit in turns + [1]]
    newer = [(col & bit) != 0 for bit in turns]
    last = len(turns) - 1
    for n in range(len(turns)):
        arrived_now = panel_moved
        if n == last:
            arrived_now = jnp.where(col == turns[n], back, panel_moved)
        source = panel_moved if last == 1 else None
        panel = jnp.where(newer[n], arrived_now, panel)
        if n + 1 == last:
            source = panel if source is None else source
            panel_moved = lax.ppermute(source, "pcol", pairs[n + 1][1:])
            back = lax.ppermute(source, "pcol", [(turns[n], turns[n + 1])])
        else:
            panel_moved = lax.ppermute(panel, "pcol", pairs[n + 1])
        message = jnp.where(newer[n], lax.ppermute(message, "pcol", pairs[n]), message)
        if n + 1 == last:
            message, panel_moved, back = lax.optimization_barrier((message, panel_moved, back))
        elif n < last:
            message, panel_moved = lax.optimization_barrier((message, panel_moved))
    if n_row == 4:
        message, to_y, to_x = lax.optimization_barrier((message, to_y, to_x))
        arrived += [send(to_y, 2), send(to_x, 1)]
    message_new = lax.ppermute(message, "pcol", pairs[-1])
    factors = factor(message, message_new, True)
    out = finish(
        mine, counts, wide, pltpu.with_memory_space_constraint(mat, pltpu.HBM), (panel, panel_moved), (message, message_new), factors, arrived
    )
    return out.reshape(matrix.shape)


def on_device(n_row, n_col, matrix, pivots):
    _, rows, _, cols = matrix.shape
    begun = begin(matrix.reshape(rows, 1, cols), pivots, n_row, capacity(n_row, pivots.shape[0]))
    return lax.cond(
        begun[2][0] > 0,
        lambda m, p, b: capped_step(n_row, n_col, m, p, b),
        lambda m, p, b: dense_step(n_row, n_col, m, p),
        matrix, pivots, begun,
    )


def solution(mesh):
    spec = P("prow", None, "pcol", None)
    n_row, n_col = mesh.shape["prow"], mesh.shape["pcol"]
    return jax.shard_map(
        functools.partial(on_device, n_row, n_col), mesh=mesh, in_specs=(spec, P()), out_specs=spec, check_vma=False
    )
```

```python
import functools

import jax
import jax.numpy as jnp
from jax import lax
from jax.experimental import pallas as pl
from jax.experimental.pallas import tpu as pltpu
from jax.sharding import PartitionSpec as P

LANES = 128
SUB = 8
HI = lax.Precision.HIGHEST


def pick_lane(tile, lane):
    return jnp.take_along_axis(tile, jnp.full((SUB, LANES), lane, jnp.int32), axis=1)


def row_of(tile, j):
    return jnp.broadcast_to(tile[j:j + 1, :], (SUB, LANES))


def factor_kernel(width, unroll, first_ref, second_ref, packed_ref, linv_ref, uinv_ref, a_ref, m_ref, v_ref, s_ref, sem):
    groups = a_ref.shape[0]
    tiles = groups * SUB // LANES
    per_tile = LANES // SUB
    per_block = width // SUB
    copies = [
        pltpu.make_async_copy(ref.at[pl.ds(0, groups * SUB), :], s_ref.at[n], sem.at[n])
        for n, ref in enumerate((first_ref, second_ref))
    ]
    for copy in copies:
        copy.start()
    sub = lax.broadcasted_iota(jnp.int32, (SUB, LANES), 0)
    lane = lax.broadcasted_iota(jnp.int32, (SUB, LANES), 1)

    for i in range(groups):
        diag = lane - (i % per_tile) * SUB == sub
        for t in range(tiles):
            block = jnp.where(diag, 1.0, 0.0) if i // per_tile == t else jnp.zeros((SUB, LANES), jnp.float32)
            m_ref[i, :, t * LANES:(t + 1) * LANES] = block
            if t > i // per_tile:
                linv_ref[i * SUB:(i + 1) * SUB, t * LANES:(t + 1) * LANES] = block

    for copy in copies:
        copy.wait()
    for i in range(groups):
        a_ref[i] = s_ref[0, i * SUB:(i + 1) * SUB, :] + s_ref[1, i * SUB:(i + 1) * SUB, :]

    def span(t):
        return slice(t * LANES, (t + 1) * LANES)

    for o in range(groups // per_block):
        base = o * per_block
        h = base // per_tile
        live = [(a_ref, t) for t in range(h + 1, tiles)] + [(m_ref, t) for t in range(h + 1)]

        def panel(i, c, base=base, h=h, live=live):
            b = base + i
            g = (b - h * per_tile) * SUB
            rows = pl.ds(pl.multiple_of(b * SUB, SUB), SUB)
            own = a_ref[b, :, span(h)]
            cols = [pick_lane(own, g + j) for j in range(SUB)]
            in_panel = (lane >= g) & (lane < g + SUB)
            after = lane >= g + SUB
            head = jnp.where(in_panel, jnp.where(lane - g == sub, -1.0, 0.0), jnp.where(after, own, 0.0))
            rest = [ref[b, :, span(t)] for ref, t in live]
            packed = own
            final = [head] + rest
            for j in range(SUB):
                at = sub == j
                coef = cols[j]
                r = 1.0 / row_of(coef, j)
                final = [jnp.where(at, x, y) for x, y in zip([head] + rest, final)]
                packed = jnp.where((lane == g + j) & (sub > j), coef * r, packed)
                for k in range(j, SUB):
                    packed = jnp.where((lane == g + k) & at, cols[k], packed)
                head_coef = jnp.where((sub < j) | after, coef, 0.0)
                v = row_of(head, j) * r
                head = jnp.where(at, v, head - head_coef * v)
                for n, x in enumerate(rest):
                    v = row_of(x, j) * r
                    rest[n] = jnp.where(at, v, x - coef * v)
                for k in range(j + 1, SUB):
                    v = row_of(cols[k], j) * r
                    cols[k] = jnp.where(at, v, cols[k] - coef * v)
            for t in range(h):
                packed_ref[rows, span(t)] = a_ref[b, :, span(t)]
            packed_ref[rows, span(h)] = jnp.where(after, final[0], packed)
            for (ref, t), x in zip(live, final[1:]):
                (packed_ref if ref is a_ref else linv_ref)[rows, span(t)] = x
            a_ref[b, :, span(h)] = head
            v_ref[0] = head
            for n, ((ref, t), x) in enumerate(zip(live, rest)):
                ref[b, :, span(t)] = x
                v_ref[n + 1] = x
            others = [base + lax.rem(i + s, per_block) for s in range(1, per_block)]
            heads = [a_ref[r, :, span(h)] for r in others]
            facs = [[pick_lane(x, g + j) for j in range(SUB)] for x in heads]
            for n, (ref, t) in enumerate([(a_ref, h)] + live):
                old = [jnp.where(in_panel, 0.0, x) for x in heads] if n == 0 else [ref[r, :, span(t)] for r in others]
                vs = [row_of([head] + rest and ([head] + rest)[n], j) for j in range(SUB)]
                for x, fac, r in zip(old, facs, others):
                    acc = [fac[j] * vs[j] for j in range(SUB)]
                    while len(acc) > 1:
                        acc = [p + q for p, q in zip(acc[::2], acc[1::2])]
                    ref[r, :, span(t)] = x - acc[0]
            return c

        lax.fori_loop(0, per_block, panel, 0, unroll=unroll)

        lo = (base % per_tile) * SUB
        pad = [jnp.zeros((n, LANES), jnp.float32) for n in (lo, LANES - lo - width)]

        def stack(x):
            return jnp.concatenate([p for p in (pad[0], x, pad[1]) if p.shape[0]], axis=0)

        def flat(ref, first, last, t):
            return ref[first:last, :, span(t)].reshape((last - first) * SUB, LANES)

        end = base + per_block
        right = [stack(flat(ref, base, end, t)) for ref, t in [(a_ref, h)] + live]
        for first, last in ((end, groups), (0, base)):
            if first == last:
                continue
            left = flat(a_ref, first, last, h)
            column = lax.broadcasted_iota(jnp.int32, left.shape, 1)
            for n, (ref, t) in enumerate([(a_ref, h)] + live):
                if ref is m_ref and first == 0:
                    continue
                old = left if n else None
                old = jnp.where((column >= lo) & (column < lo + width), 0.0, left) if n == 0 else flat(ref, first, last, t)
                new = old - jnp.dot(left, right[n], precision=HI, preferred_element_type=jnp.float32)
                ref[first:last, :, span(t)] = new.reshape(last - first, SUB, LANES)

    ri = lax.broadcasted_iota(jnp.int32, (SUB, LANES), 0)
    for i in range(groups):
        for t in range(tiles):
            x = a_ref[i, :, span(t)]
            keep = lane + t * LANES >= ri + i * SUB
            uinv_ref[i * SUB:(i + 1) * SUB, span(t)] = jnp.where(keep, -x, 0.0)


def vmem():
    return pl.BlockSpec(memory_space=pltpu.VMEM)


def smem():
    return pl.BlockSpec(memory_space=pltpu.SMEM)


def factor(square, extra, unroll, width=32):
    size = square.shape[1]
    out = jax.ShapeDtypeStruct((size, size), jnp.float32)
    return pl.pallas_call(
        functools.partial(factor_kernel, width, unroll),
        out_shape=(out, out, out),
        in_specs=[raw(), raw()],
        out_specs=(vmem(),) * 3,
        scratch_shapes=[
            pltpu.VMEM((size // SUB, SUB, size), jnp.float32),
            pltpu.VMEM((size // SUB, SUB, size), jnp.float32),
            pltpu.VMEM((1 + size // LANES, SUB, LANES), jnp.float32),
            pltpu.VMEM((2, size, size), jnp.float32),
            pltpu.SemaphoreType.DMA((2,)),
        ],
        cost_estimate=pl.CostEstimate(flops=4 * size**3, bytes_accessed=50_000_000, transcendentals=0),
        compiler_params=pltpu.CompilerParams(vmem_limit_bytes=10 << 20),
        name="factor",
    )(square, extra)


def pick_kernel(slot_ref, own_ref, block_ref, out_ref):
    def group(q, c):
        for u in range(SUB):
            j = q * SUB + u
            row = block_ref[pl.ds(slot_ref[j], 1), :]
            out_ref[pl.ds(j, 1), :] = row * own_ref[j].astype(jnp.float32)
        return c

    lax.fori_loop(0, out_ref.shape[0] // SUB, group, 0)


def pick(block, slots, owned, tiles):
    rows, width = block.shape[0], slots.shape[0]
    return pl.pallas_call(
        pick_kernel,
        grid=(tiles,),
        out_shape=jax.ShapeDtypeStruct((width, tiles * width), jnp.float32),
        in_specs=[smem(), smem(), pl.BlockSpec((rows, width), lambda t: (0, t))],
        out_specs=pl.BlockSpec((width, width), lambda t: (0, t)),
        cost_estimate=pl.CostEstimate(
            flops=width * width * tiles, bytes_accessed=4 * (rows + width) * width * tiles, transcendentals=0
        ),
        name="pick",
    )(slots, owned, block)


def place_rows(slot_ref, rows_ref, target_ref):
    def group(q, c):
        for u in range(SUB):
            j = q * SUB + u
            target_ref[pl.ds(slot_ref[j], 1), :] = rows_ref[pl.ds(j, 1), :]
        return c

    lax.fori_loop(0, rows_ref.shape[0] // SUB, group, 0)


def place_kernel(slot_ref, block_ref, rows_ref, out_ref, buf_ref):
    rows = block_ref.shape[0]
    buf_ref[:rows, :] = block_ref[...]
    place_rows(slot_ref, rows_ref, buf_ref)
    out_ref[...] = buf_ref[:rows, :]


def place(block, rows, slots):
    height, width = block.shape[0], slots.shape[0]
    return pl.pallas_call(
        place_kernel,
        grid=(1,),
        out_shape=jax.ShapeDtypeStruct((height, width), jnp.float32),
        in_specs=[
            smem(),
            pl.BlockSpec((height, width), lambda t: (0, 0)),
            pl.BlockSpec((width, width), lambda t: (0, 0)),
        ],
        out_specs=pl.BlockSpec((height, width), lambda t: (0, 0)),
        scratch_shapes=[pltpu.VMEM((height + SUB, width), jnp.float32)],
        cost_estimate=pl.CostEstimate(flops=0, bytes_accessed=8 * height * width, transcendentals=0),
        name="place",
    )(slots, block, rows)


def halves(x):
    high = x.astype(jnp.bfloat16)
    low = (x - high.astype(jnp.float32)).astype(jnp.bfloat16)
    return high, low


def wide_left(x):
    high, low = halves(x)
    return jnp.concatenate([high, low, high], axis=1)


def wide_right(x):
    high, low = halves(x)
    return jnp.concatenate([low, high, high], axis=0)


def wide_dot(left, right):
    return jnp.dot(left, right, preferred_element_type=jnp.float32)


def split_dot(left, right):
    acc = jnp.dot(left[0], right[1], preferred_element_type=jnp.float32)
    acc += jnp.dot(left[1], right[0], preferred_element_type=jnp.float32)
    return acc + jnp.dot(left[0], right[0], preferred_element_type=jnp.float32)


def update_kernel(
    slot_ref, where_ref, block_ref, panel_ref, pivot_ref, top_ref, packed_ref, linv_ref, uinv_ref,
    out_ref, high_ref, low_ref, buf_ref,
):
    rows, width = panel_ref.shape
    t = pl.program_id(0)
    first_row = where_ref[0] == 0
    first_col = (where_ref[1] == 0) & (t == 0)

    @pl.when(t == 0)
    def _():
        lower = jnp.dot(panel_ref[...], uinv_ref[...], precision=HI, preferred_element_type=jnp.float32)
        high_ref[...], low_ref[...] = halves(lower)
        out_ref[...] = lower

    upper = jnp.dot(linv_ref[...], pivot_ref[...], precision=HI, preferred_element_type=jnp.float32)

    @pl.when(jnp.logical_not(first_col))
    def _():
        buf_ref[:rows, :] = block_ref[...]
        place_rows(slot_ref, top_ref, buf_ref)
        out_ref[...] = buf_ref[:rows, :] - split_dot((high_ref[...], low_ref[...]), halves(upper))

    @pl.when(first_row)
    def _():
        out_ref[:width, :] = jnp.where(first_col, packed_ref[...], upper)


def update(block, panel, pivot_rows, old_top, packed, linv, uinv, slots, where):
    rows, cols = block.shape
    width = slots.shape[0]
    square = pl.BlockSpec((width, width), lambda t: (0, 0))
    tall = pl.BlockSpec((rows, width), lambda t: (0, t))
    flat = pl.BlockSpec((width, width), lambda t: (0, t))
    return pl.pallas_call(
        update_kernel,
        grid=(cols // width,),
        out_shape=jax.ShapeDtypeStruct((rows, cols), jnp.float32),
        in_specs=[
            smem(), smem(), tall, pl.BlockSpec((rows, width), lambda t: (0, 0)), flat, flat, square, square, square,
        ],
        out_specs=tall,
        scratch_shapes=[
            pltpu.VMEM((rows, width), jnp.bfloat16),
            pltpu.VMEM((rows, width), jnp.bfloat16),
            pltpu.VMEM((rows + SUB, width), jnp.float32),
        ],
        cost_estimate=pl.CostEstimate(
            flops=6 * rows * cols * width, bytes_accessed=8 * rows * cols, transcendentals=0
        ),
        name="update",
    )(slots, where, block, panel, pivot_rows, old_top, packed, linv, uinv)


def bits_of(n):
    return [1 << i for i in range(n.bit_length() - 1)]


def sum_over_rows(x, order, n_row):
    for bit in order:
        x = x + lax.ppermute(x, "prow", [(i, i ^ bit) for i in range(n_row)])
    return x


def spread_rows(x, order, n_row):
    have = [0]
    for bit in order:
        x = x + lax.ppermute(x, "prow", [(i, i ^ bit) for i in have])
        have = have + [i ^ bit for i in have]
    return x


def spread_cols(x, order):
    have = [0]
    for bit in order:
        x = x + lax.ppermute(x, "pcol", [(i, i ^ bit) for i in have])
        have = have + [i ^ bit for i in have]
    return x


def dense_step(n_row, n_col, matrix, pivots):
    block = matrix[0, :, 0, :]
    rows, cols = block.shape
    width = pivots.shape[0]
    row = lax.axis_index("prow")
    col = lax.axis_index("pcol")
    owner = pivots // width % n_row
    slot = pivots // (width * n_row) * width + pivots % width
    mine = owner == row
    owned = mine.astype(jnp.int32)
    target = jnp.where(mine, slot, rows)
    where = jnp.stack([row, col]).astype(jnp.int32)
    row_bits, col_bits = bits_of(n_row), bits_of(n_col)
    at_first_row = row == 0
    at_first_col = col == 0

    square = pick(block, slot, owned * at_first_col.astype(jnp.int32), 1)
    square = sum_over_rows(square, row_bits, n_row)
    square = spread_cols(square, col_bits[::-1])
    packed, linv, uinv = factor(square, jnp.zeros_like(square), False)

    top = jnp.where(at_first_row, block[:width], 0.0)
    top_panel = spread_rows(top[:, :width], row_bits, n_row)
    panel = place(block, top_panel, target)
    panel = spread_cols(jnp.where(at_first_col, panel, 0.0), col_bits[::-1])

    picked = pick(block, slot, owned, cols // width)
    half = width // 2
    pivot_rows = jnp.concatenate([
        sum_over_rows(picked[:half], row_bits, n_row),
        sum_over_rows(picked[half:], row_bits[::-1], n_row),
    ])
    old_top = jnp.concatenate([
        spread_rows(top[:half], row_bits, n_row),
        spread_rows(top[half:], row_bits[::-1], n_row),
    ])
    result = update(block, panel, pivot_rows, old_top, packed, linv, uinv, target, where)
    return result[None, :, None, :]


def raw():
    return pl.BlockSpec(memory_space=pl.ANY)


def thirds(x):
    high = x.astype(jnp.bfloat16)
    rest = x - high.astype(jnp.float32)
    middle = rest.astype(jnp.bfloat16)
    return high, middle, (rest - middle.astype(jnp.float32)).astype(jnp.bfloat16)


def select_dot(choice, parts):
    choice = choice.astype(jnp.bfloat16)
    high, middle, low = [jnp.dot(choice, x, preferred_element_type=jnp.float32) for x in parts]
    return high + (middle + low)


def pick_dot(parts, choice):
    choice = choice.astype(jnp.bfloat16)
    high, middle, low = [jnp.dot(x, choice, preferred_element_type=jnp.float32) for x in parts]
    return high + (middle + low)


def begin_kernel(n_row, pivot_ref, mat_ref, panel_ref, wide_ref, fits_ref, *refs):
    messages, sem = refs[:n_row], refs[-1]
    rows, width = panel_ref.shape
    count = messages[0].shape[0] // 2
    width_log, row_log = width.bit_length() - 1, n_row.bit_length() - 1
    row = lax.axis_index("prow")
    copy = pltpu.make_async_copy(mat_ref.at[:, 0, pl.ds(0, width)], panel_ref, sem)
    copy.start()
    pivot = pivot_ref[...]
    block = lax.shift_right_logical(pivot, width_log)
    owner = block & (n_row - 1)
    slot = lax.shift_left(lax.shift_right_logical(block, row_log), width_log) + (pivot & (width - 1))
    _, rank = owners(pivot, n_row)
    fits_ref[0] = (jnp.max(rank) < count).astype(jnp.int32)
    place = ((owner ^ row) * count + rank).astype(jnp.float32)
    eye = lax.broadcasted_iota(jnp.int32, (width, width), 0) == lax.broadcasted_iota(jnp.int32, (width, width), 1)
    spread = jnp.where(eye, place, 0.0)
    wide = jnp.dot(spread, jnp.ones((width, LANES), jnp.float32), precision=HI, preferred_element_type=jnp.float32)
    wide_ref[...] = wide.astype(jnp.int32)
    ordinal = lax.broadcasted_iota(jnp.int32, (count, width), 0)
    mine = jnp.where((ordinal == rank) & (owner == row), 1.0, 0.0).astype(jnp.bfloat16)
    at_slot = jnp.where(lax.broadcasted_iota(jnp.int32, (rows, width), 0) == slot, 1.0, 0.0).astype(jnp.bfloat16)
    choice = lax.dot_general(mine, at_slot, (((1,), (1,)), ((), ())), preferred_element_type=jnp.float32)
    copy.wait()
    own = select_dot(choice, thirds(panel_ref[...]))
    for k in range(n_row):
        messages[k][:count, :] = own

    @pl.when(row == 0)
    def _():
        top = thirds(panel_ref[:width, :])
        for p in range(n_row):
            messages[p][count:, :] = select_dot(jnp.where((ordinal == rank) & (owner == p), 1.0, 0.0), top)


def begin(mat, pivots, n_row, count):
    rows, width = mat.shape[0], pivots.shape[0]
    message = jax.ShapeDtypeStruct((2 * count, width), jnp.float32)
    return pl.pallas_call(
        functools.partial(begin_kernel, n_row),
        out_shape=(
            jax.ShapeDtypeStruct((rows, width), jnp.float32),
            jax.ShapeDtypeStruct((width, LANES), jnp.int32),
            jax.ShapeDtypeStruct((1,), jnp.int32),
        ) + (message,) * n_row,
        in_specs=[vmem(), raw()],
        out_specs=(vmem(), vmem(), smem()) + (vmem(),) * n_row,
        scratch_shapes=[pltpu.SemaphoreType.DMA],
        cost_estimate=pl.CostEstimate(flops=0, bytes_accessed=10_000_000, transcendentals=0),
        compiler_params=pltpu.CompilerParams(vmem_limit_bytes=12 << 20),
        name="begin",
    )(pivots[None, :], mat)


def parcel_kernel(n_row, mine_ref, pivot_ref, mat_ref, *refs):
    outs, own, block, sem = refs[:-3], refs[-3], refs[-2], refs[-1]
    count, cols = own.shape
    half = count // 2
    width = pivot_ref.shape[1]

    def group(q, c):
        for u in range(SUB):
            i = q * SUB + u
            pltpu.make_async_copy(mat_ref.at[mine_ref[i]], own.at[pl.ds(i, 1), :], sem.at[0]).start()
        return c

    @pl.when(lax.axis_index("prow") == 0)
    def _():
        pltpu.make_async_copy(mat_ref.at[pl.ds(0, width), 0, :], block, sem.at[1]).start()

    lax.fori_loop(0, count // SUB, group, 0)

    @pl.when(lax.axis_index("prow") == 0)
    def _():
        copy = pltpu.make_async_copy(mat_ref.at[pl.ds(0, width), 0, :], block, sem.at[1])
        owner, rank = owners(pivot_ref[...], n_row)
        ordinal = lax.broadcasted_iota(jnp.int32, (count, width), 0)
        choices = [jnp.where((ordinal == rank) & (owner == p), 1.0, 0.0) for p in range(n_row)]
        choice = jnp.concatenate(choices, axis=0)
        copy.wait()

        def piece(t, c):
            at = pl.ds(pl.multiple_of(t * width, width), width)
            tops = select_dot(choice, thirds(block[:, at]))
            for p in range(n_row):
                for part in range(2):
                    first = p * count + part * half
                    for ref, base in top_places(n_row, half, outs, p, part):
                        ref[pl.ds(base, half), at] = tops[first:first + half]
            return c

        lax.fori_loop(0, cols // width, piece, 0, unroll=True)

    pltpu.make_async_copy(mat_ref.at[pl.ds(0, count), 0, :], own, sem.at[0]).wait()
    if n_row == 4:
        outs[0][:half, :] = own[:half, :]
        outs[1][:half, :] = own[half:, :]
        outs[2][:count, :] = own[...]
    else:
        outs[0][:count, :] = own[...]
        for p in range(1, n_row):
            outs[p][:count, :] = own[...]


def top_places(n_row, half, outs, p, part):
    if n_row != 4:
        return [(outs[p], 2 * half + part * half)]
    if p == 0:
        return [(outs[2], 2 * half + part * half)]
    if p == 3:
        return [(outs[part], 2 * half)]
    if part == p - 1:
        return [(outs[part], half)]
    return [(outs[2], (4 + part) * half)]


def owners(pivot, n_row):
    width = pivot.shape[1]
    owner = lax.shift_right_logical(pivot, width.bit_length() - 1) & (n_row - 1)
    held = lax.broadcasted_iota(jnp.int32, (-(-n_row // 16) * 16, width), 0) == owner
    before = lax.broadcasted_iota(jnp.int32, (width, width), 0) < lax.broadcasted_iota(jnp.int32, (width, width), 1)
    held = jnp.where(held, 1.0, 0.0)
    earlier = jnp.dot(
        held.astype(jnp.bfloat16), jnp.where(before, 1.0, 0.0).astype(jnp.bfloat16), preferred_element_type=jnp.float32
    )
    return owner, jnp.sum(held * earlier, axis=0, keepdims=True).astype(jnp.int32)


def parcel(mat, mine, pivots, n_row):
    count, width, cols = mine.shape[0], pivots.shape[0], mat.shape[2]
    half = count // 2
    sizes = [3 * half, 3 * half, 6 * half] if n_row == 4 else [2 * count] * n_row
    return pl.pallas_call(
        functools.partial(parcel_kernel, n_row),
        out_shape=tuple(jax.ShapeDtypeStruct((size, cols), jnp.float32) for size in sizes),
        in_specs=[smem(), vmem(), raw()],
        out_specs=(vmem(),) * len(sizes),
        scratch_shapes=[
            pltpu.VMEM((count, cols), jnp.float32),
            pltpu.VMEM((width, cols), jnp.float32),
            pltpu.SemaphoreType.DMA((2,)),
        ],
        cost_estimate=pl.CostEstimate(flops=0, bytes_accessed=16_000_000, transcendentals=0),
        compiler_params=pltpu.CompilerParams(vmem_limit_bytes=16 << 20),
        name="parcel",
    )(mine, pivots[None, :], mat)


def relay_kernel(kept_ref, first_ref, second_ref, y_ref, x_ref, sem):
    half = first_ref.shape[0] // 3
    row = lax.axis_index("prow")

    def move(source, base, dest, at, n):
        return pltpu.make_async_copy(source.at[pl.ds(base, half), :], dest.at[pl.ds(at, half), :], sem.at[n])

    copies = [
        move(kept_ref, 0, y_ref, 0, 0),
        move(kept_ref, half, x_ref, 0, 1),
        move(first_ref, 0, y_ref, half, 2),
        move(second_ref, 0, x_ref, half, 3),
    ]
    for copy in copies:
        copy.start()

    @pl.when(row == 0)
    def _():
        move(kept_ref, 4 * half, y_ref, 2 * half, 4).start()
        move(kept_ref, 5 * half, x_ref, 2 * half, 5).start()

    @pl.when(row != 0)
    def _():
        move(first_ref, 2 * half, y_ref, 2 * half, 4).start()
        move(second_ref, 2 * half, x_ref, 2 * half, 5).start()

    for copy in copies:
        copy.wait()
    move(first_ref, 2 * half, y_ref, 2 * half, 4).wait()
    move(second_ref, 2 * half, x_ref, 2 * half, 5).wait()


def relay(kept, first, second):
    shape = jax.ShapeDtypeStruct(first.shape, jnp.float32)
    return pl.pallas_call(
        relay_kernel,
        out_shape=(shape, shape),
        in_specs=[raw()] * 3,
        out_specs=(vmem(), vmem()),
        scratch_shapes=[pltpu.SemaphoreType.DMA((6,))],
        cost_estimate=pl.CostEstimate(flops=0, bytes_accessed=4_000_000, transcendentals=0),
        compiler_params=pltpu.CompilerParams(vmem_limit_bytes=4 << 20),
        name="relay",
    )(kept, first, second)


def pack_kernel(n_row, wide_ref, *refs):
    parts, out_ref, stack, sem = refs[:n_row], refs[n_row], refs[n_row + 1], refs[n_row + 2]
    width = wide_ref.shape[0]
    count = out_ref.shape[0] - width
    row, col = lax.axis_index("prow"), lax.axis_index("pcol")
    total = stack.shape[0]

    @pl.when(col == 0)
    def _():
        copies = [
            pltpu.make_async_copy(parts[k].at[pl.ds(0, count), :], stack.at[pl.ds(k * count, count), :], sem.at[k])
            for k in range(n_row)
        ]
        for copy in copies:
            copy.start()
        for k in range(n_row):
            @pl.when(row == k)
            def _(k=k):
                pltpu.make_async_copy(
                    parts[k].at[pl.ds(count, count), :], out_ref.at[pl.ds(width, count), :], sem.at[n_row]
                ).start()
        if total > n_row * count:
            stack[n_row * count:, :] = jnp.zeros((total - n_row * count, width), jnp.float32)
        lanes = lax.broadcasted_iota(jnp.int32, (width, LANES), 1)
        choice = jnp.concatenate(
            [jnp.where(lanes + t * LANES == wide_ref[...], 1.0, 0.0) for t in range(total // LANES)], axis=1
        )
        for copy in copies:
            copy.wait()
        out_ref[:width, :] = select_dot(choice, thirds(stack[...]))
        pltpu.make_async_copy(
            parts[0].at[pl.ds(count, count), :], out_ref.at[pl.ds(width, count), :], sem.at[n_row]
        ).wait()

    @pl.when(col != 0)
    def _():
        out_ref[...] = jnp.zeros_like(out_ref)


def pack(wide, parts):
    n_row, width = len(parts), wide.shape[0]
    count = parts[0].shape[0] // 2
    return pl.pallas_call(
        functools.partial(pack_kernel, n_row),
        out_shape=jax.ShapeDtypeStruct((width + count, width), jnp.float32),
        in_specs=[vmem()] + [raw()] * n_row,
        out_specs=vmem(),
        scratch_shapes=[
            pltpu.VMEM((-(-n_row * count // LANES) * LANES, width), jnp.float32),
            pltpu.SemaphoreType.DMA((n_row + 1,)),
        ],
        cost_estimate=pl.CostEstimate(flops=0, bytes_accessed=4_000_000, transcendentals=0),
        compiler_params=pltpu.CompilerParams(vmem_limit_bytes=6 << 20),
        name="pack",
    )(wide, *parts)


def unpack_parcels(n_row, count, parcels):
    half = count // 2
    if n_row != 4:
        parts = [(x, part * half) for x in parcels for part in range(2)]
        return parts, [[(x, count + part * half) for part in range(2)] for x in parcels]
    kept, first, second, third, fourth = parcels
    parts = [
        (kept, 0), (kept, half), (first, 0), (fourth, 0), (third, 0), (second, 0), (third, half), (fourth, half)
    ]
    tops = [
        [(kept, 2 * half), (kept, 3 * half)],
        [(first, half), (fourth, 2 * half)],
        [(third, 2 * half), (second, half)],
        [(third, 2 * half), (fourth, 2 * half)],
    ]
    return parts, tops


def put_rows(slot_ref, held, rows_ref, target_ref):
    spare = target_ref.shape[0] - SUB

    def group(q, c):
        for u in range(SUB):
            i = q * SUB + u
            slot = jnp.where(i < held, slot_ref[i], spare)
            target_ref[pl.ds(slot, 1), :] = rows_ref[pl.ds(i, 1), :]
        return c

    lax.fori_loop(0, (held + SUB - 1) // SUB, group, 0)


def finish_kernel(
    n_row, mine_ref, counts_ref, wide_ref, mat_ref, panel_ref, panel_new_ref, square_ref, square_new_ref,
    packed_ref, linv_ref, uinv_ref, *refs,
):
    n_parcels = 5 if n_row == 4 else n_row
    parcels, refs = refs[:n_parcels], refs[n_parcels:]
    out_ref, block, pivot, panel, old, left, lower, top, sem, in_sem, out_sem = refs
    rows, _, cols = mat_ref.shape
    width = linv_ref.shape[0]
    count = mine_ref.shape[0]
    half = count // 2
    stacked = n_row * count
    parts, tops = unpack_parcels(n_row, count, parcels)
    tiles = cols // width
    row, col = lax.axis_index("prow"), lax.axis_index("pcol")

    def tile(t):
        return pl.ds(pl.multiple_of(t * width, width), width)

    @pl.when(col % 2 == 0)
    def _():
        pltpu.make_async_copy(panel_ref, panel.at[pl.ds(0, rows)], sem.at[0]).start()

    @pl.when(col % 2 == 1)
    def _():
        pltpu.make_async_copy(panel_new_ref, panel.at[pl.ds(0, rows)], sem.at[0]).start()

    top_copies = [
        pltpu.make_async_copy(ref.at[pl.ds(width, count), :], top.at[n], sem.at[1 + n])
        for n, ref in enumerate((square_ref, square_new_ref))
    ]
    for copy in top_copies:
        copy.start()

    def fetch(t, c):
        pltpu.make_async_copy(mat_ref.at[:, 0, tile(t)], block.at[pl.ds(0, rows), tile(t)], in_sem.at[0, t]).start()
        for n, (ref, base) in enumerate(parts):
            dest = pivot.at[pl.ds(n * half, half), tile(t)]
            pltpu.make_async_copy(ref.at[pl.ds(base, half), tile(t)], dest, in_sem.at[1, t]).start()
        for p in range(n_row):
            @pl.when(row == p)
            def _(p=p):
                for part, (ref, base) in enumerate(tops[p]):
                    dest = old.at[pl.ds(part * half, half), tile(t)]
                    pltpu.make_async_copy(ref.at[pl.ds(base, half), tile(t)], dest, in_sem.at[2, t]).start()
        return c

    lax.fori_loop(0, tiles, fetch, 0)
    if pivot.shape[0] > stacked:
        pivot[stacked:, :] = jnp.zeros((pivot.shape[0] - stacked, cols), jnp.float32)

    lanes = lax.broadcasted_iota(jnp.int32, (width, LANES), 1)
    places = jnp.concatenate(
        [jnp.where(lanes + t * LANES == wide_ref[...], 1.0, 0.0) for t in range(pivot.shape[0] // LANES)], axis=1
    )
    spread_inv = wide_left(pick_dot(thirds(linv_ref[...]), places))
    for copy in top_copies:
        copy.wait()
    top[0] = top[0] + top[1]
    pltpu.make_async_copy(panel_ref, panel.at[pl.ds(0, rows)], sem.at[0]).wait()
    put_rows(mine_ref, counts_ref[row], top.at[0], panel)
    lower[...] = wide_dot(wide_left(panel[:rows, :]), wide_right(uinv_ref[...]))
    left[...] = wide_left(lower[...])

    def step(t, c):
        first_col = (col == 0) & (t == 0)
        pltpu.make_async_copy(
            mat_ref.at[pl.ds(0, stacked), 0, tile(t)], pivot.at[pl.ds(0, stacked), tile(t)], in_sem.at[1, t]
        ).wait()
        upper = wide_dot(spread_inv, wide_right(pivot[:, tile(t)]))
        pltpu.make_async_copy(mat_ref.at[pl.ds(0, count), 0, tile(t)], old.at[:, tile(t)], in_sem.at[2, t]).wait()
        pltpu.make_async_copy(mat_ref.at[:, 0, tile(t)], block.at[pl.ds(0, rows), tile(t)], in_sem.at[0, t]).wait()

        @pl.when(jnp.logical_not(first_col))
        def _():
            put_rows(mine_ref, counts_ref[row], old.at[:, tile(t)], block.at[:, tile(t)])
            block[:rows, tile(t)] = block[:rows, tile(t)] - wide_dot(left[...], wide_right(upper))

        @pl.when(first_col)
        def _():
            block[:rows, tile(t)] = lower[...]

        @pl.when(row == 0)
        def _():
            block[:width, tile(t)] = jnp.where(first_col, packed_ref[...], upper)

        pltpu.make_async_copy(block.at[pl.ds(0, rows), tile(t)], out_ref.at[:, 0, tile(t)], out_sem.at[t]).start()
        return c

    lax.fori_loop(0, tiles, step, 0)

    def drain(t, c):
        pltpu.make_async_copy(block.at[pl.ds(0, rows), tile(t)], out_ref.at[:, 0, tile(t)], out_sem.at[t]).wait()
        return c

    lax.fori_loop(0, tiles, drain, 0)


def finish(mine, counts, wide, mat, panels, squares, factors, parcels):
    rows, _, cols = mat.shape
    width, n_row, count = factors[0].shape[0], counts.shape[0], mine.shape[0]
    return pl.pallas_call(
        functools.partial(finish_kernel, n_row),
        out_shape=jax.ShapeDtypeStruct(mat.shape, jnp.float32),
        in_specs=[smem(), smem(), vmem()] + [raw()] * 5 + [vmem()] * 3 + [raw()] * len(parcels),
        out_specs=raw(),
        scratch_shapes=[
            pltpu.VMEM((rows + SUB, cols), jnp.float32),
            pltpu.VMEM((-(-n_row * count // LANES) * LANES, cols), jnp.float32),
            pltpu.VMEM((rows + SUB, width), jnp.float32),
            pltpu.VMEM((count, cols), jnp.float32),
            pltpu.VMEM((rows, 3 * width), jnp.bfloat16),
            pltpu.VMEM((rows, width), jnp.float32),
            pltpu.VMEM((2, count, width), jnp.float32),
            pltpu.SemaphoreType.DMA((3,)),
            pltpu.SemaphoreType.DMA((3, cols // width)),
            pltpu.SemaphoreType.DMA((cols // width,)),
        ],
        cost_estimate=pl.CostEstimate(
            flops=6 * rows * cols * width, bytes_accessed=8 * rows * cols, transcendentals=0
        ),
        compiler_params=pltpu.CompilerParams(vmem_limit_bytes=26 << 20),
        name="finish",
    )(mine, counts, wide, mat, *panels, *squares, *factors, *parcels)


def capacity(n_row, width):
    mean = width / n_row
    return -(-int(mean + 4 * (mean * (1 - 1 / n_row)) ** 0.5) // (2 * SUB)) * (2 * SUB)


def locate(pivots, n_row, row, count):
    width = pivots.shape[0]
    owner = pivots // width % n_row
    slot = pivots // (width * n_row) * width + pivots % width
    number = jnp.arange(width, dtype=jnp.int32)
    ahead = (owner[:, None] == owner[None, :]) & (number[None, :] < number[:, None])
    rank = jnp.sum(ahead, axis=1, dtype=jnp.int32)
    every = jnp.arange(n_row, dtype=jnp.int32)[:, None]
    ordinal = jnp.arange(count, dtype=jnp.int32)[:, None]
    own = (owner[None, :] == row) & (rank[None, :] == ordinal)
    mine = jnp.sum(jnp.where(own, slot[None, :], 0), axis=1, dtype=jnp.int32)
    return mine, jnp.sum(owner[None, :] == every, axis=1, dtype=jnp.int32)


def capped_step(n_row, n_col, matrix, pivots, begun):
    _, rows, _, cols = matrix.shape
    mat = matrix.reshape(rows, 1, cols)
    panel, wide, _, *messages = begun
    count = messages[0].shape[0] // 2
    row, col = lax.axis_index("prow"), lax.axis_index("pcol")
    both = ("prow", "pcol")
    turns = bits_of(n_col)[:0:-1]

    def exchange(x, k):
        return lax.ppermute(x, both, [(i * n_col, (i ^ k) * n_col) for i in range(n_row)])

    moved = [exchange(messages[k], k) for k in range(1, n_row)]
    mine, counts = locate(pivots, n_row, row, count)
    parcels = parcel(mat, mine, pivots, n_row)

    def send(x, k):
        return lax.ppermute(x, "prow", [(i, i ^ k) for i in range(n_row)])

    *moved, kept = lax.optimization_barrier((*moved, parcels[-1]))
    parcels = parcels[:-1] + (kept,)
    message = pack(wide, messages[:1] + moved)
    panel_moved = lax.ppermute(panel, "pcol", [(i, i + turns[0]) for i in range(0, n_col, 2 * turns[0])])
    message, panel_moved = lax.optimization_barrier((message, panel_moved))
    if n_row == 4:
        first, second = send(parcels[0], 1), send(parcels[1], 2)
        kept = parcels[2]
        to_y, to_x = relay(kept, first, second)
        arrived = [kept, first, second]
    else:
        arrived = [parcels[0]] + [send(parcels[k], k) for k in range(1, n_row)]

    pairs = [[(i, i + bit) for i in range(0, n_col, 2 * bit)] for bit in turns + [1]]
    newer = [(col & bit) != 0 for bit in turns]
    last = len(turns) - 1
    for n in range(len(turns)):
        arrived_now = panel_moved
        if n == last:
            arrived_now = jnp.where(col == turns[n], back, panel_moved)
        source = panel_moved if last == 1 else None
        panel = jnp.where(newer[n], arrived_now, panel)
        if n + 1 == last:
            source = panel if source is None else source
            panel_moved = lax.ppermute(source, "pcol", pairs[n + 1][1:])
            back = lax.ppermute(source, "pcol", [(turns[n], turns[n + 1])])
        else:
            panel_moved = lax.ppermute(panel, "pcol", pairs[n + 1])
        message = jnp.where(newer[n], lax.ppermute(message, "pcol", pairs[n]), message)
        if n + 1 == last:
            message, panel_moved, back = lax.optimization_barrier((message, panel_moved, back))
        elif n < last:
            message, panel_moved = lax.optimization_barrier((message, panel_moved))
    if n_row == 4:
        arrived += [send(to_y, 2), send(to_x, 1)]
    message_new = lax.ppermute(message, "pcol", pairs[-1])
    factors = factor(message, message_new, True)
    out = finish(
        mine, counts, wide, pltpu.with_memory_space_constraint(mat, pltpu.HBM), (panel, panel_moved), (message, message_new), factors, arrived
    )
    return out.reshape(matrix.shape)


def on_device(n_row, n_col, matrix, pivots):
    _, rows, _, cols = matrix.shape
    begun = begin(matrix.reshape(rows, 1, cols), pivots, n_row, capacity(n_row, pivots.shape[0]))
    return lax.cond(
        begun[2][0] > 0,
        lambda m, p, b: capped_step(n_row, n_col, m, p, b),
        lambda m, p, b: dense_step(n_row, n_col, m, p),
        matrix, pivots, begun,
    )


def solution(mesh):
    spec = P("prow", None, "pcol", None)
    n_row, n_col = mesh.shape["prow"], mesh.shape["pcol"]
    return jax.shard_map(
        functools.partial(on_device, n_row, n_col), mesh=mesh, in_specs=(spec, P()), out_specs=spec, check_vma=False
    )
```

```python
import functools

import jax
import jax.numpy as jnp
from jax import lax
from jax.experimental import pallas as pl
from jax.experimental.pallas import tpu as pltpu
from jax.sharding import PartitionSpec as P

LANES = 128
SUB = 8
HI = lax.Precision.HIGHEST


def pick_lane(tile, lane):
    return jnp.take_along_axis(tile, jnp.full((SUB, LANES), lane, jnp.int32), axis=1)


def row_of(tile, j):
    return jnp.broadcast_to(tile[j:j + 1, :], (SUB, LANES))


def factor_kernel(width, unroll, first_ref, second_ref, packed_ref, linv_ref, uinv_ref, a_ref, m_ref, v_ref, s_ref, sem):
    groups = a_ref.shape[0]
    tiles = groups * SUB // LANES
    per_tile = LANES // SUB
    per_block = width // SUB
    copies = [
        pltpu.make_async_copy(ref.at[pl.ds(0, groups * SUB), :], s_ref.at[n], sem.at[n])
        for n, ref in enumerate((first_ref, second_ref))
    ]
    for copy in copies:
        copy.start()
    sub = lax.broadcasted_iota(jnp.int32, (SUB, LANES), 0)
    lane = lax.broadcasted_iota(jnp.int32, (SUB, LANES), 1)

    for i in range(groups):
        diag = lane - (i % per_tile) * SUB == sub
        for t in range(tiles):
            block = jnp.where(diag, 1.0, 0.0) if i // per_tile == t else jnp.zeros((SUB, LANES), jnp.float32)
            m_ref[i, :, t * LANES:(t + 1) * LANES] = block
            if t > i // per_tile:
                linv_ref[i * SUB:(i + 1) * SUB, t * LANES:(t + 1) * LANES] = block

    for copy in copies:
        copy.wait()
    for i in range(groups):
        a_ref[i] = s_ref[0, i * SUB:(i + 1) * SUB, :] + s_ref[1, i * SUB:(i + 1) * SUB, :]

    def span(t):
        return slice(t * LANES, (t + 1) * LANES)

    for o in range(groups // per_block):
        base = o * per_block
        h = base // per_tile
        live = [(a_ref, t) for t in range(h + 1, tiles)] + [(m_ref, t) for t in range(h + 1)]

        def panel(i, c, base=base, h=h, live=live):
            b = base + i
            g = (b - h * per_tile) * SUB
            rows = pl.ds(pl.multiple_of(b * SUB, SUB), SUB)
            own = a_ref[b, :, span(h)]
            cols = [pick_lane(own, g + j) for j in range(SUB)]
            in_panel = (lane >= g) & (lane < g + SUB)
            after = lane >= g + SUB
            head = jnp.where(in_panel, jnp.where(lane - g == sub, -1.0, 0.0), jnp.where(after, own, 0.0))
            rest = [ref[b, :, span(t)] for ref, t in live]
            packed = own
            final = [head] + rest
            for j in range(SUB):
                at = sub == j
                coef = cols[j]
                r = 1.0 / row_of(coef, j)
                final = [jnp.where(at, x, y) for x, y in zip([head] + rest, final)]
                packed = jnp.where((lane == g + j) & (sub > j), coef * r, packed)
                for k in range(j, SUB):
                    packed = jnp.where((lane == g + k) & at, cols[k], packed)
                head_coef = jnp.where((sub < j) | after, coef, 0.0)
                v = row_of(head, j) * r
                head = jnp.where(at, v, head - head_coef * v)
                for n, x in enumerate(rest):
                    v = row_of(x, j) * r
                    rest[n] = jnp.where(at, v, x - coef * v)
                for k in range(j + 1, SUB):
                    v = row_of(cols[k], j) * r
                    cols[k] = jnp.where(at, v, cols[k] - coef * v)
            for t in range(h):
                packed_ref[rows, span(t)] = a_ref[b, :, span(t)]
            packed_ref[rows, span(h)] = jnp.where(after, final[0], packed)
            for (ref, t), x in zip(live, final[1:]):
                (packed_ref if ref is a_ref else linv_ref)[rows, span(t)] = x
            a_ref[b, :, span(h)] = head
            v_ref[0] = head
            for n, ((ref, t), x) in enumerate(zip(live, rest)):
                ref[b, :, span(t)] = x
                v_ref[n + 1] = x
            others = [base + lax.rem(i + s, per_block) for s in range(1, per_block)]
            heads = [a_ref[r, :, span(h)] for r in others]
            facs = [[pick_lane(x, g + j) for j in range(SUB)] for x in heads]
            for n, (ref, t) in enumerate([(a_ref, h)] + live):
                old = [jnp.where(in_panel, 0.0, x) for x in heads] if n == 0 else [ref[r, :, span(t)] for r in others]
                vs = [row_of([head] + rest and ([head] + rest)[n], j) for j in range(SUB)]
                for x, fac, r in zip(old, facs, others):
                    acc = [fac[j] * vs[j] for j in range(SUB)]
                    while len(acc) > 1:
                        acc = [p + q for p, q in zip(acc[::2], acc[1::2])]
                    ref[r, :, span(t)] = x - acc[0]
            return c

        lax.fori_loop(0, per_block, panel, 0, unroll=unroll)

        lo = (base % per_tile) * SUB
        pad = [jnp.zeros((n, LANES), jnp.float32) for n in (lo, LANES - lo - width)]

        def stack(x):
            return jnp.concatenate([p for p in (pad[0], x, pad[1]) if p.shape[0]], axis=0)

        def flat(ref, first, last, t):
            return ref[first:last, :, span(t)].reshape((last - first) * SUB, LANES)

        end = base + per_block
        right = [stack(flat(ref, base, end, t)) for ref, t in [(a_ref, h)] + live]
        for first, last in ((end, groups), (0, base)):
            if first == last:
                continue
            left = flat(a_ref, first, last, h)
            column = lax.broadcasted_iota(jnp.int32, left.shape, 1)
            for n, (ref, t) in enumerate([(a_ref, h)] + live):
                if ref is m_ref and first == 0:
                    continue
                old = left if n else None
                old = jnp.where((column >= lo) & (column < lo + width), 0.0, left) if n == 0 else flat(ref, first, last, t)
                new = old - jnp.dot(left, right[n], precision=HI, preferred_element_type=jnp.float32)
                ref[first:last, :, span(t)] = new.reshape(last - first, SUB, LANES)

    ri = lax.broadcasted_iota(jnp.int32, (SUB, LANES), 0)
    for i in range(groups):
        for t in range(tiles):
            x = a_ref[i, :, span(t)]
            keep = lane + t * LANES >= ri + i * SUB
            uinv_ref[i * SUB:(i + 1) * SUB, span(t)] = jnp.where(keep, -x, 0.0)


def vmem():
    return pl.BlockSpec(memory_space=pltpu.VMEM)


def smem():
    return pl.BlockSpec(memory_space=pltpu.SMEM)


def factor(square, extra, unroll, width=32):
    size = square.shape[1]
    out = jax.ShapeDtypeStruct((size, size), jnp.float32)
    return pl.pallas_call(
        functools.partial(factor_kernel, width, unroll),
        out_shape=(out, out, out),
        in_specs=[raw(), raw()],
        out_specs=(vmem(),) * 3,
        scratch_shapes=[
            pltpu.VMEM((size // SUB, SUB, size), jnp.float32),
            pltpu.VMEM((size // SUB, SUB, size), jnp.float32),
            pltpu.VMEM((1 + size // LANES, SUB, LANES), jnp.float32),
            pltpu.VMEM((2, size, size), jnp.float32),
            pltpu.SemaphoreType.DMA((2,)),
        ],
        cost_estimate=pl.CostEstimate(flops=4 * size**3, bytes_accessed=50_000_000, transcendentals=0),
        compiler_params=pltpu.CompilerParams(vmem_limit_bytes=10 << 20),
        name="factor",
    )(square, extra)


def pick_kernel(slot_ref, own_ref, block_ref, out_ref):
    def group(q, c):
        for u in range(SUB):
            j = q * SUB + u
            row = block_ref[pl.ds(slot_ref[j], 1), :]
            out_ref[pl.ds(j, 1), :] = row * own_ref[j].astype(jnp.float32)
        return c

    lax.fori_loop(0, out_ref.shape[0] // SUB, group, 0)


def pick(block, slots, owned, tiles):
    rows, width = block.shape[0], slots.shape[0]
    return pl.pallas_call(
        pick_kernel,
        grid=(tiles,),
        out_shape=jax.ShapeDtypeStruct((width, tiles * width), jnp.float32),
        in_specs=[smem(), smem(), pl.BlockSpec((rows, width), lambda t: (0, t))],
        out_specs=pl.BlockSpec((width, width), lambda t: (0, t)),
        cost_estimate=pl.CostEstimate(
            flops=width * width * tiles, bytes_accessed=4 * (rows + width) * width * tiles, transcendentals=0
        ),
        name="pick",
    )(slots, owned, block)


def place_rows(slot_ref, rows_ref, target_ref):
    def group(q, c):
        for u in range(SUB):
            j = q * SUB + u
            target_ref[pl.ds(slot_ref[j], 1), :] = rows_ref[pl.ds(j, 1), :]
        return c

    lax.fori_loop(0, rows_ref.shape[0] // SUB, group, 0)


def place_kernel(slot_ref, block_ref, rows_ref, out_ref, buf_ref):
    rows = block_ref.shape[0]
    buf_ref[:rows, :] = block_ref[...]
    place_rows(slot_ref, rows_ref, buf_ref)
    out_ref[...] = buf_ref[:rows, :]


def place(block, rows, slots):
    height, width = block.shape[0], slots.shape[0]
    return pl.pallas_call(
        place_kernel,
        grid=(1,),
        out_shape=jax.ShapeDtypeStruct((height, width), jnp.float32),
        in_specs=[
            smem(),
            pl.BlockSpec((height, width), lambda t: (0, 0)),
            pl.BlockSpec((width, width), lambda t: (0, 0)),
        ],
        out_specs=pl.BlockSpec((height, width), lambda t: (0, 0)),
        scratch_shapes=[pltpu.VMEM((height + SUB, width), jnp.float32)],
        cost_estimate=pl.CostEstimate(flops=0, bytes_accessed=8 * height * width, transcendentals=0),
        name="place",
    )(slots, block, rows)


def halves(x):
    high = x.astype(jnp.bfloat16)
    low = (x - high.astype(jnp.float32)).astype(jnp.bfloat16)
    return high, low


def wide_left(x):
    high, low = halves(x)
    return jnp.concatenate([high, low, high], axis=1)


def wide_right(x):
    high, low = halves(x)
    return jnp.concatenate([low, high, high], axis=0)


def wide_dot(left, right):
    return jnp.dot(left, right, preferred_element_type=jnp.float32)


def split_dot(left, right):
    acc = jnp.dot(left[0], right[1], preferred_element_type=jnp.float32)
    acc += jnp.dot(left[1], right[0], preferred_element_type=jnp.float32)
    return acc + jnp.dot(left[0], right[0], preferred_element_type=jnp.float32)


def update_kernel(
    slot_ref, where_ref, block_ref, panel_ref, pivot_ref, top_ref, packed_ref, linv_ref, uinv_ref,
    out_ref, high_ref, low_ref, buf_ref,
):
    rows, width = panel_ref.shape
    t = pl.program_id(0)
    first_row = where_ref[0] == 0
    first_col = (where_ref[1] == 0) & (t == 0)

    @pl.when(t == 0)
    def _():
        lower = jnp.dot(panel_ref[...], uinv_ref[...], precision=HI, preferred_element_type=jnp.float32)
        high_ref[...], low_ref[...] = halves(lower)
        out_ref[...] = lower

    upper = jnp.dot(linv_ref[...], pivot_ref[...], precision=HI, preferred_element_type=jnp.float32)

    @pl.when(jnp.logical_not(first_col))
    def _():
        buf_ref[:rows, :] = block_ref[...]
        place_rows(slot_ref, top_ref, buf_ref)
        out_ref[...] = buf_ref[:rows, :] - split_dot((high_ref[...], low_ref[...]), halves(upper))

    @pl.when(first_row)
    def _():
        out_ref[:width, :] = jnp.where(first_col, packed_ref[...], upper)


def update(block, panel, pivot_rows, old_top, packed, linv, uinv, slots, where):
    rows, cols = block.shape
    width = slots.shape[0]
    square = pl.BlockSpec((width, width), lambda t: (0, 0))
    tall = pl.BlockSpec((rows, width), lambda t: (0, t))
    flat = pl.BlockSpec((width, width), lambda t: (0, t))
    return pl.pallas_call(
        update_kernel,
        grid=(cols // width,),
        out_shape=jax.ShapeDtypeStruct((rows, cols), jnp.float32),
        in_specs=[
            smem(), smem(), tall, pl.BlockSpec((rows, width), lambda t: (0, 0)), flat, flat, square, square, square,
        ],
        out_specs=tall,
        scratch_shapes=[
            pltpu.VMEM((rows, width), jnp.bfloat16),
            pltpu.VMEM((rows, width), jnp.bfloat16),
            pltpu.VMEM((rows + SUB, width), jnp.float32),
        ],
        cost_estimate=pl.CostEstimate(
            flops=6 * rows * cols * width, bytes_accessed=8 * rows * cols, transcendentals=0
        ),
        name="update",
    )(slots, where, block, panel, pivot_rows, old_top, packed, linv, uinv)


def bits_of(n):
    return [1 << i for i in range(n.bit_length() - 1)]


def sum_over_rows(x, order, n_row):
    for bit in order:
        x = x + lax.ppermute(x, "prow", [(i, i ^ bit) for i in range(n_row)])
    return x


def spread_rows(x, order, n_row):
    have = [0]
    for bit in order:
        x = x + lax.ppermute(x, "prow", [(i, i ^ bit) for i in have])
        have = have + [i ^ bit for i in have]
    return x


def spread_cols(x, order):
    have = [0]
    for bit in order:
        x = x + lax.ppermute(x, "pcol", [(i, i ^ bit) for i in have])
        have = have + [i ^ bit for i in have]
    return x


def dense_step(n_row, n_col, matrix, pivots):
    block = matrix[0, :, 0, :]
    rows, cols = block.shape
    width = pivots.shape[0]
    row = lax.axis_index("prow")
    col = lax.axis_index("pcol")
    owner = pivots // width % n_row
    slot = pivots // (width * n_row) * width + pivots % width
    mine = owner == row
    owned = mine.astype(jnp.int32)
    target = jnp.where(mine, slot, rows)
    where = jnp.stack([row, col]).astype(jnp.int32)
    row_bits, col_bits = bits_of(n_row), bits_of(n_col)
    at_first_row = row == 0
    at_first_col = col == 0

    square = pick(block, slot, owned * at_first_col.astype(jnp.int32), 1)
    square = sum_over_rows(square, row_bits, n_row)
    square = spread_cols(square, col_bits[::-1])
    packed, linv, uinv = factor(square, jnp.zeros_like(square), False)

    top = jnp.where(at_first_row, block[:width], 0.0)
    top_panel = spread_rows(top[:, :width], row_bits, n_row)
    panel = place(block, top_panel, target)
    panel = spread_cols(jnp.where(at_first_col, panel, 0.0), col_bits[::-1])

    picked = pick(block, slot, owned, cols // width)
    half = width // 2
    pivot_rows = jnp.concatenate([
        sum_over_rows(picked[:half], row_bits, n_row),
        sum_over_rows(picked[half:], row_bits[::-1], n_row),
    ])
    old_top = jnp.concatenate([
        spread_rows(top[:half], row_bits, n_row),
        spread_rows(top[half:], row_bits[::-1], n_row),
    ])
    result = update(block, panel, pivot_rows, old_top, packed, linv, uinv, target, where)
    return result[None, :, None, :]


def raw():
    return pl.BlockSpec(memory_space=pl.ANY)


def thirds(x):
    high = x.astype(jnp.bfloat16)
    rest = x - high.astype(jnp.float32)
    middle = rest.astype(jnp.bfloat16)
    return high, middle, (rest - middle.astype(jnp.float32)).astype(jnp.bfloat16)


def select_dot(choice, parts):
    choice = choice.astype(jnp.bfloat16)
    high, middle, low = [jnp.dot(choice, x, preferred_element_type=jnp.float32) for x in parts]
    return high + (middle + low)


def pick_dot(parts, choice):
    choice = choice.astype(jnp.bfloat16)
    high, middle, low = [jnp.dot(x, choice, preferred_element_type=jnp.float32) for x in parts]
    return high + (middle + low)


def begin_kernel(n_row, pivot_ref, mat_ref, panel_ref, wide_ref, fits_ref, *refs):
    messages, sem = refs[:n_row], refs[-1]
    rows, width = panel_ref.shape
    count = messages[0].shape[0] // 2
    width_log, row_log = width.bit_length() - 1, n_row.bit_length() - 1
    row = lax.axis_index("prow")
    copy = pltpu.make_async_copy(mat_ref.at[:, 0, pl.ds(0, width)], panel_ref, sem)
    copy.start()
    pivot = pivot_ref[...]
    block = lax.shift_right_logical(pivot, width_log)
    owner = block & (n_row - 1)
    slot = lax.shift_left(lax.shift_right_logical(block, row_log), width_log) + (pivot & (width - 1))
    _, rank = owners(pivot, n_row)
    fits_ref[0] = (jnp.max(rank) < count).astype(jnp.int32)
    place = ((owner ^ row) * count + rank).astype(jnp.float32)
    eye = lax.broadcasted_iota(jnp.int32, (width, width), 0) == lax.broadcasted_iota(jnp.int32, (width, width), 1)
    spread = jnp.where(eye, place, 0.0)
    wide = jnp.dot(spread, jnp.ones((width, LANES), jnp.float32), precision=HI, preferred_element_type=jnp.float32)
    wide_ref[...] = wide.astype(jnp.int32)
    ordinal = lax.broadcasted_iota(jnp.int32, (count, width), 0)
    mine = jnp.where((ordinal == rank) & (owner == row), 1.0, 0.0).astype(jnp.bfloat16)
    at_slot = jnp.where(lax.broadcasted_iota(jnp.int32, (rows, width), 0) == slot, 1.0, 0.0).astype(jnp.bfloat16)
    choice = lax.dot_general(mine, at_slot, (((1,), (1,)), ((), ())), preferred_element_type=jnp.float32)
    copy.wait()
    own = select_dot(choice, thirds(panel_ref[...]))
    for k in range(n_row):
        messages[k][:count, :] = own

    @pl.when(row == 0)
    def _():
        top = thirds(panel_ref[:width, :])
        for p in range(n_row):
            messages[p][count:, :] = select_dot(jnp.where((ordinal == rank) & (owner == p), 1.0, 0.0), top)


def begin(mat, pivots, n_row, count):
    rows, width = mat.shape[0], pivots.shape[0]
    message = jax.ShapeDtypeStruct((2 * count, width), jnp.float32)
    return pl.pallas_call(
        functools.partial(begin_kernel, n_row),
        out_shape=(
            jax.ShapeDtypeStruct((rows, width), jnp.float32),
            jax.ShapeDtypeStruct((width, LANES), jnp.int32),
            jax.ShapeDtypeStruct((1,), jnp.int32),
        ) + (message,) * n_row,
        in_specs=[vmem(), raw()],
        out_specs=(vmem(), vmem(), smem()) + (vmem(),) * n_row,
        scratch_shapes=[pltpu.SemaphoreType.DMA],
        cost_estimate=pl.CostEstimate(flops=0, bytes_accessed=10_000_000, transcendentals=0),
        compiler_params=pltpu.CompilerParams(vmem_limit_bytes=12 << 20),
        name="begin",
    )(pivots[None, :], mat)


def parcel_kernel(n_row, mine_ref, pivot_ref, mat_ref, *refs):
    outs, own, block, sem = refs[:-3], refs[-3], refs[-2], refs[-1]
    count, cols = own.shape
    half = count // 2
    width = pivot_ref.shape[1]

    def group(q, c):
        for u in range(SUB):
            i = q * SUB + u
            pltpu.make_async_copy(mat_ref.at[mine_ref[i]], own.at[pl.ds(i, 1), :], sem.at[0]).start()
        return c

    @pl.when(lax.axis_index("prow") == 0)
    def _():
        pltpu.make_async_copy(mat_ref.at[pl.ds(0, width), 0, :], block, sem.at[1]).start()

    lax.fori_loop(0, count // SUB, group, 0)

    @pl.when(lax.axis_index("prow") == 0)
    def _():
        copy = pltpu.make_async_copy(mat_ref.at[pl.ds(0, width), 0, :], block, sem.at[1])
        owner, rank = owners(pivot_ref[...], n_row)
        ordinal = lax.broadcasted_iota(jnp.int32, (count, width), 0)
        choices = [jnp.where((ordinal == rank) & (owner == p), 1.0, 0.0) for p in range(n_row)]
        choice = jnp.concatenate(choices, axis=0)
        copy.wait()

        def piece(t, c):
            at = pl.ds(pl.multiple_of(t * width, width), width)
            tops = select_dot(choice, thirds(block[:, at]))
            for p in range(n_row):
                for part in range(2):
                    first = p * count + part * half
                    for ref, base in top_places(n_row, half, outs, p, part):
                        ref[pl.ds(base, half), at] = tops[first:first + half]
            return c

        lax.fori_loop(0, cols // width, piece, 0, unroll=True)

    pltpu.make_async_copy(mat_ref.at[pl.ds(0, count), 0, :], own, sem.at[0]).wait()
    if n_row == 4:
        outs[0][:half, :] = own[:half, :]
        outs[1][:half, :] = own[half:, :]
        outs[2][:count, :] = own[...]
    else:
        outs[0][:count, :] = own[...]
        for p in range(1, n_row):
            outs[p][:count, :] = own[...]


def top_places(n_row, half, outs, p, part):
    if n_row != 4:
        return [(outs[p], 2 * half + part * half)]
    if p == 0:
        return [(outs[2], 2 * half + part * half)]
    if p == 3:
        return [(outs[part], 2 * half)]
    if part == p - 1:
        return [(outs[part], half)]
    return [(outs[2], (4 + part) * half)]


def owners(pivot, n_row):
    width = pivot.shape[1]
    owner = lax.shift_right_logical(pivot, width.bit_length() - 1) & (n_row - 1)
    held = lax.broadcasted_iota(jnp.int32, (-(-n_row // 16) * 16, width), 0) == owner
    before = lax.broadcasted_iota(jnp.int32, (width, width), 0) < lax.broadcasted_iota(jnp.int32, (width, width), 1)
    held = jnp.where(held, 1.0, 0.0)
    earlier = jnp.dot(
        held.astype(jnp.bfloat16), jnp.where(before, 1.0, 0.0).astype(jnp.bfloat16), preferred_element_type=jnp.float32
    )
    return owner, jnp.sum(held * earlier, axis=0, keepdims=True).astype(jnp.int32)


def parcel(mat, mine, pivots, n_row):
    count, width, cols = mine.shape[0], pivots.shape[0], mat.shape[2]
    half = count // 2
    sizes = [3 * half, 3 * half, 6 * half] if n_row == 4 else [2 * count] * n_row
    return pl.pallas_call(
        functools.partial(parcel_kernel, n_row),
        out_shape=tuple(jax.ShapeDtypeStruct((size, cols), jnp.float32) for size in sizes),
        in_specs=[smem(), vmem(), raw()],
        out_specs=(vmem(),) * len(sizes),
        scratch_shapes=[
            pltpu.VMEM((count, cols), jnp.float32),
            pltpu.VMEM((width, cols), jnp.float32),
            pltpu.SemaphoreType.DMA((2,)),
        ],
        cost_estimate=pl.CostEstimate(flops=0, bytes_accessed=16_000_000, transcendentals=0),
        compiler_params=pltpu.CompilerParams(vmem_limit_bytes=16 << 20),
        name="parcel",
    )(mine, pivots[None, :], mat)


def relay_kernel(kept_ref, first_ref, second_ref, y_ref, x_ref, sem):
    half = first_ref.shape[0] // 3
    row = lax.axis_index("prow")

    def move(source, base, dest, at, n):
        return pltpu.make_async_copy(source.at[pl.ds(base, half), :], dest.at[pl.ds(at, half), :], sem.at[n])

    copies = [
        move(kept_ref, 0, y_ref, 0, 0),
        move(kept_ref, half, x_ref, 0, 1),
        move(first_ref, 0, y_ref, half, 2),
        move(second_ref, 0, x_ref, half, 3),
    ]
    for copy in copies:
        copy.start()

    @pl.when(row == 0)
    def _():
        move(kept_ref, 4 * half, y_ref, 2 * half, 4).start()
        move(kept_ref, 5 * half, x_ref, 2 * half, 5).start()

    @pl.when(row != 0)
    def _():
        move(first_ref, 2 * half, y_ref, 2 * half, 4).start()
        move(second_ref, 2 * half, x_ref, 2 * half, 5).start()

    for copy in copies:
        copy.wait()
    move(first_ref, 2 * half, y_ref, 2 * half, 4).wait()
    move(second_ref, 2 * half, x_ref, 2 * half, 5).wait()


def relay(kept, first, second):
    shape = jax.ShapeDtypeStruct(first.shape, jnp.float32)
    return pl.pallas_call(
        relay_kernel,
        out_shape=(shape, shape),
        in_specs=[raw()] * 3,
        out_specs=(vmem(), vmem()),
        scratch_shapes=[pltpu.SemaphoreType.DMA((6,))],
        cost_estimate=pl.CostEstimate(flops=0, bytes_accessed=4_000_000, transcendentals=0),
        compiler_params=pltpu.CompilerParams(vmem_limit_bytes=4 << 20),
        name="relay",
    )(kept, first, second)


def pack_kernel(n_row, wide_ref, *refs):
    parts, out_ref, stack, sem = refs[:n_row], refs[n_row], refs[n_row + 1], refs[n_row + 2]
    width = wide_ref.shape[0]
    count = out_ref.shape[0] - width
    row, col = lax.axis_index("prow"), lax.axis_index("pcol")
    total = stack.shape[0]

    @pl.when(col == 0)
    def _():
        copies = [
            pltpu.make_async_copy(parts[k].at[pl.ds(0, count), :], stack.at[pl.ds(k * count, count), :], sem.at[k])
            for k in range(n_row)
        ]
        for copy in copies:
            copy.start()
        for k in range(n_row):
            @pl.when(row == k)
            def _(k=k):
                pltpu.make_async_copy(
                    parts[k].at[pl.ds(count, count), :], out_ref.at[pl.ds(width, count), :], sem.at[n_row]
                ).start()
        if total > n_row * count:
            stack[n_row * count:, :] = jnp.zeros((total - n_row * count, width), jnp.float32)
        lanes = lax.broadcasted_iota(jnp.int32, (width, LANES), 1)
        choice = jnp.concatenate(
            [jnp.where(lanes + t * LANES == wide_ref[...], 1.0, 0.0) for t in range(total // LANES)], axis=1
        )
        for copy in copies:
            copy.wait()
        out_ref[:width, :] = select_dot(choice, thirds(stack[...]))
        pltpu.make_async_copy(
            parts[0].at[pl.ds(count, count), :], out_ref.at[pl.ds(width, count), :], sem.at[n_row]
        ).wait()

    @pl.when(col != 0)
    def _():
        out_ref[...] = jnp.zeros_like(out_ref)


def pack(wide, parts):
    n_row, width = len(parts), wide.shape[0]
    count = parts[0].shape[0] // 2
    return pl.pallas_call(
        functools.partial(pack_kernel, n_row),
        out_shape=jax.ShapeDtypeStruct((width + count, width), jnp.float32),
        in_specs=[vmem()] + [raw()] * n_row,
        out_specs=vmem(),
        scratch_shapes=[
            pltpu.VMEM((-(-n_row * count // LANES) * LANES, width), jnp.float32),
            pltpu.SemaphoreType.DMA((n_row + 1,)),
        ],
        cost_estimate=pl.CostEstimate(flops=0, bytes_accessed=4_000_000, transcendentals=0),
        compiler_params=pltpu.CompilerParams(vmem_limit_bytes=6 << 20),
        name="pack",
    )(wide, *parts)


def unpack_parcels(n_row, count, parcels):
    half = count // 2
    if n_row != 4:
        parts = [(x, part * half) for x in parcels for part in range(2)]
        return parts, [[(x, count + part * half) for part in range(2)] for x in parcels]
    kept, first, second, third, fourth = parcels
    parts = [
        (kept, 0), (kept, half), (first, 0), (fourth, 0), (third, 0), (second, 0), (third, half), (fourth, half)
    ]
    tops = [
        [(kept, 2 * half), (kept, 3 * half)],
        [(first, half), (fourth, 2 * half)],
        [(third, 2 * half), (second, half)],
        [(third, 2 * half), (fourth, 2 * half)],
    ]
    return parts, tops


def put_rows(slot_ref, held, rows_ref, target_ref):
    spare = target_ref.shape[0] - SUB

    def group(q, c):
        for u in range(SUB):
            i = q * SUB + u
            slot = jnp.where(i < held, slot_ref[i], spare)
            target_ref[pl.ds(slot, 1), :] = rows_ref[pl.ds(i, 1), :]
        return c

    lax.fori_loop(0, (held + SUB - 1) // SUB, group, 0)


def finish_kernel(
    n_row, mine_ref, counts_ref, wide_ref, mat_ref, panel_ref, panel_new_ref, square_ref, square_new_ref,
    packed_ref, linv_ref, uinv_ref, *refs,
):
    n_parcels = 5 if n_row == 4 else n_row
    parcels, refs = refs[:n_parcels], refs[n_parcels:]
    out_ref, block, pivot, panel, old, left, lower, top, sem, in_sem, out_sem = refs
    rows, _, cols = mat_ref.shape
    width = linv_ref.shape[0]
    count = mine_ref.shape[0]
    half = count // 2
    stacked = n_row * count
    parts, tops = unpack_parcels(n_row, count, parcels)
    tiles = cols // width
    row, col = lax.axis_index("prow"), lax.axis_index("pcol")

    def tile(t):
        return pl.ds(pl.multiple_of(t * width, width), width)

    @pl.when(col % 2 == 0)
    def _():
        pltpu.make_async_copy(panel_ref, panel.at[pl.ds(0, rows)], sem.at[0]).start()

    @pl.when(col % 2 == 1)
    def _():
        pltpu.make_async_copy(panel_new_ref, panel.at[pl.ds(0, rows)], sem.at[0]).start()

    top_copies = [
        pltpu.make_async_copy(ref.at[pl.ds(width, count), :], top.at[n], sem.at[1 + n])
        for n, ref in enumerate((square_ref, square_new_ref))
    ]
    for copy in top_copies:
        copy.start()

    def fetch(t, c):
        pltpu.make_async_copy(mat_ref.at[:, 0, tile(t)], block.at[pl.ds(0, rows), tile(t)], in_sem.at[0, t]).start()
        for n, (ref, base) in enumerate(parts):
            dest = pivot.at[pl.ds(n * half, half), tile(t)]
            pltpu.make_async_copy(ref.at[pl.ds(base, half), tile(t)], dest, in_sem.at[1, t]).start()
        for p in range(n_row):
            @pl.when(row == p)
            def _(p=p):
                for part, (ref, base) in enumerate(tops[p]):
                    dest = old.at[pl.ds(part * half, half), tile(t)]
                    pltpu.make_async_copy(ref.at[pl.ds(base, half), tile(t)], dest, in_sem.at[2, t]).start()
        return c

    lax.fori_loop(0, tiles, fetch, 0)
    if pivot.shape[0] > stacked:
        pivot[stacked:, :] = jnp.zeros((pivot.shape[0] - stacked, cols), jnp.float32)

    lanes = lax.broadcasted_iota(jnp.int32, (width, LANES), 1)
    places = jnp.concatenate(
        [jnp.where(lanes + t * LANES == wide_ref[...], 1.0, 0.0) for t in range(pivot.shape[0] // LANES)], axis=1
    )
    spread_inv = wide_left(pick_dot(thirds(linv_ref[...]), places))
    for copy in top_copies:
        copy.wait()
    top[0] = top[0] + top[1]
    pltpu.make_async_copy(panel_ref, panel.at[pl.ds(0, rows)], sem.at[0]).wait()
    put_rows(mine_ref, counts_ref[row], top.at[0], panel)
    lower[...] = wide_dot(wide_left(panel[:rows, :]), wide_right(uinv_ref[...]))
    left[...] = wide_left(lower[...])

    def step(t, c):
        first_col = (col == 0) & (t == 0)
        pltpu.make_async_copy(
            mat_ref.at[pl.ds(0, stacked), 0, tile(t)], pivot.at[pl.ds(0, stacked), tile(t)], in_sem.at[1, t]
        ).wait()
        upper = wide_dot(spread_inv, wide_right(pivot[:, tile(t)]))
        pltpu.make_async_copy(mat_ref.at[pl.ds(0, count), 0, tile(t)], old.at[:, tile(t)], in_sem.at[2, t]).wait()
        pltpu.make_async_copy(mat_ref.at[:, 0, tile(t)], block.at[pl.ds(0, rows), tile(t)], in_sem.at[0, t]).wait()

        @pl.when(jnp.logical_not(first_col))
        def _():
            put_rows(mine_ref, counts_ref[row], old.at[:, tile(t)], block.at[:, tile(t)])
            block[:rows, tile(t)] = block[:rows, tile(t)] - wide_dot(left[...], wide_right(upper))

        @pl.when(first_col)
        def _():
            block[:rows, tile(t)] = lower[...]

        @pl.when(row == 0)
        def _():
            block[:width, tile(t)] = jnp.where(first_col, packed_ref[...], upper)

        pltpu.make_async_copy(block.at[pl.ds(0, rows), tile(t)], out_ref.at[:, 0, tile(t)], out_sem.at[t]).start()
        return c

    lax.fori_loop(0, tiles, step, 0)

    def drain(t, c):
        pltpu.make_async_copy(block.at[pl.ds(0, rows), tile(t)], out_ref.at[:, 0, tile(t)], out_sem.at[t]).wait()
        return c

    lax.fori_loop(0, tiles, drain, 0)


def finish(mine, counts, wide, mat, panels, squares, factors, parcels):
    rows, _, cols = mat.shape
    width, n_row, count = factors[0].shape[0], counts.shape[0], mine.shape[0]
    return pl.pallas_call(
        functools.partial(finish_kernel, n_row),
        out_shape=jax.ShapeDtypeStruct(mat.shape, jnp.float32),
        in_specs=[smem(), smem(), vmem()] + [raw()] * 5 + [vmem()] * 3 + [raw()] * len(parcels),
        out_specs=raw(),
        scratch_shapes=[
            pltpu.VMEM((rows + SUB, cols), jnp.float32),
            pltpu.VMEM((-(-n_row * count // LANES) * LANES, cols), jnp.float32),
            pltpu.VMEM((rows + SUB, width), jnp.float32),
            pltpu.VMEM((count, cols), jnp.float32),
            pltpu.VMEM((rows, 3 * width), jnp.bfloat16),
            pltpu.VMEM((rows, width), jnp.float32),
            pltpu.VMEM((2, count, width), jnp.float32),
            pltpu.SemaphoreType.DMA((3,)),
            pltpu.SemaphoreType.DMA((3, cols // width)),
            pltpu.SemaphoreType.DMA((cols // width,)),
        ],
        cost_estimate=pl.CostEstimate(
            flops=6 * rows * cols * width, bytes_accessed=8 * rows * cols, transcendentals=0
        ),
        compiler_params=pltpu.CompilerParams(vmem_limit_bytes=26 << 20),
        name="finish",
    )(mine, counts, wide, mat, *panels, *squares, *factors, *parcels)


def capacity(n_row, width):
    mean = width / n_row
    return -(-int(mean + 4 * (mean * (1 - 1 / n_row)) ** 0.5) // (2 * SUB)) * (2 * SUB)


def locate(pivots, n_row, row, count):
    width = pivots.shape[0]
    owner = pivots // width % n_row
    slot = pivots // (width * n_row) * width + pivots % width
    number = jnp.arange(width, dtype=jnp.int32)
    ahead = (owner[:, None] == owner[None, :]) & (number[None, :] < number[:, None])
    rank = jnp.sum(ahead, axis=1, dtype=jnp.int32)
    every = jnp.arange(n_row, dtype=jnp.int32)[:, None]
    ordinal = jnp.arange(count, dtype=jnp.int32)[:, None]
    own = (owner[None, :] == row) & (rank[None, :] == ordinal)
    mine = jnp.sum(jnp.where(own, slot[None, :], 0), axis=1, dtype=jnp.int32)
    return mine, jnp.sum(owner[None, :] == every, axis=1, dtype=jnp.int32)


def capped_step(n_row, n_col, matrix, pivots, begun):
    _, rows, _, cols = matrix.shape
    mat = matrix.reshape(rows, 1, cols)
    panel, wide, _, *messages = begun
    count = messages[0].shape[0] // 2
    row, col = lax.axis_index("prow"), lax.axis_index("pcol")
    both = ("prow", "pcol")
    turns = bits_of(n_col)[:0:-1]

    def exchange(x, k):
        return lax.ppermute(x, both, [(i * n_col, (i ^ k) * n_col) for i in range(n_row)])

    moved = [exchange(messages[k], k) for k in range(1, n_row)]
    mine, counts = locate(pivots, n_row, row, count)
    parcels = parcel(mat, mine, pivots, n_row)

    def send(x, k):
        return lax.ppermute(x, "prow", [(i, i ^ k) for i in range(n_row)])

    *moved, kept = lax.optimization_barrier((*moved, parcels[-1]))
    parcels = parcels[:-1] + (kept,)
    message = pack(wide, messages[:1] + moved)
    panel_moved = lax.ppermute(panel, "pcol", [(i, i + turns[0]) for i in range(0, n_col, 2 * turns[0])])
    message, panel_moved = lax.optimization_barrier((message, panel_moved))
    if n_row == 4:
        first, second = send(parcels[0], 1), send(parcels[1], 2)
        kept = parcels[2]
        to_y, to_x = relay(kept, first, second)
        arrived = [kept, first, second]
    else:
        arrived = [parcels[0]] + [send(parcels[k], k) for k in range(1, n_row)]

    pairs = [[(i, i + bit) for i in range(0, n_col, 2 * bit)] for bit in turns + [1]]
    newer = [(col & bit) != 0 for bit in turns]
    for n in range(len(turns)):
        panel = jnp.where(newer[n], panel_moved, panel)
        panel_moved = lax.ppermute(panel, "pcol", pairs[n + 1])
        message = jnp.where(newer[n], lax.ppermute(message, "pcol", pairs[n]), message)
        if n + 1 < len(turns):
            message, panel_moved = lax.optimization_barrier((message, panel_moved))
    if n_row == 4:
        arrived += [send(to_y, 2), send(to_x, 1)]
    message_new = lax.ppermute(message, "pcol", pairs[-1])
    factors = factor(message, message_new, True)
    out = finish(
        mine, counts, wide, mat, (panel, panel_moved), (message, message_new), factors, arrived
    )
    return out.reshape(matrix.shape)


def on_device(n_row, n_col, matrix, pivots):
    _, rows, _, cols = matrix.shape
    begun = begin(matrix.reshape(rows, 1, cols), pivots, n_row, capacity(n_row, pivots.shape[0]))
    return lax.cond(
        begun[2][0] > 0,
        lambda m, p, b: capped_step(n_row, n_col, m, p, b),
        lambda m, p, b: dense_step(n_row, n_col, m, p),
        matrix, pivots, begun,
    )


def solution(mesh):
    spec = P("prow", None, "pcol", None)
    n_row, n_col = mesh.shape["prow"], mesh.shape["pcol"]
    return jax.shard_map(
        functools.partial(on_device, n_row, n_col), mesh=mesh, in_specs=(spec, P()), out_specs=spec, check_vma=False
    )
```
